32 devices in a mesh: fsdp: 4 (over z), tensor: 8 (over y, x, core).
Axes of the slice: x: 2, y: 2, z: 4, core: 2. Of those that a mesh axis runs over, the one named last changes fastest.
Arguments:
- tokens: bfloat16 [5120, 2048], P(('fsdp', 'tensor')), may hold values from -6 to 6
- gain_attn: bfloat16 [2048], replicated, may hold values from 0.099609375 to 1.8984375
- gain_mlp: bfloat16 [2048], replicated, may hold values from 0.099609375 to 1.8984375
- w_query: bfloat16 [2048, 2048], P('fsdp', 'tensor'), may hold values from -0.125 to 0.125
- w_key: bfloat16 [2048, 2048], P('fsdp', 'tensor'), may hold values from -0.125 to 0.125
- w_value: bfloat16 [2048, 2048], P('fsdp', 'tensor'), may hold values from -0.125 to 0.125
- w_out: bfloat16 [2048, 2048], P('tensor', 'fsdp'), may hold values from -0.5 to 0.5
- w_gate: bfloat16 [2048, 8192], P('fsdp', 'tensor'), may hold values from -0.125 to 0.125
- w_up: bfloat16 [2048, 8192], P('fsdp', 'tensor'), may hold values from -0.125 to 0.125
- w_down: bfloat16 [8192, 2048], P('tensor', 'fsdp'), may hold values from -0.09375 to 0.09375
- segment_ids: int32 [4, 1280], P('fsdp'), may hold values from 0 to 3, never falling along the last dimension, each value on 1 to 512 neighbouring positions
- out_grad: bfloat16 [5120, 2048], P(('fsdp', 'tensor')), may hold values from -6 to 6
Outputs:
- output: bfloat16 [5120, 2048], P(('fsdp', 'tensor'))
- tokens_grad: bfloat16 [5120, 2048], P(('fsdp', 'tensor'))
- gain_attn_grad: float32 [2048], replicated
- gain_mlp_grad: float32 [2048], replicated
- w_query_grad: float32 [2048, 2048], P('fsdp', 'tensor')
- w_key_grad: float32 [2048, 2048], P('fsdp', 'tensor')
- w_value_grad: float32 [2048, 2048], P('fsdp', 'tensor')
- w_out_grad: float32 [2048, 2048], P('tensor', 'fsdp')
- w_gate_grad: float32 [2048, 8192], P('fsdp', 'tensor')
- w_up_grad: float32 [2048, 8192], P('fsdp', 'tensor')
- w_down_grad: float32 [8192, 2048], P('tensor', 'fsdp')
The draws below stay inside these ranges and needn't reach their ends.
Inputs may be any that keep to these rules, and one draw needn't show every extreme that they name: `segment_ids`: in each packed row the ids never fall; each sample has 1 to 512 tokens, and some sample in each row has exactly 512.
All inputs are finite; a program needn't handle non-finite values.
Results may differ from the reference program's by a relative error of at most 0.019.
Values may be sent and summed in bfloat16 or wider, within the bound.
A program may use at most 192 MiB of HBM per device.

```python
import math
import jax
import jax.numpy as jnp
import numpy as np
from jax import lax

D = 2048
HEADS = 32
HEAD = 64
FF = 8192
ROW_LEN = 1280
SEGS = 4
SEG_MAX = 512
TOKENS = 5120
ROWS = 4


def shard_levels(rng, extent, cuts, low, top_value):
    def one(axis_at, blocks):
        steps = jax.random.uniform(jax.random.fold_in(jax.random.fold_in(rng, 6), axis_at), (blocks,), jnp.float32, low / len(cuts), top_value / len(cuts))
        return jnp.repeat(jnp.exp(steps), extent[axis_at] // blocks).reshape((-1,) + (1,) * (len(extent) - axis_at - 1))

    loudness = one(*cuts[0])
    for cut in cuts[1:]:
        loudness = loudness * one(*cut)
    return loudness


def split_up(count, total, bound, slope):
    portions = [(1 << 20) // math.isqrt(grade ** slope) + 1 for grade in range(2, count + 1)]
    rest, given = total - bound - (count - 1), [1] * (count - 1)
    while rest > 0:
        free = [i for i in range(count - 1) if given[i] < bound]
        pool, remaining = sum([portions[i] for i in free]), rest
        for i in free:
            addition = min(bound - given[i], max(1, remaining * portions[i] // pool), rest)
            given[i] = given[i] + addition
            rest = rest - addition
    return np.array([bound] + given)


def uneven_parts(key, number_of, total, limit, skew):
    if number_of == 2:
        one = jax.random.randint(key, (), max(1, total - limit), min(limit, total - 1) + 1)
        return jnp.stack([one, total - one])
    sizes = jnp.asarray(split_up(number_of, total, limit, skew), jnp.int32)
    pairs = (number_of - 1) // 2
    source_of, receiver = sizes[1:1 + 2 * pairs:2], sizes[2:2 + 2 * pairs:2]
    room = jnp.minimum(source_of - 1, limit - receiver)
    shifted = jax.random.randint(jax.random.fold_in(key, 1), (pairs,), 0, 1 << 20) % (room + 1)
    sizes = sizes.at[1:1 + 2 * pairs:2].set(source_of - shifted).at[2:2 + 2 * pairs:2].set(receiver + shifted)
    return sizes[jax.random.permutation(jax.random.fold_in(key, 2), number_of)]


def normal_values(stream_key, extent, scale, most, pieces=(), held_as=jnp.bfloat16):
    values = jax.random.normal(stream_key, extent, jnp.float32) * scale
    if len(pieces) > 0:
        values = shard_levels(stream_key, extent, pieces, -0.22, 0.18) * values
    return jnp.clip(values, min=-most, max=most).astype(held_as)


def setup_inputs(seed: int = 0) -> dict:
    key_of = jax.random.split(jax.random.key(seed), 13)
    tokens = normal_values(key_of[0], (TOKENS, D), 1.0, 6.0, ((0, 32),))
    gain_attn = jnp.clip(1.0 + 0.18 * jax.random.normal(key_of[1], (D,), jnp.float32), 0.099609375, 1.8984375).astype(jnp.bfloat16)
    gain_mlp = jnp.clip(1.0 + 0.18 * jax.random.normal(key_of[2], (D,), jnp.float32), 0.099609375, 1.8984375).astype(jnp.bfloat16)
    w_query = normal_values(key_of[3], (D, D), D ** -0.5, 0.125, ((0, 4), (1, 8)))
    w_key = normal_values(key_of[4], (D, D), D ** -0.5, 0.125, ((0, 4), (1, 8)))
    w_value = normal_values(key_of[5], (D, D), D ** -0.5, 0.125, ((0, 4), (1, 8)))
    w_out = normal_values(key_of[6], (D, D), (D // 16) ** -0.5, 0.5, ((0, 8), (1, 4)))
    w_gate = normal_values(key_of[7], (D, FF), D ** -0.5, 0.125, ((0, 4), (1, 8)))
    w_up = normal_values(key_of[8], (D, FF), D ** -0.5, 0.125, ((0, 4), (1, 8)))
    w_down = normal_values(key_of[9], (FF, D), (FF // 2) ** -0.5, 0.09375, ((0, 8), (1, 4)))
    segment_ids = jax.vmap(lambda own: jnp.searchsorted(jnp.cumsum(uneven_parts(own, SEGS, ROW_LEN, SEG_MAX, 0)), jnp.arange(ROW_LEN), side="right"))(jax.random.split(key_of[10], ROWS)).reshape((ROWS, ROW_LEN)).astype(jnp.int32)
    out_grad = normal_values(key_of[11], (TOKENS, D), 1.0, 6.0, ((0, 32),))
    return {"tokens": tokens, "gain_attn": gain_attn, "gain_mlp": gain_mlp, "w_query": w_query, "w_key": w_key, "w_value": w_value, "w_out": w_out, "w_gate": w_gate, "w_up": w_up, "w_down": w_down, "segment_ids": segment_ids, "out_grad": out_grad}


@jax.custom_vjp
def low(v):
    return lax.optimization_barrier(v.astype(jnp.bfloat16)).astype(jnp.float32)

@jax.custom_vjp
def low_back(v):
    return v

def low_keep(v):
    return (low(v), None)

def low_pass(kept, grad):
    return (grad,)

def back_keep(v):
    return (v, None)

def back_low(kept, grad):
    return (low(grad),)
low.defvjp(low_keep, low_pass)
low_back.defvjp(back_keep, back_low)
eps = 1e-05
rope_base = 130000.0
highest = lax.Precision.HIGHEST

def matmul(left, right):
    return jnp.dot(left, right, precision=highest, preferred_element_type=jnp.float32)

def rms_norm(value, gain):
    scale = lax.rsqrt(lax.optimization_barrier(jnp.mean(value * value, axis=-1, keepdims=True)) + eps)
    return value * scale * gain

def rope_tables(segments):
    length = segments.shape[1]
    index = jnp.arange(length, dtype=jnp.int32)[None, :]
    change = jnp.concatenate([jnp.ones((segments.shape[0], 1), dtype=bool), segments[:, 1:] != segments[:, :-1]], axis=1)
    start = lax.cummax(jnp.where(change, index, 0), axis=1)
    position = (index - start).astype(jnp.float32)
    half = jnp.arange(HEAD // 2, dtype=jnp.float32)
    inverse = jnp.exp(half * (-2.0 / HEAD) * math.log(rope_base))
    angle = position[:, :, None, None] * inverse[None, None, None, :]
    return (jnp.cos(angle), jnp.sin(angle))

def rotate(value, cosine, sine):
    half = value.shape[-1] // 2
    first = value[..., :half]
    second = value[..., half:]
    return jnp.concatenate([first * cosine - second * sine, second * cosine + first * sine], axis=-1)

def attend(inputs):
    query, key, value, segments = inputs
    length = segments.shape[0]
    scores = jnp.einsum('qhd,khd->hqk', query, key, precision=highest) * HEAD ** (-0.5)
    scores = low_back(scores)
    index = jnp.arange(length, dtype=jnp.int32)
    allowed = (segments[:, None] == segments[None, :]) & (index[None, :] <= index[:, None])
    scores = jnp.where(allowed[None, :, :], scores, -1000000000.0)
    weights = jax.nn.softmax(scores, axis=-1)
    return jnp.einsum('hqk,khd->qhd', low(weights), value, precision=highest)

def layer(x, gain_a, gain_m, wq, wk, wv, wo, wg, wu, wd, segments):
    rows = segments.shape[0]
    length = segments.shape[1]
    cosine, sine = rope_tables(segments)
    normed_a = low(rms_norm(x, gain_a))

    def heads(value):
        return value.reshape(rows, length, HEADS, HEAD)
    query = low(rotate(heads(low_back(matmul(normed_a, wq))), cosine, sine))
    key = low(rotate(heads(low_back(matmul(normed_a, wk))), cosine, sine))
    value = heads(low(low_back(matmul(normed_a, wv))))
    attended = lax.map(jax.checkpoint(attend), (query, key, value, segments))
    attended = low(low_back(attended.reshape(rows * length, D)))
    hidden = x + low_back(matmul(attended, wo))
    normed_m = low(rms_norm(hidden, gain_m))
    gate = low_back(matmul(normed_m, wg))
    up = low_back(matmul(normed_m, wu))
    act = low(jax.nn.silu(gate) * up)
    return hidden + low_back(matmul(act, wd))

def reference(tokens, gain_attn, gain_mlp, w_query, w_key, w_value, w_out, w_gate, w_up, w_down, segment_ids, out_grad):
    floats = [a.astype(jnp.float32) for a in (tokens, gain_attn, gain_mlp, w_query, w_key, w_value, w_out, w_gate, w_up, w_down)]

    def forward(*values):
        return layer(*values, segment_ids)
    result, pullback = jax.vjp(forward, *floats)
    grads = pullback(out_grad.astype(jnp.float32))
    return (result.astype(jnp.bfloat16), grads[0].astype(jnp.bfloat16), grads[1], grads[2], grads[3], grads[4], grads[5], grads[6], grads[7], grads[8], grads[9])
```

```python
import functools
import math

import jax
import jax.numpy as jnp
from jax import lax
from jax.experimental import pallas as pl
from jax.experimental.pallas import tpu as pltpu
from jax.sharding import PartitionSpec as P

HEAD = 64
SAMPLE = 512
EPS = 1e-05
ROPE_BASE = 130000.0
MESH = pl.DeviceIdType.MESH
BF16 = jnp.bfloat16
F32 = jnp.float32
ANY = pl.BlockSpec(memory_space=pl.ANY)
VMEM = pl.BlockSpec(memory_space=pltpu.VMEM)


def flip(index, bit):
    return index + bit - 2 * bit * ((index // bit) % 2)


def dot_nt(left, right):
    return lax.dot_general(left, right, (((1,), (1,)), ((), ())), preferred_element_type=F32)


def dot_tn(left, right):
    return lax.dot_general(left, right, (((0,), (0,)), ((), ())), preferred_element_type=F32)


class Group:
    def __init__(self, z_size, t_size):
        self.z_size = z_size
        self.t_size = t_size
        self.size = 2 * t_size
        inner = []
        bit = 2
        while bit < t_size:
            inner.append(bit)
            bit *= 2
        self.core = 1
        self.pair = t_size
        self.orders = (tuple(inner) + (self.pair,), tuple(inner[::-1]) + (self.pair,))
        self.inner = (tuple(inner), tuple(inner[::-1]))
        self.bits = (self.core,) + tuple(inner) + (self.pair,)
        masks = [0]
        for b in self.orders[0]:
            masks = masks + [m + b for m in masks]
        self.masks = tuple(masks)

    def place(self):
        return lax.axis_index("fsdp"), lax.axis_index("tensor")

    def rank(self, mask=0):
        z, t = self.place()
        r = (z % 2) * self.t_size + t
        for b in self.bits:
            if mask & b:
                r = flip(r, b)
        return r

    def partner(self, bit):
        z, t = self.place()
        if bit == self.pair:
            return (flip(z, 1), t)
        return (z, flip(t, bit))

    def greet(self, bits=None):
        barrier = pltpu.get_barrier_semaphore()
        bits = self.bits if bits is None else bits
        for b in bits:
            pl.semaphore_signal(barrier, inc=1, device_id=self.partner(b), device_id_type=MESH)
        pl.semaphore_wait(barrier, len(bits))


def last_bit(mask, order):
    found = None
    for b in order:
        if mask & b:
            found = b
    return found


def gather_steps(grp, x_ref, o_ref, send, recv, local):
    rows = x_ref.shape[0]
    half = rows // 2

    def at(ref, mask, h):
        return ref.at[pl.ds(pl.multiple_of(grp.rank(mask) * rows + h * half, half), half)]

    own = pltpu.make_async_copy(x_ref, o_ref.at[pl.ds(pl.multiple_of(grp.rank() * rows, rows), rows)], local)
    own.start()
    full = [(grp.pair,) + grp.inner[h] + (grp.core,) for h in range(2)]
    sent = []

    def copy(h, mask, bit):
        src = x_ref.at[pl.ds(h * half, half)] if mask == 0 else at(o_ref, mask, h)
        k = mask | bit
        return pltpu.make_async_remote_copy(
            src_ref=src,
            dst_ref=at(o_ref, mask, h),
            send_sem=send.at[h, k],
            recv_sem=recv.at[h, k],
            device_id=grp.partner(bit),
            device_id_type=MESH,
        )

    def arrived(h, mask):
        bit = last_bit(mask, full[h])
        pltpu.make_async_remote_copy(
            src_ref=at(o_ref, mask, h),
            dst_ref=at(o_ref, mask, h),
            send_sem=send.at[h, mask],
            recv_sem=recv.at[h, mask],
            device_id=grp.partner(bit),
            device_id_type=MESH,
        ).wait_recv()

    def forward(h, mask):
        order = full[h]
        start = 0 if mask == 0 else order.index(last_bit(mask, order)) + 1
        for bit in order[start:]:
            c = copy(h, mask, bit)
            c.start()
            sent.append(c)

    for h in range(2):
        forward(h, 0)
    plain = sorted(
        (m for m in grp.masks if m), key=lambda m: (m & grp.pair, bin(m).count("1"))
    )
    for i, _ in enumerate(plain):
        for h in range(2):
            m = plain[i] if h == 0 else mirror(grp, plain[i])
            arrived(h, m)
            forward(h, m)
    for m in grp.masks:
        for h in range(2):
            arrived(h, m | grp.core)
    own.wait()
    for c in sent:
        c.wait_send()


def mirror(grp, mask):
    out = mask & (grp.pair | grp.core)
    a, b = grp.inner
    for p, q in zip(a, b):
        if mask & p:
            out |= q
    return out


def gather_kernel(grp, x_ref, o_ref, send, recv, local):
    grp.greet()
    gather_steps(grp, x_ref, o_ref, send, recv, local)


def gather(grp, x, cid, name):
    rows, width = x.shape
    return pl.pallas_call(
        functools.partial(gather_kernel, grp),
        out_shape=jax.ShapeDtypeStruct((rows * grp.size, width), x.dtype),
        in_specs=[ANY],
        out_specs=ANY,
        scratch_shapes=[
            pltpu.SemaphoreType.DMA((2, grp.size)),
            pltpu.SemaphoreType.DMA((2, grp.size)),
            pltpu.SemaphoreType.DMA,
        ],
        compiler_params=pltpu.CompilerParams(collective_id=cid, has_side_effects=True),
        name=name,
    )(x)


TILE = 16


def add_rows(dst, src, rows):
    @pl.loop(0, rows // TILE)
    def _(i):
        part = pl.ds(pl.multiple_of(i * TILE, TILE), TILE)
        dst[part] = (dst[part].astype(F32) + src[part].astype(F32)).astype(dst.dtype)


def scatter_scratch(grp, rows, width):
    n = len(grp.masks)
    return [
        pltpu.VMEM((n, rows, width), BF16),
        pltpu.VMEM((n, rows, width), BF16),
        pltpu.VMEM((2, n, rows // 2, width), BF16),
        pltpu.SemaphoreType.DMA((n,)),
        pltpu.SemaphoreType.DMA((n,)),
        pltpu.SemaphoreType.DMA((n,)),
        pltpu.SemaphoreType.DMA((2, n)),
        pltpu.SemaphoreType.DMA((2, n)),
    ]


def scatter_steps(grp, p_ref, acc, crecv, rbuf, local, csend, crecv_sem, send, recv):
    n, rows, _ = acc.shape
    half = rows // 2
    index = {m: i for i, m in enumerate(grp.masks)}
    order_masks = sorted(grp.masks, key=lambda m: (0 if m & grp.pair else 1, -bin(m).count("1")))

    def block(mask):
        return p_ref.at[pl.ds(pl.multiple_of(grp.rank(mask) * rows, rows), rows)]

    started = []
    loads = {}
    for m in order_masks:
        i = index[m]
        c = pltpu.make_async_remote_copy(
            src_ref=block(m | grp.core),
            dst_ref=crecv.at[i],
            send_sem=csend.at[i],
            recv_sem=crecv_sem.at[i],
            device_id=grp.partner(grp.core),
            device_id_type=MESH,
        )
        c.start()
        started.append(c)
        d = pltpu.make_async_copy(block(m), acc.at[i], local.at[i])
        d.start()
        loads[m] = (c, d)
    for m in order_masks:
        c, d = loads[m]
        d.wait()
        c.wait_recv()
        add_rows(acc.at[index[m]], crecv.at[index[m]], rows)

        def nothing():
            return None

    slots = []
    for h in range(2):
        s = {}
        order = grp.orders[h]
        for i in range(len(order)):
            later = order[i + 1 :]
            for m in grp.masks:
                if all((not m & b) or b in later for b in order):
                    s[(i, m)] = len(s)
        slots.append(s)

    def part(h, mask):
        return acc.at[index[mask], pl.ds(h * half, half)]

    def ship(h, i, mask):
        bit = grp.orders[h][i]
        k = slots[h][(i, mask - bit)]
        c = pltpu.make_async_remote_copy(
            src_ref=part(h, mask),
            dst_ref=rbuf.at[h, k],
            send_sem=send.at[h, k],
            recv_sem=recv.at[h, k],
            device_id=grp.partner(bit),
            device_id_type=MESH,
        )
        c.start()
        started.append(c)

    def take(h, i, mask):
        bit = grp.orders[h][i]
        k = slots[h][(i, mask)]
        pltpu.make_async_remote_copy(
            src_ref=part(h, mask),
            dst_ref=rbuf.at[h, k],
            send_sem=send.at[h, k],
            recv_sem=recv.at[h, k],
            device_id=grp.partner(bit),
            device_id_type=MESH,
        ).wait_recv()
        add_rows(part(h, mask), rbuf.at[h, k], half)

    last = len(grp.orders[0]) - 1
    for p in (grp.pair, 0):
        for i in range(last + 1):
            for h in range(2):
                order = grp.orders[h]
                later = order[i:]
                alive = [
                    m
                    for m in order_masks
                    if (m & grp.pair) == p and all((not m & b) or b in later for b in order)
                ]
                for m in alive:
                    if i > 0:
                        take(h, i - 1, m)
                    if m & order[i]:
                        ship(h, i, m)
    for h in range(2):
        take(h, last, 0)
    for c in started:
        c.wait_send()


def scatter_kernel(grp, rows, p_ref, o_ref, *scratch):
    grp.greet()
    scatter_steps(grp, p_ref, *scratch)
    o_ref[...] = scratch[0][0].astype(o_ref.dtype)


def scatter(grp, part, cid, name):
    rows, width = part.shape[0] // grp.size, part.shape[1]
    return pl.pallas_call(
        functools.partial(scatter_kernel, grp, rows),
        out_shape=jax.ShapeDtypeStruct((rows, width), F32),
        in_specs=[ANY],
        out_specs=VMEM,
        scratch_shapes=scatter_scratch(grp, rows, width),
        compiler_params=pltpu.CompilerParams(
            collective_id=cid, has_side_effects=True, vmem_limit_bytes=48 << 20
        ),
        name=name,
    )(part)


def sum_kernel(hops, x_ref, o_ref, buf, send, recv):
    z, t = lax.axis_index("fsdp"), lax.axis_index("tensor")

    def where(hop):
        axis, bit = hop
        return (flip(z, bit), t) if axis == "fsdp" else (z, flip(t, bit))

    barrier = pltpu.get_barrier_semaphore()
    for hop in hops:
        pl.semaphore_signal(barrier, inc=1, device_id=where(hop), device_id_type=MESH)
    pl.semaphore_wait(barrier, len(hops))
    buf[0] = x_ref[...]
    for i, hop in enumerate(hops):
        c = pltpu.make_async_remote_copy(
            src_ref=buf.at[2 * i],
            dst_ref=buf.at[2 * i + 1],
            send_sem=send.at[i],
            recv_sem=recv.at[i],
            device_id=where(hop),
            device_id_type=MESH,
        )
        c.start()
        c.wait()
        buf[2 * i + 2] = buf[2 * i] + buf[2 * i + 1]
    o_ref[...] = buf[2 * len(hops)]


def sum_all(z_size, t_size, x, cid):
    hops = []
    for axis, size in (("tensor", t_size), ("fsdp", z_size)):
        bit = 1
        while bit < size:
            hops.append((axis, bit))
            bit *= 2
    n = len(hops)
    return pl.pallas_call(
        functools.partial(sum_kernel, hops),
        out_shape=jax.ShapeDtypeStruct(x.shape, x.dtype),
        in_specs=[VMEM],
        out_specs=VMEM,
        scratch_shapes=[
            pltpu.VMEM((2 * n + 1,) + x.shape, x.dtype),
            pltpu.SemaphoreType.DMA((n,)),
            pltpu.SemaphoreType.DMA((n,)),
        ],
        compiler_params=pltpu.CompilerParams(collective_id=cid, has_side_effects=True),
        name="sum_all",
    )(x)


def swap_halves(value):
    half = HEAD // 2
    width = value.shape[1]
    pieces = []
    for at in range(0, width, HEAD):
        pieces.append(value[:, at + half : at + HEAD])
        pieces.append(value[:, at : at + half])
    if width % 128:
        return jnp.concatenate(pieces, axis=1)
    lane = lax.broadcasted_iota(jnp.int32, value.shape, 1)
    return jnp.where(
        lane % HEAD < half, pltpu.roll(value, width - half, 1), pltpu.roll(value, half, 1)
    )


QB = 256


def bands(length):
    for at in range(0, length, QB):
        first = max(0, at - SAMPLE)
        yield at, min(QB, length - at), first, at + min(QB, length - at) - first


def kept(start_row, at, size, first, width):
    key = first + lax.broadcasted_iota(jnp.int32, (width, size), 0)
    query = at + lax.broadcasted_iota(jnp.int32, (width, size), 1)
    return (key >= start_row) & (key <= query)


def attend_kernel(heads, qkv_ref, cos_ref, sin_ref, start_ref, q_ref, k_ref, v_ref, o_ref, lse_ref):
    wide = heads * HEAD
    length = qkv_ref.shape[0]

    @pl.loop(0, length // QB)
    def _(i):
        rows = pl.ds(pl.multiple_of(i * QB, QB), QB)
        cosine, sine = cos_ref[rows], sin_ref[rows]
        query, key = qkv_ref[rows, :wide], qkv_ref[rows, wide : 2 * wide]
        query = (query * cosine + swap_halves(query) * sine).astype(BF16)
        q_ref[rows] = query
        k_ref[rows] = (key * cosine + swap_halves(key) * sine).astype(BF16)
        v_ref[rows] = qkv_ref[rows, 2 * wide :].astype(BF16)

    for h in range(heads):
        lanes = slice(h * HEAD, (h + 1) * HEAD)
        for at, size, first, width in bands(length):
            query = q_ref[at : at + size, lanes] * BF16(HEAD**-0.5)
            key = k_ref[first : first + width, lanes]
            scores = dot_nt(key, query)
            mask = kept(start_ref[0, :, at : at + size], at, size, first, width)
            scores = jnp.where(mask, scores, -1e9)
            top = jnp.max(scores, axis=0, keepdims=True)
            expo = jnp.exp(scores - top)
            total = jnp.sum(expo, axis=0, keepdims=True)
            weights = (expo * (1.0 / total)).astype(BF16)
            o_ref[at : at + size, lanes] = dot_tn(
                weights, v_ref[first : first + width, lanes]
            ).astype(BF16)
            lse_ref[0, h : h + 1, at : at + size] = top + jnp.log(total)


def attend(qkv, cosine, sine, start, heads):
    rows, _, length = start.shape
    wide = heads * HEAD

    def tall(width):
        return pl.BlockSpec((length, width), lambda r: (r, 0))

    out = jax.ShapeDtypeStruct((rows * length, wide), BF16)
    return pl.pallas_call(
        functools.partial(attend_kernel, heads),
        grid=(rows,),
        out_shape=[out, out, out, out, jax.ShapeDtypeStruct((rows, heads, length), F32)],
        in_specs=[tall(3 * wide), tall(wide), tall(wide), pl.BlockSpec((1, 1, length), lambda r: (r, 0, 0))],
        out_specs=[tall(wide)] * 4 + [pl.BlockSpec((1, heads, length), lambda r: (r, 0, 0))],
        compiler_params=pltpu.CompilerParams(vmem_limit_bytes=48 << 20),
        name="attend",
    )(qkv, cosine, sine, start)


def attend_back_kernel(
    heads, q_ref, k_ref, v_ref, do_ref, lse_ref, cos_ref, sin_ref, start_ref, out_ref, dq, dk, dv
):
    wide = heads * HEAD
    length = q_ref.shape[0]
    dk[...] = jnp.zeros_like(dk)
    dv[...] = jnp.zeros_like(dv)
    for h in range(heads):
        lanes = slice(h * HEAD, (h + 1) * HEAD)
        for at, size, first, width in bands(length):
            query = q_ref[at : at + size, lanes]
            key = k_ref[first : first + width, lanes]
            value = v_ref[first : first + width, lanes]
            grad = do_ref[at : at + size, lanes]
            scores = dot_nt(key, query * BF16(HEAD**-0.5))
            mask = kept(start_ref[0, :, at : at + size], at, size, first, width)
            weights = jnp.where(
                mask, jnp.exp(jnp.where(mask, scores, -1e9) - lse_ref[0, h : h + 1, at : at + size]), 0.0
            )
            dv[first : first + width, lanes] += jnp.dot(
                weights.astype(BF16), grad, preferred_element_type=F32
            )
            grad_weights = dot_nt(value, grad)
            inner = jnp.sum(weights * grad_weights, axis=0, keepdims=True)
            grad_scores = (weights * (grad_weights - inner)).astype(BF16)
            dq[at : at + size, lanes] = dot_tn(grad_scores, key)
            dk[first : first + width, lanes] += jnp.dot(
                grad_scores, query, preferred_element_type=F32
            )

    @pl.loop(0, length // QB)
    def _(i):
        rows = pl.ds(pl.multiple_of(i * QB, QB), QB)
        cosine, sine = cos_ref[rows], sin_ref[rows]
        query, key = dq[rows] * HEAD**-0.5, dk[rows] * HEAD**-0.5
        out_ref[rows, :wide] = (query * cosine - swap_halves(query) * sine).astype(BF16)
        out_ref[rows, wide : 2 * wide] = (key * cosine - swap_halves(key) * sine).astype(BF16)
        out_ref[rows, 2 * wide :] = dv[rows].astype(BF16)


def attend_back(query, key, value, grad, lse, cosine, sine, start, heads):
    rows, _, length = start.shape
    wide = heads * HEAD

    def tall(width):
        return pl.BlockSpec((length, width), lambda r: (r, 0))

    return pl.pallas_call(
        functools.partial(attend_back_kernel, heads),
        grid=(rows,),
        out_shape=jax.ShapeDtypeStruct((rows * length, 3 * wide), BF16),
        in_specs=[tall(wide)] * 4
        + [pl.BlockSpec((1, heads, length), lambda r: (r, 0, 0)), tall(wide), tall(wide)]
        + [pl.BlockSpec((1, 1, length), lambda r: (r, 0, 0))],
        out_specs=tall(3 * wide),
        scratch_shapes=[pltpu.VMEM((length, wide), F32)] * 3,
        compiler_params=pltpu.CompilerParams(vmem_limit_bytes=48 << 20),
        name="attend_back",
    )(query, key, value, grad, lse, cosine, sine, start)


def norm_forward(value, gain):
    scale = lax.rsqrt(jnp.mean(value * value, axis=-1, keepdims=True) + EPS)
    return (value * scale * gain, scale)


def norm_backward(value, scale, gain, grad):
    scaled_grad = grad * gain
    inner = jnp.mean(value * scaled_grad, axis=-1, keepdims=True)
    back = scale * scaled_grad - value * scale * scale * scale * inner
    return (back, jnp.sum(grad * value * scale, axis=0))


def shards(
    z_size,
    t_size,
    tokens,
    gain_attn,
    gain_mlp,
    w_query,
    w_key,
    w_value,
    w_out,
    w_gate,
    w_up,
    w_down,
    segment_ids,
    out_grad,
):
    grp = Group(z_size, t_size)
    z = lax.axis_index("fsdp")
    low = z % 2

    def hop(value, mask):
        return lax.ppermute(value, "fsdp", [(i, i ^ mask) for i in range(z_size)])

    def half_of(value, which, axis):
        size = value.shape[axis] // 2
        return lax.dynamic_slice_in_dim(value, which * size, size, axis)

    def collect(sharded, half_axis, axis):
        mine = [half_of(w, low, half_axis) for w in sharded]
        other = [half_of(w, 1 - low, half_axis) for w in sharded]
        mine = mine[0] if len(mine) == 1 else jnp.concatenate(mine, axis=half_axis)
        other = other[0] if len(other) == 1 else jnp.concatenate(other, axis=half_axis)
        size = mine.shape[axis]
        shape = list(mine.shape)
        shape[axis] = size * z_size
        whole = jnp.zeros(shape, mine.dtype)
        for m in range(z_size):
            got = mine if m == 0 else hop(other if m % 2 else mine, m)
            whole = lax.dynamic_update_slice_in_dim(whole, got, (z ^ m) * size, axis)
        return whole

    def deliver(grad, half_axis, axis, parts):
        size = grad.shape[axis] // z_size
        sums = [None, None]
        for m in range(z_size):
            block = lax.dynamic_slice_in_dim(grad, (z ^ m) * size, size, axis)
            got = (block if m == 0 else hop(block, m)).astype(F32)
            sums[m % 2] = got if sums[m % 2] is None else sums[m % 2] + got
        outs = []
        piece = sums[0].shape[half_axis] // parts
        for i in range(parts):
            a, b = (lax.slice_in_dim(s, i * piece, (i + 1) * piece, axis=half_axis) for s in sums)
            outs.append(
                jnp.where(
                    low == 0,
                    jnp.concatenate([a, b], axis=half_axis),
                    jnp.concatenate([b, a], axis=half_axis),
                )
            )
        return outs

    wqkv = collect((w_query, w_key, w_value), 1, 0)
    wo = collect((w_out,), 0, 1)
    wgu = collect((w_gate, w_up), 1, 0)
    wd = collect((w_down,), 0, 1)
    wide = wqkv.shape[1] // 3
    heads = wide // HEAD
    units = wd.shape[0]

    other_ids = hop(segment_ids, 1)
    segments = jnp.where(
        low == 0,
        jnp.concatenate([segment_ids, other_ids], axis=0),
        jnp.concatenate([other_ids, segment_ids], axis=0),
    )
    rows, length = segments.shape
    start = jnp.sum(segments[:, :, None] > segments[:, None, :], axis=2, dtype=jnp.int32)
    position = (jnp.arange(length, dtype=jnp.int32)[None, :] - start).astype(F32)
    lane = jnp.arange(wide, dtype=jnp.int32)
    half = (lane % (HEAD // 2)).astype(F32)
    inverse = jnp.exp(half * (-2.0 / HEAD) * math.log(ROPE_BASE))
    angle = position.reshape(rows * length, 1) * inverse[None, :]
    cosine = jnp.cos(angle)
    sine = jnp.where(lane[None, :] % HEAD < HEAD // 2, -1.0, 1.0) * jnp.sin(angle)
    start = start.reshape(rows, 1, length)

    gain_a = gain_attn.astype(F32)
    gain_m = gain_mlp.astype(F32)
    x = tokens.astype(F32)
    normed_local, scale_a = norm_forward(x, gain_a)
    normed_a = gather(grp, normed_local.astype(BF16), 0, "gather_normed_a")
    grad_all = gather(grp, out_grad, 1, "gather_out_grad")
    qkv = jnp.dot(normed_a, wqkv, preferred_element_type=F32)
    query, key, value, attended, lse = attend(qkv, cosine, sine, start, heads)
    branch = jnp.dot(attended, wo, preferred_element_type=F32).astype(BF16)
    hidden = x + scatter(grp, branch, 2, "scatter_attn")
    normed_hidden, scale_m = norm_forward(hidden, gain_m)
    normed_m = gather(grp, normed_hidden.astype(BF16), 3, "gather_normed_m")
    gate_up = jnp.dot(normed_m, wgu, preferred_element_type=F32)
    gate, up = gate_up[:, :units], gate_up[:, units:]
    sigma = jax.nn.sigmoid(gate)
    silu_gate = gate * sigma
    act = (silu_gate * up).astype(BF16)
    grad_down = dot_tn(act, grad_all).astype(BF16)
    grad_act = dot_nt(grad_all, wd)
    grad_gate = (grad_act * up * (sigma * (1.0 + gate * (1.0 - sigma)))).astype(BF16)
    grad_up = (grad_act * silu_gate).astype(BF16)
    grad_gu = jnp.concatenate([grad_gate, grad_up], axis=1)
    grad_wgu = dot_tn(normed_m, grad_gu).astype(BF16)
    grad_nm = scatter(grp, dot_nt(grad_gu, wgu).astype(BF16), 4, "scatter_nm")
    back_m, gain_m_part = norm_backward(hidden, scale_m, gain_m, grad_nm)
    grad_hidden = out_grad.astype(F32) + back_m
    branch_all = gather(grp, grad_hidden.astype(BF16), 5, "gather_branch")
    out_part = jnp.dot(act, wd, preferred_element_type=F32).astype(BF16)
    output = hidden + scatter(grp, out_part, 6, "scatter_out")
    grad_wout = dot_tn(attended, branch_all).astype(BF16)
    grad_attended = dot_nt(branch_all, wo).astype(BF16)
    grad_qkv = attend_back(query, key, value, grad_attended, lse, cosine, sine, start, heads)
    grad_wqkv = dot_tn(normed_a, grad_qkv).astype(BF16)
    grad_na = scatter(grp, dot_nt(grad_qkv, wqkv).astype(BF16), 7, "scatter_na")
    back_a, gain_a_part = norm_backward(x, scale_a, gain_a, grad_na)
    tokens_grad = (grad_hidden + back_a).astype(BF16)
    gains = sum_all(z_size, t_size, jnp.stack([gain_a_part, gain_m_part]), 8)
    (down_out,) = deliver(grad_down, 0, 1, 1)
    gate_out, up_out = deliver(grad_wgu, 1, 0, 2)
    (out_out,) = deliver(grad_wout, 0, 1, 1)
    query_out, key_out, value_out = deliver(grad_wqkv, 1, 0, 3)
    return (
        output.astype(BF16),
        tokens_grad,
        gains[0],
        gains[1],
        query_out,
        key_out,
        value_out,
        out_out,
        gate_out,
        up_out,
        down_out,
    )


def solution(mesh):
    return jax.shard_map(
        functools.partial(shards, mesh.shape["fsdp"], mesh.shape["tensor"]),
        mesh=mesh,
        in_specs=(
            P(("fsdp", "tensor"), None),
            P(),
            P(),
            P("fsdp", "tensor"),
            P("fsdp", "tensor"),
            P("fsdp", "tensor"),
            P("tensor", "fsdp"),
            P("fsdp", "tensor"),
            P("fsdp", "tensor"),
            P("tensor", "fsdp"),
            P("fsdp", None),
            P(("fsdp", "tensor"), None),
        ),
        out_specs=(
            P(("fsdp", "tensor"), None),
            P(("fsdp", "tensor"), None),
            P(),
            P(),
            P("fsdp", "tensor"),
            P("fsdp", "tensor"),
            P("fsdp", "tensor"),
            P("tensor", "fsdp"),
            P("fsdp", "tensor"),
            P("fsdp", "tensor"),
            P("tensor", "fsdp"),
        ),
        check_vma=False,
    )
```

```python
import functools
import math

import jax
import jax.numpy as jnp
from jax import lax
from jax.experimental import pallas as pl
from jax.experimental.pallas import tpu as pltpu
from jax.sharding import PartitionSpec as P

HEAD = 64
SAMPLE = 512
EPS = 1e-05
ROPE_BASE = 130000.0
MESH = pl.DeviceIdType.MESH
BF16 = jnp.bfloat16
F32 = jnp.float32
ANY = pl.BlockSpec(memory_space=pl.ANY)
VMEM = pl.BlockSpec(memory_space=pltpu.VMEM)


def flip(index, bit):
    return index + bit - 2 * bit * ((index // bit) % 2)


def dot_nt(left, right):
    return lax.dot_general(left, right, (((1,), (1,)), ((), ())), preferred_element_type=F32)


def dot_tn(left, right):
    return lax.dot_general(left, right, (((0,), (0,)), ((), ())), preferred_element_type=F32)


class Group:
    def __init__(self, z_size, t_size):
        self.z_size = z_size
        self.t_size = t_size
        self.size = 2 * t_size
        inner = []
        bit = 2
        while bit < t_size:
            inner.append(bit)
            bit *= 2
        self.core = 1
        self.pair = t_size
        self.orders = (tuple(inner) + (self.pair,), tuple(inner[::-1]) + (self.pair,))
        self.inner = (tuple(inner), tuple(inner[::-1]))
        self.bits = (self.core,) + tuple(inner) + (self.pair,)
        masks = [0]
        for b in self.orders[0]:
            masks = masks + [m + b for m in masks]
        self.masks = tuple(masks)
        self.far = tuple(range(2, z_size))

    def place(self):
        return lax.axis_index("fsdp"), lax.axis_index("tensor")

    def rank(self, mask=0):
        z, t = self.place()
        r = (z % 2) * self.t_size + t
        for b in self.bits:
            if mask & b:
                r = flip(r, b)
        return r

    def partner(self, bit):
        z, t = self.place()
        if bit == self.pair:
            return (flip(z, 1), t)
        return (z, flip(t, bit))

    def across(self, mask):
        z, t = self.place()
        bit = 1
        while bit < self.z_size:
            if mask & bit:
                z = flip(z, bit)
            bit *= 2
        return (z, t)

    def greet(self):
        barrier = pltpu.get_barrier_semaphore()
        peers = [self.partner(b) for b in self.bits if b != self.pair]
        peers += [self.across(m) for m in range(1, self.z_size)]
        for peer in peers:
            pl.semaphore_signal(barrier, inc=1, device_id=peer, device_id_type=MESH)
        pl.semaphore_wait(barrier, len(peers))


def last_bit(mask, order):
    found = None
    for b in order:
        if mask & b:
            found = b
    return found


class Gather:
    def __init__(self, grp, x_ref, o_ref, send, recv, local):
        self.grp, self.x, self.o = grp, x_ref, o_ref
        self.send, self.recv = send, recv
        self.rows = x_ref.shape[0]
        self.half = self.rows // 2
        self.order = [(grp.pair,) + grp.inner[h] + (grp.core,) for h in range(2)]
        self.sent = []
        own = pl.ds(pl.multiple_of(grp.rank() * self.rows, self.rows), self.rows)
        self.own = pltpu.make_async_copy(x_ref, o_ref.at[own], local)

    def at(self, mask, h):
        first = self.grp.rank(mask) * self.rows + h * self.half
        return self.o.at[pl.ds(pl.multiple_of(first, self.half), self.half)]

    def copy(self, src, mask, h, key, bit):
        return pltpu.make_async_remote_copy(
            src_ref=src,
            dst_ref=self.at(mask, h),
            send_sem=self.send.at[h, key],
            recv_sem=self.recv.at[h, key],
            device_id=self.grp.partner(bit),
            device_id_type=MESH,
        )

    def forward(self, h, mask, bits=None):
        order = self.order[h]
        start = 0 if mask == 0 else order.index(last_bit(mask, order)) + 1
        for bit in order[start:] if bits is None else bits:
            src = self.x.at[pl.ds(h * self.half, self.half)] if mask == 0 else self.at(mask, h)
            c = self.copy(src, mask, h, mask | bit, bit)
            c.start()
            self.sent.append(c)

    def arrived(self, h, mask):
        bit = last_bit(mask, self.order[h])
        self.copy(self.at(mask, h), mask, h, mask, bit).wait_recv()

    def begin(self):
        self.own.start()
        for h in range(2):
            self.forward(h, 0, (self.grp.pair,))
        for h in range(2):
            self.forward(h, 0, self.order[h][1:])
        grp = self.grp
        plain = sorted(
            (m for m in grp.masks if m), key=lambda m: (m & grp.pair, bin(m).count("1"))
        )
        if len(plain) > 3:
            plain.remove(grp.pair)
            plain.insert(2, grp.pair)

        def step(h, m):
            self.arrived(h, m)
            self.forward(h, m)

        return [
            functools.partial(step, h, m if h == 0 else mirror(grp, m))
            for m in plain
            for h in range(2)
        ]

    def finish(self):
        for m in self.grp.masks:
            for h in range(2):
                self.arrived(h, m | self.grp.core)
        self.own.wait()
        for c in self.sent:
            c.wait_send()


def mirror(grp, mask):
    out = mask & (grp.pair | grp.core)
    a, b = grp.inner
    for p, q in zip(a, b):
        if mask & p:
            out |= q
    return out


TILE = 16


def add_rows(dst, src, rows):
    @pl.loop(0, rows // TILE)
    def _(i):
        part = pl.ds(pl.multiple_of(i * TILE, TILE), TILE)
        dst[part] = (dst[part].astype(F32) + src[part].astype(F32)).astype(dst.dtype)


def scatter_scratch(grp, rows, width):
    n = len(grp.masks)
    return [
        pltpu.VMEM((n, rows, width), BF16),
        pltpu.VMEM((2, n - 1, rows // 2, width), BF16),
        pltpu.SemaphoreType.DMA((n,)),
        pltpu.SemaphoreType.DMA((n,)),
        pltpu.SemaphoreType.DMA((2, n)),
        pltpu.SemaphoreType.DMA((2, n)),
    ]


N_SCATTER = 6


class Scatter:
    def __init__(self, grp, p, rows, got, rbuf, csend, crecv, send, recv):
        self.grp, self.p, self.rows, self.half = grp, p, rows, rows // 2
        self.got, self.rbuf = got, rbuf
        self.csend, self.crecv, self.send, self.recv = csend, crecv, send, recv
        self.index = {m: i for i, m in enumerate(grp.masks)}
        self.started = []
        self.slots = []
        for h in range(2):
            s = {}
            order = grp.orders[h]
            for i in range(len(order)):
                later = order[i + 1 :]
                for m in grp.masks:
                    if all((not m & b) or b in later for b in order):
                        s[(i, m)] = len(s)
            self.slots.append(s)

    def masks(self, pair):
        chosen = [m for m in self.grp.masks if bool(m & self.grp.pair) == pair]
        return sorted(chosen, key=lambda m: -bin(m).count("1"))

    def block(self, mask, h=None):
        first = self.grp.rank(mask) * self.rows
        if h is None:
            return self.p.at[pl.ds(pl.multiple_of(first, self.rows), self.rows)]
        return self.p.at[pl.ds(pl.multiple_of(first + h * self.half, self.half), self.half)]

    def core_copy(self, mask):
        i = self.index[mask]
        return pltpu.make_async_remote_copy(
            src_ref=self.block(mask | self.grp.core),
            dst_ref=self.got.at[i],
            send_sem=self.csend.at[i],
            recv_sem=self.crecv.at[i],
            device_id=self.grp.partner(self.grp.core),
            device_id_type=MESH,
        )

    def begin(self, masks):
        for m in masks:
            c = self.core_copy(m)
            c.start()
            self.started.append(c)

    def core_step(self, mask):
        self.core_copy(mask).wait_recv()
        add_rows(self.block(mask), self.got.at[self.index[mask]], self.rows)
        for h in range(2):
            if mask & self.grp.orders[h][0]:
                self.ship(h, 0, mask)

    def link_copy(self, h, i, mask, k):
        return pltpu.make_async_remote_copy(
            src_ref=self.block(mask, h),
            dst_ref=self.rbuf.at[h, k],
            send_sem=self.send.at[h, k],
            recv_sem=self.recv.at[h, k],
            device_id=self.grp.partner(self.grp.orders[h][i]),
            device_id_type=MESH,
        )

    def ship(self, h, i, mask):
        c = self.link_copy(h, i, mask, self.slots[h][(i, mask - self.grp.orders[h][i])])
        c.start()
        self.started.append(c)

    def take(self, h, i, mask):
        k = self.slots[h][(i, mask)]
        self.link_copy(h, i, mask, k).wait_recv()
        add_rows(self.block(mask, h), self.rbuf.at[h, k], self.half)

    def core_steps(self, pair):
        return [functools.partial(self.core_step, m) for m in self.masks(pair)]

    def link_steps(self, pair):
        steps = []
        for i in range(1, len(self.grp.orders[0])):
            for m in self.masks(pair):
                for h in range(2):
                    order = self.grp.orders[h]
                    mine = m if h == 0 else mirror(self.grp, m)
                    if any(mine & b for b in order[:i]):
                        continue

                    def step(h=h, i=i, mine=mine, order=order):
                        self.take(h, i - 1, mine)
                        if mine & order[i]:
                            self.ship(h, i, mine)

                    steps.append(step)
        return steps

    def finish(self):
        for h in range(2):
            self.take(h, len(self.grp.orders[h]) - 1, 0)

    def drain(self):
        for c in self.started:
            c.wait_send()


def plain_scatter(grp, p, rows, refs):
    scat = Scatter(grp, p, rows, *refs)
    scat.begin(scat.masks(True) + scat.masks(False))
    run(scat.core_steps(True) + scat.core_steps(False))
    run(scat.link_steps(True) + scat.link_steps(False))
    scat.finish()
    scat.drain()
    return scat.block(0)


def run(*lists):
    for i in range(max(len(x) for x in lists)):
        for steps in lists:
            if i < len(steps):
                steps[i]()


class Spread:
    def __init__(self, grp, send, recv):
        self.grp, self.send, self.recv = grp, send, recv
        self.used = 0
        self.copies = []

    def to(self, mask, src, dst):
        if mask == 0:
            c = pltpu.make_async_copy(src, dst, self.send.at[self.used])
        else:
            c = pltpu.make_async_remote_copy(
                src_ref=src,
                dst_ref=dst,
                send_sem=self.send.at[self.used],
                recv_sem=self.recv.at[self.used],
                device_id=self.grp.across(mask),
                device_id_type=MESH,
            )
        self.used += 1
        c.start()
        self.copies.append(c)

    def wait(self):
        for c in self.copies:
            c.wait()


def spread_sems(grp, parts):
    return [pltpu.SemaphoreType.DMA((grp.z_size * parts,))] * 2


def spread_weight(grp, spread, shard, whole, half_axis, at, masks=None):
    z, _ = grp.place()
    axis = 1 - half_axis
    mine, other = shard
    for m in grp.far + (0, 1) if masks is None else masks:
        src = other if m % 2 else mine
        size, width = src.shape[axis], src.shape[half_axis]
        place = pl.ds(pl.multiple_of(z * size, size), size)
        if axis == 0:
            dst = whole.at[place, at : at + width]
        else:
            dst = whole.at[at : at + width, place]
        spread.to(m, src, dst)


def halves_of(grp, ref, axis):
    z, _ = grp.place()
    size = ref.shape[axis] // 2
    out = []
    for which in (z % 2, 1 - z % 2):
        part = pl.ds(pl.multiple_of(which * size, size), size)
        out.append(ref.at[:, part] if axis == 1 else ref.at[part])
    return out


def spread_grad(grp, spread, grad, got, axis, masks=None):
    for m in grp.far + (1,) if masks is None else masks:
        place = grp.across(m)[0]
        size = grad.shape[axis] // grp.z_size
        part = pl.ds(pl.multiple_of(place * size, size), size)
        spread.to(m, grad.at[part] if axis == 0 else grad.at[:, part], got.at[m - 1])


def staged_gather(gather, after_pair):
    steps = gather.begin()
    cut = 6 if len(steps) > 6 else len(steps)
    run(steps[:cut])
    after_pair()
    run(steps[cut:])
    gather.finish()


def tiles(rows, body):
    @pl.loop(0, rows // TILE)
    def _(i):
        body(pl.ds(pl.multiple_of(i * TILE, TILE), TILE))


def norm_scale(value):
    return lax.rsqrt(jnp.mean(value * value, axis=-1, keepdims=True) + EPS)


def gather_scratch(grp):
    return [
        pltpu.SemaphoreType.DMA((2, grp.size)),
        pltpu.SemaphoreType.DMA((2, grp.size)),
        pltpu.SemaphoreType.DMA,
    ]


def params(cid):
    return pltpu.CompilerParams(
        collective_id=cid, has_side_effects=True, vmem_limit_bytes=60 << 20
    )


def sds(shape, dtype):
    return jax.ShapeDtypeStruct(shape, dtype)


def weight_views(grp, refs, axis, presliced):
    if presliced:
        return [(refs[2 * i], refs[2 * i + 1]) for i in range(len(refs) // 2)]
    return [tuple(halves_of(grp, r, axis)) for r in refs]


def shard_args(low, shards_, axis):
    aligned = shards_[0].shape[axis] // 2 % (128 if axis == 1 else 16) == 0
    if aligned:
        return False, list(shards_)
    out = []
    for w in shards_:
        size = w.shape[axis] // 2
        out += [
            lax.dynamic_slice_in_dim(w, low * size, size, axis),
            lax.dynamic_slice_in_dim(w, (1 - low) * size, size, axis),
        ]
    return True, out


def first_kernel(grp, flags, n_qkv, x_ref, gain_ref, *rest):
    pre_qkv, pre_o = flags
    qkv_refs, rest = rest[:n_qkv], rest[n_qkv:]
    n_o = 2 if pre_o else 1
    o_refs, rest = rest[:n_o], rest[n_o:]
    all_ref, wqkv_ref, wo_ref, local, send, recv, sem, zs, zr = rest
    grp.greet()
    spread = Spread(grp, zs, zr)

    def weights(masks):
        at = 0
        for pair in weight_views(grp, qkv_refs, 1, pre_qkv):
            spread_weight(grp, spread, pair, wqkv_ref, 1, at, masks)
            at += pair[0].shape[1]
        for pair in weight_views(grp, o_refs, 0, pre_o):
            spread_weight(grp, spread, pair, wo_ref, 0, 0, masks)

    def norm(rows):
        x = x_ref[rows].astype(F32)
        local[rows] = (x * norm_scale(x) * gain_ref[...]).astype(BF16)

    tiles(x_ref.shape[0], norm)
    gather = Gather(grp, local, all_ref, send, recv, sem)
    steps = gather.begin()
    weights(grp.far + (0,))
    run(steps[:6])
    weights((1,))
    run(steps[6:] or [lambda: None])
    gather.finish()
    spread.wait()


def first(grp, low, x, gain, w_query, w_key, w_value, w_out, cid):
    pre_qkv, qkv = shard_args(low, (w_query, w_key, w_value), 1)
    pre_o, out = shard_args(low, (w_out,), 0)
    rows, width = x.shape
    if pre_qkv:
        qkv = [jnp.concatenate(qkv[i::2], axis=1) for i in range(2)]
    deep = w_query.shape[0] * grp.z_size
    thin = 3 * w_query.shape[1] // 2
    return pl.pallas_call(
        functools.partial(first_kernel, grp, (pre_qkv, pre_o), len(qkv)),
        out_shape=[
            sds((rows * grp.size, width), BF16),
            sds((deep, thin), BF16),
            sds((w_out.shape[0] // 2, w_out.shape[1] * grp.z_size), BF16),
        ],
        in_specs=[VMEM, VMEM] + [ANY] * (len(qkv) + len(out)),
        out_specs=[ANY] * 3,
        scratch_shapes=[pltpu.VMEM((rows, width), BF16)]
        + gather_scratch(grp)
        + spread_sems(grp, 4),
        compiler_params=params(cid),
        name="first",
    )(x, gain, *qkv, *out)


def attend_rows(length, heads, q_ref, k_ref, v_ref, start_ref, o_ref, lse_ref, row):
    base = row * length

    def band(h, at, first, width, size):
        lanes = slice(h * HEAD, (h + 1) * HEAD)
        mine = pl.ds(pl.multiple_of(base + at, QB), size)
        keys = pl.ds(pl.multiple_of(base + first, QB), width)
        cols = pl.ds(pl.multiple_of(at, QB), size)
        query = q_ref[mine, lanes] * BF16(HEAD**-0.5)
        scores = dot_nt(k_ref[keys, lanes], query)
        mask = kept(start_ref[row, :, cols], at, size, first, width)
        scores = jnp.where(mask, scores, -1e9)
        top = jnp.max(scores, axis=0, keepdims=True)
        expo = jnp.exp(scores - top)
        total = jnp.sum(expo, axis=0, keepdims=True)
        weights = (expo * (1.0 / total)).astype(BF16)
        o_ref[mine, lanes] = dot_tn(weights, v_ref[keys, lanes]).astype(BF16)
        lse_ref[row, h : h + 1, cols] = top + jnp.log(total)

    return banded(length, heads, band)


def banded(length, heads, band):
    parts = []
    for h in range(heads):
        whole = [b for b in bands(length) if b[3] == SAMPLE + QB]
        for at, size, first, width in bands(length):
            if width != SAMPLE + QB:
                parts.append(functools.partial(band, h, at, first, width, size))

        def loop(h=h, whole=whole):
            @pl.loop(0, len(whole))
            def _(i):
                at = whole[0][0] + i * QB
                band(h, at, at - SAMPLE, SAMPLE + QB, QB)

        if whole:
            parts.append(loop)
    return parts


def middle_kernel(
    grp,
    heads,
    na_ref,
    wqkv_ref,
    wo_ref,
    cos_ref,
    sin_ref,
    start_ref,
    dy_ref,
    x_ref,
    gain_ref,
    gate_ref,
    up_ref,
    down_ref,
    q_ref,
    k_ref,
    v_ref,
    o_ref,
    lse_ref,
    h_ref,
    nm_ref,
    dyall_ref,
    wg_ref,
    wu_ref,
    wd_ref,
    p,
    rowbuf,
    rowsem,
    local,
    *rest,
):
    scat_refs, rest = rest[:N_SCATTER], rest[N_SCATTER:]
    dsend, drecv, dsem, send, recv, sem, zs, zr = rest
    rows_all, _, length = start_ref.shape
    wide = heads * HEAD
    z, _ = grp.place()
    n = rows_all // 2
    rows = [(1 - z % 2) * n + j for j in range(n)] + [(z % 2) * n + j for j in range(n)]

    blocks = length // QB

    def load(i, j):
        part = pl.ds(pl.multiple_of(rows[i] * length + j * QB, QB), QB)
        return pltpu.make_async_copy(na_ref.at[part], rowbuf.at[j % 2], rowsem.at[j % 2])

    load(0, 0).start()
    grp.greet()
    spread = Spread(grp, zs, zr)
    views = [
        (halves_of(grp, gate_ref, 1), wg_ref, 1),
        (halves_of(grp, up_ref, 1), wu_ref, 1),
        (halves_of(grp, down_ref, 0), wd_ref, 0),
    ]
    outer = Gather(grp, dy_ref, dyall_ref, dsend, drecv, dsem)
    outer_steps = outer.begin()
    for masks in (grp.far, (0, 1)):
        for pair, whole, axis in views:
            spread_weight(grp, spread, pair, whole, axis, 0, masks)
    scat = Scatter(grp, p, x_ref.shape[0], *scat_refs)

    def project(i):
        base = rows[i] * length
        if i:
            load(i, 0).start()

        @pl.loop(0, blocks)
        def _(j):
            @pl.when(j + 1 < blocks)
            def _():
                load(i, j + 1).start()

            load(i, j).wait()
            there = pl.ds(pl.multiple_of(base + j * QB, QB), QB)
            qkv = jnp.dot(rowbuf[j % 2], wqkv_ref[...], preferred_element_type=F32)
            cosine, sine = cos_ref[there], sin_ref[there]
            query, key = qkv[:, :wide], qkv[:, wide : 2 * wide]
            q_ref[there] = (query * cosine + swap_halves(query) * sine).astype(BF16)
            k_ref[there] = (key * cosine + swap_halves(key) * sine).astype(BF16)
            v_ref[there] = qkv[:, 2 * wide :].astype(BF16)

    def branch(i):
        base = rows[i] * length

        @pl.loop(0, length // QB)
        def _(j):
            there = pl.ds(pl.multiple_of(base + j * QB, QB), QB)
            p[there] = jnp.dot(o_ref[there], wo_ref[...], preferred_element_type=F32).astype(BF16)

    def parts(i):
        return (
            [functools.partial(project, i)]
            + attend_rows(length, heads, q_ref, k_ref, v_ref, start_ref, o_ref, lse_ref, rows[i])
            + [functools.partial(branch, i)]
        )

    for i in range(n):
        run(parts(i))
    scat.begin(scat.masks(True))
    run(outer_steps[:4])
    pair_steps = scat.core_steps(True)
    for i in range(n, 2 * n):
        todo = parts(i)
        run(todo, pair_steps)
        pair_steps = pair_steps[len(todo) :]
    scat.begin(scat.masks(False))
    run(pair_steps or [lambda: None])
    run(scat.core_steps(False), outer_steps[4:8])
    run(scat.link_steps(True), outer_steps[8:])
    run(scat.link_steps(False))
    scat.finish()
    summed = scat.block(0)

    def norm(part):
        h = x_ref[part].astype(F32) + summed[part].astype(F32)
        h_ref[part] = h
        local[part] = (h * norm_scale(h) * gain_ref[...]).astype(BF16)

    tiles(x_ref.shape[0], norm)
    gather = Gather(grp, local, nm_ref, send, recv, sem)
    run(gather.begin())
    scat.drain()
    outer.finish()
    gather.finish()
    spread.wait()


def middle(grp, heads, normed, wqkv, wo, cosine, sine, start, dy, x, gain, w_gate, w_up, w_down, cid):
    rows, width = x.shape
    total = rows * grp.size
    wide = heads * HEAD
    rows_all, _, length = start.shape
    thin = sds((total, wide), BF16)
    return pl.pallas_call(
        functools.partial(middle_kernel, grp, heads),
        out_shape=[thin] * 4
        + [
            sds((rows_all, heads, length), F32),
            sds((rows, width), F32),
            sds((total, width), BF16),
            sds((total, width), BF16),
            sds((w_gate.shape[0] * grp.z_size, w_gate.shape[1] // 2), BF16),
            sds((w_up.shape[0] * grp.z_size, w_up.shape[1] // 2), BF16),
            sds((w_down.shape[0] // 2, w_down.shape[1] * grp.z_size), BF16),
        ],
        in_specs=[ANY, VMEM, VMEM, VMEM, VMEM, VMEM, ANY, VMEM, VMEM, ANY, ANY, ANY],
        out_specs=[VMEM] * 6 + [ANY] * 5,
        scratch_shapes=[
            pltpu.VMEM((total, width), BF16),
            pltpu.VMEM((2, QB, width), BF16),
            pltpu.SemaphoreType.DMA((2,)),
            pltpu.VMEM((rows, width), BF16),
        ]
        + scatter_scratch(grp, rows, width)
        + gather_scratch(grp)
        + gather_scratch(grp)
        + spread_sems(grp, 3),
        compiler_params=params(cid),
        name="middle",
    )(normed, wqkv, wo, cosine, sine, start, dy, x, gain, w_gate, w_up, w_down)


def norm_back_tile(value, gain, grad):
    scale = norm_scale(value)
    scaled = grad * gain
    inner = jnp.mean(value * scaled, axis=-1, keepdims=True)
    back = scale * scaled - value * (scale * scale * scale * inner)
    return back, jnp.sum(grad * value * scale, axis=0, keepdims=True)


def got_shape(grp, grad, axis):
    shape = list(grad.shape)
    shape[axis] //= grp.z_size
    return sds((grp.z_size - 1, *shape), BF16)


def fourth_kernel(
    grp, p_ref, h_ref, dy_ref, gain_ref, gdown_ref, ggate_ref, dh_ref, gm_ref, all_ref, down_ref, gate_ref, *rest
):
    p, psem, rest = rest[0], rest[1], rest[2:]
    scat, rest = rest[:N_SCATTER], rest[N_SCATTER:]
    local, send, recv, sem, zs, zr = rest
    pltpu.make_async_copy(p_ref, p, psem).start()
    grp.greet()
    spread = Spread(grp, zs, zr)
    spread_grad(grp, spread, gdown_ref, down_ref, 1)
    spread_grad(grp, spread, ggate_ref, gate_ref, 0, grp.far)
    pltpu.make_async_copy(p_ref, p, psem).wait()
    acc = plain_scatter(grp, p, h_ref.shape[0], scat)
    gm_ref[...] = jnp.zeros_like(gm_ref)

    def back(rows):
        dn, gain_part = norm_back_tile(h_ref[rows], gain_ref[...], acc[rows].astype(F32))
        gm_ref[...] += gain_part
        dh = dy_ref[rows].astype(F32) + dn
        dh_ref[rows] = dh
        local[rows] = dh.astype(BF16)

    tiles(h_ref.shape[0], back)
    staged_gather(
        Gather(grp, local, all_ref, send, recv, sem),
        lambda: spread_grad(grp, spread, ggate_ref, gate_ref, 0, (1,)),
    )
    spread.wait()


def fourth(grp, part, hidden, out_grad, gain, grad_down, grad_gate, cid):
    rows, width = hidden.shape
    return pl.pallas_call(
        functools.partial(fourth_kernel, grp),
        out_shape=[
            sds((rows, width), F32),
            sds((1, width), F32),
            sds((rows * grp.size, width), BF16),
            got_shape(grp, grad_down, 1),
            got_shape(grp, grad_gate, 0),
        ],
        in_specs=[ANY, VMEM, VMEM, VMEM, ANY, ANY],
        out_specs=[VMEM, VMEM, ANY, ANY, ANY],
        scratch_shapes=[pltpu.VMEM((rows * grp.size, width), BF16), pltpu.SemaphoreType.DMA]
        + scatter_scratch(grp, rows, width)
        + [pltpu.VMEM((rows, width), BF16)]
        + gather_scratch(grp)
        + spread_sems(grp, 2),
        compiler_params=params(cid),
        name="fourth",
    )(part, hidden, out_grad, gain, grad_down, grad_gate)


def fifth_kernel(grp, p_ref, h_ref, gup_ref, out_ref, up_ref, *rest):
    p, psem, rest = rest[0], rest[1], rest[2:]
    scat, rest = rest[:N_SCATTER], rest[N_SCATTER:]
    zs, zr = rest
    pltpu.make_async_copy(p_ref, p, psem).start()
    grp.greet()
    spread = Spread(grp, zs, zr)
    spread_grad(grp, spread, gup_ref, up_ref, 0)
    pltpu.make_async_copy(p_ref, p, psem).wait()
    acc = plain_scatter(grp, p, h_ref.shape[0], scat)

    def finish(rows):
        out_ref[rows] = (h_ref[rows] + acc[rows].astype(F32)).astype(BF16)

    tiles(h_ref.shape[0], finish)
    spread.wait()


def fifth(grp, part, hidden, grad_up, cid):
    rows, width = hidden.shape
    return pl.pallas_call(
        functools.partial(fifth_kernel, grp),
        out_shape=[sds((rows, width), BF16), got_shape(grp, grad_up, 0)],
        in_specs=[ANY, VMEM, ANY],
        out_specs=[VMEM, ANY],
        scratch_shapes=[pltpu.VMEM((rows * grp.size, width), BF16), pltpu.SemaphoreType.DMA]
        + scatter_scratch(grp, rows, width)
        + spread_sems(grp, 1),
        compiler_params=params(cid),
        name="fifth",
    )(part, hidden, grad_up)


def sixth_kernel(
    grp, p_ref, x_ref, dh_ref, gain_ref, gm_ref, gout_ref, gqkv_ref, tok_ref, gains_ref, o_ref, qkv_ref, *rest
):
    p, psem, rest = rest[0], rest[1], rest[2:]
    scat, rest = rest[:N_SCATTER], rest[N_SCATTER:]
    buf, gs, gr, zs, zr = rest
    pltpu.make_async_copy(p_ref, p, psem).start()
    grp.greet()
    spread = Spread(grp, zs, zr)
    spread_grad(grp, spread, gout_ref, o_ref, 1)
    spread_grad(grp, spread, gqkv_ref, qkv_ref, 0)
    pltpu.make_async_copy(p_ref, p, psem).wait()
    acc = plain_scatter(grp, p, x_ref.shape[0], scat)
    buf[0, 0:1] = jnp.zeros_like(gm_ref)
    buf[0, 1:2] = gm_ref[...]

    def back(rows):
        dn, gain_part = norm_back_tile(
            x_ref[rows].astype(F32), gain_ref[...], acc[rows].astype(F32)
        )
        buf[0, 0:1] += gain_part
        tok_ref[rows] = (dh_ref[rows] + dn).astype(BF16)

    tiles(x_ref.shape[0], back)
    hops = [grp.partner(b) for b in grp.bits if b != grp.pair]
    bit = 1
    while bit < grp.z_size:
        hops.append(grp.across(bit))
        bit *= 2
    for i, hop in enumerate(hops):
        c = pltpu.make_async_remote_copy(
            src_ref=buf.at[2 * i],
            dst_ref=buf.at[2 * i + 1],
            send_sem=gs.at[i],
            recv_sem=gr.at[i],
            device_id=hop,
            device_id_type=MESH,
        )
        c.start()
        c.wait()
        buf[2 * i + 2] = buf[2 * i] + buf[2 * i + 1]
    gains_ref[...] = buf[2 * len(hops)]
    spread.wait()


def sixth(grp, part, x, dh, gain, gain_m, grad_out, grad_qkv, cid):
    rows, width = x.shape
    n = len(grp.bits) - 1 + (grp.z_size - 1).bit_length()
    return pl.pallas_call(
        functools.partial(sixth_kernel, grp),
        out_shape=[
            sds((rows, width), BF16),
            sds((2, width), F32),
            got_shape(grp, grad_out, 1),
            got_shape(grp, grad_qkv, 0),
        ],
        in_specs=[ANY, VMEM, VMEM, VMEM, VMEM, ANY, ANY],
        out_specs=[VMEM, VMEM, ANY, ANY],
        scratch_shapes=[pltpu.VMEM((rows * grp.size, width), BF16), pltpu.SemaphoreType.DMA]
        + scatter_scratch(grp, rows, width)
        + [
            pltpu.VMEM((2 * n + 1, 2, width), F32),
            pltpu.SemaphoreType.DMA((n,)),
            pltpu.SemaphoreType.DMA((n,)),
        ]
        + spread_sems(grp, 2),
        compiler_params=params(cid),
        name="sixth",
    )(part, x, dh, gain, gain_m, grad_out, grad_qkv)


def swap_halves(value):
    half = HEAD // 2
    width = value.shape[1]
    pieces = []
    for at in range(0, width, HEAD):
        pieces.append(value[:, at + half : at + HEAD])
        pieces.append(value[:, at : at + half])
    if width % 128:
        return jnp.concatenate(pieces, axis=1)
    lane = lax.broadcasted_iota(jnp.int32, value.shape, 1)
    return jnp.where(
        lane % HEAD < half, pltpu.roll(value, width - half, 1), pltpu.roll(value, half, 1)
    )


QB = 256


def bands(length):
    for at in range(0, length, QB):
        first = max(0, at - SAMPLE)
        yield at, min(QB, length - at), first, at + min(QB, length - at) - first


def kept(start_row, at, size, first, width):
    key = first + lax.broadcasted_iota(jnp.int32, (width, size), 0)
    query = at + lax.broadcasted_iota(jnp.int32, (width, size), 1)
    return (key >= start_row) & (key <= query)


def attend_back_kernel(
    heads, q_ref, k_ref, v_ref, do_ref, lse_ref, cos_ref, sin_ref, start_ref, out_ref, dq, dk, dv
):
    wide = heads * HEAD
    length = q_ref.shape[0]
    dk[...] = jnp.zeros_like(dk)
    dv[...] = jnp.zeros_like(dv)
    for h in range(heads):
        lanes = slice(h * HEAD, (h + 1) * HEAD)
        for at, size, first, width in bands(length):
            query = q_ref[at : at + size, lanes]
            key = k_ref[first : first + width, lanes]
            value = v_ref[first : first + width, lanes]
            grad = do_ref[at : at + size, lanes]
            scores = dot_nt(key, query * BF16(HEAD**-0.5))
            mask = kept(start_ref[0, :, at : at + size], at, size, first, width)
            weights = jnp.where(
                mask, jnp.exp(jnp.where(mask, scores, -1e9) - lse_ref[0, h : h + 1, at : at + size]), 0.0
            )
            dv[first : first + width, lanes] += jnp.dot(
                weights.astype(BF16), grad, preferred_element_type=F32
            )
            grad_weights = dot_nt(value, grad)
            inner = jnp.sum(weights * grad_weights, axis=0, keepdims=True)
            grad_scores = (weights * (grad_weights - inner)).astype(BF16)
            dq[at : at + size, lanes] = dot_tn(grad_scores, key)
            dk[first : first + width, lanes] += jnp.dot(
                grad_scores, query, preferred_element_type=F32
            )

    @pl.loop(0, length // QB)
    def _(i):
        rows = pl.ds(pl.multiple_of(i * QB, QB), QB)
        cosine, sine = cos_ref[rows], sin_ref[rows]
        query, key = dq[rows] * HEAD**-0.5, dk[rows] * HEAD**-0.5
        out_ref[rows, :wide] = (query * cosine - swap_halves(query) * sine).astype(BF16)
        out_ref[rows, wide : 2 * wide] = (key * cosine - swap_halves(key) * sine).astype(BF16)
        out_ref[rows, 2 * wide :] = dv[rows].astype(BF16)


def attend_back(query, key, value, grad, lse, cosine, sine, start, heads):
    rows, _, length = start.shape
    wide = heads * HEAD

    def tall(width):
        return pl.BlockSpec((length, width), lambda r: (r, 0))

    return pl.pallas_call(
        functools.partial(attend_back_kernel, heads),
        grid=(rows,),
        out_shape=jax.ShapeDtypeStruct((rows * length, 3 * wide), BF16),
        in_specs=[tall(wide)] * 4
        + [pl.BlockSpec((1, heads, length), lambda r: (r, 0, 0)), tall(wide), tall(wide)]
        + [pl.BlockSpec((1, 1, length), lambda r: (r, 0, 0))],
        out_specs=tall(3 * wide),
        scratch_shapes=[pltpu.VMEM((length, wide), F32)] * 3,
        compiler_params=pltpu.CompilerParams(vmem_limit_bytes=48 << 20),
        name="attend_back",
    )(query, key, value, grad, lse, cosine, sine, start)


def shards(
    z_size,
    t_size,
    tokens,
    gain_attn,
    gain_mlp,
    w_query,
    w_key,
    w_value,
    w_out,
    w_gate,
    w_up,
    w_down,
    segment_ids,
    out_grad,
):
    grp = Group(z_size, t_size)
    z = lax.axis_index("fsdp")
    low = z % 2

    def hop(value, mask):
        return lax.ppermute(value, "fsdp", [(i, i ^ mask) for i in range(z_size)])

    def deliver(grad, got, half_axis, axis, parts=1):
        size = grad.shape[axis] // z_size
        sums = [lax.dynamic_slice_in_dim(grad, z * size, size, axis).astype(F32), None]
        for m in range(1, z_size):
            term = got[m - 1].astype(F32)
            sums[m % 2] = term if sums[m % 2] is None else sums[m % 2] + term
        outs = []
        piece = sums[0].shape[half_axis] // parts
        for i in range(parts):
            a, b = (lax.slice_in_dim(s, i * piece, (i + 1) * piece, axis=half_axis) for s in sums)
            outs.append(
                jnp.where(
                    low == 0,
                    jnp.concatenate([a, b], axis=half_axis),
                    jnp.concatenate([b, a], axis=half_axis),
                )
            )
        return outs

    wide = w_query.shape[1] // 2
    heads = wide // HEAD

    other_ids = hop(segment_ids, 1)
    segments = jnp.where(
        low == 0,
        jnp.concatenate([segment_ids, other_ids], axis=0),
        jnp.concatenate([other_ids, segment_ids], axis=0),
    )
    rows, length = segments.shape
    start = jnp.sum(segments[:, :, None] > segments[:, None, :], axis=2, dtype=jnp.int32)
    position = (jnp.arange(length, dtype=jnp.int32)[None, :] - start).astype(F32)
    lane = jnp.arange(wide, dtype=jnp.int32)
    half = (lane % (HEAD // 2)).astype(F32)
    inverse = jnp.exp(half * (-2.0 / HEAD) * math.log(ROPE_BASE))
    angle = position.reshape(rows * length, 1) * inverse[None, :]
    cosine = jnp.cos(angle)
    sine = jnp.where(lane[None, :] % HEAD < HEAD // 2, -1.0, 1.0) * jnp.sin(angle)
    start = start.reshape(rows, 1, length)

    gain_a = gain_attn.astype(F32)[None, :]
    gain_m = gain_mlp.astype(F32)[None, :]
    normed_a, wqkv, wo = first(grp, low, tokens, gain_a, w_query, w_key, w_value, w_out, 0)
    query, key, value, attended, lse, hidden, normed_m, grad_all, wg, wu, wd = middle(
        grp,
        heads,
        normed_a,
        wqkv,
        wo,
        cosine,
        sine,
        start,
        out_grad,
        tokens,
        gain_m,
        w_gate,
        w_up,
        w_down,
        1,
    )
    gate = jnp.dot(normed_m, wg, preferred_element_type=F32)
    up = jnp.dot(normed_m, wu, preferred_element_type=F32)
    sigma = jax.nn.sigmoid(gate)
    silu_gate = gate * sigma
    act = (silu_gate * up).astype(BF16)
    grad_down = dot_tn(act, grad_all).astype(BF16)
    grad_act = dot_nt(grad_all, wd)
    grad_gate = (grad_act * up * (sigma * (1.0 + gate * (1.0 - sigma)))).astype(BF16)
    grad_up = (grad_act * silu_gate).astype(BF16)
    grad_wg = dot_tn(normed_m, grad_gate).astype(BF16)
    grad_wu = dot_tn(normed_m, grad_up).astype(BF16)
    grad_nm = (dot_nt(grad_gate, wg) + dot_nt(grad_up, wu)).astype(BF16)
    grad_hidden, gain_m_part, branch_all, got_down, got_gate = fourth(
        grp, grad_nm, hidden, out_grad, gain_m, grad_down, grad_wg, 3
    )
    out_part = jnp.dot(act, wd, preferred_element_type=F32).astype(BF16)
    output, got_up = fifth(grp, out_part, hidden, grad_wu, 4)
    grad_wout = dot_tn(attended, branch_all).astype(BF16)
    grad_attended = dot_nt(branch_all, wo).astype(BF16)
    grad_qkv = attend_back(query, key, value, grad_attended, lse, cosine, sine, start, heads)
    grad_wqkv = dot_tn(normed_a, grad_qkv).astype(BF16)
    grad_na = dot_nt(grad_qkv, wqkv).astype(BF16)
    tokens_grad, gains, got_out, got_qkv = sixth(
        grp, grad_na, tokens, grad_hidden, gain_a, gain_m_part, grad_wout, grad_wqkv, 5
    )
    (down_out,) = deliver(grad_down, got_down, 0, 1)
    (gate_out,) = deliver(grad_wg, got_gate, 1, 0)
    (up_out,) = deliver(grad_wu, got_up, 1, 0)
    (out_out,) = deliver(grad_wout, got_out, 0, 1)
    query_out, key_out, value_out = deliver(grad_wqkv, got_qkv, 1, 0, 3)
    return (
        output,
        tokens_grad,
        gains[0],
        gains[1],
        query_out,
        key_out,
        value_out,
        out_out,
        gate_out,
        up_out,
        down_out,
    )


def solution(mesh):
    return jax.shard_map(
        functools.partial(shards, mesh.shape["fsdp"], mesh.shape["tensor"]),
        mesh=mesh,
        in_specs=(
            P(("fsdp", "tensor"), None),
            P(),
            P(),
            P("fsdp", "tensor"),
            P("fsdp", "tensor"),
            P("fsdp", "tensor"),
            P("tensor", "fsdp"),
            P("fsdp", "tensor"),
            P("fsdp", "tensor"),
            P("tensor", "fsdp"),
            P("fsdp", None),
            P(("fsdp", "tensor"), None),
        ),
        out_specs=(
            P(("fsdp", "tensor"), None),
            P(("fsdp", "tensor"), None),
            P(),
            P(),
            P("fsdp", "tensor"),
            P("fsdp", "tensor"),
            P("fsdp", "tensor"),
            P("tensor", "fsdp"),
            P("fsdp", "tensor"),
            P("fsdp", "tensor"),
            P("tensor", "fsdp"),
        ),
        check_vma=False,
    )
```

```python
import functools
import math

import jax
import jax.numpy as jnp
from jax import lax
from jax.experimental import pallas as pl
from jax.experimental.pallas import tpu as pltpu
from jax.sharding import PartitionSpec as P

HEAD = 64
SAMPLE = 512
EPS = 1e-05
LANES = 128
ROPE_BASE = 130000.0
MESH = pl.DeviceIdType.MESH
BF16 = jnp.bfloat16
F32 = jnp.float32
ANY = pl.BlockSpec(memory_space=pl.ANY)
VMEM = pl.BlockSpec(memory_space=pltpu.VMEM)


def flip(index, bit):
    return index + bit - 2 * bit * ((index // bit) % 2)


def dot_nt(left, right):
    return lax.dot_general(left, right, (((1,), (1,)), ((), ())), preferred_element_type=F32)


def dot_tn(left, right):
    return lax.dot_general(left, right, (((0,), (0,)), ((), ())), preferred_element_type=F32)


class Group:
    def __init__(self, z_size, t_size):
        self.z_size = z_size
        self.t_size = t_size
        self.size = 2 * t_size
        inner = []
        bit = 2
        while bit < t_size:
            inner.append(bit)
            bit *= 2
        self.core = 1
        self.pair = t_size
        self.orders = (tuple(inner) + (self.pair,), tuple(inner[::-1]) + (self.pair,))
        self.inner = (tuple(inner), tuple(inner[::-1]))
        self.bits = (self.core,) + tuple(inner) + (self.pair,)
        masks = [0]
        for b in self.orders[0]:
            masks = masks + [m + b for m in masks]
        self.masks = tuple(masks)
        self.far = tuple(range(2, z_size))

    def place(self):
        return lax.axis_index("fsdp"), lax.axis_index("tensor")

    def rank(self, mask=0):
        z, t = self.place()
        r = (z % 2) * self.t_size + t
        for b in self.bits:
            if mask & b:
                r = flip(r, b)
        return r

    def chip_at(self, j):
        chip = self.rank() // 2
        mask = len(self.masks) - 1 - j
        out = 0
        bit = 1
        while bit < len(self.masks):
            a, b = (chip // bit) % 2, (mask // bit) % 2
            out = out + (a + b - 2 * a * b) * bit
            bit *= 2
        return out

    def partner(self, bit):
        z, t = self.place()
        if bit == self.pair:
            return (flip(z, 1), t)
        return (z, flip(t, bit))

    def across(self, mask):
        z, t = self.place()
        bit = 1
        while bit < self.z_size:
            if mask & bit:
                z = flip(z, bit)
            bit *= 2
        return (z, t)

    def greet(self):
        barrier = pltpu.get_barrier_semaphore()
        peers = [self.partner(b) for b in self.bits if b != self.pair]
        peers += [self.across(m) for m in range(1, self.z_size)]
        for peer in peers:
            pl.semaphore_signal(barrier, inc=1, device_id=peer, device_id_type=MESH)
        pl.semaphore_wait(barrier, len(peers))


def last_bit(mask, order):
    found = None
    for b in order:
        if mask & b:
            found = b
    return found


class Gather:
    def __init__(self, grp, x_ref, o_ref, send, recv, local):
        self.grp, self.x, self.o = grp, x_ref, o_ref
        self.send, self.recv = send, recv
        self.rows = x_ref.shape[0]
        self.half = self.rows // 2
        self.order = [(grp.pair,) + grp.inner[h] + (grp.core,) for h in range(2)]
        self.sent = []
        own = pl.ds(pl.multiple_of(grp.rank() * self.rows, self.rows), self.rows)
        self.own = pltpu.make_async_copy(x_ref, o_ref.at[own], local)

    def at(self, mask, h):
        first = self.grp.rank(mask) * self.rows + h * self.half
        return self.o.at[pl.ds(pl.multiple_of(first, self.half), self.half)]

    def copy(self, src, mask, h, key, bit):
        return pltpu.make_async_remote_copy(
            src_ref=src,
            dst_ref=self.at(mask, h),
            send_sem=self.send.at[h, key],
            recv_sem=self.recv.at[h, key],
            device_id=self.grp.partner(bit),
            device_id_type=MESH,
        )

    def forward(self, h, mask, bits=None):
        order = self.order[h]
        start = 0 if mask == 0 else order.index(last_bit(mask, order)) + 1
        for bit in order[start:] if bits is None else bits:
            self.own_copy(h, mask, bit).start()
            self.sent.append((h, mask, bit))

    def own_copy(self, h, mask, bit):
        src = self.x.at[pl.ds(h * self.half, self.half)] if mask == 0 else self.at(mask, h)
        return self.copy(src, mask, h, mask | bit, bit)

    def arrived(self, h, mask):
        bit = last_bit(mask, self.order[h])
        self.copy(self.at(mask, h), mask, h, mask, bit).wait_recv()

    def begin(self):
        self.own.start()
        for h in range(2):
            self.forward(h, 0, (self.grp.pair,))
        for k in range(1, len(self.order[0])):
            for h in range(2):
                self.forward(h, 0, (self.order[h][k],))
        grp = self.grp
        plain = sorted(
            (m for m in grp.masks if m), key=lambda m: (m & grp.pair, bin(m).count("1"))
        )
        if len(plain) > 3:
            plain.remove(grp.pair)
            plain.insert(2, grp.pair)

        def step(h, m):
            self.arrived(h, m)
            self.forward(h, m)

        return [
            functools.partial(step, h, m if h == 0 else mirror(grp, m))
            for m in plain
            for h in range(2)
        ]

    def finish(self):
        for m in self.grp.masks:
            for h in range(2):
                self.arrived(h, m | self.grp.core)
        self.own.wait()
        for sent in self.sent:
            self.own_copy(*sent).wait_send()


def mirror(grp, mask):
    out = mask & (grp.pair | grp.core)
    a, b = grp.inner
    for p, q in zip(a, b):
        if mask & p:
            out |= q
    return out


TILE = 16


def add_rows(dst, src, rows):
    @pl.loop(0, rows // TILE)
    def _(i):
        part = pl.ds(pl.multiple_of(i * TILE, TILE), TILE)
        dst[part] = (dst[part].astype(F32) + src[part].astype(F32)).astype(dst.dtype)


def scatter_scratch(grp, rows, width):
    n = len(grp.masks)
    return [
        pltpu.VMEM((n, rows, width), BF16),
        pltpu.VMEM((2, n - 1, rows // 2, width), BF16),
        pltpu.SemaphoreType.DMA((n,)),
        pltpu.SemaphoreType.DMA((n,)),
        pltpu.SemaphoreType.DMA((2, n)),
        pltpu.SemaphoreType.DMA((2, n)),
    ]


N_SCATTER = 6


class Scatter:
    def __init__(self, grp, p, rows, got, rbuf, csend, crecv, send, recv, own=None):
        self.grp, self.p, self.rows, self.half = grp, p, rows, rows // 2
        self.own = own
        self.got, self.rbuf = got, rbuf
        self.csend, self.crecv, self.send, self.recv = csend, crecv, send, recv
        self.index = {m: len(grp.masks) - 1 - m // 2 for m in grp.masks}
        self.started = []
        self.slots = []
        for h in range(2):
            s = {}
            order = grp.orders[h]
            for i in range(len(order)):
                later = order[i + 1 :]
                for m in grp.masks:
                    if all((not m & b) or b in later for b in order):
                        s[(i, m)] = len(s)
            self.slots.append(s)

    def masks(self, pair):
        chosen = [m for m in self.grp.masks if bool(m & self.grp.pair) == pair]
        return sorted(chosen, reverse=True)

    def begin_tile(self, j):
        _, t = self.grp.place()
        first = (self.grp.chip_at(j) * 2 + 1 - t % 2) * self.rows
        pltpu.make_async_remote_copy(
            src_ref=self.p.at[pl.ds(pl.multiple_of(first, self.rows), self.rows)],
            dst_ref=self.got.at[j],
            send_sem=self.csend.at[j],
            recv_sem=self.crecv.at[j],
            device_id=self.grp.partner(self.grp.core),
            device_id_type=MESH,
        ).start()

    def block(self, mask, h=None):
        if self.own is not None and not mask & self.grp.core:
            mine = self.own.at[self.index[mask]]
            return mine if h is None else mine.at[pl.ds(h * self.half, self.half)]
        first = self.grp.rank(mask) * self.rows
        if h is None:
            return self.p.at[pl.ds(pl.multiple_of(first, self.rows), self.rows)]
        return self.p.at[pl.ds(pl.multiple_of(first + h * self.half, self.half), self.half)]

    def core_copy(self, mask):
        i = self.index[mask]
        return pltpu.make_async_remote_copy(
            src_ref=self.block(mask | self.grp.core),
            dst_ref=self.got.at[i],
            send_sem=self.csend.at[i],
            recv_sem=self.crecv.at[i],
            device_id=self.grp.partner(self.grp.core),
            device_id_type=MESH,
        )

    def begin(self, masks):
        for m in masks:
            self.core_copy(m).start()

    def load(self, mask, sem):
        first = pl.multiple_of(self.grp.rank(mask) * self.rows, self.rows)
        i = self.index[mask]
        return pltpu.make_async_copy(self.p.at[pl.ds(first, self.rows)], self.own.at[i], sem.at[i])

    def core_step(self, mask):
        self.core_copy(mask).wait_recv()
        add_rows(self.block(mask), self.got.at[self.index[mask]], self.rows)
        for h in range(2):
            if mask & self.grp.orders[h][0]:
                self.ship(h, 0, mask)

    def link_copy(self, h, i, mask, k):
        return pltpu.make_async_remote_copy(
            src_ref=self.block(mask, h),
            dst_ref=self.rbuf.at[h, k],
            send_sem=self.send.at[h, k],
            recv_sem=self.recv.at[h, k],
            device_id=self.grp.partner(self.grp.orders[h][i]),
            device_id_type=MESH,
        )

    def ship(self, h, i, mask):
        self.out_copy(h, i, mask).start()
        self.started.append((h, i, mask))

    def out_copy(self, h, i, mask):
        return self.link_copy(h, i, mask, self.slots[h][(i, mask - self.grp.orders[h][i])])

    def take(self, h, i, mask):
        k = self.slots[h][(i, mask)]
        self.link_copy(h, i, mask, k).wait_recv()
        add_rows(self.block(mask, h), self.rbuf.at[h, k], self.half)

    def core_steps(self, pair):
        return [functools.partial(self.core_step, m) for m in self.masks(pair)]

    def link_steps(self, pair):
        steps = []
        for i in range(1, len(self.grp.orders[0])):
            for m in self.masks(pair):
                for h in range(2):
                    order = self.grp.orders[h]
                    mine = m if h == 0 else mirror(self.grp, m)
                    if any(mine & b for b in order[:i]):
                        continue

                    def step(h=h, i=i, mine=mine, order=order):
                        self.take(h, i - 1, mine)
                        if mine & order[i]:
                            self.ship(h, i, mine)

                    steps.append(step)
        return steps

    def finish(self):
        for h in range(2):
            self.take(h, len(self.grp.orders[h]) - 1, 0)

    def drain(self):
        for m in self.grp.masks:
            self.core_copy(m).wait_send()
        for sent in self.started:
            self.out_copy(*sent).wait_send()


def plain_scatter(grp, p, rows, refs):
    scat = Scatter(grp, p, rows, *refs)
    scat.begin(scat.masks(True) + scat.masks(False))
    run(scat.core_steps(True) + scat.core_steps(False))
    run(scat.link_steps(True) + scat.link_steps(False))
    scat.finish()
    scat.drain()
    return scat.block(0)


def run(*lists):
    for i in range(max(len(x) for x in lists)):
        for steps in lists:
            if i < len(steps):
                steps[i]()


class Spread:
    def __init__(self, grp, send, recv):
        self.grp, self.send, self.recv = grp, send, recv
        self.used = 0
        self.makers = []

    def to(self, mask, views):
        k = self.used
        self.used += 1

        def make():
            src, dst = views()
            if mask == 0:
                return pltpu.make_async_copy(src, dst, self.send.at[k])
            return pltpu.make_async_remote_copy(
                src_ref=src,
                dst_ref=dst,
                send_sem=self.send.at[k],
                recv_sem=self.recv.at[k],
                device_id=self.grp.across(mask),
                device_id_type=MESH,
            )

        make().start()
        self.makers.append(make)

    def wait(self):
        self.wait_first(len(self.makers))

    def wait_first(self, count):
        for make in self.makers[:count]:
            make().wait()
        self.makers = self.makers[count:]


def spread_sems(grp, parts):
    return [pltpu.SemaphoreType.DMA((grp.z_size * parts,))] * 2


def spread_weight(grp, spread, shard, whole, half_axis, at, masks=None):
    axis = 1 - half_axis
    mine, other = shard
    for m in grp.far + (0, 1) if masks is None else masks:

        def views(src=other if m % 2 else mine):
            z, _ = grp.place()
            size, width = src.shape[axis], src.shape[half_axis]
            place = pl.ds(pl.multiple_of(z * size, size), size)
            if axis == 0:
                return src, whole.at[place, at : at + width]
            return src, whole.at[at : at + width, place]

        spread.to(m, views)


def halves_of(grp, ref, axis):
    z, _ = grp.place()
    size = ref.shape[axis] // 2
    out = []
    for which in (z % 2, 1 - z % 2):
        part = pl.ds(pl.multiple_of(which * size, size), size)
        out.append(ref.at[:, part] if axis == 1 else ref.at[part])
    return out


def weight_jobs(grp, spread, shard, whole, half_axis, pieces):
    axis = 1 - half_axis
    mine, other = shard
    jobs = {m: [] for m in range(grp.z_size)}
    for i in range(pieces):
        for m in range(grp.z_size):

            def views(i=i, src=other if m % 2 else mine):
                z, _ = grp.place()
                size, width = src.shape[0] // pieces, src.shape[1]
                piece = src.at[pl.ds(i * size, size)]
                if axis == 0:
                    first = pl.multiple_of(z * (size * pieces) + i * size, size)
                    return piece, whole.at[pl.ds(first, size)]
                place = pl.ds(pl.multiple_of(z * width, width), width)
                return piece, whole.at[pl.ds(i * size, size), place]

            jobs[m].append(functools.partial(spread.to, m, views))
    return by_distance(grp, jobs)


def grad_jobs(grp, spread, grad, got, axis, pieces):
    jobs = {m: [] for m in range(1, grp.z_size)}
    for i in range(pieces):
        for m in range(1, grp.z_size):

            def views(i=i, m=m):
                place = grp.across(m)[0]
                size = got.shape[1] // pieces
                land = got.at[m - 1, pl.ds(i * size, size)]
                if axis == 0:
                    first = pl.multiple_of(place * (size * pieces) + i * size, size)
                    return grad.at[pl.ds(first, size)], land
                width = got.shape[2]
                part = pl.ds(pl.multiple_of(place * width, width), width)
                return grad.at[pl.ds(i * size, size), part], land

            jobs[m].append(functools.partial(spread.to, m, views))
    return by_distance(grp, jobs)


def by_distance(grp, jobs):
    far = [job for jobs_i in zip(*(jobs[m] for m in grp.far)) for job in jobs_i]
    near = [job for jobs_i in zip(*(jobs[m] for m in (1, 0) if m in jobs)) for job in jobs_i]
    return far, near


def mixed(steps, jobs, first=0):
    out = list(steps[:first])
    tail = steps[first:]
    done = 0
    for i, step in enumerate(tail):
        upto = (i + 1) * len(jobs) // len(tail)
        out.append(functools.partial(run, [step] + jobs[done:upto]))
        done = upto
    return out + (jobs if not tail else [])


PIECES = 1


def top_rows(views, which):
    size = views[0].shape[0] // 2
    return [v.at[pl.ds(which * size, size)] for v in views]


def spread_grad(grp, spread, grad, got, axis, masks=None):
    for m in grp.far + (1,) if masks is None else masks:

        def views(m=m):
            size = grad.shape[axis] // grp.z_size
            part = pl.ds(pl.multiple_of(grp.across(m)[0] * size, size), size)
            return (grad.at[part] if axis == 0 else grad.at[:, part]), got.at[m - 1]

        spread.to(m, views)


def staged_gather(gather, after_pair):
    steps = gather.begin()
    cut = 6 if len(steps) > 6 else len(steps)
    run(steps[:cut])
    after_pair()
    run(steps[cut:])
    gather.finish()


def tiles(rows, body):
    @pl.loop(0, rows // TILE)
    def _(i):
        body(pl.ds(pl.multiple_of(i * TILE, TILE), TILE))


def norm_scale(value):
    return lax.rsqrt(jnp.mean(value * value, axis=-1, keepdims=True) + EPS)


def gather_scratch(grp):
    return [
        pltpu.SemaphoreType.DMA((2, grp.size)),
        pltpu.SemaphoreType.DMA((2, grp.size)),
        pltpu.SemaphoreType.DMA,
    ]


def params(cid):
    return pltpu.CompilerParams(
        collective_id=cid, has_side_effects=True, vmem_limit_bytes=61952 << 10
    )


def sds(shape, dtype):
    return jax.ShapeDtypeStruct(shape, dtype)


def weight_views(grp, refs, axis, presliced):
    if presliced:
        return [(refs[2 * i], refs[2 * i + 1]) for i in range(len(refs) // 2)]
    return [tuple(halves_of(grp, r, axis)) for r in refs]


def shard_args(low, shards_, axis):
    aligned = shards_[0].shape[axis] // 2 % (128 if axis == 1 else 16) == 0
    if aligned:
        return False, list(shards_)
    out = []
    for w in shards_:
        size = w.shape[axis] // 2
        out += [
            lax.dynamic_slice_in_dim(w, low * size, size, axis),
            lax.dynamic_slice_in_dim(w, (1 - low) * size, size, axis),
        ]
    return True, out


def first_kernel(grp, flags, n_qkv, x_ref, gain_ref, *rest):
    pre_qkv, pre_o = flags
    qkv_refs, rest = rest[:n_qkv], rest[n_qkv:]
    n_o = 2 if pre_o else 1
    o_refs, rest = rest[:n_o], rest[n_o:]
    seg_ref, all_ref, wqkv_ref, wo_ref, start_ref, cos_ref, sin_ref, local, ids, send, recv, sem, zs, zr = rest
    grp.greet()
    spread = Spread(grp, zs, zr)
    z, _ = grp.place()
    spread.to(0, lambda: (seg_ref, ids.at[z % 2]))
    spread.to(1, lambda: (seg_ref, ids.at[z % 2]))

    def weights(masks):
        at = 0
        for pair in weight_views(grp, qkv_refs, 1, pre_qkv):
            spread_weight(grp, spread, pair, wqkv_ref, 1, at, masks)
            at += pair[0].shape[1]
        for pair in weight_views(grp, o_refs, 0, pre_o):
            spread_weight(grp, spread, pair, wo_ref, 0, 0, masks)

    def norm(rows):
        x = x_ref[rows].astype(F32)
        local[rows] = (x * norm_scale(x) * gain_ref[...].astype(F32)).astype(BF16)

    tiles(x_ref.shape[0], norm)
    gather = Gather(grp, local, all_ref, send, recv, sem)
    steps = gather.begin()
    weights(grp.far + (0,))
    spread.wait_first(2)
    places(ids, start_ref, cos_ref, sin_ref)
    run(steps[:6])
    weights((1,))
    run(steps[6:] or [lambda: None])
    gather.finish()
    spread.wait()


def places(ids, start_ref, cos_ref, sin_ref):
    planes, rows, length = ids.shape
    wide = cos_ref.shape[1]
    place = lax.broadcasted_iota(jnp.int32, (1, length), 1)
    lane = lax.broadcasted_iota(jnp.int32, (LANES, LANES), 1)
    pair = (lane % (HEAD // 2)).astype(F32)
    inverse = jnp.exp(pair * (-2.0 / HEAD) * math.log(ROPE_BASE))
    sign = jnp.where(lane % HEAD < HEAD // 2, -1.0, 1.0)
    for a in range(planes):
        for r in range(rows):
            row = a * rows + r
            own = ids[a, r : r + 1]
            change = (place == 0) | (own != pltpu.roll(own, 1, 1))
            start = jnp.where(change, place, 0)
            step = 1
            while step < length:
                start = jnp.maximum(start, jnp.where(place >= step, pltpu.roll(start, step, 1), 0))
                step *= 2
            start_ref[row] = start
            position = (place - start).astype(F32)
            for c in range(0, length, LANES):
                angle = jnp.broadcast_to(position[:, c : c + LANES], (LANES, LANES)).T * inverse
                here = slice(row * length + c, row * length + c + LANES)
                cos_ref[here] = jnp.cos(angle)[:, :wide]
                sin_ref[here] = (sign * jnp.sin(angle))[:, :wide]


def first(grp, low, x, gain, w_query, w_key, w_value, w_out, ids, cid):
    pre_qkv, qkv = shard_args(low, (w_query, w_key, w_value), 1)
    pre_o, out = shard_args(low, (w_out,), 0)
    rows, width = x.shape
    if pre_qkv:
        qkv = [jnp.concatenate(qkv[i::2], axis=1) for i in range(2)]
    deep = w_query.shape[0] * grp.z_size
    thin = 3 * w_query.shape[1] // 2
    table = sds((2 * ids.shape[0] * ids.shape[1], thin // 3), F32)
    return pl.pallas_call(
        functools.partial(first_kernel, grp, (pre_qkv, pre_o), len(qkv)),
        out_shape=[
            sds((rows * grp.size, width), BF16),
            sds((deep, thin), BF16),
            sds((w_out.shape[0] // 2, w_out.shape[1] * grp.z_size), BF16),
            sds((2 * ids.shape[0], 1, ids.shape[1]), jnp.int32),
            table,
            table,
        ],
        in_specs=[VMEM, VMEM] + [ANY] * (len(qkv) + len(out)) + [VMEM],
        out_specs=[ANY] * 3 + [VMEM] * 3,
        scratch_shapes=[
            pltpu.VMEM((rows, width), BF16),
            pltpu.VMEM((2,) + ids.shape, jnp.int32),
        ]
        + gather_scratch(grp)
        + spread_sems(grp, 5),
        compiler_params=params(cid),
        name="first",
    )(x, gain, *qkv, *out, ids)


def attend_rows(length, heads, q_ref, k_ref, v_ref, start_ref, o_ref, lse_ref, row):
    base = row * length

    def band(h, at, first, width, size):
        lanes = slice(h * HEAD, (h + 1) * HEAD)
        mine = pl.ds(pl.multiple_of(base + at, QB), size)
        keys = pl.ds(pl.multiple_of(base + first, QB), width)
        cols = pl.ds(pl.multiple_of(at, QB), size)
        query = q_ref[mine, lanes] * BF16(HEAD**-0.5)
        scores = dot_nt(k_ref[keys, lanes], query)
        mask = kept(start_ref[row, :, cols], at, size, first, width)
        scores = jnp.where(mask, scores, -1e9)
        top = jnp.max(scores, axis=0, keepdims=True)
        expo = jnp.exp(scores - top)
        total = jnp.sum(expo, axis=0, keepdims=True)
        weights = (expo * (1.0 / total)).astype(BF16)
        o_ref[mine, lanes] = dot_tn(weights, v_ref[keys, lanes]).astype(BF16)
        lse_ref[row, h : h + 1, cols] = top + jnp.log(total)

    return banded(length, heads, band)


def banded(length, heads, band):
    parts = []
    for h in range(heads):
        whole = [b for b in bands(length) if b[3] == SAMPLE + QB]
        for at, size, first, width in bands(length):
            if width != SAMPLE + QB:
                parts.append(functools.partial(band, h, at, first, width, size))

        def loop(h=h, whole=whole):
            @pl.loop(0, len(whole))
            def _(i):
                at = whole[0][0] + i * QB
                band(h, at, at - SAMPLE, SAMPLE + QB, QB)

        if whole:
            parts.append(loop)
    return parts


def middle_kernel(
    grp,
    heads,
    na_ref,
    wqkv_ref,
    wo_ref,
    cos_ref,
    sin_ref,
    start_ref,
    dy_ref,
    x_ref,
    gain_ref,
    gate_ref,
    up_ref,
    down_ref,
    q_ref,
    k_ref,
    v_ref,
    o_ref,
    lse_ref,
    h_ref,
    nm_ref,
    dyall_ref,
    wg_ref,
    wu_ref,
    wd_ref,
    p,
    rowbuf,
    rowsem,
    local,
    *rest,
):
    scat_refs, rest = rest[:N_SCATTER], rest[N_SCATTER:]
    dsend, drecv, dsem, send, recv, sem, zs, zr = rest
    rows_all, _, length = start_ref.shape
    wide = heads * HEAD
    z, _ = grp.place()
    n = rows_all // 2
    rows = [(1 - z % 2) * n + j for j in range(n)] + [(z % 2) * n + j for j in range(n)]

    blocks = length // QB

    def load(i, j):
        part = pl.ds(pl.multiple_of(rows[i] * length + j * QB, QB), QB)
        return pltpu.make_async_copy(na_ref.at[part], rowbuf.at[j % 2], rowsem.at[j % 2])

    load(0, 0).start()
    grp.greet()
    spread = Spread(grp, zs, zr)
    views = [
        (halves_of(grp, gate_ref, 1), wg_ref, 1),
        (halves_of(grp, up_ref, 1), wu_ref, 1),
        (top_rows(halves_of(grp, down_ref, 0), 0), wd_ref, 0),
    ]
    outer = Gather(grp, dy_ref, dyall_ref, dsend, drecv, dsem)
    outer_steps = outer.begin()
    for masks in (grp.far, (0, 1)):
        for pair, whole, axis in views:
            spread_weight(grp, spread, pair, whole, axis, 0, masks)
    scat = Scatter(grp, p, x_ref.shape[0], *scat_refs)

    def project(i):
        base = rows[i] * length
        if i:
            load(i, 0).start()

        @pl.loop(0, blocks)
        def _(j):
            @pl.when(j + 1 < blocks)
            def _():
                load(i, j + 1).start()

            load(i, j).wait()
            there = pl.ds(pl.multiple_of(base + j * QB, QB), QB)
            qkv = jnp.dot(rowbuf[j % 2], wqkv_ref[...], preferred_element_type=F32)
            cosine, sine = cos_ref[there], sin_ref[there]
            query, key = qkv[:, :wide], qkv[:, wide : 2 * wide]
            q_ref[there] = (query * cosine + swap_halves(query) * sine).astype(BF16)
            k_ref[there] = (key * cosine + swap_halves(key) * sine).astype(BF16)
            v_ref[there] = qkv[:, 2 * wide :].astype(BF16)

    def branch(i):
        base = rows[i] * length

        @pl.loop(0, length // QB)
        def _(j):
            there = pl.ds(pl.multiple_of(base + j * QB, QB), QB)
            p[there] = jnp.dot(o_ref[there], wo_ref[...], preferred_element_type=F32).astype(BF16)

    def parts(i):
        return (
            [functools.partial(project, i)]
            + attend_rows(length, heads, q_ref, k_ref, v_ref, start_ref, o_ref, lse_ref, rows[i])
            + [functools.partial(branch, i)]
        )

    for i in range(n):
        run(parts(i))
    scat.begin(scat.masks(True))
    run(outer_steps[:4])
    pair_steps = scat.core_steps(True)
    for i in range(n, 2 * n):
        todo = parts(i)
        run(todo, pair_steps)
        pair_steps = pair_steps[len(todo) :]
    scat.begin(scat.masks(False))
    run(pair_steps or [lambda: None])
    run(scat.core_steps(False), outer_steps[4:8])
    run(scat.link_steps(True), outer_steps[8:])
    run(scat.link_steps(False))
    scat.finish()
    summed = scat.block(0)

    def norm(part):
        h = x_ref[part].astype(F32) + summed[part].astype(F32)
        h_ref[part] = h
        local[part] = (h * norm_scale(h) * gain_ref[...].astype(F32)).astype(BF16)

    tiles(x_ref.shape[0], norm)
    gather = Gather(grp, local, nm_ref, send, recv, sem)
    run(gather.begin())
    scat.drain()
    outer.finish()
    gather.finish()
    spread.wait()


def middle(grp, heads, normed, wqkv, wo, cosine, sine, start, dy, x, gain, w_gate, w_up, w_down, cid):
    rows, width = x.shape
    total = rows * grp.size
    wide = heads * HEAD
    rows_all, _, length = start.shape
    thin = sds((total, wide), BF16)
    return pl.pallas_call(
        functools.partial(middle_kernel, grp, heads),
        out_shape=[thin] * 4
        + [
            sds((rows_all, heads, length), F32),
            sds((rows, width), F32),
            sds((total, width), BF16),
            sds((total, width), BF16),
            sds((w_gate.shape[0] * grp.z_size, w_gate.shape[1] // 2), BF16),
            sds((w_up.shape[0] * grp.z_size, w_up.shape[1] // 2), BF16),
            sds((w_down.shape[0] // 4, w_down.shape[1] * grp.z_size), BF16),
        ],
        in_specs=[ANY, VMEM, VMEM, VMEM, VMEM, VMEM, ANY, VMEM, VMEM, ANY, ANY, ANY],
        out_specs=[VMEM] * 6 + [ANY] * 5,
        scratch_shapes=[
            pltpu.VMEM((total, width), BF16),
            pltpu.VMEM((2, QB, width), BF16),
            pltpu.SemaphoreType.DMA((2,)),
            pltpu.VMEM((rows, width), BF16),
        ]
        + scatter_scratch(grp, rows, width)
        + gather_scratch(grp)
        + gather_scratch(grp)
        + spread_sems(grp, 3 * PIECES),
        compiler_params=params(cid),
        name="middle",
    )(normed, wqkv, wo, cosine, sine, start, dy, x, gain, w_gate, w_up, w_down)


def norm_back_tile(value, gain, grad):
    scale = norm_scale(value)
    scaled = grad * gain
    inner = jnp.mean(value * scaled, axis=-1, keepdims=True)
    back = scale * scaled - value * (scale * scale * scale * inner)
    return back, jnp.sum(grad * value * scale, axis=0, keepdims=True)


def weave(parts, steps, each=1):
    for part in parts:
        part()
        for step in steps[:each]:
            step()
        steps = steps[each:]
    return steps


def last_kernel(
    grp,
    heads,
    branch_ref,
    na_ref,
    part_ref,
    gup_ref,
    q_ref,
    k_ref,
    v_ref,
    o_ref,
    lse_ref,
    cos_ref,
    sin_ref,
    start_ref,
    wqkv_ref,
    wo_ref,
    h_ref,
    x_ref,
    dh_ref,
    gain_ref,
    gm_ref,
    out_ref,
    tok_ref,
    gains_ref,
    gout_ref,
    gqkv_ref,
    upgot_ref,
    outgot_ref,
    qkvgot_ref,
    p,
    own,
    ownsem,
    rowbuf,
    rowsem,
    cols,
    csem,
    do,
    dqkv,
    dq,
    dk,
    dv,
    gacc,
    buf,
    gs,
    gr,
    *rest,
):
    na_scat, rest = rest[:N_SCATTER], rest[N_SCATTER:]
    out_scat, rest = rest[:N_SCATTER], rest[N_SCATTER:]
    zs, zr = rest
    rows_all, _, length = start_ref.shape
    rows, width = h_ref.shape
    wide = heads * HEAD
    z, _ = grp.place()
    n = rows_all // 2
    order = [(1 - z % 2) * n + j for j in range(n)] + [(z % 2) * n + j for j in range(n)]
    blocks = length // QB
    step = cols.shape[2]

    def load(i, j):
        part = pl.ds(pl.multiple_of(order[i] * length + j * QB, QB), QB)
        return pltpu.make_async_copy(branch_ref.at[part], rowbuf.at[j % 2], rowsem.at[j % 2])

    def load_cols(c):
        part = pl.ds(pl.multiple_of(c * step, step), step)
        return pltpu.make_async_copy(na_ref.at[:, part], cols.at[c % 2], csem.at[c % 2])

    load(0, 0).start()
    load_cols(0).start()
    outer = Scatter(grp, part_ref, rows, *out_scat, own=own)
    for m in outer.masks(True) + outer.masks(False):
        outer.load(m, ownsem).start()
    grp.greet()
    outer.begin(outer.masks(True) + outer.masks(False))
    spread = Spread(grp, zs, zr)
    spread_grad(grp, spread, gup_ref, upgot_ref, 0)
    scat = Scatter(grp, p, rows, *na_scat)
    gacc[...] = jnp.zeros_like(gacc)

    def outer_core(m):
        outer.load(m, ownsem).wait()
        outer.core_step(m)

    outer_steps = [
        functools.partial(outer_core, m) for m in outer.masks(True) + outer.masks(False)
    ]
    outer_steps += outer.link_steps(True) + outer.link_steps(False)

    def prepare(i):
        base = order[i] * length
        if i:
            load(i, 0).start()
        dk[...] = jnp.zeros_like(dk)
        dv[...] = jnp.zeros_like(dv)

        @pl.loop(0, blocks)
        def _(j):
            @pl.when(j + 1 < blocks)
            def _():
                load(i, j + 1).start()

            load(i, j).wait()
            there = pl.ds(pl.multiple_of(base + j * QB, QB), QB)
            here = pl.ds(pl.multiple_of(j * QB, QB), QB)
            branch = rowbuf[j % 2]
            do[here] = dot_nt(branch, wo_ref[...]).astype(BF16)
            gacc[...] += dot_tn(o_ref[there], branch)

    def banded_back(i):
        row = order[i]
        base = row * length

        def band(h, at, first, width, size):
            lanes = slice(h * HEAD, (h + 1) * HEAD)
            cols_at = pl.ds(pl.multiple_of(at, QB), size)
            keys_at = pl.ds(pl.multiple_of(first, QB), width)
            mine = pl.ds(pl.multiple_of(base + at, QB), size)
            keys = pl.ds(pl.multiple_of(base + first, QB), width)
            query = q_ref[mine, lanes]
            key = k_ref[keys, lanes]
            grad = do[cols_at, lanes]
            scores = dot_nt(key, query * BF16(HEAD**-0.5))
            mask = kept(start_ref[row, :, cols_at], at, size, first, width)
            scores = jnp.where(mask, scores, -1e9)
            weights = jnp.exp(scores - lse_ref[row, h : h + 1, cols_at])
            dv[keys_at, lanes] += jnp.dot(weights.astype(BF16), grad, preferred_element_type=F32)
            grad_weights = dot_nt(v_ref[keys, lanes], grad)
            inner = jnp.sum(weights * grad_weights, axis=0, keepdims=True)
            grad_scores = (weights * (grad_weights - inner)).astype(BF16)
            dq[cols_at, lanes] = dot_tn(grad_scores, key)
            dk[keys_at, lanes] += jnp.dot(grad_scores, query, preferred_element_type=F32)

        return banded(length, heads, band)

    def turn_back(i):
        base = order[i] * length

        @pl.loop(0, blocks)
        def _(j):
            there = pl.ds(pl.multiple_of(base + j * QB, QB), QB)
            here = pl.ds(pl.multiple_of(j * QB, QB), QB)
            cosine, sine = cos_ref[there], sin_ref[there]
            query, key = dq[here] * HEAD**-0.5, dk[here] * HEAD**-0.5
            dqkv[there, :wide] = (query * cosine - swap_halves(query) * sine).astype(BF16)
            dqkv[there, wide : 2 * wide] = (key * cosine - swap_halves(key) * sine).astype(BF16)
            dqkv[there, 2 * wide :] = dv[here].astype(BF16)
            p[there] = dot_nt(dqkv[there], wqkv_ref[...]).astype(BF16)

    def parts(i):
        return (
            [functools.partial(prepare, i)] + banded_back(i) + [functools.partial(turn_back, i)]
        )

    for i in range(n):
        outer_steps = weave(parts(i), outer_steps)
    scat.begin(scat.masks(True))
    pair_core = scat.core_steps(True)
    for i in range(n, 2 * n):
        todo = parts(i)
        merged = []
        for a in range(len(todo)):
            merged += [x[a] for x in (outer_steps, pair_core) if a < len(x)]
        outer_steps, pair_core = outer_steps[len(todo) :], pair_core[len(todo) :]
        merged = weave(todo, merged, 2)
        outer_steps = merged + outer_steps
    scat.begin(scat.masks(False))
    gout_ref[...] = gacc[...].astype(BF16)
    spread_grad(grp, spread, gout_ref, outgot_ref, 1)

    def qkv_cols(c):
        @pl.when(c + 1 < width // step)
        def _():
            load_cols(c + 1).start()

        load_cols(c).wait()
        part = pl.ds(pl.multiple_of(c * step, step), step)
        gqkv_ref[part] = dot_tn(cols[c % 2], dqkv[...]).astype(BF16)

    paced(width // step, qkv_cols, outer_steps + pair_core + scat.core_steps(False))
    spread_grad(grp, spread, gqkv_ref, qkvgot_ref, 0)
    run(scat.link_steps(True) + scat.link_steps(False))
    outer.finish()
    whole = outer.block(0)

    def output(part):
        out_ref[part] = (h_ref[part] + whole[part].astype(F32)).astype(BF16)

    tiles(rows, output)
    scat.finish()
    summed = scat.block(0)
    buf[0, 0:1] = jnp.zeros_like(gm_ref)
    buf[0, 1:2] = gm_ref[...]

    def back(part):
        dn, gain_part = norm_back_tile(
            x_ref[part].astype(F32), gain_ref[...].astype(F32), summed[part].astype(F32)
        )
        buf[0, 0:1] += gain_part
        tok_ref[part] = (dh_ref[part] + dn).astype(BF16)

    tiles(rows, back)
    sum_gains(grp, buf, gs, gr)
    gains_ref[...] = buf[buf.shape[0] - 1]
    outer.drain()
    scat.drain()
    spread.wait()


def sum_gains(grp, buf, send, recv):
    hops = [grp.partner(b) for b in grp.bits if b != grp.pair]
    bit = 1
    while bit < grp.z_size:
        hops.append(grp.across(bit))
        bit *= 2
    for i, hop in enumerate(hops):
        c = pltpu.make_async_remote_copy(
            src_ref=buf.at[2 * i],
            dst_ref=buf.at[2 * i + 1],
            send_sem=send.at[i],
            recv_sem=recv.at[i],
            device_id=hop,
            device_id_type=MESH,
        )
        c.start()
        c.wait()
        buf[2 * i + 2] = buf[2 * i] + buf[2 * i + 1]


def last(
    grp, heads, branch, normed, part, grad_up, query, key, value, attended, lse, cosine, sine, start,
    wqkv, wo, hidden, x, dh, gain, gain_m, cid,
):
    rows, width = x.shape
    total = rows * grp.size
    wide = heads * HEAD
    length = start.shape[2]
    hops = len(grp.bits) - 1 + (grp.z_size - 1).bit_length()
    n = len(grp.masks)
    gout, gqkv = sds((wide, width), BF16), sds((width, 3 * wide), BF16)
    return pl.pallas_call(
        functools.partial(last_kernel, grp, heads),
        out_shape=[
            sds((rows, width), BF16),
            sds((rows, width), BF16),
            sds((2, width), F32),
            gout,
            gqkv,
            got_shape(grp, grad_up, 0),
            got_shape(grp, gout, 1),
            got_shape(grp, gqkv, 0),
        ],
        in_specs=[ANY] * 4 + [VMEM] * 15,
        out_specs=[VMEM] * 5 + [ANY] * 3,
        scratch_shapes=[
            pltpu.VMEM((total, width), BF16),
            pltpu.VMEM((n, rows, width), BF16),
            pltpu.SemaphoreType.DMA((n,)),
            pltpu.VMEM((2, QB, width), BF16),
            pltpu.SemaphoreType.DMA((2,)),
            pltpu.VMEM((2, total, cols_of(total)), BF16),
            pltpu.SemaphoreType.DMA((2,)),
            pltpu.VMEM((length, wide), BF16),
            pltpu.VMEM((total, 3 * wide), BF16),
            pltpu.VMEM((length, wide), F32),
            pltpu.VMEM((length, wide), F32),
            pltpu.VMEM((length, wide), F32),
            pltpu.VMEM((wide, width), F32),
            pltpu.VMEM((2 * hops + 1, 2, width), F32),
            pltpu.SemaphoreType.DMA((hops,)),
            pltpu.SemaphoreType.DMA((hops,)),
        ]
        + scatter_scratch(grp, rows, width)
        + scatter_scratch(grp, rows, width)
        + spread_sems(grp, 3 * PIECES),
        compiler_params=params(cid),
        name="last",
    )(
        branch, normed, part, grad_up, query, key, value, attended, lse, cosine, sine, start,
        wqkv, wo, hidden, x, dh, gain, gain_m,
    )


def got_shape(grp, grad, axis):
    shape = list(grad.shape)
    shape[axis] //= grp.z_size
    return sds((grp.z_size - 1, *shape), BF16)


def paced(count, body, steps, first=0):
    turns = count - first
    each = -(-len(steps) // turns) if steps else 0

    @pl.loop(0, count)
    def _(i):
        body(i)
        for k in range(turns):
            mine = steps[k * each : (k + 1) * each]
            if mine:

                @pl.when(i == first + k)
                def _(mine=mine):
                    for step in mine:
                        step()


def cols_of(total):
    return max(128, 655360 // total // 128 * 128)


def mlp_kernel(
    grp,
    nm_ref,
    dyall_ref,
    wg_ref,
    wu_ref,
    top_ref,
    h_ref,
    dy_ref,
    gain_ref,
    down_ref,
    dh_ref,
    gm_ref,
    gdown_ref,
    ggate_ref,
    gup_ref,
    branch_ref,
    out_ref,
    downgot_ref,
    gategot_ref,
    p,
    wd,
    tile_n,
    tsem,
    act,
    dgu,
    cols,
    csem,
    dsem,
    *rest,
):
    scat_refs, rest = rest[:N_SCATTER], rest[N_SCATTER:]
    send, recv, sem, zs, zr = rest
    rows, width = h_ref.shape
    size = 2 * rows
    n = len(grp.masks)
    units = wd.shape[0]
    step = cols.shape[2]

    def at(j):
        return pl.ds(pl.multiple_of(grp.chip_at(j) * size, size), size)

    def load(src, buf, k, j):
        return pltpu.make_async_copy(src.at[at(j)], buf.at[j % 2], tsem.at[k, j % 2])

    def load_cols(src, c):
        part = pl.ds(pl.multiple_of(c * step, step), step)
        return pltpu.make_async_copy(src.at[:, part], cols.at[c % 2], csem.at[c % 2])

    load(nm_ref, tile_n, 0, 0).start()
    grp.greet()
    spread = Spread(grp, zs, zr)
    spread.to(0, lambda: (top_ref, wd.at[pl.ds(0, units // 2)]))
    spread_weight(
        grp,
        spread,
        top_rows(halves_of(grp, down_ref, 0), 1),
        wd.at[pl.ds(units // 2, units // 2)],
        0,
        0,
    )

    def forward(j):
        @pl.when(j + 1 < n)
        def _():
            load(nm_ref, tile_n, 0, j + 1).start()

        load(nm_ref, tile_n, 0, j).wait()
        normed = tile_n[j % 2]
        gate = jnp.dot(normed, wg_ref[...], preferred_element_type=F32)
        up = jnp.dot(normed, wu_ref[...], preferred_element_type=F32)
        here = at(j)
        act[here] = (gate * jax.nn.sigmoid(gate) * up).astype(BF16)
        dgu[here, :units] = gate.astype(BF16)
        dgu[here, units:] = up.astype(BF16)

    load_cols(dyall_ref, 0).start()
    paced(n, forward, [])
    blocks = width // step

    def down_cols(c):
        @pl.when(c + 1 < blocks)
        def _():
            load_cols(dyall_ref, c + 1).start()

        load_cols(dyall_ref, c).wait()
        part = pl.ds(pl.multiple_of(c * step, step), step)
        gdown_ref[:, part] = dot_tn(cols[c % 2], act[...]).T.astype(BF16)

    load(dyall_ref, tile_n, 1, 0).start()
    paced(blocks, down_cols, [])
    spread.wait()
    spread_grad(grp, spread, gdown_ref, downgot_ref, 1)

    scat = Scatter(grp, p, rows, *scat_refs)
    chunk = min(512, width)

    def backward(j):
        @pl.when(j + 1 < n)
        def _():
            load(dyall_ref, tile_n, 1, j + 1).start()

        load(dyall_ref, tile_n, 1, j).wait()
        here = at(j)
        grad_act = dot_nt(tile_n[j % 2], wd[...])
        gate, up = dgu[here, :units].astype(F32), dgu[here, units:].astype(F32)
        sigma = jax.nn.sigmoid(gate)
        grad_gate = (grad_act * up * (sigma * (1.0 + gate * (1.0 - sigma)))).astype(BF16)
        grad_up = (grad_act * (gate * sigma)).astype(BF16)
        dgu[here, :units] = grad_gate
        dgu[here, units:] = grad_up
        for c in range(0, width, chunk):
            p[here, c : c + chunk] = (
                dot_nt(grad_gate, wg_ref[c : c + chunk]) + dot_nt(grad_up, wu_ref[c : c + chunk])
            ).astype(BF16)
        scat.begin_tile(j)

    core = scat.core_steps(True) + scat.core_steps(False)
    pair_links = scat.link_steps(True)
    todo = []
    late = n // 2
    share = -(-len(pair_links) // max(1, late - 1))
    for j in range(1, n):
        todo.append([core[j - 1]])
        if j > late:
            k = (j - late - 1) * share
            todo[-1] += pair_links[k : k + share]
    done = share * max(0, late - 1)
    paced(n, backward, [functools.partial(run, x) for x in todo], 1)
    rest_steps = [core[n - 1]] + pair_links[done:] + scat.link_steps(False)

    def gate_up_cols(c):
        @pl.when(c + 1 < blocks)
        def _():
            load_cols(nm_ref, c + 1).start()

        load_cols(nm_ref, c).wait()
        part = pl.ds(pl.multiple_of(c * step, step), step)
        grads = dot_tn(cols[c % 2], dgu[...]).astype(BF16)
        ggate_ref[part] = grads[:, :units]
        gup_ref[part] = grads[:, units:]

    load_cols(nm_ref, 0).start()
    paced(blocks, gate_up_cols, rest_steps)
    spread_grad(grp, spread, ggate_ref, gategot_ref, 0, grp.far)
    dy = scat_refs[0].at[n - 1]
    fetches = [
        pltpu.make_async_copy(dy_ref, dy, dsem.at[0]),
        pltpu.make_async_copy(h_ref, dh_ref, dsem.at[1]),
    ]
    for fetch in fetches:
        fetch.start()
    scat.finish()
    summed = scat.block(0)
    for fetch in fetches:
        fetch.wait()
    gm_ref[...] = jnp.zeros_like(gm_ref)

    def back(part):
        dn, gain_part = norm_back_tile(dh_ref[part], gain_ref[...].astype(F32), summed[part].astype(F32))
        gm_ref[...] += gain_part
        dh = dy[part].astype(F32) + dn
        dh_ref[part] = dh
        summed[part] = dh.astype(BF16)

    tiles(rows, back)
    gather = Gather(grp, summed, branch_ref, send, recv, sem)
    steps = gather.begin()
    scat.drain()

    def save(j):
        return pltpu.make_async_copy(tile_n.at[j % 2], out_ref.at[at(j)], tsem.at[0, j % 2])

    def branch(j):
        @pl.when(j > 1)
        def _():
            save(j - 2).wait()

        tile_n[j % 2] = jnp.dot(act[at(j)], wd[...], preferred_element_type=F32).astype(BF16)
        save(j).start()

    near = functools.partial(spread_grad, grp, spread, ggate_ref, gategot_ref, 0, (1,))
    paced(n, branch, steps[:6] + [near] + steps[6:], 1)
    save(n - 2).wait()
    save(n - 1).wait()
    gather.finish()
    spread.wait()


def mlp(grp, normed, dy_all, wg, wu, wd_top, hidden, dy, gain, w_down, cid):
    rows, width = hidden.shape
    total = rows * grp.size
    n = len(grp.masks)
    units = wg.shape[1]
    gdown, ggate = sds((units, width), BF16), sds((width, units), BF16)
    return pl.pallas_call(
        functools.partial(mlp_kernel, grp),
        out_shape=[
            sds((rows, width), F32),
            sds((1, width), F32),
            gdown,
            ggate,
            ggate,
            sds((total, width), BF16),
            sds((total, width), BF16),
            got_shape(grp, gdown, 1),
            got_shape(grp, ggate, 0),
        ],
        in_specs=[ANY, ANY, VMEM, VMEM, ANY, ANY, ANY, VMEM, ANY],
        out_specs=[VMEM] * 5 + [ANY] * 4,
        scratch_shapes=[
            pltpu.VMEM((total, width), BF16),
            pltpu.VMEM((units, width), BF16),
            pltpu.VMEM((2, 2 * rows, width), BF16),
            pltpu.SemaphoreType.DMA((2, 2)),
            pltpu.VMEM((total, units), BF16),
            pltpu.VMEM((total, 2 * units), BF16),
            pltpu.VMEM((2, total, cols_of(total)), BF16),
            pltpu.SemaphoreType.DMA((2,)),
            pltpu.SemaphoreType.DMA((2,)),
        ]
        + scatter_scratch(grp, rows, width)
        + gather_scratch(grp)
        + spread_sems(grp, 4),
        compiler_params=params(cid),
        name="mlp",
    )(normed, dy_all, wg, wu, wd_top, hidden, dy, gain, w_down)


def fifth_kernel(grp, p_ref, h_ref, gup_ref, out_ref, up_ref, *rest):
    p, psem, rest = rest[0], rest[1], rest[2:]
    scat, rest = rest[:N_SCATTER], rest[N_SCATTER:]
    zs, zr = rest
    pltpu.make_async_copy(p_ref, p, psem).start()
    grp.greet()
    spread = Spread(grp, zs, zr)
    spread_grad(grp, spread, gup_ref, up_ref, 0)
    pltpu.make_async_copy(p_ref, p, psem).wait()
    acc = plain_scatter(grp, p, h_ref.shape[0], scat)

    def finish(rows):
        out_ref[rows] = (h_ref[rows] + acc[rows].astype(F32)).astype(BF16)

    tiles(h_ref.shape[0], finish)
    spread.wait()


def fifth(grp, part, hidden, grad_up, cid):
    rows, width = hidden.shape
    return pl.pallas_call(
        functools.partial(fifth_kernel, grp),
        out_shape=[sds((rows, width), BF16), got_shape(grp, grad_up, 0)],
        in_specs=[ANY, VMEM, ANY],
        out_specs=[VMEM, ANY],
        scratch_shapes=[pltpu.VMEM((rows * grp.size, width), BF16), pltpu.SemaphoreType.DMA]
        + scatter_scratch(grp, rows, width)
        + spread_sems(grp, 1),
        compiler_params=params(cid),
        name="fifth",
    )(part, hidden, grad_up)


def sixth_kernel(
    grp, p_ref, x_ref, dh_ref, gain_ref, gm_ref, gout_ref, gqkv_ref, tok_ref, gains_ref, o_ref, qkv_ref, *rest
):
    p, psem, rest = rest[0], rest[1], rest[2:]
    scat, rest = rest[:N_SCATTER], rest[N_SCATTER:]
    buf, gs, gr, zs, zr = rest
    pltpu.make_async_copy(p_ref, p, psem).start()
    grp.greet()
    spread = Spread(grp, zs, zr)
    spread_grad(grp, spread, gout_ref, o_ref, 1)
    spread_grad(grp, spread, gqkv_ref, qkv_ref, 0)
    pltpu.make_async_copy(p_ref, p, psem).wait()
    acc = plain_scatter(grp, p, x_ref.shape[0], scat)
    buf[0, 0:1] = jnp.zeros_like(gm_ref)
    buf[0, 1:2] = gm_ref[...]

    def back(rows):
        dn, gain_part = norm_back_tile(
            x_ref[rows].astype(F32), gain_ref[...].astype(F32), acc[rows].astype(F32)
        )
        buf[0, 0:1] += gain_part
        tok_ref[rows] = (dh_ref[rows] + dn).astype(BF16)

    tiles(x_ref.shape[0], back)
    sum_gains(grp, buf, gs, gr)
    gains_ref[...] = buf[buf.shape[0] - 1]
    spread.wait()


def sixth(grp, part, x, dh, gain, gain_m, grad_out, grad_qkv, cid):
    rows, width = x.shape
    n = len(grp.bits) - 1 + (grp.z_size - 1).bit_length()
    return pl.pallas_call(
        functools.partial(sixth_kernel, grp),
        out_shape=[
            sds((rows, width), BF16),
            sds((2, width), F32),
            got_shape(grp, grad_out, 1),
            got_shape(grp, grad_qkv, 0),
        ],
        in_specs=[ANY, VMEM, VMEM, VMEM, VMEM, ANY, ANY],
        out_specs=[VMEM, VMEM, ANY, ANY],
        scratch_shapes=[pltpu.VMEM((rows * grp.size, width), BF16), pltpu.SemaphoreType.DMA]
        + scatter_scratch(grp, rows, width)
        + [
            pltpu.VMEM((2 * n + 1, 2, width), F32),
            pltpu.SemaphoreType.DMA((n,)),
            pltpu.SemaphoreType.DMA((n,)),
        ]
        + spread_sems(grp, 2),
        compiler_params=params(cid),
        name="sixth",
    )(part, x, dh, gain, gain_m, grad_out, grad_qkv)


def swap_halves(value):
    half = HEAD // 2
    width = value.shape[1]
    pieces = []
    for at in range(0, width, HEAD):
        pieces.append(value[:, at + half : at + HEAD])
        pieces.append(value[:, at : at + half])
    if width % 128:
        return jnp.concatenate(pieces, axis=1)
    lane = lax.broadcasted_iota(jnp.int32, value.shape, 1)
    return jnp.where(
        lane % HEAD < half, pltpu.roll(value, width - half, 1), pltpu.roll(value, half, 1)
    )


QB = 256


def bands(length):
    for at in range(0, length, QB):
        first = max(0, at - SAMPLE)
        yield at, min(QB, length - at), first, at + min(QB, length - at) - first


def kept(start_row, at, size, first, width):
    key = first + lax.broadcasted_iota(jnp.int32, (width, size), 0)
    query = at + lax.broadcasted_iota(jnp.int32, (width, size), 1)
    return (key >= start_row) & (key <= query)


def attend_back_kernel(
    heads, q_ref, k_ref, v_ref, do_ref, lse_ref, cos_ref, sin_ref, start_ref, out_ref, dq, dk, dv
):
    wide = heads * HEAD
    length = q_ref.shape[0]
    dk[...] = jnp.zeros_like(dk)
    dv[...] = jnp.zeros_like(dv)
    for h in range(heads):
        lanes = slice(h * HEAD, (h + 1) * HEAD)
        for at, size, first, width in bands(length):
            query = q_ref[at : at + size, lanes]
            key = k_ref[first : first + width, lanes]
            value = v_ref[first : first + width, lanes]
            grad = do_ref[at : at + size, lanes]
            scores = dot_nt(key, query * BF16(HEAD**-0.5))
            mask = kept(start_ref[0, :, at : at + size], at, size, first, width)
            weights = jnp.where(
                mask, jnp.exp(jnp.where(mask, scores, -1e9) - lse_ref[0, h : h + 1, at : at + size]), 0.0
            )
            dv[first : first + width, lanes] += jnp.dot(
                weights.astype(BF16), grad, preferred_element_type=F32
            )
            grad_weights = dot_nt(value, grad)
            inner = jnp.sum(weights * grad_weights, axis=0, keepdims=True)
            grad_scores = (weights * (grad_weights - inner)).astype(BF16)
            dq[at : at + size, lanes] = dot_tn(grad_scores, key)
            dk[first : first + width, lanes] += jnp.dot(
                grad_scores, query, preferred_element_type=F32
            )

    @pl.loop(0, length // QB)
    def _(i):
        rows = pl.ds(pl.multiple_of(i * QB, QB), QB)
        cosine, sine = cos_ref[rows], sin_ref[rows]
        query, key = dq[rows] * HEAD**-0.5, dk[rows] * HEAD**-0.5
        out_ref[rows, :wide] = (query * cosine - swap_halves(query) * sine).astype(BF16)
        out_ref[rows, wide : 2 * wide] = (key * cosine - swap_halves(key) * sine).astype(BF16)
        out_ref[rows, 2 * wide :] = dv[rows].astype(BF16)


def attend_back(query, key, value, grad, lse, cosine, sine, start, heads):
    rows, _, length = start.shape
    wide = heads * HEAD

    def tall(width):
        return pl.BlockSpec((length, width), lambda r: (r, 0))

    return pl.pallas_call(
        functools.partial(attend_back_kernel, heads),
        grid=(rows,),
        out_shape=jax.ShapeDtypeStruct((rows * length, 3 * wide), BF16),
        in_specs=[tall(wide)] * 4
        + [pl.BlockSpec((1, heads, length), lambda r: (r, 0, 0)), tall(wide), tall(wide)]
        + [pl.BlockSpec((1, 1, length), lambda r: (r, 0, 0))],
        out_specs=tall(3 * wide),
        scratch_shapes=[pltpu.VMEM((length, wide), F32)] * 3,
        compiler_params=pltpu.CompilerParams(vmem_limit_bytes=48 << 20),
        name="attend_back",
    )(query, key, value, grad, lse, cosine, sine, start)


def finish_kernel(z_size, parts, z_ref, *refs):
    low = z_ref[0] % 2
    n = len(parts)
    owns, gots, outs = refs[:n], refs[n : 2 * n], list(refs[2 * n :])
    for own, got, (axis, count) in zip(owns, gots, parts):
        sums = [own[...].astype(F32), None]
        for m in range(1, z_size):
            term = got[m - 1].astype(F32)
            sums[m % 2] = term if sums[m % 2] is None else sums[m % 2] + term
        if axis == 0:
            out = outs.pop(0)
            out[low] = sums[0]
            out[1 - low] = sums[1]
            continue
        width = sums[0].shape[1] // count
        for i in range(count):
            out = outs.pop(0)
            for which, total in ((low, sums[0]), (1 - low, sums[1])):
                place = pl.ds(pl.multiple_of(which * width, width), width)
                out[:, place] = total[:, i * width : (i + 1) * width]


def finish(z_size, z, grads, gots, axes):
    steps = 4
    owns, blocks, outs, shapes = [], [], [], []
    for grad, got, (axis, count) in zip(grads, gots, axes):
        rows, cols = got.shape[1] // steps, got.shape[2]
        if axis == 0:
            owns.append(pl.BlockSpec((rows, cols), lambda i, z_ref: (i, z_ref[0])))
            outs.append(pl.BlockSpec((2, rows, cols), lambda i, z_ref: (0, i, 0)))
            shapes.append(sds((2, rows * steps, cols), F32))
        else:
            owns.append(pl.BlockSpec((rows, cols), lambda i, z_ref: (z_ref[0] * steps + i, 0)))
            wide = 2 * cols // count
            outs += [pl.BlockSpec((rows, wide), lambda i, z_ref: (i, 0))] * count
            shapes += [sds((rows * steps, wide), F32)] * count
        blocks.append(pl.BlockSpec((z_size - 1, rows, cols), lambda i, z_ref: (0, i, 0)))
    return pl.pallas_call(
        functools.partial(finish_kernel, z_size, axes),
        out_shape=shapes,
        grid_spec=pltpu.PrefetchScalarGridSpec(
            num_scalar_prefetch=1, grid=(steps,), in_specs=owns + blocks, out_specs=outs
        ),
        compiler_params=pltpu.CompilerParams(vmem_limit_bytes=56 << 20),
        name="finish",
    )(jnp.reshape(z, (1,)), *grads, *gots)


def shards(
    z_size,
    t_size,
    tokens,
    gain_attn,
    gain_mlp,
    w_query,
    w_key,
    w_value,
    w_out,
    w_gate,
    w_up,
    w_down,
    segment_ids,
    out_grad,
):
    grp = Group(z_size, t_size)
    z = lax.axis_index("fsdp")
    low = z % 2

    def deliver(grad, got, half_axis, axis, parts=1):
        size = grad.shape[axis] // z_size
        sums = [lax.dynamic_slice_in_dim(grad, z * size, size, axis).astype(F32), None]
        for m in range(1, z_size):
            term = got[m - 1].astype(F32)
            sums[m % 2] = term if sums[m % 2] is None else sums[m % 2] + term
        outs = []
        piece = sums[0].shape[half_axis] // parts
        for i in range(parts):
            a, b = (lax.slice_in_dim(s, i * piece, (i + 1) * piece, axis=half_axis) for s in sums)
            outs.append(
                jnp.where(
                    low == 0,
                    jnp.concatenate([a, b], axis=half_axis),
                    jnp.concatenate([b, a], axis=half_axis),
                )
            )
        return outs

    wide = w_query.shape[1] // 2
    heads = wide // HEAD

    gain_a = gain_attn[None, :]
    gain_m = gain_mlp[None, :]
    normed_a, wqkv, wo, start, cosine, sine = first(
        grp, low, tokens, gain_a, w_query, w_key, w_value, w_out, segment_ids, 0
    )
    query, key, value, attended, lse, hidden, normed_m, grad_all, wg, wu, wd_top = middle(
        grp,
        heads,
        normed_a,
        wqkv,
        wo,
        cosine,
        sine,
        start,
        out_grad,
        tokens,
        gain_m,
        w_gate,
        w_up,
        w_down,
        1,
    )
    grad_hidden, gain_m_part, grad_down, grad_wg, grad_wu, branch_all, out_part, got_down, got_gate = mlp(
        grp, normed_m, grad_all, wg, wu, wd_top, hidden, out_grad, gain_m, w_down, 3
    )
    if grp.size <= 16:
        output, tokens_grad, gains, grad_wout, grad_wqkv, got_up, got_out, got_qkv = last(
            grp, heads, branch_all, normed_a, out_part, grad_wu, query, key, value, attended, lse,
            cosine, sine, start, wqkv, wo, hidden, tokens, grad_hidden, gain_a, gain_m_part, 4,
        )
    else:
        output, got_up = fifth(grp, out_part, hidden, grad_wu, 4)
        grad_wout = dot_tn(attended, branch_all).astype(BF16)
        grad_attended = dot_nt(branch_all, wo).astype(BF16)
        grad_qkv = attend_back(query, key, value, grad_attended, lse, cosine, sine, start, heads)
        grad_wqkv = dot_tn(normed_a, grad_qkv).astype(BF16)
        grad_na = dot_nt(grad_qkv, wqkv).astype(BF16)
        tokens_grad, gains, got_out, got_qkv = sixth(
            grp, grad_na, tokens, grad_hidden, gain_a, gain_m_part, grad_wout, grad_wqkv, 5
        )
    grads = (grad_down, grad_wg, grad_wu, grad_wout, grad_wqkv)
    gots = (got_down, got_gate, got_up, got_out, got_qkv)
    axes = ((0, 1), (1, 1), (1, 1), (0, 1), (1, 3))
    if wide % LANES == 0:
        outs = finish(z_size, z, grads, gots, axes)
        down_out, out_out = (x.reshape(-1, x.shape[2]) for x in (outs[0], outs[3]))
        gate_out, up_out = outs[1:3]
        query_out, key_out, value_out = outs[4:]
    else:
        (down_out,) = deliver(grad_down, got_down, 0, 1)
        (gate_out,) = deliver(grad_wg, got_gate, 1, 0)
        (up_out,) = deliver(grad_wu, got_up, 1, 0)
        (out_out,) = deliver(grad_wout, got_out, 0, 1)
        query_out, key_out, value_out = deliver(grad_wqkv, got_qkv, 1, 0, 3)
    return (
        output,
        tokens_grad,
        gains[0],
        gains[1],
        query_out,
        key_out,
        value_out,
        out_out,
        gate_out,
        up_out,
        down_out,
    )


def solution(mesh):
    return jax.shard_map(
        functools.partial(shards, mesh.shape["fsdp"], mesh.shape["tensor"]),
        mesh=mesh,
        in_specs=(
            P(("fsdp", "tensor"), None),
            P(),
            P(),
            P("fsdp", "tensor"),
            P("fsdp", "tensor"),
            P("fsdp", "tensor"),
            P("tensor", "fsdp"),
            P("fsdp", "tensor"),
            P("fsdp", "tensor"),
            P("tensor", "fsdp"),
            P("fsdp", None),
            P(("fsdp", "tensor"), None),
        ),
        out_specs=(
            P(("fsdp", "tensor"), None),
            P(("fsdp", "tensor"), None),
            P(),
            P(),
            P("fsdp", "tensor"),
            P("fsdp", "tensor"),
            P("fsdp", "tensor"),
            P("tensor", "fsdp"),
            P("fsdp", "tensor"),
            P("fsdp", "tensor"),
            P("tensor", "fsdp"),
        ),
        check_vma=False,
    )
```

```python
import functools
import math

import jax
import jax.numpy as jnp
from jax import lax
from jax.experimental import pallas as pl
from jax.experimental.pallas import tpu as pltpu
from jax.sharding import PartitionSpec as P

HEAD = 64
SAMPLE = 512
EPS = 1e-05
LANES = 128
ROPE_BASE = 130000.0
MESH = pl.DeviceIdType.MESH
BF16 = jnp.bfloat16
F32 = jnp.float32
ANY = pl.BlockSpec(memory_space=pl.ANY)
VMEM = pl.BlockSpec(memory_space=pltpu.VMEM)


def flip(index, bit):
    return index + bit - 2 * bit * ((index // bit) % 2)


def dot_nt(left, right):
    return lax.dot_general(left, right, (((1,), (1,)), ((), ())), preferred_element_type=F32)


def dot_tn(left, right):
    return lax.dot_general(left, right, (((0,), (0,)), ((), ())), preferred_element_type=F32)


class Group:
    def __init__(self, z_size, t_size):
        self.z_size = z_size
        self.t_size = t_size
        self.size = 2 * t_size
        inner = []
        bit = 2
        while bit < t_size:
            inner.append(bit)
            bit *= 2
        self.core = 1
        self.pair = t_size
        self.orders = (tuple(inner) + (self.pair,), tuple(inner[::-1]) + (self.pair,))
        self.inner = (tuple(inner), tuple(inner[::-1]))
        self.bits = (self.core,) + tuple(inner) + (self.pair,)
        masks = [0]
        for b in self.orders[0]:
            masks = masks + [m + b for m in masks]
        self.masks = tuple(masks)
        self.far = tuple(range(2, z_size))

    def place(self):
        return lax.axis_index("fsdp"), lax.axis_index("tensor")

    def rank(self, mask=0):
        z, t = self.place()
        r = (z % 2) * self.t_size + t
        for b in self.bits:
            if mask & b:
                r = flip(r, b)
        return r

    def chip_at(self, j):
        chip = self.rank() // 2
        mask = len(self.masks) - 1 - j
        out = 0
        bit = 1
        while bit < len(self.masks):
            a, b = (chip // bit) % 2, (mask // bit) % 2
            out = out + (a + b - 2 * a * b) * bit
            bit *= 2
        return out

    def partner(self, bit):
        z, t = self.place()
        if bit == self.pair:
            return (flip(z, 1), t)
        return (z, flip(t, bit))

    def across(self, mask):
        z, t = self.place()
        bit = 1
        while bit < self.z_size:
            if mask & bit:
                z = flip(z, bit)
            bit *= 2
        return (z, t)

    def beside(self, mask):
        z, t = self.place()
        bit = 1
        while bit < self.t_size:
            if mask & bit:
                t = flip(t, bit)
            bit *= 2
        return (z, t)

    def greet(self, everyone=False):
        barrier = pltpu.get_barrier_semaphore()
        if everyone:
            peers = [self.beside(m) for m in range(1, self.t_size)]
        else:
            peers = [self.partner(b) for b in self.bits if b != self.pair]
        peers += [self.across(m) for m in range(1, self.z_size)]
        for peer in peers:
            pl.semaphore_signal(barrier, inc=1, device_id=peer, device_id_type=MESH)
        pl.semaphore_wait(barrier, len(peers))


def last_bit(mask, order):
    found = None
    for b in order:
        if mask & b:
            found = b
    return found


class Gather:
    def __init__(self, grp, x_ref, o_ref, send, recv, local):
        self.grp, self.x, self.o = grp, x_ref, o_ref
        self.send, self.recv = send, recv
        self.rows = x_ref.shape[0]
        self.half = self.rows // 2
        self.order = [(grp.pair,) + grp.inner[h] + (grp.core,) for h in range(2)]
        self.sent = []
        own = pl.ds(pl.multiple_of(grp.rank() * self.rows, self.rows), self.rows)
        self.own = pltpu.make_async_copy(x_ref, o_ref.at[own], local)

    def at(self, mask, h):
        first = self.grp.rank(mask) * self.rows + h * self.half
        return self.o.at[pl.ds(pl.multiple_of(first, self.half), self.half)]

    def copy(self, src, mask, h, key, bit):
        return pltpu.make_async_remote_copy(
            src_ref=src,
            dst_ref=self.at(mask, h),
            send_sem=self.send.at[h, key],
            recv_sem=self.recv.at[h, key],
            device_id=self.grp.partner(bit),
            device_id_type=MESH,
        )

    def forward(self, h, mask, bits=None):
        order = self.order[h]
        start = 0 if mask == 0 else order.index(last_bit(mask, order)) + 1
        for bit in order[start:] if bits is None else bits:
            self.own_copy(h, mask, bit).start()
            self.sent.append((h, mask, bit))

    def own_copy(self, h, mask, bit):
        src = self.x.at[pl.ds(h * self.half, self.half)] if mask == 0 else self.at(mask, h)
        return self.copy(src, mask, h, mask | bit, bit)

    def arrived(self, h, mask):
        bit = last_bit(mask, self.order[h])
        self.copy(self.at(mask, h), mask, h, mask, bit).wait_recv()

    def begin(self):
        self.own.start()
        for h in range(2):
            self.forward(h, 0, (self.grp.pair,))
        for k in range(1, len(self.order[0])):
            for h in range(2):
                self.forward(h, 0, (self.order[h][k],))
        grp = self.grp
        plain = sorted(
            (m for m in grp.masks if m), key=lambda m: (m & grp.pair, bin(m).count("1"))
        )
        if len(plain) > 3:
            plain.remove(grp.pair)
            plain.insert(2, grp.pair)

        def step(h, m):
            self.arrived(h, m)
            self.forward(h, m)

        return [
            functools.partial(step, h, m if h == 0 else mirror(grp, m))
            for m in plain
            for h in range(2)
        ]

    def finish(self):
        for m in self.grp.masks:
            for h in range(2):
                self.arrived(h, m | self.grp.core)
        self.own.wait()
        for sent in self.sent:
            self.own_copy(*sent).wait_send()


def mirror(grp, mask):
    out = mask & (grp.pair | grp.core)
    a, b = grp.inner
    for p, q in zip(a, b):
        if mask & p:
            out |= q
    return out


TILE = 16


def add_rows(dst, src, rows):
    @pl.loop(0, rows // TILE)
    def _(i):
        part = pl.ds(pl.multiple_of(i * TILE, TILE), TILE)
        dst[part] = (dst[part].astype(F32) + src[part].astype(F32)).astype(dst.dtype)


def scatter_scratch(grp, rows, width):
    n = len(grp.masks)
    return [
        pltpu.VMEM((n, rows, width), BF16),
        pltpu.VMEM((2, n - 1, rows // 2, width), BF16),
        pltpu.SemaphoreType.DMA((n,)),
        pltpu.SemaphoreType.DMA((n,)),
        pltpu.SemaphoreType.DMA((2, n)),
        pltpu.SemaphoreType.DMA((2, n)),
    ]


N_SCATTER = 6


class Scatter:
    def __init__(self, grp, p, rows, got, rbuf, csend, crecv, send, recv, own=None):
        self.grp, self.p, self.rows, self.half = grp, p, rows, rows // 2
        self.own = own
        self.got, self.rbuf = got, rbuf
        self.csend, self.crecv, self.send, self.recv = csend, crecv, send, recv
        self.index = {m: len(grp.masks) - 1 - m // 2 for m in grp.masks}
        self.started = []
        self.slots = []
        for h in range(2):
            s = {}
            order = grp.orders[h]
            for i in range(len(order)):
                later = order[i + 1 :]
                for m in grp.masks:
                    if all((not m & b) or b in later for b in order):
                        s[(i, m)] = len(s)
            self.slots.append(s)

    def masks(self, pair):
        chosen = [m for m in self.grp.masks if bool(m & self.grp.pair) == pair]
        return sorted(chosen, reverse=True)

    def begin_tile(self, j):
        _, t = self.grp.place()
        first = (self.grp.chip_at(j) * 2 + 1 - t % 2) * self.rows
        pltpu.make_async_remote_copy(
            src_ref=self.p.at[pl.ds(pl.multiple_of(first, self.rows), self.rows)],
            dst_ref=self.got.at[j],
            send_sem=self.csend.at[j],
            recv_sem=self.crecv.at[j],
            device_id=self.grp.partner(self.grp.core),
            device_id_type=MESH,
        ).start()

    def block(self, mask, h=None):
        if self.own is not None and not mask & self.grp.core:
            mine = self.own.at[self.index[mask]]
            return mine if h is None else mine.at[pl.ds(h * self.half, self.half)]
        first = self.grp.rank(mask) * self.rows
        if h is None:
            return self.p.at[pl.ds(pl.multiple_of(first, self.rows), self.rows)]
        return self.p.at[pl.ds(pl.multiple_of(first + h * self.half, self.half), self.half)]

    def core_copy(self, mask):
        i = self.index[mask]
        return pltpu.make_async_remote_copy(
            src_ref=self.block(mask | self.grp.core),
            dst_ref=self.got.at[i],
            send_sem=self.csend.at[i],
            recv_sem=self.crecv.at[i],
            device_id=self.grp.partner(self.grp.core),
            device_id_type=MESH,
        )

    def begin(self, masks):
        for m in masks:
            self.core_copy(m).start()

    def load(self, mask, sem):
        first = pl.multiple_of(self.grp.rank(mask) * self.rows, self.rows)
        i = self.index[mask]
        return pltpu.make_async_copy(self.p.at[pl.ds(first, self.rows)], self.own.at[i], sem.at[i])

    def core_step(self, mask):
        self.core_copy(mask).wait_recv()
        add_rows(self.block(mask), self.got.at[self.index[mask]], self.rows)
        for h in range(2):
            if mask & self.grp.orders[h][0]:
                self.ship(h, 0, mask)

    def link_copy(self, h, i, mask, k):
        return pltpu.make_async_remote_copy(
            src_ref=self.block(mask, h),
            dst_ref=self.rbuf.at[h, k],
            send_sem=self.send.at[h, k],
            recv_sem=self.recv.at[h, k],
            device_id=self.grp.partner(self.grp.orders[h][i]),
            device_id_type=MESH,
        )

    def ship(self, h, i, mask):
        self.out_copy(h, i, mask).start()
        self.started.append((h, i, mask))

    def out_copy(self, h, i, mask):
        return self.link_copy(h, i, mask, self.slots[h][(i, mask - self.grp.orders[h][i])])

    def take(self, h, i, mask):
        k = self.slots[h][(i, mask)]
        self.link_copy(h, i, mask, k).wait_recv()
        add_rows(self.block(mask, h), self.rbuf.at[h, k], self.half)

    def core_steps(self, pair):
        return [functools.partial(self.core_step, m) for m in self.masks(pair)]

    def link_steps(self, pair):
        steps = []
        for i in range(1, len(self.grp.orders[0])):
            for m in self.masks(pair):
                for h in range(2):
                    order = self.grp.orders[h]
                    mine = m if h == 0 else mirror(self.grp, m)
                    if any(mine & b for b in order[:i]):
                        continue

                    def step(h=h, i=i, mine=mine, order=order):
                        self.take(h, i - 1, mine)
                        if mine & order[i]:
                            self.ship(h, i, mine)

                    steps.append(step)
        return steps

    def finish(self):
        for h in range(2):
            self.take(h, len(self.grp.orders[h]) - 1, 0)

    def drain(self):
        for m in self.grp.masks:
            self.core_copy(m).wait_send()
        for sent in self.started:
            self.out_copy(*sent).wait_send()


def plain_scatter(grp, p, rows, refs):
    scat = Scatter(grp, p, rows, *refs)
    scat.begin(scat.masks(True) + scat.masks(False))
    run(scat.core_steps(True) + scat.core_steps(False))
    run(scat.link_steps(True) + scat.link_steps(False))
    scat.finish()
    scat.drain()
    return scat.block(0)


def run(*lists):
    for i in range(max(len(x) for x in lists)):
        for steps in lists:
            if i < len(steps):
                steps[i]()


class Spread:
    def __init__(self, grp, send, recv):
        self.grp, self.send, self.recv = grp, send, recv
        self.used = 0
        self.makers = []

    def to(self, mask, views):
        k = self.used
        self.used += 1

        def make():
            src, dst = views()
            if mask == 0:
                return pltpu.make_async_copy(src, dst, self.send.at[k])
            return pltpu.make_async_remote_copy(
                src_ref=src,
                dst_ref=dst,
                send_sem=self.send.at[k],
                recv_sem=self.recv.at[k],
                device_id=self.grp.across(mask),
                device_id_type=MESH,
            )

        make().start()
        self.makers.append(make)

    def wait(self):
        self.wait_first(len(self.makers))

    def wait_first(self, count):
        for make in self.makers[:count]:
            make().wait()
        self.makers = self.makers[count:]


def spread_sems(grp, parts):
    return [pltpu.SemaphoreType.DMA((grp.z_size * parts,))] * 2


def spread_weight(grp, spread, shard, whole, half_axis, at, masks=None):
    axis = 1 - half_axis
    mine, other = shard
    for m in grp.far + (0, 1) if masks is None else masks:

        def views(src=other if m % 2 else mine):
            z, _ = grp.place()
            size, width = src.shape[axis], src.shape[half_axis]
            place = pl.ds(pl.multiple_of(z * size, size), size)
            if axis == 0:
                return src, whole.at[place, at : at + width]
            return src, whole.at[at : at + width, place]

        spread.to(m, views)


def halves_of(grp, ref, axis):
    z, _ = grp.place()
    size = ref.shape[axis] // 2
    out = []
    for which in (z % 2, 1 - z % 2):
        part = pl.ds(pl.multiple_of(which * size, size), size)
        out.append(ref.at[:, part] if axis == 1 else ref.at[part])
    return out


def weight_jobs(grp, spread, shard, whole, half_axis, pieces):
    axis = 1 - half_axis
    mine, other = shard
    jobs = {m: [] for m in range(grp.z_size)}
    for i in range(pieces):
        for m in range(grp.z_size):

            def views(i=i, src=other if m % 2 else mine):
                z, _ = grp.place()
                size, width = src.shape[0] // pieces, src.shape[1]
                piece = src.at[pl.ds(i * size, size)]
                if axis == 0:
                    first = pl.multiple_of(z * (size * pieces) + i * size, size)
                    return piece, whole.at[pl.ds(first, size)]
                place = pl.ds(pl.multiple_of(z * width, width), width)
                return piece, whole.at[pl.ds(i * size, size), place]

            jobs[m].append(functools.partial(spread.to, m, views))
    return by_distance(grp, jobs)


def grad_jobs(grp, spread, grad, got, axis, pieces):
    jobs = {m: [] for m in range(1, grp.z_size)}
    for i in range(pieces):
        for m in range(1, grp.z_size):

            def views(i=i, m=m):
                place = grp.across(m)[0]
                size = got.shape[1] // pieces
                land = got.at[m - 1, pl.ds(i * size, size)]
                if axis == 0:
                    first = pl.multiple_of(place * (size * pieces) + i * size, size)
                    return grad.at[pl.ds(first, size)], land
                width = got.shape[2]
                part = pl.ds(pl.multiple_of(place * width, width), width)
                return grad.at[pl.ds(i * size, size), part], land

            jobs[m].append(functools.partial(spread.to, m, views))
    return by_distance(grp, jobs)


def by_distance(grp, jobs):
    far = [job for jobs_i in zip(*(jobs[m] for m in grp.far)) for job in jobs_i]
    near = [job for jobs_i in zip(*(jobs[m] for m in (1, 0) if m in jobs)) for job in jobs_i]
    return far, near


def mixed(steps, jobs, first=0):
    out = list(steps[:first])
    tail = steps[first:]
    done = 0
    for i, step in enumerate(tail):
        upto = (i + 1) * len(jobs) // len(tail)
        out.append(functools.partial(run, [step] + jobs[done:upto]))
        done = upto
    return out + (jobs if not tail else [])


PIECES = 1


def top_rows(views, which):
    size = views[0].shape[0] // 2
    return [v.at[pl.ds(which * size, size)] for v in views]


def spread_grad(grp, spread, grad, got, axis, masks=None):
    for m in grp.far + (1,) if masks is None else masks:

        def views(m=m):
            size = grad.shape[axis] // grp.z_size
            part = pl.ds(pl.multiple_of(grp.across(m)[0] * size, size), size)
            return (grad.at[part] if axis == 0 else grad.at[:, part]), got.at[m - 1]

        spread.to(m, views)


def staged_gather(gather, after_pair):
    steps = gather.begin()
    cut = 6 if len(steps) > 6 else len(steps)
    run(steps[:cut])
    after_pair()
    run(steps[cut:])
    gather.finish()


def tiles(rows, body):
    @pl.loop(0, rows // TILE)
    def _(i):
        body(pl.ds(pl.multiple_of(i * TILE, TILE), TILE))


def norm_scale(value):
    return lax.rsqrt(jnp.mean(value * value, axis=-1, keepdims=True) + EPS)


def gather_scratch(grp):
    return [
        pltpu.SemaphoreType.DMA((2, grp.size)),
        pltpu.SemaphoreType.DMA((2, grp.size)),
        pltpu.SemaphoreType.DMA,
    ]


def params(cid):
    return pltpu.CompilerParams(
        collective_id=cid, has_side_effects=True, vmem_limit_bytes=61952 << 10
    )


def sds(shape, dtype):
    return jax.ShapeDtypeStruct(shape, dtype)


def weight_views(grp, refs, axis, presliced):
    if presliced:
        return [(refs[2 * i], refs[2 * i + 1]) for i in range(len(refs) // 2)]
    return [tuple(halves_of(grp, r, axis)) for r in refs]


def shard_args(low, shards_, axis):
    aligned = shards_[0].shape[axis] // 2 % (128 if axis == 1 else 16) == 0
    if aligned:
        return False, list(shards_)
    out = []
    for w in shards_:
        size = w.shape[axis] // 2
        out += [
            lax.dynamic_slice_in_dim(w, low * size, size, axis),
            lax.dynamic_slice_in_dim(w, (1 - low) * size, size, axis),
        ]
    return True, out


def first_kernel(grp, flags, n_qkv, x_ref, gain_ref, *rest):
    pre_qkv, pre_o = flags
    qkv_refs, rest = rest[:n_qkv], rest[n_qkv:]
    n_o = 2 if pre_o else 1
    o_refs, rest = rest[:n_o], rest[n_o:]
    seg_ref, all_ref, wqkv_ref, wo_ref, start_ref, cos_ref, sin_ref, local, ids, send, recv, sem, zs, zr = rest
    grp.greet()
    spread = Spread(grp, zs, zr)
    z, _ = grp.place()
    spread.to(0, lambda: (seg_ref, ids.at[z % 2]))
    spread.to(1, lambda: (seg_ref, ids.at[z % 2]))

    def weights(masks):
        at = 0
        for pair in weight_views(grp, qkv_refs, 1, pre_qkv):
            spread_weight(grp, spread, pair, wqkv_ref, 1, at, masks)
            at += pair[0].shape[1]
        for pair in weight_views(grp, o_refs, 0, pre_o):
            spread_weight(grp, spread, pair, wo_ref, 0, 0, masks)

    def norm(rows):
        x = x_ref[rows].astype(F32)
        local[rows] = (x * norm_scale(x) * gain_ref[...].astype(F32)).astype(BF16)

    tiles(x_ref.shape[0], norm)
    gather = Gather(grp, local, all_ref, send, recv, sem)
    steps = gather.begin()
    weights(grp.far + (0,))
    spread.wait_first(2)
    places(ids, start_ref, cos_ref, sin_ref)
    run(steps[:6])
    weights((1,))
    run(steps[6:] or [lambda: None])
    gather.finish()
    spread.wait()


def places(ids, start_ref, cos_ref, sin_ref):
    planes, rows, length = ids.shape
    wide = cos_ref.shape[1]
    place = lax.broadcasted_iota(jnp.int32, (1, length), 1)
    lane = lax.broadcasted_iota(jnp.int32, (LANES, LANES), 1)
    pair = (lane % (HEAD // 2)).astype(F32)
    inverse = jnp.exp(pair * (-2.0 / HEAD) * math.log(ROPE_BASE))
    sign = jnp.where(lane % HEAD < HEAD // 2, -1.0, 1.0)
    for a in range(planes):
        for r in range(rows):
            row = a * rows + r
            own = ids[a, r : r + 1]
            change = (place == 0) | (own != pltpu.roll(own, 1, 1))
            start = jnp.where(change, place, 0)
            step = 1
            while step < length:
                start = jnp.maximum(start, jnp.where(place >= step, pltpu.roll(start, step, 1), 0))
                step *= 2
            start_ref[row] = start

    @pl.loop(0, planes * rows)
    def _(row):
        @pl.loop(0, length // LANES)
        def _(c):
            here = pl.ds(pl.multiple_of(c * LANES, LANES), LANES)
            token = c * LANES + lax.broadcasted_iota(jnp.int32, (1, LANES), 1)
            position = (token - start_ref[row, :, here]).astype(F32)
            angle = jnp.broadcast_to(position, (LANES, LANES)).T * inverse
            there = pl.ds(pl.multiple_of(row * length + c * LANES, LANES), LANES)
            cos_ref[there] = jnp.cos(angle)[:, :wide]
            sin_ref[there] = (sign * jnp.sin(angle))[:, :wide]


def first(grp, low, x, gain, w_query, w_key, w_value, w_out, ids, cid):
    pre_qkv, qkv = shard_args(low, (w_query, w_key, w_value), 1)
    pre_o, out = shard_args(low, (w_out,), 0)
    rows, width = x.shape
    if pre_qkv:
        qkv = [jnp.concatenate(qkv[i::2], axis=1) for i in range(2)]
    deep = w_query.shape[0] * grp.z_size
    thin = 3 * w_query.shape[1] // 2
    table = sds((2 * ids.shape[0] * ids.shape[1], thin // 3), F32)
    return pl.pallas_call(
        functools.partial(first_kernel, grp, (pre_qkv, pre_o), len(qkv)),
        out_shape=[
            sds((rows * grp.size, width), BF16),
            sds((deep, thin), BF16),
            sds((w_out.shape[0] // 2, w_out.shape[1] * grp.z_size), BF16),
            sds((2 * ids.shape[0], 1, ids.shape[1]), jnp.int32),
            table,
            table,
        ],
        in_specs=[VMEM, VMEM] + [ANY] * (len(qkv) + len(out)) + [VMEM],
        out_specs=[ANY] * 3 + [VMEM] * 3,
        scratch_shapes=[
            pltpu.VMEM((rows, width), BF16),
            pltpu.VMEM((2,) + ids.shape, jnp.int32),
        ]
        + gather_scratch(grp)
        + spread_sems(grp, 5),
        compiler_params=params(cid),
        name="first",
    )(x, gain, *qkv, *out, ids)


def attend_rows(length, heads, q_ref, k_ref, v_ref, start_ref, o_ref, lse_ref, row):
    base = row * length

    def band(h, at, first, width, size):
        lanes = slice(h * HEAD, (h + 1) * HEAD)
        mine = pl.ds(pl.multiple_of(base + at, QB), size)
        keys = pl.ds(pl.multiple_of(base + first, QB), width)
        cols = pl.ds(pl.multiple_of(at, QB), size)
        query = q_ref[mine, lanes] * BF16(HEAD**-0.5)
        scores = dot_nt(k_ref[keys, lanes], query)
        mask = kept(start_ref[row, :, cols], at, size, first, width)
        scores = jnp.where(mask, scores, -1e9)
        top = jnp.max(scores, axis=0, keepdims=True)
        expo = jnp.exp(scores - top)
        total = jnp.sum(expo, axis=0, keepdims=True)
        weights = (expo * (1.0 / total)).astype(BF16)
        o_ref[mine, lanes] = dot_tn(weights, v_ref[keys, lanes]).astype(BF16)
        lse_ref[row, h : h + 1, cols] = top + jnp.log(total)

    return banded(length, heads, band)


def banded(length, heads, band):
    parts = []
    for h in range(heads):
        whole = [b for b in bands(length) if b[3] == SAMPLE + QB]
        for at, size, first, width in bands(length):
            if width != SAMPLE + QB:
                parts.append(functools.partial(band, h, at, first, width, size))

        def loop(h=h, whole=whole):
            @pl.loop(0, len(whole))
            def _(i):
                at = whole[0][0] + i * QB
                band(h, at, at - SAMPLE, SAMPLE + QB, QB)

        if whole:
            parts.append(loop)
    return parts


def middle_kernel(
    grp,
    heads,
    na_ref,
    wqkv_ref,
    wo_ref,
    cos_ref,
    sin_ref,
    start_ref,
    dy_ref,
    x_ref,
    gain_ref,
    gate_ref,
    up_ref,
    down_ref,
    q_ref,
    k_ref,
    v_ref,
    o_ref,
    lse_ref,
    h_ref,
    nm_ref,
    dyall_ref,
    wg_ref,
    wu_ref,
    wd_ref,
    p,
    rowbuf,
    rowsem,
    local,
    *rest,
):
    scat_refs, rest = rest[:N_SCATTER], rest[N_SCATTER:]
    dsend, drecv, dsem, send, recv, sem, zs, zr = rest
    rows_all, _, length = start_ref.shape
    wide = heads * HEAD
    z, _ = grp.place()
    n = rows_all // 2
    rows = [(1 - z % 2) * n + j for j in range(n)] + [(z % 2) * n + j for j in range(n)]

    blocks = length // QB

    def load(i, j):
        part = pl.ds(pl.multiple_of(rows[i] * length + j * QB, QB), QB)
        return pltpu.make_async_copy(na_ref.at[part], rowbuf.at[j % 2], rowsem.at[j % 2])

    load(0, 0).start()
    grp.greet()
    spread = Spread(grp, zs, zr)
    views = [
        (halves_of(grp, gate_ref, 1), wg_ref, 1),
        (halves_of(grp, up_ref, 1), wu_ref, 1),
        (top_rows(halves_of(grp, down_ref, 0), 0), wd_ref, 0),
    ]
    outer = Gather(grp, dy_ref, dyall_ref, dsend, drecv, dsem)
    outer_steps = outer.begin()
    for masks in (grp.far, (0, 1)):
        for pair, whole, axis in views:
            spread_weight(grp, spread, pair, whole, axis, 0, masks)
    scat = Scatter(grp, p, x_ref.shape[0], *scat_refs)

    def project(i):
        base = rows[i] * length
        if i:
            load(i, 0).start()

        @pl.loop(0, blocks)
        def _(j):
            @pl.when(j + 1 < blocks)
            def _():
                load(i, j + 1).start()

            load(i, j).wait()
            there = pl.ds(pl.multiple_of(base + j * QB, QB), QB)
            qkv = jnp.dot(rowbuf[j % 2], wqkv_ref[...], preferred_element_type=F32)
            cosine, sine = cos_ref[there], sin_ref[there]
            query, key = qkv[:, :wide], qkv[:, wide : 2 * wide]
            q_ref[there] = (query * cosine + swap_halves(query) * sine).astype(BF16)
            k_ref[there] = (key * cosine + swap_halves(key) * sine).astype(BF16)
            v_ref[there] = qkv[:, 2 * wide :].astype(BF16)

    def branch(i):
        base = rows[i] * length

        @pl.loop(0, length // QB)
        def _(j):
            there = pl.ds(pl.multiple_of(base + j * QB, QB), QB)
            p[there] = jnp.dot(o_ref[there], wo_ref[...], preferred_element_type=F32).astype(BF16)

    def parts(i):
        return (
            [functools.partial(project, i)]
            + attend_rows(length, heads, q_ref, k_ref, v_ref, start_ref, o_ref, lse_ref, rows[i])
            + [functools.partial(branch, i)]
        )

    for i in range(n):
        run(parts(i))
    scat.begin(scat.masks(True))
    run(outer_steps[:4])
    pair_steps = scat.core_steps(True)
    for i in range(n, 2 * n):
        todo = parts(i)
        run(todo, pair_steps)
        pair_steps = pair_steps[len(todo) :]
    scat.begin(scat.masks(False))
    run(pair_steps or [lambda: None])
    run(scat.core_steps(False), outer_steps[4:8])
    run(scat.link_steps(True), outer_steps[8:])
    run(scat.link_steps(False))
    scat.finish()
    summed = scat.block(0)

    def norm(part):
        h = x_ref[part].astype(F32) + summed[part].astype(F32)
        h_ref[part] = h
        local[part] = (h * norm_scale(h) * gain_ref[...].astype(F32)).astype(BF16)

    tiles(x_ref.shape[0], norm)
    gather = Gather(grp, local, nm_ref, send, recv, sem)
    run(gather.begin())
    scat.drain()
    outer.finish()
    gather.finish()
    spread.wait()


def middle(grp, heads, normed, wqkv, wo, cosine, sine, start, dy, x, gain, w_gate, w_up, w_down, cid):
    rows, width = x.shape
    total = rows * grp.size
    wide = heads * HEAD
    rows_all, _, length = start.shape
    thin = sds((total, wide), BF16)
    return pl.pallas_call(
        functools.partial(middle_kernel, grp, heads),
        out_shape=[thin] * 4
        + [
            sds((rows_all, heads, length), F32),
            sds((rows, width), F32),
            sds((total, width), BF16),
            sds((total, width), BF16),
            sds((w_gate.shape[0] * grp.z_size, w_gate.shape[1] // 2), BF16),
            sds((w_up.shape[0] * grp.z_size, w_up.shape[1] // 2), BF16),
            sds((w_down.shape[0] // 4, w_down.shape[1] * grp.z_size), BF16),
        ],
        in_specs=[ANY, VMEM, VMEM, VMEM, VMEM, VMEM, ANY, VMEM, VMEM, ANY, ANY, ANY],
        out_specs=[VMEM] * 6 + [ANY] * 5,
        scratch_shapes=[
            pltpu.VMEM((total, width), BF16),
            pltpu.VMEM((2, QB, width), BF16),
            pltpu.SemaphoreType.DMA((2,)),
            pltpu.VMEM((rows, width), BF16),
        ]
        + scatter_scratch(grp, rows, width)
        + gather_scratch(grp)
        + gather_scratch(grp)
        + spread_sems(grp, 3 * PIECES),
        compiler_params=params(cid),
        name="middle",
    )(normed, wqkv, wo, cosine, sine, start, dy, x, gain, w_gate, w_up, w_down)


def norm_back_tile(value, gain, grad):
    scale = norm_scale(value)
    scaled = grad * gain
    inner = jnp.mean(value * scaled, axis=-1, keepdims=True)
    back = scale * scaled - value * (scale * scale * scale * inner)
    return back, jnp.sum(grad * value * scale, axis=0, keepdims=True)


def weave(parts, steps, each=1):
    for part in parts:
        part()
        for step in steps[:each]:
            step()
        steps = steps[each:]
    return steps


def last_kernel(
    grp,
    heads,
    branch_ref,
    na_ref,
    part_ref,
    gup_ref,
    q_ref,
    k_ref,
    v_ref,
    o_ref,
    lse_ref,
    cos_ref,
    sin_ref,
    start_ref,
    wqkv_ref,
    wo_ref,
    h_ref,
    x_ref,
    dh_ref,
    gain_ref,
    gm_ref,
    out_ref,
    tok_ref,
    gains_ref,
    gout_ref,
    gqkv_ref,
    upgot_ref,
    outgot_ref,
    qkvgot_ref,
    p,
    own,
    ownsem,
    rowbuf,
    rowsem,
    cols,
    csem,
    do,
    dqkv,
    dq,
    dk,
    dv,
    gacc,
    buf,
    gs,
    gr,
    *rest,
):
    na_scat, rest = rest[:N_SCATTER], rest[N_SCATTER:]
    out_scat, rest = rest[:N_SCATTER], rest[N_SCATTER:]
    zs, zr = rest
    rows_all, _, length = start_ref.shape
    rows, width = h_ref.shape
    wide = heads * HEAD
    z, _ = grp.place()
    n = rows_all // 2
    order = [(1 - z % 2) * n + j for j in range(n)] + [(z % 2) * n + j for j in range(n)]
    blocks = length // QB
    step = cols.shape[2]

    def load(i, j):
        part = pl.ds(pl.multiple_of(order[i] * length + j * QB, QB), QB)
        return pltpu.make_async_copy(branch_ref.at[part], rowbuf.at[j % 2], rowsem.at[j % 2])

    def load_cols(c):
        part = pl.ds(pl.multiple_of(c * step, step), step)
        return pltpu.make_async_copy(na_ref.at[:, part], cols.at[c % 2], csem.at[c % 2])

    load(0, 0).start()
    load_cols(0).start()
    outer = Scatter(grp, part_ref, rows, *out_scat, own=own)
    for m in outer.masks(True) + outer.masks(False):
        outer.load(m, ownsem).start()
    grp.greet(everyone=True)
    outer.begin(outer.masks(True) + outer.masks(False))
    spread = Spread(grp, zs, zr)
    spread_grad(grp, spread, gup_ref, upgot_ref, 0)
    scat = Scatter(grp, p, rows, *na_scat)
    gacc[...] = jnp.zeros_like(gacc)

    def outer_core(m):
        outer.load(m, ownsem).wait()
        outer.core_step(m)

    outer_steps = [
        functools.partial(outer_core, m) for m in outer.masks(True) + outer.masks(False)
    ]
    outer_steps += outer.link_steps(True) + outer.link_steps(False)

    def prepare(i):
        base = order[i] * length
        if i:
            load(i, 0).start()
        dk[...] = jnp.zeros_like(dk)
        dv[...] = jnp.zeros_like(dv)

        @pl.loop(0, blocks)
        def _(j):
            @pl.when(j + 1 < blocks)
            def _():
                load(i, j + 1).start()

            load(i, j).wait()
            there = pl.ds(pl.multiple_of(base + j * QB, QB), QB)
            here = pl.ds(pl.multiple_of(j * QB, QB), QB)
            branch = rowbuf[j % 2]
            do[here] = dot_nt(branch, wo_ref[...]).astype(BF16)
            gacc[...] += dot_tn(o_ref[there], branch)

    def banded_back(i):
        row = order[i]
        base = row * length

        def band(h, at, first, width, size):
            lanes = slice(h * HEAD, (h + 1) * HEAD)
            cols_at = pl.ds(pl.multiple_of(at, QB), size)
            keys_at = pl.ds(pl.multiple_of(first, QB), width)
            mine = pl.ds(pl.multiple_of(base + at, QB), size)
            keys = pl.ds(pl.multiple_of(base + first, QB), width)
            query = q_ref[mine, lanes]
            key = k_ref[keys, lanes]
            grad = do[cols_at, lanes]
            scores = dot_nt(key, query * BF16(HEAD**-0.5))
            mask = kept(start_ref[row, :, cols_at], at, size, first, width)
            scores = jnp.where(mask, scores, -1e9)
            weights = jnp.exp(scores - lse_ref[row, h : h + 1, cols_at])
            dv[keys_at, lanes] += jnp.dot(weights.astype(BF16), grad, preferred_element_type=F32)
            grad_weights = dot_nt(v_ref[keys, lanes], grad)
            inner = jnp.sum(weights * grad_weights, axis=0, keepdims=True)
            grad_scores = (weights * (grad_weights - inner)).astype(BF16)
            dq[cols_at, lanes] = dot_tn(grad_scores, key)
            dk[keys_at, lanes] += jnp.dot(grad_scores, query, preferred_element_type=F32)

        return banded(length, heads, band)

    def turn_back(i):
        base = order[i] * length

        @pl.loop(0, blocks)
        def _(j):
            there = pl.ds(pl.multiple_of(base + j * QB, QB), QB)
            here = pl.ds(pl.multiple_of(j * QB, QB), QB)
            cosine, sine = cos_ref[there], sin_ref[there]
            query, key = dq[here] * HEAD**-0.5, dk[here] * HEAD**-0.5
            dqkv[there, :wide] = (query * cosine - swap_halves(query) * sine).astype(BF16)
            dqkv[there, wide : 2 * wide] = (key * cosine - swap_halves(key) * sine).astype(BF16)
            dqkv[there, 2 * wide :] = dv[here].astype(BF16)
            p[there] = dot_nt(dqkv[there], wqkv_ref[...]).astype(BF16)

    def parts(i):
        return (
            [functools.partial(prepare, i)] + banded_back(i) + [functools.partial(turn_back, i)]
        )

    for i in range(n):
        outer_steps = weave(parts(i), outer_steps)
    scat.begin(scat.masks(True))
    pair_core = scat.core_steps(True)
    for i in range(n, 2 * n):
        todo = parts(i)
        merged = []
        for a in range(len(todo)):
            merged += [x[a] for x in (outer_steps, pair_core) if a < len(x)]
        outer_steps, pair_core = outer_steps[len(todo) :], pair_core[len(todo) :]
        merged = weave(todo, merged, 2)
        outer_steps = merged + outer_steps
    scat.begin(scat.masks(False))
    gout_ref[...] = gacc[...].astype(BF16)
    spread_grad(grp, spread, gout_ref, outgot_ref, 1)

    def qkv_cols(c):
        @pl.when(c + 1 < width // step)
        def _():
            load_cols(c + 1).start()

        load_cols(c).wait()
        part = pl.ds(pl.multiple_of(c * step, step), step)
        gqkv_ref[part] = dot_tn(cols[c % 2], dqkv[...]).astype(BF16)

    paced(width // step, qkv_cols, outer_steps + pair_core + scat.core_steps(False))
    spread_grad(grp, spread, gqkv_ref, qkvgot_ref, 0)
    run(scat.link_steps(True) + scat.link_steps(False))
    outer.finish()
    whole = outer.block(0)

    def output(part):
        out_ref[part] = (h_ref[part] + whole[part].astype(F32)).astype(BF16)

    tiles(rows, output)
    scat.finish()
    summed = scat.block(0)
    buf[0, 0:1] = jnp.zeros_like(gm_ref)
    buf[0, 1:2] = gm_ref[...]

    def back(part):
        dn, gain_part = norm_back_tile(
            x_ref[part].astype(F32), gain_ref[...].astype(F32), summed[part].astype(F32)
        )
        buf[0, 0:1] += gain_part
        tok_ref[part] = (dh_ref[part] + dn).astype(BF16)

    tiles(rows, back)
    sum_gains(grp, buf, gs, gr)
    gains_ref[...] = buf[buf.shape[0] - 1]
    outer.drain()
    scat.drain()
    spread.wait()


def gain_scratch(grp, width):
    n = grp.t_size + grp.z_size - 2
    return [
        pltpu.VMEM((grp.t_size + grp.z_size + 3, 2, width), F32),
        pltpu.SemaphoreType.DMA((n,)),
        pltpu.SemaphoreType.DMA((n,)),
    ]


def sum_gains(grp, buf, send, recv):
    z, t = grp.place()
    at, sem = 0, 0
    for index, size, peer in ((t, grp.t_size, grp.beside), (z, grp.z_size, grp.across)):
        copies = []
        for m in range(1, size):
            c = pltpu.make_async_remote_copy(
                src_ref=buf.at[at],
                dst_ref=buf.at[at + 1 + index],
                send_sem=send.at[sem],
                recv_sem=recv.at[sem],
                device_id=peer(m),
                device_id_type=MESH,
            )
            c.start()
            copies.append(c)
            sem += 1
        buf[at + 1 + index] = buf[at]
        for c in copies:
            c.wait()
        total = buf[at + 1]
        for i in range(1, size):
            total = total + buf[at + 1 + i]
        at += size + 1
        buf[at] = total


def last(
    grp, heads, branch, normed, part, grad_up, query, key, value, attended, lse, cosine, sine, start,
    wqkv, wo, hidden, x, dh, gain, gain_m, cid,
):
    rows, width = x.shape
    total = rows * grp.size
    wide = heads * HEAD
    length = start.shape[2]
    n = len(grp.masks)
    gout, gqkv = sds((wide, width), BF16), sds((width, 3 * wide), BF16)
    return pl.pallas_call(
        functools.partial(last_kernel, grp, heads),
        out_shape=[
            sds((rows, width), BF16),
            sds((rows, width), BF16),
            sds((2, width), F32),
            gout,
            gqkv,
            got_shape(grp, grad_up, 0),
            got_shape(grp, gout, 1),
            got_shape(grp, gqkv, 0),
        ],
        in_specs=[ANY] * 4 + [VMEM] * 15,
        out_specs=[VMEM] * 5 + [ANY] * 3,
        scratch_shapes=[
            pltpu.VMEM((total, width), BF16),
            pltpu.VMEM((n, rows, width), BF16),
            pltpu.SemaphoreType.DMA((n,)),
            pltpu.VMEM((2, QB, width), BF16),
            pltpu.SemaphoreType.DMA((2,)),
            pltpu.VMEM((2, total, cols_of(total)), BF16),
            pltpu.SemaphoreType.DMA((2,)),
            pltpu.VMEM((length, wide), BF16),
            pltpu.VMEM((total, 3 * wide), BF16),
            pltpu.VMEM((length, wide), F32),
            pltpu.VMEM((length, wide), F32),
            pltpu.VMEM((length, wide), F32),
            pltpu.VMEM((wide, width), F32),
        ]
        + gain_scratch(grp, width)
        + scatter_scratch(grp, rows, width)
        + scatter_scratch(grp, rows, width)
        + spread_sems(grp, 3 * PIECES),
        compiler_params=params(cid),
        name="last",
    )(
        branch, normed, part, grad_up, query, key, value, attended, lse, cosine, sine, start,
        wqkv, wo, hidden, x, dh, gain, gain_m,
    )


def got_shape(grp, grad, axis):
    shape = list(grad.shape)
    shape[axis] //= grp.z_size
    return sds((grp.z_size - 1, *shape), BF16)


def paced(count, body, steps, first=0):
    turns = count - first
    each = -(-len(steps) // turns) if steps else 0

    @pl.loop(0, count)
    def _(i):
        body(i)
        for k in range(turns):
            mine = steps[k * each : (k + 1) * each]
            if mine:

                @pl.when(i == first + k)
                def _(mine=mine):
                    for step in mine:
                        step()


def cols_of(total):
    return max(128, 655360 // total // 128 * 128)


def mlp_kernel(
    grp,
    nm_ref,
    dyall_ref,
    wg_ref,
    wu_ref,
    top_ref,
    h_ref,
    dy_ref,
    gain_ref,
    down_ref,
    dh_ref,
    gm_ref,
    gdown_ref,
    ggate_ref,
    gup_ref,
    branch_ref,
    out_ref,
    downgot_ref,
    gategot_ref,
    p,
    wd,
    tile_n,
    tsem,
    act,
    dgu,
    cols,
    csem,
    dsem,
    *rest,
):
    scat_refs, rest = rest[:N_SCATTER], rest[N_SCATTER:]
    send, recv, sem, zs, zr = rest
    rows, width = h_ref.shape
    size = 2 * rows
    n = len(grp.masks)
    units = wd.shape[0]
    step = cols.shape[2]

    def at(j):
        return pl.ds(pl.multiple_of(grp.chip_at(j) * size, size), size)

    def load(src, buf, k, j):
        return pltpu.make_async_copy(src.at[at(j)], buf.at[j % 2], tsem.at[k, j % 2])

    def load_cols(src, c):
        part = pl.ds(pl.multiple_of(c * step, step), step)
        return pltpu.make_async_copy(src.at[:, part], cols.at[c % 2], csem.at[c % 2])

    load(nm_ref, tile_n, 0, 0).start()
    grp.greet()
    spread = Spread(grp, zs, zr)
    spread.to(0, lambda: (top_ref, wd.at[pl.ds(0, units // 2)]))
    spread_weight(
        grp,
        spread,
        top_rows(halves_of(grp, down_ref, 0), 1),
        wd.at[pl.ds(units // 2, units // 2)],
        0,
        0,
    )

    def forward(j):
        @pl.when(j + 1 < n)
        def _():
            load(nm_ref, tile_n, 0, j + 1).start()

        load(nm_ref, tile_n, 0, j).wait()
        normed = tile_n[j % 2]
        gate = jnp.dot(normed, wg_ref[...], preferred_element_type=F32)
        up = jnp.dot(normed, wu_ref[...], preferred_element_type=F32)
        here = at(j)
        act[here] = (gate * jax.nn.sigmoid(gate) * up).astype(BF16)
        dgu[here, :units] = gate.astype(BF16)
        dgu[here, units:] = up.astype(BF16)

    load_cols(dyall_ref, 0).start()
    paced(n, forward, [])
    blocks = width // step

    def down_cols(c):
        @pl.when(c + 1 < blocks)
        def _():
            load_cols(dyall_ref, c + 1).start()

        load_cols(dyall_ref, c).wait()
        part = pl.ds(pl.multiple_of(c * step, step), step)
        gdown_ref[:, part] = dot_tn(cols[c % 2], act[...]).T.astype(BF16)

    load(dyall_ref, tile_n, 1, 0).start()
    paced(blocks, down_cols, [])
    spread.wait()
    spread_grad(grp, spread, gdown_ref, downgot_ref, 1)

    scat = Scatter(grp, p, rows, *scat_refs)
    chunk = min(512, width)

    def backward(j):
        @pl.when(j + 1 < n)
        def _():
            load(dyall_ref, tile_n, 1, j + 1).start()

        load(dyall_ref, tile_n, 1, j).wait()
        here = at(j)
        grad_act = dot_nt(tile_n[j % 2], wd[...])
        gate, up = dgu[here, :units].astype(F32), dgu[here, units:].astype(F32)
        sigma = jax.nn.sigmoid(gate)
        grad_gate = (grad_act * up * (sigma * (1.0 + gate * (1.0 - sigma)))).astype(BF16)
        grad_up = (grad_act * (gate * sigma)).astype(BF16)
        dgu[here, :units] = grad_gate
        dgu[here, units:] = grad_up
        for c in range(0, width, chunk):
            p[here, c : c + chunk] = (
                dot_nt(grad_gate, wg_ref[c : c + chunk]) + dot_nt(grad_up, wu_ref[c : c + chunk])
            ).astype(BF16)
        scat.begin_tile(j)

    core = scat.core_steps(True) + scat.core_steps(False)
    pair_links = scat.link_steps(True)
    todo = []
    late = n // 2
    share = -(-len(pair_links) // max(1, late - 1))
    for j in range(1, n):
        todo.append([core[j - 1]])
        if j > late:
            k = (j - late - 1) * share
            todo[-1] += pair_links[k : k + share]
    done = share * max(0, late - 1)
    paced(n, backward, [functools.partial(run, x) for x in todo], 1)
    rest_steps = [core[n - 1]] + pair_links[done:] + scat.link_steps(False)

    def gate_up_cols(c):
        @pl.when(c + 1 < blocks)
        def _():
            load_cols(nm_ref, c + 1).start()

        load_cols(nm_ref, c).wait()
        part = pl.ds(pl.multiple_of(c * step, step), step)
        grads = dot_tn(cols[c % 2], dgu[...]).astype(BF16)
        ggate_ref[part] = grads[:, :units]
        gup_ref[part] = grads[:, units:]

    load_cols(nm_ref, 0).start()
    paced(blocks, gate_up_cols, rest_steps)
    dy = scat_refs[0].at[n - 1]
    fetches = [
        pltpu.make_async_copy(dy_ref, dy, dsem.at[0]),
        pltpu.make_async_copy(h_ref, dh_ref, dsem.at[1]),
    ]
    for fetch in fetches:
        fetch.start()
    scat.finish()
    summed = scat.block(0)
    for fetch in fetches:
        fetch.wait()
    gm_ref[...] = jnp.zeros_like(gm_ref)

    def back(part):
        dn, gain_part = norm_back_tile(dh_ref[part], gain_ref[...].astype(F32), summed[part].astype(F32))
        gm_ref[...] += gain_part
        dh = dy[part].astype(F32) + dn
        dh_ref[part] = dh
        summed[part] = dh.astype(BF16)

    tiles(rows, back)
    gather = Gather(grp, summed, branch_ref, send, recv, sem)
    steps = gather.begin()
    spread_grad(grp, spread, ggate_ref, gategot_ref, 0, grp.far)
    scat.drain()

    def save(j):
        return pltpu.make_async_copy(tile_n.at[j % 2], out_ref.at[at(j)], tsem.at[0, j % 2])

    def branch(j):
        @pl.when(j > 1)
        def _():
            save(j - 2).wait()

        tile_n[j % 2] = jnp.dot(act[at(j)], wd[...], preferred_element_type=F32).astype(BF16)
        save(j).start()

    near = functools.partial(spread_grad, grp, spread, ggate_ref, gategot_ref, 0, (1,))
    paced(n, branch, steps[:6] + [near] + steps[6:], 1)
    save(n - 2).wait()
    save(n - 1).wait()
    gather.finish()
    spread.wait()


def mlp(grp, normed, dy_all, wg, wu, wd_top, hidden, dy, gain, w_down, cid):
    rows, width = hidden.shape
    total = rows * grp.size
    n = len(grp.masks)
    units = wg.shape[1]
    gdown, ggate = sds((units, width), BF16), sds((width, units), BF16)
    return pl.pallas_call(
        functools.partial(mlp_kernel, grp),
        out_shape=[
            sds((rows, width), F32),
            sds((1, width), F32),
            gdown,
            ggate,
            ggate,
            sds((total, width), BF16),
            sds((total, width), BF16),
            got_shape(grp, gdown, 1),
            got_shape(grp, ggate, 0),
        ],
        in_specs=[ANY, ANY, VMEM, VMEM, ANY, ANY, ANY, VMEM, ANY],
        out_specs=[VMEM] * 5 + [ANY] * 4,
        scratch_shapes=[
            pltpu.VMEM((total, width), BF16),
            pltpu.VMEM((units, width), BF16),
            pltpu.VMEM((2, 2 * rows, width), BF16),
            pltpu.SemaphoreType.DMA((2, 2)),
            pltpu.VMEM((total, units), BF16),
            pltpu.VMEM((total, 2 * units), BF16),
            pltpu.VMEM((2, total, cols_of(total)), BF16),
            pltpu.SemaphoreType.DMA((2,)),
            pltpu.SemaphoreType.DMA((2,)),
        ]
        + scatter_scratch(grp, rows, width)
        + gather_scratch(grp)
        + spread_sems(grp, 4),
        compiler_params=params(cid),
        name="mlp",
    )(normed, dy_all, wg, wu, wd_top, hidden, dy, gain, w_down)


def fifth_kernel(grp, p_ref, h_ref, gup_ref, out_ref, up_ref, *rest):
    p, psem, rest = rest[0], rest[1], rest[2:]
    scat, rest = rest[:N_SCATTER], rest[N_SCATTER:]
    zs, zr = rest
    pltpu.make_async_copy(p_ref, p, psem).start()
    grp.greet()
    spread = Spread(grp, zs, zr)
    spread_grad(grp, spread, gup_ref, up_ref, 0)
    pltpu.make_async_copy(p_ref, p, psem).wait()
    acc = plain_scatter(grp, p, h_ref.shape[0], scat)

    def finish(rows):
        out_ref[rows] = (h_ref[rows] + acc[rows].astype(F32)).astype(BF16)

    tiles(h_ref.shape[0], finish)
    spread.wait()


def fifth(grp, part, hidden, grad_up, cid):
    rows, width = hidden.shape
    return pl.pallas_call(
        functools.partial(fifth_kernel, grp),
        out_shape=[sds((rows, width), BF16), got_shape(grp, grad_up, 0)],
        in_specs=[ANY, VMEM, ANY],
        out_specs=[VMEM, ANY],
        scratch_shapes=[pltpu.VMEM((rows * grp.size, width), BF16), pltpu.SemaphoreType.DMA]
        + scatter_scratch(grp, rows, width)
        + spread_sems(grp, 1),
        compiler_params=params(cid),
        name="fifth",
    )(part, hidden, grad_up)


def sixth_kernel(
    grp, p_ref, x_ref, dh_ref, gain_ref, gm_ref, gout_ref, gqkv_ref, tok_ref, gains_ref, o_ref, qkv_ref, *rest
):
    p, psem, rest = rest[0], rest[1], rest[2:]
    scat, rest = rest[:N_SCATTER], rest[N_SCATTER:]
    buf, gs, gr, zs, zr = rest
    pltpu.make_async_copy(p_ref, p, psem).start()
    grp.greet(everyone=True)
    spread = Spread(grp, zs, zr)
    spread_grad(grp, spread, gout_ref, o_ref, 1)
    spread_grad(grp, spread, gqkv_ref, qkv_ref, 0)
    pltpu.make_async_copy(p_ref, p, psem).wait()
    acc = plain_scatter(grp, p, x_ref.shape[0], scat)
    buf[0, 0:1] = jnp.zeros_like(gm_ref)
    buf[0, 1:2] = gm_ref[...]

    def back(rows):
        dn, gain_part = norm_back_tile(
            x_ref[rows].astype(F32), gain_ref[...].astype(F32), acc[rows].astype(F32)
        )
        buf[0, 0:1] += gain_part
        tok_ref[rows] = (dh_ref[rows] + dn).astype(BF16)

    tiles(x_ref.shape[0], back)
    sum_gains(grp, buf, gs, gr)
    gains_ref[...] = buf[buf.shape[0] - 1]
    spread.wait()


def sixth(grp, part, x, dh, gain, gain_m, grad_out, grad_qkv, cid):
    rows, width = x.shape
    return pl.pallas_call(
        functools.partial(sixth_kernel, grp),
        out_shape=[
            sds((rows, width), BF16),
            sds((2, width), F32),
            got_shape(grp, grad_out, 1),
            got_shape(grp, grad_qkv, 0),
        ],
        in_specs=[ANY, VMEM, VMEM, VMEM, VMEM, ANY, ANY],
        out_specs=[VMEM, VMEM, ANY, ANY],
        scratch_shapes=[pltpu.VMEM((rows * grp.size, width), BF16), pltpu.SemaphoreType.DMA]
        + scatter_scratch(grp, rows, width)
        + gain_scratch(grp, width)
        + spread_sems(grp, 2),
        compiler_params=params(cid),
        name="sixth",
    )(part, x, dh, gain, gain_m, grad_out, grad_qkv)


def swap_halves(value):
    half = HEAD // 2
    width = value.shape[1]
    pieces = []
    for at in range(0, width, HEAD):
        pieces.append(value[:, at + half : at + HEAD])
        pieces.append(value[:, at : at + half])
    if width % 128:
        return jnp.concatenate(pieces, axis=1)
    lane = lax.broadcasted_iota(jnp.int32, value.shape, 1)
    return jnp.where(
        lane % HEAD < half, pltpu.roll(value, width - half, 1), pltpu.roll(value, half, 1)
    )


QB = 256


def bands(length):
    for at in range(0, length, QB):
        first = max(0, at - SAMPLE)
        yield at, min(QB, length - at), first, at + min(QB, length - at) - first


def kept(start_row, at, size, first, width):
    key = first + lax.broadcasted_iota(jnp.int32, (width, size), 0)
    query = at + lax.broadcasted_iota(jnp.int32, (width, size), 1)
    return (key >= start_row) & (key <= query)


def attend_back_kernel(
    heads, q_ref, k_ref, v_ref, do_ref, lse_ref, cos_ref, sin_ref, start_ref, out_ref, dq, dk, dv
):
    wide = heads * HEAD
    length = q_ref.shape[0]
    dk[...] = jnp.zeros_like(dk)
    dv[...] = jnp.zeros_like(dv)
    for h in range(heads):
        lanes = slice(h * HEAD, (h + 1) * HEAD)
        for at, size, first, width in bands(length):
            query = q_ref[at : at + size, lanes]
            key = k_ref[first : first + width, lanes]
            value = v_ref[first : first + width, lanes]
            grad = do_ref[at : at + size, lanes]
            scores = dot_nt(key, query * BF16(HEAD**-0.5))
            mask = kept(start_ref[0, :, at : at + size], at, size, first, width)
            weights = jnp.where(
                mask, jnp.exp(jnp.where(mask, scores, -1e9) - lse_ref[0, h : h + 1, at : at + size]), 0.0
            )
            dv[first : first + width, lanes] += jnp.dot(
                weights.astype(BF16), grad, preferred_element_type=F32
            )
            grad_weights = dot_nt(value, grad)
            inner = jnp.sum(weights * grad_weights, axis=0, keepdims=True)
            grad_scores = (weights * (grad_weights - inner)).astype(BF16)
            dq[at : at + size, lanes] = dot_tn(grad_scores, key)
            dk[first : first + width, lanes] += jnp.dot(
                grad_scores, query, preferred_element_type=F32
            )

    @pl.loop(0, length // QB)
    def _(i):
        rows = pl.ds(pl.multiple_of(i * QB, QB), QB)
        cosine, sine = cos_ref[rows], sin_ref[rows]
        query, key = dq[rows] * HEAD**-0.5, dk[rows] * HEAD**-0.5
        out_ref[rows, :wide] = (query * cosine - swap_halves(query) * sine).astype(BF16)
        out_ref[rows, wide : 2 * wide] = (key * cosine - swap_halves(key) * sine).astype(BF16)
        out_ref[rows, 2 * wide :] = dv[rows].astype(BF16)


def attend_back(query, key, value, grad, lse, cosine, sine, start, heads):
    rows, _, length = start.shape
    wide = heads * HEAD

    def tall(width):
        return pl.BlockSpec((length, width), lambda r: (r, 0))

    return pl.pallas_call(
        functools.partial(attend_back_kernel, heads),
        grid=(rows,),
        out_shape=jax.ShapeDtypeStruct((rows * length, 3 * wide), BF16),
        in_specs=[tall(wide)] * 4
        + [pl.BlockSpec((1, heads, length), lambda r: (r, 0, 0)), tall(wide), tall(wide)]
        + [pl.BlockSpec((1, 1, length), lambda r: (r, 0, 0))],
        out_specs=tall(3 * wide),
        scratch_shapes=[pltpu.VMEM((length, wide), F32)] * 3,
        compiler_params=pltpu.CompilerParams(vmem_limit_bytes=48 << 20),
        name="attend_back",
    )(query, key, value, grad, lse, cosine, sine, start)


def finish_kernel(z_size, parts, z_ref, *refs):
    low = z_ref[0] % 2
    n = len(parts)
    owns, gots, outs = refs[:n], refs[n : 2 * n], list(refs[2 * n :])
    for own, got, (axis, count) in zip(owns, gots, parts):
        sums = [own[...].astype(F32), None]
        for m in range(1, z_size):
            term = got[m - 1].astype(F32)
            sums[m % 2] = term if sums[m % 2] is None else sums[m % 2] + term
        if axis == 0:
            out = outs.pop(0)
            out[low] = sums[0]
            out[1 - low] = sums[1]
            continue
        width = sums[0].shape[1] // count
        for i in range(count):
            out = outs.pop(0)
            for which, total in ((low, sums[0]), (1 - low, sums[1])):
                place = pl.ds(pl.multiple_of(which * width, width), width)
                out[:, place] = total[:, i * width : (i + 1) * width]


def finish(z_size, z, grads, gots, axes):
    steps = 4
    owns, blocks, outs, shapes = [], [], [], []
    for grad, got, (axis, count) in zip(grads, gots, axes):
        rows, cols = got.shape[1] // steps, got.shape[2]
        if axis == 0:
            owns.append(pl.BlockSpec((rows, cols), lambda i, z_ref: (i, z_ref[0])))
            outs.append(pl.BlockSpec((2, rows, cols), lambda i, z_ref: (0, i, 0)))
            shapes.append(sds((2, rows * steps, cols), F32))
        else:
            owns.append(pl.BlockSpec((rows, cols), lambda i, z_ref: (z_ref[0] * steps + i, 0)))
            wide = 2 * cols // count
            outs += [pl.BlockSpec((rows, wide), lambda i, z_ref: (i, 0))] * count
            shapes += [sds((rows * steps, wide), F32)] * count
        blocks.append(pl.BlockSpec((z_size - 1, rows, cols), lambda i, z_ref: (0, i, 0)))
    return pl.pallas_call(
        functools.partial(finish_kernel, z_size, axes),
        out_shape=shapes,
        grid_spec=pltpu.PrefetchScalarGridSpec(
            num_scalar_prefetch=1, grid=(steps,), in_specs=owns + blocks, out_specs=outs
        ),
        compiler_params=pltpu.CompilerParams(vmem_limit_bytes=56 << 20),
        name="finish",
    )(jnp.reshape(z, (1,)), *grads, *gots)


def shards(
    z_size,
    t_size,
    tokens,
    gain_attn,
    gain_mlp,
    w_query,
    w_key,
    w_value,
    w_out,
    w_gate,
    w_up,
    w_down,
    segment_ids,
    out_grad,
):
    grp = Group(z_size, t_size)
    z = lax.axis_index("fsdp")
    low = z % 2

    def deliver(grad, got, half_axis, axis, parts=1):
        size = grad.shape[axis] // z_size
        sums = [lax.dynamic_slice_in_dim(grad, z * size, size, axis).astype(F32), None]
        for m in range(1, z_size):
            term = got[m - 1].astype(F32)
            sums[m % 2] = term if sums[m % 2] is None else sums[m % 2] + term
        outs = []
        piece = sums[0].shape[half_axis] // parts
        for i in range(parts):
            a, b = (lax.slice_in_dim(s, i * piece, (i + 1) * piece, axis=half_axis) for s in sums)
            outs.append(
                jnp.where(
                    low == 0,
                    jnp.concatenate([a, b], axis=half_axis),
                    jnp.concatenate([b, a], axis=half_axis),
                )
            )
        return outs

    wide = w_query.shape[1] // 2
    heads = wide // HEAD

    gain_a = gain_attn[None, :]
    gain_m = gain_mlp[None, :]
    normed_a, wqkv, wo, start, cosine, sine = first(
        grp, low, tokens, gain_a, w_query, w_key, w_value, w_out, segment_ids, 0
    )
    query, key, value, attended, lse, hidden, normed_m, grad_all, wg, wu, wd_top = middle(
        grp,
        heads,
        normed_a,
        wqkv,
        wo,
        cosine,
        sine,
        start,
        out_grad,
        tokens,
        gain_m,
        w_gate,
        w_up,
        w_down,
        1,
    )
    grad_hidden, gain_m_part, grad_down, grad_wg, grad_wu, branch_all, out_part, got_down, got_gate = mlp(
        grp, normed_m, grad_all, wg, wu, wd_top, hidden, out_grad, gain_m, w_down, 3
    )
    if grp.size <= 16:
        output, tokens_grad, gains, grad_wout, grad_wqkv, got_up, got_out, got_qkv = last(
            grp, heads, branch_all, normed_a, out_part, grad_wu, query, key, value, attended, lse,
            cosine, sine, start, wqkv, wo, hidden, tokens, grad_hidden, gain_a, gain_m_part, 4,
        )
    else:
        output, got_up = fifth(grp, out_part, hidden, grad_wu, 4)
        grad_wout = dot_tn(attended, branch_all).astype(BF16)
        grad_attended = dot_nt(branch_all, wo).astype(BF16)
        grad_qkv = attend_back(query, key, value, grad_attended, lse, cosine, sine, start, heads)
        grad_wqkv = dot_tn(normed_a, grad_qkv).astype(BF16)
        grad_na = dot_nt(grad_qkv, wqkv).astype(BF16)
        tokens_grad, gains, got_out, got_qkv = sixth(
            grp, grad_na, tokens, grad_hidden, gain_a, gain_m_part, grad_wout, grad_wqkv, 5
        )
    grads = (grad_down, grad_wg, grad_wu, grad_wout, grad_wqkv)
    gots = (got_down, got_gate, got_up, got_out, got_qkv)
    axes = ((0, 1), (1, 1), (1, 1), (0, 1), (1, 3))
    if wide % LANES == 0:
        outs = finish(z_size, z, grads, gots, axes)
        down_out, out_out = (x.reshape(-1, x.shape[2]) for x in (outs[0], outs[3]))
        gate_out, up_out = outs[1:3]
        query_out, key_out, value_out = outs[4:]
    else:
        (down_out,) = deliver(grad_down, got_down, 0, 1)
        (gate_out,) = deliver(grad_wg, got_gate, 1, 0)
        (up_out,) = deliver(grad_wu, got_up, 1, 0)
        (out_out,) = deliver(grad_wout, got_out, 0, 1)
        query_out, key_out, value_out = deliver(grad_wqkv, got_qkv, 1, 0, 3)
    return (
        output,
        tokens_grad,
        gains[0],
        gains[1],
        query_out,
        key_out,
        value_out,
        out_out,
        gate_out,
        up_out,
        down_out,
    )


def solution(mesh):
    return jax.shard_map(
        functools.partial(shards, mesh.shape["fsdp"], mesh.shape["tensor"]),
        mesh=mesh,
        in_specs=(
            P(("fsdp", "tensor"), None),
            P(),
            P(),
            P("fsdp", "tensor"),
            P("fsdp", "tensor"),
            P("fsdp", "tensor"),
            P("tensor", "fsdp"),
            P("fsdp", "tensor"),
            P("fsdp", "tensor"),
            P("tensor", "fsdp"),
            P("fsdp", None),
            P(("fsdp", "tensor"), None),
        ),
        out_specs=(
            P(("fsdp", "tensor"), None),
            P(("fsdp", "tensor"), None),
            P(),
            P(),
            P("fsdp", "tensor"),
            P("fsdp", "tensor"),
            P("fsdp", "tensor"),
            P("tensor", "fsdp"),
            P("fsdp", "tensor"),
            P("fsdp", "tensor"),
            P("tensor", "fsdp"),
        ),
        check_vma=False,
    )
```

```python
import functools
import math

import jax
import jax.numpy as jnp
from jax import lax
from jax.experimental import pallas as pl
from jax.experimental.pallas import tpu as pltpu
from jax.sharding import PartitionSpec as P

HEAD = 64
SAMPLE = 512
EPS = 1e-05
LANES = 128
ROPE_BASE = 130000.0
MESH = pl.DeviceIdType.MESH
BF16 = jnp.bfloat16
F32 = jnp.float32
ANY = pl.BlockSpec(memory_space=pl.ANY)
VMEM = pl.BlockSpec(memory_space=pltpu.VMEM)


def flip(index, bit):
    return index + bit - 2 * bit * ((index // bit) % 2)


def dot_nt(left, right):
    return lax.dot_general(left, right, (((1,), (1,)), ((), ())), preferred_element_type=F32)


def dot_tn(left, right):
    return lax.dot_general(left, right, (((0,), (0,)), ((), ())), preferred_element_type=F32)


class Group:
    def __init__(self, z_size, t_size):
        self.z_size = z_size
        self.t_size = t_size
        self.size = 2 * t_size
        inner = []
        bit = 2
        while bit < t_size:
            inner.append(bit)
            bit *= 2
        self.core = 1
        self.pair = t_size
        self.orders = (tuple(inner) + (self.pair,), tuple(inner[::-1]) + (self.pair,))
        self.inner = (tuple(inner), tuple(inner[::-1]))
        self.bits = (self.core,) + tuple(inner) + (self.pair,)
        masks = [0]
        for b in self.orders[0]:
            masks = masks + [m + b for m in masks]
        self.masks = tuple(masks)
        self.far = tuple(range(2, z_size))

    def place(self):
        return lax.axis_index("fsdp"), lax.axis_index("tensor")

    def rank(self, mask=0):
        z, t = self.place()
        r = (z % 2) * self.t_size + t
        for b in self.bits:
            if mask & b:
                r = flip(r, b)
        return r

    def chip_at(self, j, near=False):
        chip = self.rank() // 2
        mask = j if near else len(self.masks) - 1 - j
        out = 0
        bit = 1
        while bit < len(self.masks):
            a, b = (chip // bit) % 2, (mask // bit) % 2
            out = out + (a + b - 2 * a * b) * bit
            bit *= 2
        return out

    def partner(self, bit):
        z, t = self.place()
        if bit == self.pair:
            return (flip(z, 1), t)
        return (z, flip(t, bit))

    def across(self, mask):
        z, t = self.place()
        bit = 1
        while bit < self.z_size:
            if mask & bit:
                z = flip(z, bit)
            bit *= 2
        return (z, t)

    def beside(self, mask):
        z, t = self.place()
        bit = 1
        while bit < self.t_size:
            if mask & bit:
                t = flip(t, bit)
            bit *= 2
        return (z, t)

    def greet(self, everyone=False):
        barrier = pltpu.get_barrier_semaphore()
        if everyone:
            peers = [self.beside(m) for m in range(1, self.t_size)]
        else:
            peers = [self.partner(b) for b in self.bits if b != self.pair]
        peers += [self.across(m) for m in range(1, self.z_size)]
        for peer in peers:
            pl.semaphore_signal(barrier, inc=1, device_id=peer, device_id_type=MESH)
        pl.semaphore_wait(barrier, len(peers))


def last_bit(mask, order):
    found = None
    for b in order:
        if mask & b:
            found = b
    return found


class Gather:
    def __init__(self, grp, x_ref, o_ref, send, recv, local):
        self.grp, self.x, self.o = grp, x_ref, o_ref
        self.send, self.recv = send, recv
        self.rows = x_ref.shape[0]
        self.half = self.rows // 2
        self.order = [(grp.pair,) + grp.inner[h] + (grp.core,) for h in range(2)]
        self.sent = []
        own = pl.ds(pl.multiple_of(grp.rank() * self.rows, self.rows), self.rows)
        self.own = pltpu.make_async_copy(x_ref, o_ref.at[own], local)

    def at(self, mask, h):
        first = self.grp.rank(mask) * self.rows + h * self.half
        return self.o.at[pl.ds(pl.multiple_of(first, self.half), self.half)]

    def copy(self, src, mask, h, key, bit):
        return pltpu.make_async_remote_copy(
            src_ref=src,
            dst_ref=self.at(mask, h),
            send_sem=self.send.at[h, key],
            recv_sem=self.recv.at[h, key],
            device_id=self.grp.partner(bit),
            device_id_type=MESH,
        )

    def forward(self, h, mask, bits=None):
        order = self.order[h]
        start = 0 if mask == 0 else order.index(last_bit(mask, order)) + 1
        for bit in order[start:] if bits is None else bits:
            self.own_copy(h, mask, bit).start()
            self.sent.append((h, mask, bit))

    def own_copy(self, h, mask, bit):
        src = self.x.at[pl.ds(h * self.half, self.half)] if mask == 0 else self.at(mask, h)
        return self.copy(src, mask, h, mask | bit, bit)

    def arrived(self, h, mask):
        bit = last_bit(mask, self.order[h])
        self.copy(self.at(mask, h), mask, h, mask, bit).wait_recv()

    def begin(self):
        self.own.start()
        for h in range(2):
            self.forward(h, 0, (self.grp.pair,))
        for k in range(1, len(self.order[0])):
            for h in range(2):
                self.forward(h, 0, (self.order[h][k],))
        grp = self.grp
        plain = sorted(
            (m for m in grp.masks if m), key=lambda m: (m & grp.pair, bin(m).count("1"))
        )
        if len(plain) > 3:
            plain.remove(grp.pair)
            plain.insert(2, grp.pair)
        self.plain = plain

        def step(h, m):
            self.arrived(h, m)
            self.forward(h, m)

        return [
            functools.partial(step, h, m if h == 0 else mirror(grp, m))
            for m in plain
            for h in range(2)
        ]

    def chip_arrived(self, mask):
        for h in range(2):
            self.arrived(h, mask | self.grp.core)
        if mask == 0:
            self.own.wait()

    def needs(self, steps):
        plain = self.plain
        done = 0
        out = []
        for m in sorted(self.grp.masks):
            upto = done
            if m:
                other = next(k for k in plain if mirror(self.grp, k) == m)
                upto = 2 * (max(plain.index(m), plain.index(other)) + 1)
            out.append(steps[done : max(done, upto)] + [functools.partial(self.chip_arrived, m)])
            done = max(done, upto)
        return out

    def finish(self):
        for m in self.grp.masks:
            self.chip_arrived(m)
        self.drain()

    def drain(self):
        for sent in self.sent:
            self.own_copy(*sent).wait_send()


def mirror(grp, mask):
    out = mask & (grp.pair | grp.core)
    a, b = grp.inner
    for p, q in zip(a, b):
        if mask & p:
            out |= q
    return out


TILE = 16


def add_rows(dst, src, rows):
    @pl.loop(0, rows // TILE)
    def _(i):
        part = pl.ds(pl.multiple_of(i * TILE, TILE), TILE)
        dst[part] = (dst[part].astype(F32) + src[part].astype(F32)).astype(dst.dtype)


def scatter_scratch(grp, rows, width):
    n = len(grp.masks)
    return [
        pltpu.VMEM((n, rows, width), BF16),
        pltpu.VMEM((2, n - 1, rows // 2, width), BF16),
        pltpu.SemaphoreType.DMA((n,)),
        pltpu.SemaphoreType.DMA((n,)),
        pltpu.SemaphoreType.DMA((2, n)),
        pltpu.SemaphoreType.DMA((2, n)),
    ]


N_SCATTER = 6


class Scatter:
    def __init__(self, grp, p, rows, got, rbuf, csend, crecv, send, recv, own=None):
        self.grp, self.p, self.rows, self.half = grp, p, rows, rows // 2
        self.own = own
        self.got, self.rbuf = got, rbuf
        self.csend, self.crecv, self.send, self.recv = csend, crecv, send, recv
        self.index = {m: len(grp.masks) - 1 - m // 2 for m in grp.masks}
        self.started = []
        self.slots = []
        for h in range(2):
            s = {}
            order = grp.orders[h]
            for i in range(len(order)):
                later = order[i + 1 :]
                for m in grp.masks:
                    if all((not m & b) or b in later for b in order):
                        s[(i, m)] = len(s)
            self.slots.append(s)

    def masks(self, pair):
        chosen = [m for m in self.grp.masks if bool(m & self.grp.pair) == pair]
        return sorted(chosen, reverse=True)

    def begin_tile(self, j):
        _, t = self.grp.place()
        first = (self.grp.chip_at(j) * 2 + 1 - t % 2) * self.rows
        pltpu.make_async_remote_copy(
            src_ref=self.p.at[pl.ds(pl.multiple_of(first, self.rows), self.rows)],
            dst_ref=self.got.at[j],
            send_sem=self.csend.at[j],
            recv_sem=self.crecv.at[j],
            device_id=self.grp.partner(self.grp.core),
            device_id_type=MESH,
        ).start()

    def block(self, mask, h=None):
        if self.own is not None and not mask & self.grp.core:
            mine = self.own.at[self.index[mask]]
            return mine if h is None else mine.at[pl.ds(h * self.half, self.half)]
        first = self.grp.rank(mask) * self.rows
        if h is None:
            return self.p.at[pl.ds(pl.multiple_of(first, self.rows), self.rows)]
        return self.p.at[pl.ds(pl.multiple_of(first + h * self.half, self.half), self.half)]

    def core_copy(self, mask):
        i = self.index[mask]
        return pltpu.make_async_remote_copy(
            src_ref=self.block(mask | self.grp.core),
            dst_ref=self.got.at[i],
            send_sem=self.csend.at[i],
            recv_sem=self.crecv.at[i],
            device_id=self.grp.partner(self.grp.core),
            device_id_type=MESH,
        )

    def begin(self, masks):
        for m in masks:
            self.core_copy(m).start()

    def load(self, mask, sem):
        first = pl.multiple_of(self.grp.rank(mask) * self.rows, self.rows)
        i = self.index[mask]
        return pltpu.make_async_copy(self.p.at[pl.ds(first, self.rows)], self.own.at[i], sem.at[i])

    def core_step(self, mask):
        self.core_copy(mask).wait_recv()
        add_rows(self.block(mask), self.got.at[self.index[mask]], self.rows)
        for h in range(2):
            if mask & self.grp.orders[h][0]:
                self.ship(h, 0, mask)

    def link_copy(self, h, i, mask, k):
        return pltpu.make_async_remote_copy(
            src_ref=self.block(mask, h),
            dst_ref=self.rbuf.at[h, k],
            send_sem=self.send.at[h, k],
            recv_sem=self.recv.at[h, k],
            device_id=self.grp.partner(self.grp.orders[h][i]),
            device_id_type=MESH,
        )

    def ship(self, h, i, mask):
        self.out_copy(h, i, mask).start()
        self.started.append((h, i, mask))

    def out_copy(self, h, i, mask):
        return self.link_copy(h, i, mask, self.slots[h][(i, mask - self.grp.orders[h][i])])

    def take(self, h, i, mask):
        k = self.slots[h][(i, mask)]
        self.link_copy(h, i, mask, k).wait_recv()
        add_rows(self.block(mask, h), self.rbuf.at[h, k], self.half)

    def core_steps(self, pair):
        return [functools.partial(self.core_step, m) for m in self.masks(pair)]

    def link_steps(self, pair):
        steps = []
        for i in range(1, len(self.grp.orders[0])):
            for m in self.masks(pair):
                for h in range(2):
                    order = self.grp.orders[h]
                    mine = m if h == 0 else mirror(self.grp, m)
                    if any(mine & b for b in order[:i]):
                        continue

                    def step(h=h, i=i, mine=mine, order=order):
                        self.take(h, i - 1, mine)
                        if mine & order[i]:
                            self.ship(h, i, mine)

                    steps.append(step)
        return steps

    def finish(self):
        for h in range(2):
            self.take(h, len(self.grp.orders[h]) - 1, 0)

    def drain(self):
        for m in self.grp.masks:
            self.core_copy(m).wait_send()
        for sent in self.started:
            self.out_copy(*sent).wait_send()


def plain_scatter(grp, p, rows, refs):
    scat = Scatter(grp, p, rows, *refs)
    scat.begin(scat.masks(True) + scat.masks(False))
    run(scat.core_steps(True) + scat.core_steps(False))
    run(scat.link_steps(True) + scat.link_steps(False))
    scat.finish()
    scat.drain()
    return scat.block(0)


def run(*lists):
    for i in range(max(len(x) for x in lists)):
        for steps in lists:
            if i < len(steps):
                steps[i]()


class Spread:
    def __init__(self, grp, send, recv):
        self.grp, self.send, self.recv = grp, send, recv
        self.used = 0
        self.makers = []

    def to(self, mask, views, start=True):
        k = self.used
        self.used += 1

        def make():
            src, dst = views()
            if mask == 0:
                return pltpu.make_async_copy(src, dst, self.send.at[k])
            return pltpu.make_async_remote_copy(
                src_ref=src,
                dst_ref=dst,
                send_sem=self.send.at[k],
                recv_sem=self.recv.at[k],
                device_id=self.grp.across(mask),
                device_id_type=MESH,
            )

        if start:
            make().start()
        self.makers.append(make)
        return make

    def wait(self):
        self.wait_first(len(self.makers))

    def wait_first(self, count):
        for make in self.makers[:count]:
            make().wait()
        self.makers = self.makers[count:]


def spread_sems(grp, parts):
    return [pltpu.SemaphoreType.DMA((grp.z_size * parts,))] * 2


def spread_weight(grp, spread, shard, whole, half_axis, at, masks=None, start=True):
    axis = 1 - half_axis
    mine, other = shard
    makers = []
    for m in grp.far + (0, 1) if masks is None else masks:

        def views(src=other if m % 2 else mine):
            z, _ = grp.place()
            size, width = src.shape[axis], src.shape[half_axis]
            place = pl.ds(pl.multiple_of(z * size, size), size)
            if axis == 0:
                return src, whole.at[place, at : at + width]
            return src, whole.at[at : at + width, place]

        makers.append(spread.to(m, views, start))
    return makers


def halves_of(grp, ref, axis):
    z, _ = grp.place()
    size = ref.shape[axis] // 2
    out = []
    for which in (z % 2, 1 - z % 2):
        part = pl.ds(pl.multiple_of(which * size, size), size)
        out.append(ref.at[:, part] if axis == 1 else ref.at[part])
    return out


def weight_jobs(grp, spread, shard, whole, half_axis, pieces):
    axis = 1 - half_axis
    mine, other = shard
    jobs = {m: [] for m in range(grp.z_size)}
    for i in range(pieces):
        for m in range(grp.z_size):

            def views(i=i, src=other if m % 2 else mine):
                z, _ = grp.place()
                size, width = src.shape[0] // pieces, src.shape[1]
                piece = src.at[pl.ds(i * size, size)]
                if axis == 0:
                    first = pl.multiple_of(z * (size * pieces) + i * size, size)
                    return piece, whole.at[pl.ds(first, size)]
                place = pl.ds(pl.multiple_of(z * width, width), width)
                return piece, whole.at[pl.ds(i * size, size), place]

            jobs[m].append(functools.partial(spread.to, m, views))
    return by_distance(grp, jobs)


def grad_jobs(grp, spread, grad, got, axis, pieces):
    jobs = {m: [] for m in range(1, grp.z_size)}
    for i in range(pieces):
        for m in range(1, grp.z_size):

            def views(i=i, m=m):
                place = grp.across(m)[0]
                size = got.shape[1] // pieces
                land = got.at[m - 1, pl.ds(i * size, size)]
                if axis == 0:
                    first = pl.multiple_of(place * (size * pieces) + i * size, size)
                    return grad.at[pl.ds(first, size)], land
                width = got.shape[2]
                part = pl.ds(pl.multiple_of(place * width, width), width)
                return grad.at[pl.ds(i * size, size), part], land

            jobs[m].append(functools.partial(spread.to, m, views))
    return by_distance(grp, jobs)


def by_distance(grp, jobs):
    far = [job for jobs_i in zip(*(jobs[m] for m in grp.far)) for job in jobs_i]
    near = [job for jobs_i in zip(*(jobs[m] for m in (1, 0) if m in jobs)) for job in jobs_i]
    return far, near


def mixed(steps, jobs, first=0):
    out = list(steps[:first])
    tail = steps[first:]
    done = 0
    for i, step in enumerate(tail):
        upto = (i + 1) * len(jobs) // len(tail)
        out.append(functools.partial(run, [step] + jobs[done:upto]))
        done = upto
    return out + (jobs if not tail else [])


PIECES = 1


def spread_grad(grp, spread, grad, got, axis, masks=None, start=True):
    makers = []
    for m in grp.far + (1,) if masks is None else masks:

        def views(m=m):
            size = grad.shape[axis] // grp.z_size
            part = pl.ds(pl.multiple_of(grp.across(m)[0] * size, size), size)
            return (grad.at[part] if axis == 0 else grad.at[:, part]), got.at[m - 1]

        makers.append(spread.to(m, views, start))
    return makers


def launch(makers, where=None):
    if where is None:
        for make in makers:
            make().start()
    else:

        @pl.when(where)
        def _():
            for make in makers:
                make().start()


def inner_plane(grp):
    z, _ = grp.place()
    return (z * 4 >= grp.z_size) & (z * 4 < 3 * grp.z_size)


def staged_gather(gather, after_pair):
    steps = gather.begin()
    cut = 6 if len(steps) > 6 else len(steps)
    run(steps[:cut])
    after_pair()
    run(steps[cut:])
    gather.finish()


def tiles(rows, body):
    @pl.loop(0, rows // TILE)
    def _(i):
        body(pl.ds(pl.multiple_of(i * TILE, TILE), TILE))


def norm_scale(value):
    return lax.rsqrt(jnp.mean(value * value, axis=-1, keepdims=True) + EPS)


def gather_scratch(grp):
    return [
        pltpu.SemaphoreType.DMA((2, grp.size)),
        pltpu.SemaphoreType.DMA((2, grp.size)),
        pltpu.SemaphoreType.DMA,
    ]


def params(cid):
    return pltpu.CompilerParams(
        collective_id=cid, has_side_effects=True, vmem_limit_bytes=61952 << 10
    )


def sds(shape, dtype):
    return jax.ShapeDtypeStruct(shape, dtype)


def weight_views(grp, refs, axis, presliced):
    if presliced:
        return [(refs[2 * i], refs[2 * i + 1]) for i in range(len(refs) // 2)]
    return [tuple(halves_of(grp, r, axis)) for r in refs]


def shard_args(low, shards_, axis):
    aligned = shards_[0].shape[axis] // 2 % (128 if axis == 1 else 16) == 0
    if aligned:
        return False, list(shards_)
    out = []
    for w in shards_:
        size = w.shape[axis] // 2
        out += [
            lax.dynamic_slice_in_dim(w, low * size, size, axis),
            lax.dynamic_slice_in_dim(w, (1 - low) * size, size, axis),
        ]
    return True, out


def first_kernel(grp, flags, n_qkv, x_ref, gain_ref, *rest):
    pre_qkv, pre_o = flags
    qkv_refs, rest = rest[:n_qkv], rest[n_qkv:]
    n_o = 2 if pre_o else 1
    o_refs, rest = rest[:n_o], rest[n_o:]
    seg_ref, all_ref, wqkv_ref, wo_ref, start_ref, cos_ref, sin_ref, local, ids, send, recv, sem, zs, zr = rest
    grp.greet()
    spread = Spread(grp, zs, zr)
    z, _ = grp.place()
    spread.to(0, lambda: (seg_ref, ids.at[z % 2]))
    spread.to(1, lambda: (seg_ref, ids.at[z % 2]))

    def weights(masks):
        at = 0
        for pair in weight_views(grp, qkv_refs, 1, pre_qkv):
            spread_weight(grp, spread, pair, wqkv_ref, 1, at, masks)
            at += pair[0].shape[1]
        for pair in weight_views(grp, o_refs, 0, pre_o):
            spread_weight(grp, spread, pair, wo_ref, 0, 0, masks)

    def norm(rows):
        x = x_ref[rows].astype(F32)
        local[rows] = (x * norm_scale(x) * gain_ref[...].astype(F32)).astype(BF16)

    tiles(x_ref.shape[0], norm)
    gather = Gather(grp, local, all_ref, send, recv, sem)
    steps = gather.begin()
    weights(grp.far + (0,))
    spread.wait_first(2)
    places(ids, start_ref, cos_ref, sin_ref)
    run(steps[:6])
    weights((1,))
    run(steps[6:] or [lambda: None])
    gather.finish()
    spread.wait()


def places(ids, start_ref, cos_ref, sin_ref):
    planes, rows, length = ids.shape
    wide = cos_ref.shape[1]
    place = lax.broadcasted_iota(jnp.int32, (1, length), 1)
    lane = lax.broadcasted_iota(jnp.int32, (LANES, LANES), 1)
    pair = (lane % (HEAD // 2)).astype(F32)
    inverse = jnp.exp(pair * (-2.0 / HEAD) * math.log(ROPE_BASE))
    sign = jnp.where(lane % HEAD < HEAD // 2, -1.0, 1.0)
    for a in range(planes):
        for r in range(rows):
            row = a * rows + r
            own = ids[a, r : r + 1]
            change = (place == 0) | (own != pltpu.roll(own, 1, 1))
            start = jnp.where(change, place, 0)
            step = 1
            while step < length:
                start = jnp.maximum(start, jnp.where(place >= step, pltpu.roll(start, step, 1), 0))
                step *= 2
            start_ref[row] = start

    @pl.loop(0, planes * rows)
    def _(row):
        @pl.loop(0, length // LANES)
        def _(c):
            here = pl.ds(pl.multiple_of(c * LANES, LANES), LANES)
            token = c * LANES + lax.broadcasted_iota(jnp.int32, (1, LANES), 1)
            position = (token - start_ref[row, :, here]).astype(F32)
            angle = jnp.broadcast_to(position, (LANES, LANES)).T * inverse
            there = pl.ds(pl.multiple_of(row * length + c * LANES, LANES), LANES)
            cos_ref[there] = jnp.cos(angle)[:, :wide]
            sin_ref[there] = (sign * jnp.sin(angle))[:, :wide]


def first(grp, low, x, gain, w_query, w_key, w_value, w_out, ids, cid):
    pre_qkv, qkv = shard_args(low, (w_query, w_key, w_value), 1)
    pre_o, out = shard_args(low, (w_out,), 0)
    rows, width = x.shape
    if pre_qkv:
        qkv = [jnp.concatenate(qkv[i::2], axis=1) for i in range(2)]
    deep = w_query.shape[0] * grp.z_size
    thin = 3 * w_query.shape[1] // 2
    table = sds((2 * ids.shape[0] * ids.shape[1], thin // 3), F32)
    return pl.pallas_call(
        functools.partial(first_kernel, grp, (pre_qkv, pre_o), len(qkv)),
        out_shape=[
            sds((rows * grp.size, width), BF16),
            sds((deep, thin), BF16),
            sds((w_out.shape[0] // 2, w_out.shape[1] * grp.z_size), BF16),
            sds((2 * ids.shape[0], 1, ids.shape[1]), jnp.int32),
            table,
            table,
        ],
        in_specs=[VMEM, VMEM] + [ANY] * (len(qkv) + len(out)) + [VMEM],
        out_specs=[ANY] * 3 + [VMEM] * 3,
        scratch_shapes=[
            pltpu.VMEM((rows, width), BF16),
            pltpu.VMEM((2,) + ids.shape, jnp.int32),
        ]
        + gather_scratch(grp)
        + spread_sems(grp, 5),
        compiler_params=params(cid),
        name="first",
    )(x, gain, *qkv, *out, ids)


def attend_rows(length, heads, q_ref, k_ref, v_ref, start_ref, o_ref, lse_ref, row):
    base = row * length

    def band(h, at, first, width, size):
        lanes = slice(h * HEAD, (h + 1) * HEAD)
        mine = pl.ds(pl.multiple_of(base + at, QB), size)
        keys = pl.ds(pl.multiple_of(base + first, QB), width)
        cols = pl.ds(pl.multiple_of(at, QB), size)
        query = q_ref[mine, lanes] * BF16(HEAD**-0.5)
        scores = dot_nt(k_ref[keys, lanes], query)
        mask = kept(start_ref[row, :, cols], at, size, first, width)
        scores = jnp.where(mask, scores, -1e9)
        top = jnp.max(scores, axis=0, keepdims=True)
        expo = jnp.exp(scores - top)
        total = jnp.sum(expo, axis=0, keepdims=True)
        weights = (expo * (1.0 / total)).astype(BF16)
        o_ref[mine, lanes] = dot_tn(weights, v_ref[keys, lanes]).astype(BF16)
        lse_ref[row, h : h + 1, cols] = top + jnp.log(total)

    return banded(length, heads, band)


def banded(length, heads, band):
    parts = []
    for h in range(heads):
        whole = [b for b in bands(length) if b[3] == SAMPLE + QB]
        for at, size, first, width in bands(length):
            if width != SAMPLE + QB:
                parts.append(functools.partial(band, h, at, first, width, size))

        def loop(h=h, whole=whole):
            @pl.loop(0, len(whole))
            def _(i):
                at = whole[0][0] + i * QB
                band(h, at, at - SAMPLE, SAMPLE + QB, QB)

        if whole:
            parts.append(loop)
    return parts


def middle_kernel(
    grp,
    heads,
    fused,
    na_ref,
    wqkv_ref,
    wo_ref,
    cos_ref,
    sin_ref,
    start_ref,
    dy_ref,
    x_ref,
    gain_ref,
    gate_ref,
    up_ref,
    down_ref,
    q_ref,
    k_ref,
    v_ref,
    o_ref,
    lse_ref,
    h_ref,
    nm_ref,
    dyall_ref,
    wg_ref,
    wu_ref,
    wd_ref,
    *rest,
):
    early, rest = (rest[:2], rest[2:]) if fused else (None, rest)
    p, rowbuf, rowsem, local = rest[:4]
    rest = rest[4:]
    if fused:
        wg, wu, tile, tilesem, stage_a, stage_g, stagesem = rest[:7]
        rest = rest[7:]
    scat_refs, rest = rest[:N_SCATTER], rest[N_SCATTER:]
    dsend, drecv, dsem, send, recv, sem, zs, zr = rest
    rows_all, _, length = start_ref.shape
    wide = heads * HEAD
    z, _ = grp.place()
    n = rows_all // 2
    rows = [(1 - z % 2) * n + j for j in range(n)] + [(z % 2) * n + j for j in range(n)]

    blocks = length // QB

    def load(i, j):
        part = pl.ds(pl.multiple_of(rows[i] * length + j * QB, QB), QB)
        return pltpu.make_async_copy(na_ref.at[part], rowbuf.at[j % 2], rowsem.at[j % 2])

    load(0, 0).start()
    grp.greet()
    spread = Spread(grp, zs, zr)
    views = [
        (halves_of(grp, gate_ref, 1), wg_ref, 1),
        (halves_of(grp, up_ref, 1), wu_ref, 1),
        (halves_of(grp, down_ref, 0), wd_ref, 0),
    ]
    outer = Gather(grp, dy_ref, dyall_ref, dsend, drecv, dsem)
    outer_steps = outer.begin()
    for pair, whole, axis in views[:2]:
        spread_weight(grp, spread, pair, whole, axis, 0, (1, 0))
    far = []
    for pair, whole, axis in views[:2]:
        far += spread_weight(grp, spread, pair, whole, axis, 0, grp.far, start=False)
    inner = inner_plane(grp)
    outer_plane = jnp.logical_not(inner)
    cut = len(far) // 2
    launch(far[:cut])
    launch(far[cut:], inner)
    scat = Scatter(grp, p, x_ref.shape[0], *scat_refs)

    def project(i):
        base = rows[i] * length
        if i:
            load(i, 0).start()

        @pl.loop(0, blocks)
        def _(j):
            @pl.when(j + 1 < blocks)
            def _():
                load(i, j + 1).start()

            load(i, j).wait()
            there = pl.ds(pl.multiple_of(base + j * QB, QB), QB)
            qkv = jnp.dot(rowbuf[j % 2], wqkv_ref[...], preferred_element_type=F32)
            cosine, sine = cos_ref[there], sin_ref[there]
            query, key = qkv[:, :wide], qkv[:, wide : 2 * wide]
            q_ref[there] = (query * cosine + swap_halves(query) * sine).astype(BF16)
            k_ref[there] = (key * cosine + swap_halves(key) * sine).astype(BF16)
            v_ref[there] = qkv[:, 2 * wide :].astype(BF16)

    def branch(i):
        base = rows[i] * length

        @pl.loop(0, length // QB)
        def _(j):
            there = pl.ds(pl.multiple_of(base + j * QB, QB), QB)
            p[there] = jnp.dot(o_ref[there], wo_ref[...], preferred_element_type=F32).astype(BF16)

    def parts(i):
        return (
            [functools.partial(project, i)]
            + attend_rows(length, heads, q_ref, k_ref, v_ref, start_ref, o_ref, lse_ref, rows[i])
            + [functools.partial(branch, i)]
        )

    todo = [part for i in range(n) for part in parts(i)]
    wait = max(0, len(todo) - 4)
    run(todo[:wait])
    outer_steps = weave(todo[wait:], outer_steps)
    scat.begin(scat.masks(True))
    todo = [part for i in range(n, 2 * n) for part in parts(i)]
    links = scat.link_steps(True)
    beside = scat.core_steps(True) + links[:-2]
    beside = weave(todo, beside, -(-len(beside) // len(todo)))
    scat.begin(scat.masks(False))
    run(beside + scat.core_steps(False)[:1] + links[-2:])
    launch(far[cut:], outer_plane)
    run(scat.core_steps(False)[1:])
    run(scat.link_steps(False), outer_steps)
    scat.finish()
    summed = scat.block(0)

    def norm(part):
        h = x_ref[part].astype(F32) + summed[part].astype(F32)
        h_ref[part] = h
        local[part] = (h * norm_scale(h) * gain_ref[...].astype(F32)).astype(BF16)

    tiles(x_ref.shape[0], norm)
    gather = Gather(grp, local, nm_ref, send, recv, sem)
    steps = gather.begin()
    pair, whole, axis = views[2]
    spread_weight(grp, spread, pair, whole, axis, 0)
    if not fused:
        run(steps)
        scat.drain()
        outer.finish()
        gather.finish()
        spread.wait()
        return
    spread.wait_first(2 * grp.z_size)
    loads = [
        pltpu.make_async_copy(src, dst, tilesem.at[i])
        for i, (src, dst) in enumerate(((wg_ref, wg), (wu_ref, wu)))
    ]
    for c in loads:
        c.start()
    scat.drain()
    for c in loads:
        c.wait()
    size = tile.shape[0]
    units = wg.shape[1]

    def saves(j):
        here = pl.ds(pl.multiple_of(grp.chip_at(j, near=True) * size, size), size)
        return (
            pltpu.make_async_copy(stage_a.at[j % 2], early[0].at[here], stagesem.at[0, j % 2]),
            pltpu.make_async_copy(stage_g.at[j % 2], early[1].at[here], stagesem.at[1, j % 2]),
        )

    def forward(j):
        here = pl.ds(pl.multiple_of(grp.chip_at(j, near=True) * size, size), size)
        load = pltpu.make_async_copy(nm_ref.at[here], tile, tilesem.at[0])
        load.start()

        @pl.when(j > 1)
        def _():
            for c in saves(j - 2):
                c.wait()

        load.wait()
        act, gate, up = gate_up(tile[...], wg[...], wu[...])
        stage_a[j % 2] = act
        stage_g[j % 2, :, :units] = gate
        stage_g[j % 2, :, units:] = up
        for c in saves(j):
            c.start()

    count = len(grp.masks)
    led(count, forward, gather.needs(steps))
    for j in (count - 2, count - 1):
        for c in saves(j):
            c.wait()
    outer.finish()
    gather.drain()
    spread.wait()


def middle(grp, heads, normed, wqkv, wo, cosine, sine, start, dy, x, gain, w_gate, w_up, w_down, cid):
    rows, width = x.shape
    total = rows * grp.size
    wide = heads * HEAD
    rows_all, _, length = start.shape
    thin = sds((total, wide), BF16)
    fused = grp.size <= 16
    units = w_gate.shape[1] // 2
    early, beside = [], []
    if fused:
        early = [sds((total, units), BF16), sds((total, 2 * units), BF16)]
        beside = [
            pltpu.VMEM((width, units), BF16),
            pltpu.VMEM((width, units), BF16),
            pltpu.VMEM((2 * rows, width), BF16),
            pltpu.SemaphoreType.DMA((2,)),
            pltpu.VMEM((2, 2 * rows, units), BF16),
            pltpu.VMEM((2, 2 * rows, 2 * units), BF16),
            pltpu.SemaphoreType.DMA((2, 2)),
        ]
    return pl.pallas_call(
        functools.partial(middle_kernel, grp, heads, fused),
        out_shape=[thin] * 4
        + [
            sds((rows_all, heads, length), F32),
            sds((rows, width), F32),
            sds((total, width), BF16),
            sds((total, width), BF16),
            sds((w_gate.shape[0] * grp.z_size, w_gate.shape[1] // 2), BF16),
            sds((w_up.shape[0] * grp.z_size, w_up.shape[1] // 2), BF16),
            sds((w_down.shape[0] // 2, w_down.shape[1] * grp.z_size), BF16),
        ]
        + early,
        in_specs=[ANY, VMEM, VMEM, VMEM, VMEM, VMEM, ANY, VMEM, VMEM, ANY, ANY, ANY],
        out_specs=[VMEM] * 6 + [ANY] * (5 + len(early)),
        scratch_shapes=[
            pltpu.VMEM((total, width), BF16),
            pltpu.VMEM((2, QB, width), BF16),
            pltpu.SemaphoreType.DMA((2,)),
            pltpu.VMEM((rows, width), BF16),
        ]
        + beside
        + scatter_scratch(grp, rows, width)
        + gather_scratch(grp)
        + gather_scratch(grp)
        + spread_sems(grp, 3 * PIECES),
        compiler_params=params(cid),
        name="middle",
    )(normed, wqkv, wo, cosine, sine, start, dy, x, gain, w_gate, w_up, w_down)


def norm_back_tile(value, gain, grad):
    scale = norm_scale(value)
    scaled = grad * gain
    inner = jnp.mean(value * scaled, axis=-1, keepdims=True)
    back = scale * scaled - value * (scale * scale * scale * inner)
    return back, jnp.sum(grad * value * scale, axis=0, keepdims=True)


def weave(parts, steps, each=1):
    for part in parts:
        part()
        for step in steps[:each]:
            step()
        steps = steps[each:]
    return steps


def last_kernel(
    grp,
    heads,
    branch_ref,
    na_ref,
    part_ref,
    gup_ref,
    q_ref,
    k_ref,
    v_ref,
    o_ref,
    lse_ref,
    cos_ref,
    sin_ref,
    start_ref,
    wqkv_ref,
    wo_ref,
    h_ref,
    x_ref,
    dh_ref,
    gain_ref,
    gm_ref,
    out_ref,
    tok_ref,
    gains_ref,
    gout_ref,
    gqkv_ref,
    upgot_ref,
    outgot_ref,
    qkvgot_ref,
    p,
    own,
    ownsem,
    rowbuf,
    rowsem,
    cols,
    csem,
    do,
    dqkv,
    dq,
    dk,
    dv,
    gacc,
    buf,
    gs,
    gr,
    *rest,
):
    na_scat, rest = rest[:N_SCATTER], rest[N_SCATTER:]
    out_scat, rest = rest[:N_SCATTER], rest[N_SCATTER:]
    zs, zr = rest
    rows_all, _, length = start_ref.shape
    rows, width = h_ref.shape
    wide = heads * HEAD
    z, _ = grp.place()
    n = rows_all // 2
    order = [(1 - z % 2) * n + j for j in range(n)] + [(z % 2) * n + j for j in range(n)]
    blocks = length // QB
    step = cols.shape[2]

    def load(i, j):
        part = pl.ds(pl.multiple_of(order[i] * length + j * QB, QB), QB)
        return pltpu.make_async_copy(branch_ref.at[part], rowbuf.at[j % 2], rowsem.at[j % 2])

    def load_cols(c):
        part = pl.ds(pl.multiple_of(c * step, step), step)
        return pltpu.make_async_copy(na_ref.at[:, part], cols.at[c % 2], csem.at[c % 2])

    load(0, 0).start()
    load_cols(0).start()
    outer = Scatter(grp, part_ref, rows, *out_scat, own=own)
    for m in outer.masks(True) + outer.masks(False):
        outer.load(m, ownsem).start()
    grp.greet(everyone=True)
    outer.begin(outer.masks(True) + outer.masks(False))
    spread = Spread(grp, zs, zr)
    spread_grad(grp, spread, gup_ref, upgot_ref, 0)
    scat = Scatter(grp, p, rows, *na_scat)
    gacc[...] = jnp.zeros_like(gacc)

    def outer_core(m):
        outer.load(m, ownsem).wait()
        outer.core_step(m)

    outer_steps = [
        functools.partial(outer_core, m) for m in outer.masks(True) + outer.masks(False)
    ]
    outer_steps += outer.link_steps(True) + outer.link_steps(False)

    def prepare(i):
        base = order[i] * length
        if i:
            load(i, 0).start()
        dk[...] = jnp.zeros_like(dk)
        dv[...] = jnp.zeros_like(dv)

        @pl.loop(0, blocks)
        def _(j):
            @pl.when(j + 1 < blocks)
            def _():
                load(i, j + 1).start()

            load(i, j).wait()
            there = pl.ds(pl.multiple_of(base + j * QB, QB), QB)
            here = pl.ds(pl.multiple_of(j * QB, QB), QB)
            branch = rowbuf[j % 2]
            do[here] = dot_nt(branch, wo_ref[...]).astype(BF16)
            gacc[...] += dot_tn(o_ref[there], branch)

    def banded_back(i):
        row = order[i]
        base = row * length

        def band(h, at, first, width, size):
            lanes = slice(h * HEAD, (h + 1) * HEAD)
            cols_at = pl.ds(pl.multiple_of(at, QB), size)
            keys_at = pl.ds(pl.multiple_of(first, QB), width)
            mine = pl.ds(pl.multiple_of(base + at, QB), size)
            keys = pl.ds(pl.multiple_of(base + first, QB), width)
            query = q_ref[mine, lanes]
            key = k_ref[keys, lanes]
            grad = do[cols_at, lanes]
            scores = dot_nt(key, query * BF16(HEAD**-0.5))
            mask = kept(start_ref[row, :, cols_at], at, size, first, width)
            scores = jnp.where(mask, scores, -1e9)
            weights = jnp.exp(scores - lse_ref[row, h : h + 1, cols_at])
            dv[keys_at, lanes] += jnp.dot(weights.astype(BF16), grad, preferred_element_type=F32)
            grad_weights = dot_nt(v_ref[keys, lanes], grad)
            inner = jnp.sum(weights * grad_weights, axis=0, keepdims=True)
            grad_scores = (weights * (grad_weights - inner)).astype(BF16)
            dq[cols_at, lanes] = dot_tn(grad_scores, key)
            dk[keys_at, lanes] += jnp.dot(grad_scores, query, preferred_element_type=F32)

        return banded(length, heads, band)

    def turn_back(i):
        base = order[i] * length

        @pl.loop(0, blocks)
        def _(j):
            there = pl.ds(pl.multiple_of(base + j * QB, QB), QB)
            here = pl.ds(pl.multiple_of(j * QB, QB), QB)
            cosine, sine = cos_ref[there], sin_ref[there]
            query, key = dq[here] * HEAD**-0.5, dk[here] * HEAD**-0.5
            dqkv[there, :wide] = (query * cosine - swap_halves(query) * sine).astype(BF16)
            dqkv[there, wide : 2 * wide] = (key * cosine - swap_halves(key) * sine).astype(BF16)
            dqkv[there, 2 * wide :] = dv[here].astype(BF16)
            p[there] = dot_nt(dqkv[there], wqkv_ref[...]).astype(BF16)

    def parts(i):
        return (
            [functools.partial(prepare, i)] + banded_back(i) + [functools.partial(turn_back, i)]
        )

    for i in range(n):
        outer_steps = weave(parts(i), outer_steps)
    scat.begin(scat.masks(True))
    pair_core = scat.core_steps(True)
    for i in range(n, 2 * n):
        todo = parts(i)
        merged = []
        for a in range(len(todo)):
            merged += [x[a] for x in (outer_steps, pair_core) if a < len(x)]
        outer_steps, pair_core = outer_steps[len(todo) :], pair_core[len(todo) :]
        merged = weave(todo, merged, 2)
        outer_steps = merged + outer_steps
    scat.begin(scat.masks(False))
    gout_ref[...] = gacc[...].astype(BF16)
    spread_grad(grp, spread, gout_ref, outgot_ref, 1)

    def qkv_cols(c):
        @pl.when(c + 1 < width // step)
        def _():
            load_cols(c + 1).start()

        load_cols(c).wait()
        part = pl.ds(pl.multiple_of(c * step, step), step)
        gqkv_ref[part] = dot_tn(cols[c % 2], dqkv[...]).astype(BF16)

    paced(width // step, qkv_cols, outer_steps + pair_core + scat.core_steps(False))
    spread_grad(grp, spread, gqkv_ref, qkvgot_ref, 0)
    run(scat.link_steps(True) + scat.link_steps(False))
    outer.finish()
    whole = outer.block(0)

    def output(part):
        out_ref[part] = (h_ref[part] + whole[part].astype(F32)).astype(BF16)

    tiles(rows, output)
    scat.finish()
    summed = scat.block(0)
    buf[0, 0:1] = jnp.zeros_like(gm_ref)
    buf[0, 1:2] = gm_ref[...]

    def back(part):
        dn, gain_part = norm_back_tile(
            x_ref[part].astype(F32), gain_ref[...].astype(F32), summed[part].astype(F32)
        )
        buf[0, 0:1] += gain_part
        tok_ref[part] = (dh_ref[part] + dn).astype(BF16)

    tiles(rows, back)
    sum_gains(grp, buf, gs, gr)
    gains_ref[...] = buf[buf.shape[0] - 1]
    outer.drain()
    scat.drain()
    spread.wait()


def gain_scratch(grp, width):
    n = grp.t_size + grp.z_size - 2
    return [
        pltpu.VMEM((grp.t_size + grp.z_size + 3, 2, width), F32),
        pltpu.SemaphoreType.DMA((n,)),
        pltpu.SemaphoreType.DMA((n,)),
    ]


def sum_gains(grp, buf, send, recv):
    z, t = grp.place()
    at, sem = 0, 0
    for index, size, peer in ((t, grp.t_size, grp.beside), (z, grp.z_size, grp.across)):
        copies = []
        for m in range(1, size):
            c = pltpu.make_async_remote_copy(
                src_ref=buf.at[at],
                dst_ref=buf.at[at + 1 + index],
                send_sem=send.at[sem],
                recv_sem=recv.at[sem],
                device_id=peer(m),
                device_id_type=MESH,
            )
            c.start()
            copies.append(c)
            sem += 1
        buf[at + 1 + index] = buf[at]
        for c in copies:
            c.wait()
        total = buf[at + 1]
        for i in range(1, size):
            total = total + buf[at + 1 + i]
        at += size + 1
        buf[at] = total


def last(
    grp, heads, branch, normed, part, grad_up, query, key, value, attended, lse, cosine, sine, start,
    wqkv, wo, hidden, x, dh, gain, gain_m, cid,
):
    rows, width = x.shape
    total = rows * grp.size
    wide = heads * HEAD
    length = start.shape[2]
    n = len(grp.masks)
    gout, gqkv = sds((wide, width), BF16), sds((width, 3 * wide), BF16)
    return pl.pallas_call(
        functools.partial(last_kernel, grp, heads),
        out_shape=[
            sds((rows, width), BF16),
            sds((rows, width), BF16),
            sds((2, width), F32),
            gout,
            gqkv,
            got_shape(grp, grad_up, 0),
            got_shape(grp, gout, 1),
            got_shape(grp, gqkv, 0),
        ],
        in_specs=[ANY] * 4 + [VMEM] * 15,
        out_specs=[VMEM] * 5 + [ANY] * 3,
        scratch_shapes=[
            pltpu.VMEM((total, width), BF16),
            pltpu.VMEM((n, rows, width), BF16),
            pltpu.SemaphoreType.DMA((n,)),
            pltpu.VMEM((2, QB, width), BF16),
            pltpu.SemaphoreType.DMA((2,)),
            pltpu.VMEM((2, total, cols_of(total)), BF16),
            pltpu.SemaphoreType.DMA((2,)),
            pltpu.VMEM((length, wide), BF16),
            pltpu.VMEM((total, 3 * wide), BF16),
            pltpu.VMEM((length, wide), F32),
            pltpu.VMEM((length, wide), F32),
            pltpu.VMEM((length, wide), F32),
            pltpu.VMEM((wide, width), F32),
        ]
        + gain_scratch(grp, width)
        + scatter_scratch(grp, rows, width)
        + scatter_scratch(grp, rows, width)
        + spread_sems(grp, 3 * PIECES),
        compiler_params=params(cid),
        name="last",
    )(
        branch, normed, part, grad_up, query, key, value, attended, lse, cosine, sine, start,
        wqkv, wo, hidden, x, dh, gain, gain_m,
    )


def got_shape(grp, grad, axis):
    shape = list(grad.shape)
    shape[axis] //= grp.z_size
    return sds((grp.z_size - 1, *shape), BF16)


def paced(count, body, steps, first=0):
    turns = count - first
    each = -(-len(steps) // turns) if steps else 0

    @pl.loop(0, count)
    def _(i):
        body(i)
        for k in range(turns):
            mine = steps[k * each : (k + 1) * each]
            if mine:

                @pl.when(i == first + k)
                def _(mine=mine):
                    for step in mine:
                        step()


def led(count, body, lists):
    @pl.loop(0, count)
    def _(i):
        for k, steps in enumerate(lists):

            @pl.when(i == k)
            def _(steps=steps):
                run(steps)

        body(i)


def gate_up(normed, wg, wu):
    gate = jnp.dot(normed, wg, preferred_element_type=F32)
    up = jnp.dot(normed, wu, preferred_element_type=F32)
    return (gate * jax.nn.sigmoid(gate) * up).astype(BF16), gate.astype(BF16), up.astype(BF16)


def cols_of(total):
    return max(128, 655360 // total // 128 * 128)


def mlp_kernel(grp, n_early, *refs):
    early, refs = refs[:n_early], refs[n_early:]
    (
        nm_ref,
        dyall_ref,
        wg_ref,
        wu_ref,
        down_all_ref,
        h_ref,
        dy_ref,
        gain_ref,
        down_ref,
        dh_ref,
        gm_ref,
        gdown_ref,
        ggate_ref,
        gup_ref,
        branch_ref,
        out_ref,
        downgot_ref,
        gategot_ref,
        p,
        wd,
        tile_n,
        tsem,
        act,
        dgu,
        cols,
        csem,
        dsem,
        *rest,
    ) = refs
    scat_refs, rest = rest[:N_SCATTER], rest[N_SCATTER:]
    send, recv, sem, zs, zr = rest
    rows, width = h_ref.shape
    size = 2 * rows
    n = len(grp.masks)
    units = wd.shape[0]
    step = cols.shape[2]

    def at(j):
        return pl.ds(pl.multiple_of(grp.chip_at(j) * size, size), size)

    def load(src, buf, k, j):
        return pltpu.make_async_copy(src.at[at(j)], buf.at[j % 2], tsem.at[k, j % 2])

    def load_cols(src, c):
        part = pl.ds(pl.multiple_of(c * step, step), step)
        return pltpu.make_async_copy(src.at[:, part], cols.at[c % 2], csem.at[c % 2])

    takes = []
    if n_early:
        takes = [
            pltpu.make_async_copy(src, dst, tsem.at[0, i])
            for i, (src, dst) in enumerate(zip(early, (act, dgu)))
        ]
        for c in takes:
            c.start()
    else:
        load(nm_ref, tile_n, 0, 0).start()
    grp.greet()
    spread = Spread(grp, zs, zr)
    spread.to(0, lambda: (down_all_ref, wd))

    def forward(j):
        @pl.when(j + 1 < n)
        def _():
            load(nm_ref, tile_n, 0, j + 1).start()

        load(nm_ref, tile_n, 0, j).wait()
        here = at(j)
        act[here], dgu[here, :units], dgu[here, units:] = gate_up(
            tile_n[j % 2], wg_ref[...], wu_ref[...]
        )

    load_cols(dyall_ref, 0).start()
    if n_early:
        for c in takes:
            c.wait()
    else:
        paced(n, forward, [])
    blocks = width // step

    def down_cols(c):
        @pl.when(c + 1 < blocks)
        def _():
            load_cols(dyall_ref, c + 1).start()

        load_cols(dyall_ref, c).wait()
        part = pl.ds(pl.multiple_of(c * step, step), step)
        gdown_ref[:, part] = dot_tn(cols[c % 2], act[...]).T.astype(BF16)

    load(dyall_ref, tile_n, 1, 0).start()
    paced(blocks, down_cols, [])
    spread.wait()
    spread_grad(grp, spread, gdown_ref, downgot_ref, 1)

    scat = Scatter(grp, p, rows, *scat_refs)
    chunk = min(512, width)

    def backward(j):
        @pl.when(j + 1 < n)
        def _():
            load(dyall_ref, tile_n, 1, j + 1).start()

        load(dyall_ref, tile_n, 1, j).wait()
        here = at(j)
        grad_act = dot_nt(tile_n[j % 2], wd[...])
        gate, up = dgu[here, :units].astype(F32), dgu[here, units:].astype(F32)
        sigma = jax.nn.sigmoid(gate)
        grad_gate = (grad_act * up * (sigma * (1.0 + gate * (1.0 - sigma)))).astype(BF16)
        grad_up = (grad_act * (gate * sigma)).astype(BF16)
        dgu[here, :units] = grad_gate
        dgu[here, units:] = grad_up
        for c in range(0, width, chunk):
            p[here, c : c + chunk] = (
                dot_nt(grad_gate, wg_ref[c : c + chunk]) + dot_nt(grad_up, wu_ref[c : c + chunk])
            ).astype(BF16)
        scat.begin_tile(j)

    core = scat.core_steps(True) + scat.core_steps(False)
    pair_links = scat.link_steps(True)
    todo = []
    late = n // 2
    share = -(-len(pair_links) // max(1, late - 1))
    for j in range(1, n):
        todo.append([core[j - 1]])
        if j > late:
            k = (j - late - 1) * share
            todo[-1] += pair_links[k : k + share]
    done = share * max(0, late - 1)
    paced(n, backward, [functools.partial(run, x) for x in todo], 1)
    rest_steps = [core[n - 1]] + pair_links[done:] + scat.link_steps(False)

    def gate_up_cols(c):
        @pl.when(c + 1 < blocks)
        def _():
            load_cols(nm_ref, c + 1).start()

        load_cols(nm_ref, c).wait()
        part = pl.ds(pl.multiple_of(c * step, step), step)
        grads = dot_tn(cols[c % 2], dgu[...]).astype(BF16)
        ggate_ref[part] = grads[:, :units]
        gup_ref[part] = grads[:, units:]

    load_cols(nm_ref, 0).start()
    paced(blocks, gate_up_cols, rest_steps)
    dy = scat_refs[0].at[n - 1]
    fetches = [
        pltpu.make_async_copy(dy_ref, dy, dsem.at[0]),
        pltpu.make_async_copy(h_ref, dh_ref, dsem.at[1]),
    ]
    for fetch in fetches:
        fetch.start()
    scat.finish()
    summed = scat.block(0)
    for fetch in fetches:
        fetch.wait()
    gm_ref[...] = jnp.zeros_like(gm_ref)

    def back(part):
        dn, gain_part = norm_back_tile(dh_ref[part], gain_ref[...].astype(F32), summed[part].astype(F32))
        gm_ref[...] += gain_part
        dh = dy[part].astype(F32) + dn
        dh_ref[part] = dh
        summed[part] = dh.astype(BF16)

    tiles(rows, back)
    gather = Gather(grp, summed, branch_ref, send, recv, sem)
    steps = gather.begin()
    spread_grad(grp, spread, ggate_ref, gategot_ref, 0, grp.far)
    scat.drain()

    def save(j):
        return pltpu.make_async_copy(tile_n.at[j % 2], out_ref.at[at(j)], tsem.at[0, j % 2])

    def branch(j):
        @pl.when(j > 1)
        def _():
            save(j - 2).wait()

        tile_n[j % 2] = jnp.dot(act[at(j)], wd[...], preferred_element_type=F32).astype(BF16)
        save(j).start()

    near = functools.partial(spread_grad, grp, spread, ggate_ref, gategot_ref, 0, (1,))
    paced(n, branch, steps[:6] + [near] + steps[6:], 1)
    save(n - 2).wait()
    save(n - 1).wait()
    gather.finish()
    spread.wait()


def mlp(grp, early, normed, dy_all, wg, wu, wd, hidden, dy, gain, w_down, cid):
    rows, width = hidden.shape
    total = rows * grp.size
    n = len(grp.masks)
    units = wg.shape[1]
    gdown, ggate = sds((units, width), BF16), sds((width, units), BF16)
    return pl.pallas_call(
        functools.partial(mlp_kernel, grp, len(early)),
        out_shape=[
            sds((rows, width), F32),
            sds((1, width), F32),
            gdown,
            ggate,
            ggate,
            sds((total, width), BF16),
            sds((total, width), BF16),
            got_shape(grp, gdown, 1),
            got_shape(grp, ggate, 0),
        ],
        in_specs=[ANY] * len(early) + [ANY, ANY, VMEM, VMEM, ANY, ANY, ANY, VMEM, ANY],
        out_specs=[VMEM] * 5 + [ANY] * 4,
        scratch_shapes=[
            pltpu.VMEM((total, width), BF16),
            pltpu.VMEM((units, width), BF16),
            pltpu.VMEM((2, 2 * rows, width), BF16),
            pltpu.SemaphoreType.DMA((2, 2)),
            pltpu.VMEM((total, units), BF16),
            pltpu.VMEM((total, 2 * units), BF16),
            pltpu.VMEM((2, total, cols_of(total)), BF16),
            pltpu.SemaphoreType.DMA((2,)),
            pltpu.SemaphoreType.DMA((2,)),
        ]
        + scatter_scratch(grp, rows, width)
        + gather_scratch(grp)
        + spread_sems(grp, 4),
        compiler_params=params(cid),
        name="mlp",
    )(*early, normed, dy_all, wg, wu, wd, hidden, dy, gain, w_down)


def fifth_kernel(grp, p_ref, h_ref, gup_ref, out_ref, up_ref, *rest):
    p, psem, rest = rest[0], rest[1], rest[2:]
    scat, rest = rest[:N_SCATTER], rest[N_SCATTER:]
    zs, zr = rest
    pltpu.make_async_copy(p_ref, p, psem).start()
    grp.greet()
    spread = Spread(grp, zs, zr)
    spread_grad(grp, spread, gup_ref, up_ref, 0)
    pltpu.make_async_copy(p_ref, p, psem).wait()
    acc = plain_scatter(grp, p, h_ref.shape[0], scat)

    def finish(rows):
        out_ref[rows] = (h_ref[rows] + acc[rows].astype(F32)).astype(BF16)

    tiles(h_ref.shape[0], finish)
    spread.wait()


def fifth(grp, part, hidden, grad_up, cid):
    rows, width = hidden.shape
    return pl.pallas_call(
        functools.partial(fifth_kernel, grp),
        out_shape=[sds((rows, width), BF16), got_shape(grp, grad_up, 0)],
        in_specs=[ANY, VMEM, ANY],
        out_specs=[VMEM, ANY],
        scratch_shapes=[pltpu.VMEM((rows * grp.size, width), BF16), pltpu.SemaphoreType.DMA]
        + scatter_scratch(grp, rows, width)
        + spread_sems(grp, 1),
        compiler_params=params(cid),
        name="fifth",
    )(part, hidden, grad_up)


def sixth_kernel(
    grp, p_ref, x_ref, dh_ref, gain_ref, gm_ref, gout_ref, gqkv_ref, tok_ref, gains_ref, o_ref, qkv_ref, *rest
):
    p, psem, rest = rest[0], rest[1], rest[2:]
    scat, rest = rest[:N_SCATTER], rest[N_SCATTER:]
    buf, gs, gr, zs, zr = rest
    pltpu.make_async_copy(p_ref, p, psem).start()
    grp.greet(everyone=True)
    spread = Spread(grp, zs, zr)
    spread_grad(grp, spread, gout_ref, o_ref, 1)
    spread_grad(grp, spread, gqkv_ref, qkv_ref, 0)
    pltpu.make_async_copy(p_ref, p, psem).wait()
    acc = plain_scatter(grp, p, x_ref.shape[0], scat)
    buf[0, 0:1] = jnp.zeros_like(gm_ref)
    buf[0, 1:2] = gm_ref[...]

    def back(rows):
        dn, gain_part = norm_back_tile(
            x_ref[rows].astype(F32), gain_ref[...].astype(F32), acc[rows].astype(F32)
        )
        buf[0, 0:1] += gain_part
        tok_ref[rows] = (dh_ref[rows] + dn).astype(BF16)

    tiles(x_ref.shape[0], back)
    sum_gains(grp, buf, gs, gr)
    gains_ref[...] = buf[buf.shape[0] - 1]
    spread.wait()


def sixth(grp, part, x, dh, gain, gain_m, grad_out, grad_qkv, cid):
    rows, width = x.shape
    return pl.pallas_call(
        functools.partial(sixth_kernel, grp),
        out_shape=[
            sds((rows, width), BF16),
            sds((2, width), F32),
            got_shape(grp, grad_out, 1),
            got_shape(grp, grad_qkv, 0),
        ],
        in_specs=[ANY, VMEM, VMEM, VMEM, VMEM, ANY, ANY],
        out_specs=[VMEM, VMEM, ANY, ANY],
        scratch_shapes=[pltpu.VMEM((rows * grp.size, width), BF16), pltpu.SemaphoreType.DMA]
        + scatter_scratch(grp, rows, width)
        + gain_scratch(grp, width)
        + spread_sems(grp, 2),
        compiler_params=params(cid),
        name="sixth",
    )(part, x, dh, gain, gain_m, grad_out, grad_qkv)


def swap_halves(value):
    half = HEAD // 2
    width = value.shape[1]
    pieces = []
    for at in range(0, width, HEAD):
        pieces.append(value[:, at + half : at + HEAD])
        pieces.append(value[:, at : at + half])
    if width % 128:
        return jnp.concatenate(pieces, axis=1)
    lane = lax.broadcasted_iota(jnp.int32, value.shape, 1)
    return jnp.where(
        lane % HEAD < half, pltpu.roll(value, width - half, 1), pltpu.roll(value, half, 1)
    )


QB = 256


def bands(length):
    for at in range(0, length, QB):
        first = max(0, at - SAMPLE)
        yield at, min(QB, length - at), first, at + min(QB, length - at) - first


def kept(start_row, at, size, first, width):
    key = first + lax.broadcasted_iota(jnp.int32, (width, size), 0)
    query = at + lax.broadcasted_iota(jnp.int32, (width, size), 1)
    return (key >= start_row) & (key <= query)


def attend_back_kernel(
    heads, q_ref, k_ref, v_ref, do_ref, lse_ref, cos_ref, sin_ref, start_ref, out_ref, dq, dk, dv
):
    wide = heads * HEAD
    length = q_ref.shape[0]
    dk[...] = jnp.zeros_like(dk)
    dv[...] = jnp.zeros_like(dv)
    for h in range(heads):
        lanes = slice(h * HEAD, (h + 1) * HEAD)
        for at, size, first, width in bands(length):
            query = q_ref[at : at + size, lanes]
            key = k_ref[first : first + width, lanes]
            value = v_ref[first : first + width, lanes]
            grad = do_ref[at : at + size, lanes]
            scores = dot_nt(key, query * BF16(HEAD**-0.5))
            mask = kept(start_ref[0, :, at : at + size], at, size, first, width)
            weights = jnp.where(
                mask, jnp.exp(jnp.where(mask, scores, -1e9) - lse_ref[0, h : h + 1, at : at + size]), 0.0
            )
            dv[first : first + width, lanes] += jnp.dot(
                weights.astype(BF16), grad, preferred_element_type=F32
            )
            grad_weights = dot_nt(value, grad)
            inner = jnp.sum(weights * grad_weights, axis=0, keepdims=True)
            grad_scores = (weights * (grad_weights - inner)).astype(BF16)
            dq[at : at + size, lanes] = dot_tn(grad_scores, key)
            dk[first : first + width, lanes] += jnp.dot(
                grad_scores, query, preferred_element_type=F32
            )

    @pl.loop(0, length // QB)
    def _(i):
        rows = pl.ds(pl.multiple_of(i * QB, QB), QB)
        cosine, sine = cos_ref[rows], sin_ref[rows]
        query, key = dq[rows] * HEAD**-0.5, dk[rows] * HEAD**-0.5
        out_ref[rows, :wide] = (query * cosine - swap_halves(query) * sine).astype(BF16)
        out_ref[rows, wide : 2 * wide] = (key * cosine - swap_halves(key) * sine).astype(BF16)
        out_ref[rows, 2 * wide :] = dv[rows].astype(BF16)


def attend_back(query, key, value, grad, lse, cosine, sine, start, heads):
    rows, _, length = start.shape
    wide = heads * HEAD

    def tall(width):
        return pl.BlockSpec((length, width), lambda r: (r, 0))

    return pl.pallas_call(
        functools.partial(attend_back_kernel, heads),
        grid=(rows,),
        out_shape=jax.ShapeDtypeStruct((rows * length, 3 * wide), BF16),
        in_specs=[tall(wide)] * 4
        + [pl.BlockSpec((1, heads, length), lambda r: (r, 0, 0)), tall(wide), tall(wide)]
        + [pl.BlockSpec((1, 1, length), lambda r: (r, 0, 0))],
        out_specs=tall(3 * wide),
        scratch_shapes=[pltpu.VMEM((length, wide), F32)] * 3,
        compiler_params=pltpu.CompilerParams(vmem_limit_bytes=48 << 20),
        name="attend_back",
    )(query, key, value, grad, lse, cosine, sine, start)


def finish_kernel(z_size, parts, z_ref, *refs):
    low = z_ref[0] % 2
    n = len(parts)
    owns, gots, outs = refs[:n], refs[n : 2 * n], list(refs[2 * n :])
    for own, got, (axis, count) in zip(owns, gots, parts):
        sums = [own[...].astype(F32), None]
        for m in range(1, z_size):
            term = got[m - 1].astype(F32)
            sums[m % 2] = term if sums[m % 2] is None else sums[m % 2] + term
        if axis == 0:
            out = outs.pop(0)
            out[low] = sums[0]
            out[1 - low] = sums[1]
            continue
        width = sums[0].shape[1] // count
        for i in range(count):
            out = outs.pop(0)
            for which, total in ((low, sums[0]), (1 - low, sums[1])):
                place = pl.ds(pl.multiple_of(which * width, width), width)
                out[:, place] = total[:, i * width : (i + 1) * width]


def finish(z_size, z, grads, gots, axes):
    steps = 4
    owns, blocks, outs, shapes = [], [], [], []
    for grad, got, (axis, count) in zip(grads, gots, axes):
        rows, cols = got.shape[1] // steps, got.shape[2]
        if axis == 0:
            owns.append(pl.BlockSpec((rows, cols), lambda i, z_ref: (i, z_ref[0])))
            outs.append(pl.BlockSpec((2, rows, cols), lambda i, z_ref: (0, i, 0)))
            shapes.append(sds((2, rows * steps, cols), F32))
        else:
            owns.append(pl.BlockSpec((rows, cols), lambda i, z_ref: (z_ref[0] * steps + i, 0)))
            wide = 2 * cols // count
            outs += [pl.BlockSpec((rows, wide), lambda i, z_ref: (i, 0))] * count
            shapes += [sds((rows * steps, wide), F32)] * count
        blocks.append(pl.BlockSpec((z_size - 1, rows, cols), lambda i, z_ref: (0, i, 0)))
    return pl.pallas_call(
        functools.partial(finish_kernel, z_size, axes),
        out_shape=shapes,
        grid_spec=pltpu.PrefetchScalarGridSpec(
            num_scalar_prefetch=1, grid=(steps,), in_specs=owns + blocks, out_specs=outs
        ),
        compiler_params=pltpu.CompilerParams(vmem_limit_bytes=56 << 20),
        name="finish",
    )(jnp.reshape(z, (1,)), *grads, *gots)


def shards(
    z_size,
    t_size,
    tokens,
    gain_attn,
    gain_mlp,
    w_query,
    w_key,
    w_value,
    w_out,
    w_gate,
    w_up,
    w_down,
    segment_ids,
    out_grad,
):
    grp = Group(z_size, t_size)
    z = lax.axis_index("fsdp")
    low = z % 2

    def deliver(grad, got, half_axis, axis, parts=1):
        size = grad.shape[axis] // z_size
        sums = [lax.dynamic_slice_in_dim(grad, z * size, size, axis).astype(F32), None]
        for m in range(1, z_size):
            term = got[m - 1].astype(F32)
            sums[m % 2] = term if sums[m % 2] is None else sums[m % 2] + term
        outs = []
        piece = sums[0].shape[half_axis] // parts
        for i in range(parts):
            a, b = (lax.slice_in_dim(s, i * piece, (i + 1) * piece, axis=half_axis) for s in sums)
            outs.append(
                jnp.where(
                    low == 0,
                    jnp.concatenate([a, b], axis=half_axis),
                    jnp.concatenate([b, a], axis=half_axis),
                )
            )
        return outs

    wide = w_query.shape[1] // 2
    heads = wide // HEAD

    gain_a = gain_attn[None, :]
    gain_m = gain_mlp[None, :]
    normed_a, wqkv, wo, start, cosine, sine = first(
        grp, low, tokens, gain_a, w_query, w_key, w_value, w_out, segment_ids, 0
    )
    query, key, value, attended, lse, hidden, normed_m, grad_all, wg, wu, wd, *early = middle(
        grp,
        heads,
        normed_a,
        wqkv,
        wo,
        cosine,
        sine,
        start,
        out_grad,
        tokens,
        gain_m,
        w_gate,
        w_up,
        w_down,
        1,
    )
    grad_hidden, gain_m_part, grad_down, grad_wg, grad_wu, branch_all, out_part, got_down, got_gate = mlp(
        grp, early, normed_m, grad_all, wg, wu, wd, hidden, out_grad, gain_m, w_down, 3
    )
    if grp.size <= 16:
        output, tokens_grad, gains, grad_wout, grad_wqkv, got_up, got_out, got_qkv = last(
            grp, heads, branch_all, normed_a, out_part, grad_wu, query, key, value, attended, lse,
            cosine, sine, start, wqkv, wo, hidden, tokens, grad_hidden, gain_a, gain_m_part, 4,
        )
    else:
        output, got_up = fifth(grp, out_part, hidden, grad_wu, 4)
        grad_wout = dot_tn(attended, branch_all).astype(BF16)
        grad_attended = dot_nt(branch_all, wo).astype(BF16)
        grad_qkv = attend_back(query, key, value, grad_attended, lse, cosine, sine, start, heads)
        grad_wqkv = dot_tn(normed_a, grad_qkv).astype(BF16)
        grad_na = dot_nt(grad_qkv, wqkv).astype(BF16)
        tokens_grad, gains, got_out, got_qkv = sixth(
            grp, grad_na, tokens, grad_hidden, gain_a, gain_m_part, grad_wout, grad_wqkv, 5
        )
    grads = (grad_down, grad_wg, grad_wu, grad_wout, grad_wqkv)
    gots = (got_down, got_gate, got_up, got_out, got_qkv)
    axes = ((0, 1), (1, 1), (1, 1), (0, 1), (1, 3))
    if wide % LANES == 0:
        outs = finish(z_size, z, grads, gots, axes)
        down_out, out_out = (x.reshape(-1, x.shape[2]) for x in (outs[0], outs[3]))
        gate_out, up_out = outs[1:3]
        query_out, key_out, value_out = outs[4:]
    else:
        (down_out,) = deliver(grad_down, got_down, 0, 1)
        (gate_out,) = deliver(grad_wg, got_gate, 1, 0)
        (up_out,) = deliver(grad_wu, got_up, 1, 0)
        (out_out,) = deliver(grad_wout, got_out, 0, 1)
        query_out, key_out, value_out = deliver(grad_wqkv, got_qkv, 1, 0, 3)
    return (
        output,
        tokens_grad,
        gains[0],
        gains[1],
        query_out,
        key_out,
        value_out,
        out_out,
        gate_out,
        up_out,
        down_out,
    )


def solution(mesh):
    return jax.shard_map(
        functools.partial(shards, mesh.shape["fsdp"], mesh.shape["tensor"]),
        mesh=mesh,
        in_specs=(
            P(("fsdp", "tensor"), None),
            P(),
            P(),
            P("fsdp", "tensor"),
            P("fsdp", "tensor"),
            P("fsdp", "tensor"),
            P("tensor", "fsdp"),
            P("fsdp", "tensor"),
            P("fsdp", "tensor"),
            P("tensor", "fsdp"),
            P("fsdp", None),
            P(("fsdp", "tensor"), None),
        ),
        out_specs=(
            P(("fsdp", "tensor"), None),
            P(("fsdp", "tensor"), None),
            P(),
            P(),
            P("fsdp", "tensor"),
            P("fsdp", "tensor"),
            P("fsdp", "tensor"),
            P("tensor", "fsdp"),
            P("fsdp", "tensor"),
            P("fsdp", "tensor"),
            P("tensor", "fsdp"),
        ),
        check_vma=False,
    )
```

```python
import functools
import math

import jax
import jax.numpy as jnp
from jax import lax
from jax.experimental import pallas as pl
from jax.experimental.pallas import tpu as pltpu
from jax.sharding import PartitionSpec as P

HEAD = 64
SAMPLE = 512
EPS = 1e-05
LANES = 128
ROPE_BASE = 130000.0
MESH = pl.DeviceIdType.MESH
BF16 = jnp.bfloat16
F32 = jnp.float32
ANY = pl.BlockSpec(memory_space=pl.ANY)
VMEM = pl.BlockSpec(memory_space=pltpu.VMEM)


def flip(index, bit):
    return index + bit - 2 * bit * ((index // bit) % 2)


def dot_nt(left, right):
    return lax.dot_general(left, right, (((1,), (1,)), ((), ())), preferred_element_type=F32)


def dot_tn(left, right):
    return lax.dot_general(left, right, (((0,), (0,)), ((), ())), preferred_element_type=F32)


class Group:
    def __init__(self, z_size, t_size):
        self.z_size = z_size
        self.t_size = t_size
        self.size = 2 * t_size
        inner = []
        bit = 2
        while bit < t_size:
            inner.append(bit)
            bit *= 2
        self.core = 1
        self.pair = t_size
        self.orders = (tuple(inner) + (self.pair,), tuple(inner[::-1]) + (self.pair,))
        self.inner = (tuple(inner), tuple(inner[::-1]))
        self.bits = (self.core,) + tuple(inner) + (self.pair,)
        masks = [0]
        for b in self.orders[0]:
            masks = masks + [m + b for m in masks]
        self.masks = tuple(masks)
        self.far = tuple(range(2, z_size))

    def place(self):
        return lax.axis_index("fsdp"), lax.axis_index("tensor")

    def rank(self, mask=0):
        z, t = self.place()
        r = (z % 2) * self.t_size + t
        for b in self.bits:
            if mask & b:
                r = flip(r, b)
        return r

    def chip_at(self, j, near=False):
        chip = self.rank() // 2
        mask = j if near else len(self.masks) - 1 - j
        out = 0
        bit = 1
        while bit < len(self.masks):
            a, b = (chip // bit) % 2, (mask // bit) % 2
            out = out + (a + b - 2 * a * b) * bit
            bit *= 2
        return out

    def partner(self, bit):
        z, t = self.place()
        if bit == self.pair:
            return (flip(z, 1), t)
        return (z, flip(t, bit))

    def across(self, mask):
        z, t = self.place()
        bit = 1
        while bit < self.z_size:
            if mask & bit:
                z = flip(z, bit)
            bit *= 2
        return (z, t)

    def beside(self, mask):
        z, t = self.place()
        bit = 1
        while bit < self.t_size:
            if mask & bit:
                t = flip(t, bit)
            bit *= 2
        return (z, t)

    def greet(self, everyone=False):
        barrier = pltpu.get_barrier_semaphore()
        if everyone:
            peers = [self.beside(m) for m in range(1, self.t_size)]
        else:
            peers = [self.partner(b) for b in self.bits if b != self.pair]
        peers += [self.across(m) for m in range(1, self.z_size)]
        for peer in peers:
            pl.semaphore_signal(barrier, inc=1, device_id=peer, device_id_type=MESH)
        pl.semaphore_wait(barrier, len(peers))


def last_bit(mask, order):
    found = None
    for b in order:
        if mask & b:
            found = b
    return found


class Gather:
    def __init__(self, grp, x_ref, o_ref, send, recv, local):
        self.grp, self.x, self.o = grp, x_ref, o_ref
        self.send, self.recv = send, recv
        self.rows = x_ref.shape[0]
        self.half = self.rows // 2
        self.order = [(grp.pair,) + grp.inner[h] + (grp.core,) for h in range(2)]
        self.sent = []
        own = pl.ds(pl.multiple_of(grp.rank() * self.rows, self.rows), self.rows)
        self.own = pltpu.make_async_copy(x_ref, o_ref.at[own], local)

    def at(self, mask, h):
        first = self.grp.rank(mask) * self.rows + h * self.half
        return self.o.at[pl.ds(pl.multiple_of(first, self.half), self.half)]

    def copy(self, src, mask, h, key, bit):
        return pltpu.make_async_remote_copy(
            src_ref=src,
            dst_ref=self.at(mask, h),
            send_sem=self.send.at[h, key],
            recv_sem=self.recv.at[h, key],
            device_id=self.grp.partner(bit),
            device_id_type=MESH,
        )

    def forward(self, h, mask, bits=None):
        order = self.order[h]
        start = 0 if mask == 0 else order.index(last_bit(mask, order)) + 1
        for bit in order[start:] if bits is None else bits:
            self.own_copy(h, mask, bit).start()
            self.sent.append((h, mask, bit))

    def own_copy(self, h, mask, bit):
        src = self.x.at[pl.ds(h * self.half, self.half)] if mask == 0 else self.at(mask, h)
        return self.copy(src, mask, h, mask | bit, bit)

    def arrived(self, h, mask):
        bit = last_bit(mask, self.order[h])
        self.copy(self.at(mask, h), mask, h, mask, bit).wait_recv()

    def begin(self):
        self.own.start()
        for h in range(2):
            self.forward(h, 0, (self.grp.pair,))
        for k in range(1, len(self.order[0])):
            for h in range(2):
                self.forward(h, 0, (self.order[h][k],))
        grp = self.grp
        plain = sorted(
            (m for m in grp.masks if m), key=lambda m: (m & grp.pair, bin(m).count("1"))
        )
        if len(plain) > 3:
            plain.remove(grp.pair)
            plain.insert(2, grp.pair)
        self.plain = plain

        def step(h, m):
            self.arrived(h, m)
            self.forward(h, m)

        return [
            functools.partial(step, h, m if h == 0 else mirror(grp, m))
            for m in plain
            for h in range(2)
        ]

    def chip_arrived(self, mask):
        for h in range(2):
            self.arrived(h, mask | self.grp.core)
        if mask == 0:
            self.own.wait()

    def needs(self, steps):
        plain = self.plain
        done = 0
        out = []
        for m in sorted(self.grp.masks):
            upto = done
            if m:
                other = next(k for k in plain if mirror(self.grp, k) == m)
                upto = 2 * (max(plain.index(m), plain.index(other)) + 1)
            out.append(steps[done : max(done, upto)] + [functools.partial(self.chip_arrived, m)])
            done = max(done, upto)
        return out

    def finish(self):
        for m in self.grp.masks:
            self.chip_arrived(m)
        self.drain()

    def drain(self):
        for sent in self.sent:
            self.own_copy(*sent).wait_send()


def mirror(grp, mask):
    out = mask & (grp.pair | grp.core)
    a, b = grp.inner
    for p, q in zip(a, b):
        if mask & p:
            out |= q
    return out


TILE = 16


def add_rows(dst, src, rows):
    @pl.loop(0, rows // TILE)
    def _(i):
        part = pl.ds(pl.multiple_of(i * TILE, TILE), TILE)
        dst[part] = (dst[part].astype(F32) + src[part].astype(F32)).astype(dst.dtype)


def scatter_scratch(grp, rows, width):
    n = len(grp.masks)
    return [
        pltpu.VMEM((n, rows, width), BF16),
        pltpu.VMEM((2, n - 1, rows // 2, width), BF16),
        pltpu.SemaphoreType.DMA((n,)),
        pltpu.SemaphoreType.DMA((n,)),
        pltpu.SemaphoreType.DMA((2, n)),
        pltpu.SemaphoreType.DMA((2, n)),
    ]


N_SCATTER = 6


class Scatter:
    def __init__(self, grp, p, rows, got, rbuf, csend, crecv, send, recv, own=None):
        self.grp, self.p, self.rows, self.half = grp, p, rows, rows // 2
        self.own = own
        self.got, self.rbuf = got, rbuf
        self.csend, self.crecv, self.send, self.recv = csend, crecv, send, recv
        self.index = {m: len(grp.masks) - 1 - m // 2 for m in grp.masks}
        self.started = []
        self.slots = []
        for h in range(2):
            s = {}
            order = grp.orders[h]
            for i in range(len(order)):
                later = order[i + 1 :]
                for m in grp.masks:
                    if all((not m & b) or b in later for b in order):
                        s[(i, m)] = len(s)
            self.slots.append(s)

    def masks(self, pair):
        chosen = [m for m in self.grp.masks if bool(m & self.grp.pair) == pair]
        return sorted(chosen, reverse=True)

    def begin_tile(self, j):
        _, t = self.grp.place()
        first = (self.grp.chip_at(j) * 2 + 1 - t % 2) * self.rows
        pltpu.make_async_remote_copy(
            src_ref=self.p.at[pl.ds(pl.multiple_of(first, self.rows), self.rows)],
            dst_ref=self.got.at[j],
            send_sem=self.csend.at[j],
            recv_sem=self.crecv.at[j],
            device_id=self.grp.partner(self.grp.core),
            device_id_type=MESH,
        ).start()

    def block(self, mask, h=None):
        if self.own is not None and not mask & self.grp.core:
            mine = self.own.at[self.index[mask]]
            return mine if h is None else mine.at[pl.ds(h * self.half, self.half)]
        first = self.grp.rank(mask) * self.rows
        if h is None:
            return self.p.at[pl.ds(pl.multiple_of(first, self.rows), self.rows)]
        return self.p.at[pl.ds(pl.multiple_of(first + h * self.half, self.half), self.half)]

    def core_copy(self, mask):
        i = self.index[mask]
        return pltpu.make_async_remote_copy(
            src_ref=self.block(mask | self.grp.core),
            dst_ref=self.got.at[i],
            send_sem=self.csend.at[i],
            recv_sem=self.crecv.at[i],
            device_id=self.grp.partner(self.grp.core),
            device_id_type=MESH,
        )

    def begin(self, masks):
        for m in masks:
            self.core_copy(m).start()

    def load(self, mask, sem):
        first = pl.multiple_of(self.grp.rank(mask) * self.rows, self.rows)
        i = self.index[mask]
        return pltpu.make_async_copy(self.p.at[pl.ds(first, self.rows)], self.own.at[i], sem.at[i])

    def core_step(self, mask):
        self.core_copy(mask).wait_recv()
        add_rows(self.block(mask), self.got.at[self.index[mask]], self.rows)
        for h in range(2):
            if mask & self.grp.orders[h][0]:
                self.ship(h, 0, mask)

    def link_copy(self, h, i, mask, k):
        return pltpu.make_async_remote_copy(
            src_ref=self.block(mask, h),
            dst_ref=self.rbuf.at[h, k],
            send_sem=self.send.at[h, k],
            recv_sem=self.recv.at[h, k],
            device_id=self.grp.partner(self.grp.orders[h][i]),
            device_id_type=MESH,
        )

    def ship(self, h, i, mask):
        self.out_copy(h, i, mask).start()
        self.started.append((h, i, mask))

    def out_copy(self, h, i, mask):
        return self.link_copy(h, i, mask, self.slots[h][(i, mask - self.grp.orders[h][i])])

    def take(self, h, i, mask):
        k = self.slots[h][(i, mask)]
        self.link_copy(h, i, mask, k).wait_recv()
        add_rows(self.block(mask, h), self.rbuf.at[h, k], self.half)

    def core_steps(self, pair):
        return [functools.partial(self.core_step, m) for m in self.masks(pair)]

    def link_steps(self, pair):
        steps = []
        for i in range(1, len(self.grp.orders[0])):
            for m in self.masks(pair):
                for h in range(2):
                    order = self.grp.orders[h]
                    mine = m if h == 0 else mirror(self.grp, m)
                    if any(mine & b for b in order[:i]):
                        continue

                    def step(h=h, i=i, mine=mine, order=order):
                        self.take(h, i - 1, mine)
                        if mine & order[i]:
                            self.ship(h, i, mine)

                    steps.append(step)
        return steps

    def finish(self):
        for h in range(2):
            self.take(h, len(self.grp.orders[h]) - 1, 0)

    def drain(self):
        for m in self.grp.masks:
            self.core_copy(m).wait_send()
        for sent in self.started:
            self.out_copy(*sent).wait_send()


def plain_scatter(grp, p, rows, refs):
    scat = Scatter(grp, p, rows, *refs)
    scat.begin(scat.masks(True) + scat.masks(False))
    run(scat.core_steps(True) + scat.core_steps(False))
    run(scat.link_steps(True) + scat.link_steps(False))
    scat.finish()
    scat.drain()
    return scat.block(0)


def run(*lists):
    for i in range(max(len(x) for x in lists)):
        for steps in lists:
            if i < len(steps):
                steps[i]()


class Spread:
    def __init__(self, grp, send, recv):
        self.grp, self.send, self.recv = grp, send, recv
        self.used = 0
        self.makers = []

    def to(self, mask, views, start=True):
        k = self.used
        self.used += 1

        def make():
            src, dst = views()
            if mask == 0:
                return pltpu.make_async_copy(src, dst, self.send.at[k])
            return pltpu.make_async_remote_copy(
                src_ref=src,
                dst_ref=dst,
                send_sem=self.send.at[k],
                recv_sem=self.recv.at[k],
                device_id=self.grp.across(mask),
                device_id_type=MESH,
            )

        if start:
            make().start()
        self.makers.append(make)
        return make

    def wait(self):
        self.wait_first(len(self.makers))

    def wait_first(self, count):
        for make in self.makers[:count]:
            make().wait()
        self.makers = self.makers[count:]


def spread_sems(grp, parts):
    return [pltpu.SemaphoreType.DMA((grp.z_size * parts,))] * 2


def spread_weight(grp, spread, shard, whole, half_axis, at, masks=None, start=True):
    axis = 1 - half_axis
    mine, other = shard
    makers = []
    for m in grp.far + (0, 1) if masks is None else masks:

        def views(src=other if m % 2 else mine):
            z, _ = grp.place()
            size, width = src.shape[axis], src.shape[half_axis]
            place = pl.ds(pl.multiple_of(z * size, size), size)
            if axis == 0:
                return src, whole.at[place, at : at + width]
            return src, whole.at[at : at + width, place]

        makers.append(spread.to(m, views, start))
    return makers


def halves_of(grp, ref, axis):
    z, _ = grp.place()
    size = ref.shape[axis] // 2
    out = []
    for which in (z % 2, 1 - z % 2):
        part = pl.ds(pl.multiple_of(which * size, size), size)
        out.append(ref.at[:, part] if axis == 1 else ref.at[part])
    return out


def weight_jobs(grp, spread, shard, whole, half_axis, pieces):
    axis = 1 - half_axis
    mine, other = shard
    jobs = {m: [] for m in range(grp.z_size)}
    for i in range(pieces):
        for m in range(grp.z_size):

            def views(i=i, src=other if m % 2 else mine):
                z, _ = grp.place()
                size, width = src.shape[0] // pieces, src.shape[1]
                piece = src.at[pl.ds(i * size, size)]
                if axis == 0:
                    first = pl.multiple_of(z * (size * pieces) + i * size, size)
                    return piece, whole.at[pl.ds(first, size)]
                place = pl.ds(pl.multiple_of(z * width, width), width)
                return piece, whole.at[pl.ds(i * size, size), place]

            jobs[m].append(functools.partial(spread.to, m, views))
    return by_distance(grp, jobs)


def grad_jobs(grp, spread, grad, got, axis, pieces):
    jobs = {m: [] for m in range(1, grp.z_size)}
    for i in range(pieces):
        for m in range(1, grp.z_size):

            def views(i=i, m=m):
                place = grp.across(m)[0]
                size = got.shape[1] // pieces
                land = got.at[m - 1, pl.ds(i * size, size)]
                if axis == 0:
                    first = pl.multiple_of(place * (size * pieces) + i * size, size)
                    return grad.at[pl.ds(first, size)], land
                width = got.shape[2]
                part = pl.ds(pl.multiple_of(place * width, width), width)
                return grad.at[pl.ds(i * size, size), part], land

            jobs[m].append(functools.partial(spread.to, m, views))
    return by_distance(grp, jobs)


def by_distance(grp, jobs):
    far = [job for jobs_i in zip(*(jobs[m] for m in grp.far)) for job in jobs_i]
    near = [job for jobs_i in zip(*(jobs[m] for m in (1, 0) if m in jobs)) for job in jobs_i]
    return far, near


def mixed(steps, jobs, first=0):
    out = list(steps[:first])
    tail = steps[first:]
    done = 0
    for i, step in enumerate(tail):
        upto = (i + 1) * len(jobs) // len(tail)
        out.append(functools.partial(run, [step] + jobs[done:upto]))
        done = upto
    return out + (jobs if not tail else [])


PIECES = 1


def spread_grad(grp, spread, grad, got, axis, masks=None, start=True):
    makers = []
    for m in grp.far + (1,) if masks is None else masks:

        def views(m=m):
            size = grad.shape[axis] // grp.z_size
            part = pl.ds(pl.multiple_of(grp.across(m)[0] * size, size), size)
            return (grad.at[part] if axis == 0 else grad.at[:, part]), got.at[m - 1]

        makers.append(spread.to(m, views, start))
    return makers


def launch(makers, where=None):
    if where is None:
        for make in makers:
            make().start()
    else:

        @pl.when(where)
        def _():
            for make in makers:
                make().start()


def inner_plane(grp):
    z, _ = grp.place()
    return (z * 4 >= grp.z_size) & (z * 4 < 3 * grp.z_size)


def staged_gather(gather, after_pair):
    steps = gather.begin()
    cut = 6 if len(steps) > 6 else len(steps)
    run(steps[:cut])
    after_pair()
    run(steps[cut:])
    gather.finish()


def tiles(rows, body):
    @pl.loop(0, rows // TILE)
    def _(i):
        body(pl.ds(pl.multiple_of(i * TILE, TILE), TILE))


def norm_scale(value):
    return lax.rsqrt(jnp.mean(value * value, axis=-1, keepdims=True) + EPS)


def gather_scratch(grp):
    return [
        pltpu.SemaphoreType.DMA((2, grp.size)),
        pltpu.SemaphoreType.DMA((2, grp.size)),
        pltpu.SemaphoreType.DMA,
    ]


def params(cid):
    return pltpu.CompilerParams(
        collective_id=cid, has_side_effects=True, vmem_limit_bytes=61952 << 10
    )


def sds(shape, dtype):
    return jax.ShapeDtypeStruct(shape, dtype)


def weight_views(grp, refs, axis, presliced):
    if presliced:
        return [(refs[2 * i], refs[2 * i + 1]) for i in range(len(refs) // 2)]
    return [tuple(halves_of(grp, r, axis)) for r in refs]


def shard_args(low, shards_, axis):
    aligned = shards_[0].shape[axis] // 2 % (128 if axis == 1 else 16) == 0
    if aligned:
        return False, list(shards_)
    out = []
    for w in shards_:
        size = w.shape[axis] // 2
        out += [
            lax.dynamic_slice_in_dim(w, low * size, size, axis),
            lax.dynamic_slice_in_dim(w, (1 - low) * size, size, axis),
        ]
    return True, out


def first_kernel(grp, flags, n_qkv, x_ref, gain_ref, *rest):
    pre_qkv, pre_o = flags
    qkv_refs, rest = rest[:n_qkv], rest[n_qkv:]
    n_o = 2 if pre_o else 1
    o_refs, rest = rest[:n_o], rest[n_o:]
    seg_ref, all_ref, wqkv_ref, wo_ref, start_ref, cos_ref, sin_ref, local, ids, send, recv, sem, zs, zr = rest
    grp.greet()
    spread = Spread(grp, zs, zr)
    z, _ = grp.place()
    spread.to(0, lambda: (seg_ref, ids.at[z % 2]))
    spread.to(1, lambda: (seg_ref, ids.at[z % 2]))

    def weights(masks):
        at = 0
        for pair in weight_views(grp, qkv_refs, 1, pre_qkv):
            spread_weight(grp, spread, pair, wqkv_ref, 1, at, masks)
            at += pair[0].shape[1]
        for pair in weight_views(grp, o_refs, 0, pre_o):
            spread_weight(grp, spread, pair, wo_ref, 0, 0, masks)

    def norm(rows):
        x = x_ref[rows].astype(F32)
        local[rows] = (x * norm_scale(x) * gain_ref[0:1].astype(F32)).astype(BF16)

    tiles(x_ref.shape[0], norm)
    gather = Gather(grp, local, all_ref, send, recv, sem)
    steps = gather.begin()
    weights((1,) + grp.far + (0,))
    spread.wait_first(2)
    places(ids, start_ref, cos_ref, sin_ref)
    run(steps[:6])
    run(steps[6:] or [lambda: None])
    gather.finish()
    spread.wait()


def places(ids, start_ref, cos_ref, sin_ref):
    planes, rows, length = ids.shape
    wide = cos_ref.shape[1]
    place = lax.broadcasted_iota(jnp.int32, (1, length), 1)
    lane = lax.broadcasted_iota(jnp.int32, (LANES, LANES), 1)
    pair = (lane % (HEAD // 2)).astype(F32)
    inverse = jnp.exp(pair * (-2.0 / HEAD) * math.log(ROPE_BASE))
    sign = jnp.where(lane % HEAD < HEAD // 2, -1.0, 1.0)
    for a in range(planes):
        for r in range(rows):
            row = a * rows + r
            own = ids[a, r : r + 1]
            change = (place == 0) | (own != pltpu.roll(own, 1, 1))
            start = jnp.where(change, place, 0)
            step = 1
            while step < length:
                start = jnp.maximum(start, jnp.where(place >= step, pltpu.roll(start, step, 1), 0))
                step *= 2
            start_ref[row] = start

    @pl.loop(0, planes * rows)
    def _(row):
        @pl.loop(0, length // LANES)
        def _(c):
            here = pl.ds(pl.multiple_of(c * LANES, LANES), LANES)
            token = c * LANES + lax.broadcasted_iota(jnp.int32, (1, LANES), 1)
            position = (token - start_ref[row, :, here]).astype(F32)
            angle = jnp.broadcast_to(position, (LANES, LANES)).T * inverse
            there = pl.ds(pl.multiple_of(row * length + c * LANES, LANES), LANES)
            cos_ref[there] = jnp.cos(angle)[:, :wide]
            sin_ref[there] = (sign * jnp.sin(angle))[:, :wide]


def first(grp, low, x, gain, w_query, w_key, w_value, w_out, ids, cid):
    pre_qkv, qkv = shard_args(low, (w_query, w_key, w_value), 1)
    pre_o, out = shard_args(low, (w_out,), 0)
    rows, width = x.shape
    if pre_qkv:
        qkv = [jnp.concatenate(qkv[i::2], axis=1) for i in range(2)]
    deep = w_query.shape[0] * grp.z_size
    thin = 3 * w_query.shape[1] // 2
    table = sds((2 * ids.shape[0] * ids.shape[1], thin // 3), F32)
    return pl.pallas_call(
        functools.partial(first_kernel, grp, (pre_qkv, pre_o), len(qkv)),
        out_shape=[
            sds((rows * grp.size, width), BF16),
            sds((deep, thin), BF16),
            sds((w_out.shape[0] // 2, w_out.shape[1] * grp.z_size), BF16),
            sds((2 * ids.shape[0], 1, ids.shape[1]), jnp.int32),
            table,
            table,
        ],
        in_specs=[VMEM, VMEM] + [ANY] * (len(qkv) + len(out)) + [VMEM],
        out_specs=[ANY] * 3 + [VMEM] * 3,
        scratch_shapes=[
            pltpu.VMEM((rows, width), BF16),
            pltpu.VMEM((2,) + ids.shape, jnp.int32),
        ]
        + gather_scratch(grp)
        + spread_sems(grp, 5),
        compiler_params=params(cid),
        name="first",
    )(x, gain, *qkv, *out, ids)


def attend_rows(length, heads, q_ref, k_ref, v_ref, start_ref, o_ref, lse_ref, row):
    base = row * length

    def band(h, at, first, width, size):
        lanes = slice(h * HEAD, (h + 1) * HEAD)
        mine = pl.ds(pl.multiple_of(base + at, QB), size)
        keys = pl.ds(pl.multiple_of(base + first, QB), width)
        cols = pl.ds(pl.multiple_of(at, QB), size)
        query = q_ref[mine, lanes] * BF16(HEAD**-0.5)
        scores = dot_nt(k_ref[keys, lanes], query)
        mask = kept(start_ref[row, :, cols], at, size, first, width)
        scores = jnp.where(mask, scores, -1e9)
        top = jnp.max(scores, axis=0, keepdims=True)
        expo = jnp.exp(scores - top)
        total = jnp.sum(expo, axis=0, keepdims=True)
        weights = (expo * (1.0 / total)).astype(BF16)
        o_ref[mine, lanes] = dot_tn(weights, v_ref[keys, lanes]).astype(BF16)
        lse_ref[row, h : h + 1, cols] = top + jnp.log(total)

    return banded(length, heads, band)


def banded(length, heads, band):
    parts = []
    for h in range(heads):
        whole = [b for b in bands(length) if b[3] == SAMPLE + QB]
        for at, size, first, width in bands(length):
            if width != SAMPLE + QB:
                parts.append(functools.partial(band, h, at, first, width, size))

        def loop(h=h, whole=whole):
            @pl.loop(0, len(whole))
            def _(i):
                at = whole[0][0] + i * QB
                band(h, at, at - SAMPLE, SAMPLE + QB, QB)

        if whole:
            parts.append(loop)
    return parts


def middle_kernel(
    grp,
    heads,
    fused,
    na_ref,
    wqkv_ref,
    wo_ref,
    cos_ref,
    sin_ref,
    start_ref,
    dy_ref,
    x_ref,
    gain_ref,
    gate_ref,
    up_ref,
    down_ref,
    q_ref,
    k_ref,
    v_ref,
    o_ref,
    lse_ref,
    h_ref,
    nm_ref,
    dyall_ref,
    wg_ref,
    wu_ref,
    wd_ref,
    *rest,
):
    early, rest = (rest[:2], rest[2:]) if fused else (None, rest)
    p, rowbuf, rowsem, local = rest[:4]
    rest = rest[4:]
    if fused:
        wg, wu, tile, tilesem, stage_a, stage_g, stagesem = rest[:7]
        rest = rest[7:]
    scat_refs, rest = rest[:N_SCATTER], rest[N_SCATTER:]
    dsend, drecv, dsem, send, recv, sem, zs, zr = rest
    rows_all, _, length = start_ref.shape
    wide = heads * HEAD
    z, _ = grp.place()
    n = rows_all // 2
    rows = [(1 - z % 2) * n + j for j in range(n)] + [(z % 2) * n + j for j in range(n)]

    blocks = length // QB

    def load(i, j):
        part = pl.ds(pl.multiple_of(rows[i] * length + j * QB, QB), QB)
        return pltpu.make_async_copy(na_ref.at[part], rowbuf.at[j % 2], rowsem.at[j % 2])

    load(0, 0).start()
    grp.greet()
    spread = Spread(grp, zs, zr)
    views = [
        (halves_of(grp, gate_ref, 1), wg_ref, 1),
        (halves_of(grp, up_ref, 1), wu_ref, 1),
        (halves_of(grp, down_ref, 0), wd_ref, 0),
    ]
    outer = Gather(grp, dy_ref, dyall_ref, dsend, drecv, dsem)
    outer_steps = outer.begin()
    for pair, whole, axis in views[:2]:
        spread_weight(grp, spread, pair, whole, axis, 0, (1, 0))
    far = []
    for pair, whole, axis in views[:2]:
        far += spread_weight(grp, spread, pair, whole, axis, 0, grp.far, start=False)
    inner = inner_plane(grp)
    outer_plane = jnp.logical_not(inner)
    cut = len(far) // 2
    launch(far[:cut])
    launch(far[cut:], inner)
    scat = Scatter(grp, p, x_ref.shape[0], *scat_refs)

    def project(i):
        base = rows[i] * length
        if i:
            load(i, 0).start()

        @pl.loop(0, blocks)
        def _(j):
            @pl.when(j + 1 < blocks)
            def _():
                load(i, j + 1).start()

            load(i, j).wait()
            there = pl.ds(pl.multiple_of(base + j * QB, QB), QB)
            qkv = jnp.dot(rowbuf[j % 2], wqkv_ref[...], preferred_element_type=F32)
            cosine, sine = cos_ref[there], sin_ref[there]
            query, key = qkv[:, :wide], qkv[:, wide : 2 * wide]
            q_ref[there] = (query * cosine + swap_halves(query) * sine).astype(BF16)
            k_ref[there] = (key * cosine + swap_halves(key) * sine).astype(BF16)
            v_ref[there] = qkv[:, 2 * wide :].astype(BF16)

    def branch(i):
        base = rows[i] * length

        @pl.loop(0, length // QB)
        def _(j):
            there = pl.ds(pl.multiple_of(base + j * QB, QB), QB)
            p[there] = jnp.dot(o_ref[there], wo_ref[...], preferred_element_type=F32).astype(BF16)

    def parts(i):
        return (
            [functools.partial(project, i)]
            + attend_rows(length, heads, q_ref, k_ref, v_ref, start_ref, o_ref, lse_ref, rows[i])
            + [functools.partial(branch, i)]
        )

    todo = [part for i in range(n) for part in parts(i)]
    wait = max(0, len(todo) - 4)
    run(todo[:wait])
    outer_steps = weave(todo[wait:], outer_steps)
    scat.begin(scat.masks(True))
    todo = [part for i in range(n, 2 * n) for part in parts(i)]
    links = scat.link_steps(True)
    beside = scat.core_steps(True) + links[:-2]
    beside = weave(todo, beside, -(-len(beside) // len(todo)))
    scat.begin(scat.masks(False))
    run(beside + scat.core_steps(False)[:1] + links[-2:])
    launch(far[cut:], outer_plane)
    run(scat.core_steps(False)[1:])
    run(scat.link_steps(False), outer_steps)
    scat.finish()
    summed = scat.block(0)

    def norm(part):
        h = x_ref[part].astype(F32) + summed[part].astype(F32)
        h_ref[part] = h
        local[part] = (h * norm_scale(h) * gain_ref[1:2].astype(F32)).astype(BF16)

    tiles(x_ref.shape[0], norm)
    gather = Gather(grp, local, nm_ref, send, recv, sem)
    steps = gather.begin()
    pair, whole, axis = views[2]
    spread_weight(grp, spread, pair, whole, axis, 0)
    if not fused:
        run(steps)
        scat.drain()
        outer.finish()
        gather.finish()
        spread.wait()
        return
    spread.wait_first(2 * grp.z_size)
    loads = [
        pltpu.make_async_copy(src, dst, tilesem.at[i])
        for i, (src, dst) in enumerate(((wg_ref, wg), (wu_ref, wu)))
    ]
    for c in loads:
        c.start()
    scat.drain()
    for c in loads:
        c.wait()
    size = tile.shape[0]
    units = wg.shape[1]

    def saves(j):
        here = pl.ds(pl.multiple_of(grp.chip_at(j, near=True) * size, size), size)
        return (
            pltpu.make_async_copy(stage_a.at[j % 2], early[0].at[here], stagesem.at[0, j % 2]),
            pltpu.make_async_copy(stage_g.at[j % 2], early[1].at[here], stagesem.at[1, j % 2]),
        )

    def forward(j):
        here = pl.ds(pl.multiple_of(grp.chip_at(j, near=True) * size, size), size)
        load = pltpu.make_async_copy(nm_ref.at[here], tile, tilesem.at[0])
        load.start()

        @pl.when(j > 1)
        def _():
            for c in saves(j - 2):
                c.wait()

        load.wait()
        act, gate, up = gate_up(tile[...], wg[...], wu[...])
        stage_a[j % 2] = act
        stage_g[j % 2, :, :units] = gate
        stage_g[j % 2, :, units:] = up
        for c in saves(j):
            c.start()

    count = len(grp.masks)
    led(count, forward, gather.needs(steps))
    for j in (count - 2, count - 1):
        for c in saves(j):
            c.wait()
    outer.finish()
    gather.drain()
    spread.wait()


def middle(grp, heads, normed, wqkv, wo, cosine, sine, start, dy, x, gain, w_gate, w_up, w_down, cid):
    rows, width = x.shape
    total = rows * grp.size
    wide = heads * HEAD
    rows_all, _, length = start.shape
    thin = sds((total, wide), BF16)
    fused = grp.size <= 16
    units = w_gate.shape[1] // 2
    early, beside = [], []
    if fused:
        early = [sds((total, units), BF16), sds((total, 2 * units), BF16)]
        beside = [
            pltpu.VMEM((width, units), BF16),
            pltpu.VMEM((width, units), BF16),
            pltpu.VMEM((2 * rows, width), BF16),
            pltpu.SemaphoreType.DMA((2,)),
            pltpu.VMEM((2, 2 * rows, units), BF16),
            pltpu.VMEM((2, 2 * rows, 2 * units), BF16),
            pltpu.SemaphoreType.DMA((2, 2)),
        ]
    return pl.pallas_call(
        functools.partial(middle_kernel, grp, heads, fused),
        out_shape=[thin] * 4
        + [
            sds((rows_all, heads, length), F32),
            sds((rows, width), F32),
            sds((total, width), BF16),
            sds((total, width), BF16),
            sds((w_gate.shape[0] * grp.z_size, w_gate.shape[1] // 2), BF16),
            sds((w_up.shape[0] * grp.z_size, w_up.shape[1] // 2), BF16),
            sds((w_down.shape[0] // 2, w_down.shape[1] * grp.z_size), BF16),
        ]
        + early,
        in_specs=[ANY, VMEM, VMEM, VMEM, VMEM, VMEM, ANY, VMEM, VMEM, ANY, ANY, ANY],
        out_specs=[VMEM] * 6 + [ANY] * (5 + len(early)),
        scratch_shapes=[
            pltpu.VMEM((total, width), BF16),
            pltpu.VMEM((2, QB, width), BF16),
            pltpu.SemaphoreType.DMA((2,)),
            pltpu.VMEM((rows, width), BF16),
        ]
        + beside
        + scatter_scratch(grp, rows, width)
        + gather_scratch(grp)
        + gather_scratch(grp)
        + spread_sems(grp, 3 * PIECES),
        compiler_params=params(cid),
        name="middle",
    )(normed, wqkv, wo, cosine, sine, start, dy, x, gain, w_gate, w_up, w_down)


def norm_back_tile(value, gain, grad):
    scale = norm_scale(value)
    scaled = grad * gain
    inner = jnp.mean(value * scaled, axis=-1, keepdims=True)
    back = scale * scaled - value * (scale * scale * scale * inner)
    return back, jnp.sum(grad * value * scale, axis=0, keepdims=True)


class Fetch:
    def __init__(self, sems, *pairs):
        self.copies = [
            pltpu.make_async_copy(src, dst, sems.at[i]) for i, (src, dst) in enumerate(pairs)
        ]
        for c in self.copies:
            c.start()

    def wait(self):
        for c in self.copies:
            c.wait()


def weave(parts, steps, each=1):
    for part in parts:
        part()
        for step in steps[:each]:
            step()
        steps = steps[each:]
    return steps


def last_kernel(
    grp,
    heads,
    branch_ref,
    na_ref,
    part_ref,
    gup_ref,
    q_ref,
    k_ref,
    v_ref,
    o_ref,
    lse_ref,
    cos_in,
    sin_in,
    start_ref,
    wqkv_in,
    wo_ref,
    h_in,
    x_in,
    dh_in,
    gain_ref,
    gm_ref,
    out_ref,
    tok_ref,
    gains_ref,
    gout_ref,
    gqkv_ref,
    upgot_ref,
    outgot_ref,
    qkvgot_ref,
    p,
    own,
    ownsem,
    rowbuf,
    rowsem,
    cols,
    csem,
    do,
    dqkv,
    dq,
    dk,
    dv,
    gacc,
    cos_ref,
    sin_ref,
    wqkv_ref,
    h_ref,
    x_ref,
    dh_ref,
    fsem,
    buf,
    gs,
    gr,
    *rest,
):
    na_scat, rest = rest[:N_SCATTER], rest[N_SCATTER:]
    out_scat, rest = rest[:N_SCATTER], rest[N_SCATTER:]
    zs, zr = rest
    rows_all, _, length = start_ref.shape
    rows, width = h_in.shape
    wide = heads * HEAD
    z, _ = grp.place()
    n = rows_all // 2
    order = [(1 - z % 2) * n + j for j in range(n)] + [(z % 2) * n + j for j in range(n)]
    blocks = length // QB
    step = cols.shape[2]

    def load(i, j):
        part = pl.ds(pl.multiple_of(order[i] * length + j * QB, QB), QB)
        return pltpu.make_async_copy(branch_ref.at[part], rowbuf.at[j % 2], rowsem.at[j % 2])

    def load_cols(c):
        part = pl.ds(pl.multiple_of(c * step, step), step)
        return pltpu.make_async_copy(na_ref.at[:, part], cols.at[c % 2], csem.at[c % 2])

    load(0, 0).start()
    fetch = Fetch(
        fsem,
        (cos_in, cos_ref),
        (sin_in, sin_ref),
        (wqkv_in, wqkv_ref),
        (h_in, h_ref),
        (x_in, x_ref),
        (dh_in, dh_ref),
    )
    load_cols(0).start()
    outer = Scatter(grp, part_ref, rows, *out_scat, own=own)
    for m in outer.masks(True) + outer.masks(False):
        outer.load(m, ownsem).start()
    grp.greet(everyone=True)
    outer.begin(outer.masks(True) + outer.masks(False))
    spread = Spread(grp, zs, zr)
    spread_grad(grp, spread, gup_ref, upgot_ref, 0, (1,) + grp.far)
    scat = Scatter(grp, p, rows, *na_scat)
    gacc[...] = jnp.zeros_like(gacc)

    def outer_core(m):
        outer.load(m, ownsem).wait()
        outer.core_step(m)

    outer_steps = [
        functools.partial(outer_core, m) for m in outer.masks(True) + outer.masks(False)
    ]
    outer_steps += outer.link_steps(True) + outer.link_steps(False)

    def prepare(i):
        base = order[i] * length
        if i:
            load(i, 0).start()
        dk[...] = jnp.zeros_like(dk)
        dv[...] = jnp.zeros_like(dv)

        @pl.loop(0, blocks)
        def _(j):
            @pl.when(j + 1 < blocks)
            def _():
                load(i, j + 1).start()

            load(i, j).wait()
            there = pl.ds(pl.multiple_of(base + j * QB, QB), QB)
            here = pl.ds(pl.multiple_of(j * QB, QB), QB)
            branch = rowbuf[j % 2]
            do[here] = dot_nt(branch, wo_ref[...]).astype(BF16)
            gacc[...] += dot_tn(o_ref[there], branch)

    def banded_back(i):
        row = order[i]
        base = row * length

        def band(h, at, first, width, size):
            lanes = slice(h * HEAD, (h + 1) * HEAD)
            cols_at = pl.ds(pl.multiple_of(at, QB), size)
            keys_at = pl.ds(pl.multiple_of(first, QB), width)
            mine = pl.ds(pl.multiple_of(base + at, QB), size)
            keys = pl.ds(pl.multiple_of(base + first, QB), width)
            query = q_ref[mine, lanes]
            key = k_ref[keys, lanes]
            grad = do[cols_at, lanes]
            scores = dot_nt(key, query * BF16(HEAD**-0.5))
            mask = kept(start_ref[row, :, cols_at], at, size, first, width)
            scores = jnp.where(mask, scores, -1e9)
            weights = jnp.exp(scores - lse_ref[row, h : h + 1, cols_at])
            dv[keys_at, lanes] += jnp.dot(weights.astype(BF16), grad, preferred_element_type=F32)
            grad_weights = dot_nt(v_ref[keys, lanes], grad)
            inner = jnp.sum(weights * grad_weights, axis=0, keepdims=True)
            grad_scores = (weights * (grad_weights - inner)).astype(BF16)
            dq[cols_at, lanes] = dot_tn(grad_scores, key)
            dk[keys_at, lanes] += jnp.dot(grad_scores, query, preferred_element_type=F32)

        return banded(length, heads, band)

    def turn_back(i):
        base = order[i] * length
        if i == 0:
            fetch.wait()

        @pl.loop(0, blocks)
        def _(j):
            there = pl.ds(pl.multiple_of(base + j * QB, QB), QB)
            here = pl.ds(pl.multiple_of(j * QB, QB), QB)
            cosine, sine = cos_ref[there], sin_ref[there]
            query, key = dq[here] * HEAD**-0.5, dk[here] * HEAD**-0.5
            dqkv[there, :wide] = (query * cosine - swap_halves(query) * sine).astype(BF16)
            dqkv[there, wide : 2 * wide] = (key * cosine - swap_halves(key) * sine).astype(BF16)
            dqkv[there, 2 * wide :] = dv[here].astype(BF16)
            p[there] = dot_nt(dqkv[there], wqkv_ref[...]).astype(BF16)

    def parts(i):
        return (
            [functools.partial(prepare, i)] + banded_back(i) + [functools.partial(turn_back, i)]
        )

    for i in range(n):
        outer_steps = weave(parts(i), outer_steps)
    scat.begin(scat.masks(True))
    pair_core = scat.core_steps(True)
    for i in range(n, 2 * n):
        todo = parts(i)
        beside = [
            functools.partial(run, pair_core[a : a + 1] + outer_steps[a : a + 1])
            for a in range(len(todo))
        ]
        outer_steps, pair_core = outer_steps[len(todo) :], pair_core[len(todo) :]
        weave(todo, beside)
    scat.begin(scat.masks(False))
    gout_ref[...] = gacc[...].astype(BF16)
    inner = inner_plane(grp)
    spread_grad(grp, spread, gout_ref, outgot_ref, 1, (1,) + grp.far)

    def qkv_cols(c):
        @pl.when(c + 1 < width // step)
        def _():
            load_cols(c + 1).start()

        load_cols(c).wait()
        part = pl.ds(pl.multiple_of(c * step, step), step)
        gqkv_ref[part] = dot_tn(cols[c % 2], dqkv[...]).astype(BF16)

    paced(width // step, qkv_cols, pair_core + scat.core_steps(False))
    spread_grad(grp, spread, gqkv_ref, qkvgot_ref, 0, (1,))
    far = spread_grad(grp, spread, gqkv_ref, qkvgot_ref, 0, grp.far, start=False)
    launch(far, inner)
    run(scat.link_steps(True))
    launch(far, jnp.logical_not(inner))
    run(scat.link_steps(False), outer_steps)
    outer.finish()
    whole = outer.block(0)

    def output(part):
        out_ref[part] = (h_ref[part] + whole[part].astype(F32)).astype(BF16)

    tiles(rows, output)
    scat.finish()
    summed = scat.block(0)
    buf[0, 0:1] = jnp.zeros_like(gm_ref)
    buf[0, 1:2] = gm_ref[...]

    def back(part):
        dn, gain_part = norm_back_tile(
            x_ref[part].astype(F32), gain_ref[0:1].astype(F32), summed[part].astype(F32)
        )
        buf[0, 0:1] += gain_part
        tok_ref[part] = (dh_ref[part] + dn).astype(BF16)

    tiles(rows, back)
    sum_gains(grp, buf, gs, gr)
    gains_ref[...] = buf[buf.shape[0] - 1]
    outer.drain()
    scat.drain()
    spread.wait()


def gain_scratch(grp, width):
    n = grp.t_size + grp.z_size - 2
    return [
        pltpu.VMEM((grp.t_size + grp.z_size + 3, 2, width), F32),
        pltpu.SemaphoreType.DMA((n,)),
        pltpu.SemaphoreType.DMA((n,)),
    ]


def sum_gains(grp, buf, send, recv):
    z, t = grp.place()
    at, sem = 0, 0
    for index, size, peer in ((t, grp.t_size, grp.beside), (z, grp.z_size, grp.across)):
        copies = []
        for m in range(1, size):
            c = pltpu.make_async_remote_copy(
                src_ref=buf.at[at],
                dst_ref=buf.at[at + 1 + index],
                send_sem=send.at[sem],
                recv_sem=recv.at[sem],
                device_id=peer(m),
                device_id_type=MESH,
            )
            c.start()
            copies.append(c)
            sem += 1
        buf[at + 1 + index] = buf[at]
        for c in copies:
            c.wait()
        total = buf[at + 1]
        for i in range(1, size):
            total = total + buf[at + 1 + i]
        at += size + 1
        buf[at] = total


def last(
    grp, heads, branch, normed, part, grad_up, query, key, value, attended, lse, cosine, sine, start,
    wqkv, wo, hidden, x, dh, gain, gain_m, cid,
):
    rows, width = x.shape
    total = rows * grp.size
    wide = heads * HEAD
    length = start.shape[2]
    n = len(grp.masks)
    gout, gqkv = sds((wide, width), BF16), sds((width, 3 * wide), BF16)
    return pl.pallas_call(
        functools.partial(last_kernel, grp, heads),
        out_shape=[
            sds((rows, width), BF16),
            sds((rows, width), BF16),
            sds((2, width), F32),
            gout,
            gqkv,
            got_shape(grp, grad_up, 0),
            got_shape(grp, gout, 1),
            got_shape(grp, gqkv, 0),
        ],
        in_specs=[ANY] * 4 + [VMEM] * 5 + [ANY] * 2 + [VMEM, ANY, VMEM] + [ANY] * 3 + [VMEM] * 2,
        out_specs=[VMEM] * 5 + [ANY] * 3,
        scratch_shapes=[
            pltpu.VMEM((total, width), BF16),
            pltpu.VMEM((n, rows, width), BF16),
            pltpu.SemaphoreType.DMA((n,)),
            pltpu.VMEM((2, QB, width), BF16),
            pltpu.SemaphoreType.DMA((2,)),
            pltpu.VMEM((2, total, cols_of(total)), BF16),
            pltpu.SemaphoreType.DMA((2,)),
            pltpu.VMEM((length, wide), BF16),
            pltpu.VMEM((total, 3 * wide), BF16),
            pltpu.VMEM((length, wide), F32),
            pltpu.VMEM((length, wide), F32),
            pltpu.VMEM((length, wide), F32),
            pltpu.VMEM((wide, width), F32),
            pltpu.VMEM((total, wide), F32),
            pltpu.VMEM((total, wide), F32),
            pltpu.VMEM((width, 3 * wide), BF16),
            pltpu.VMEM((rows, width), F32),
            pltpu.VMEM((rows, width), BF16),
            pltpu.VMEM((rows, width), F32),
            pltpu.SemaphoreType.DMA((6,)),
        ]
        + gain_scratch(grp, width)
        + scatter_scratch(grp, rows, width)
        + scatter_scratch(grp, rows, width)
        + spread_sems(grp, 3 * PIECES),
        compiler_params=params(cid),
        name="last",
    )(
        branch, normed, part, grad_up, query, key, value, attended, lse, cosine, sine, start,
        wqkv, wo, hidden, x, dh, gain, gain_m,
    )


def got_shape(grp, grad, axis):
    shape = list(grad.shape)
    shape[axis] //= grp.z_size
    return sds((grp.z_size - 1, *shape), BF16)


def paced(count, body, steps, first=0):
    turns = count - first
    each = -(-len(steps) // turns) if steps else 0

    @pl.loop(0, count)
    def _(i):
        body(i)
        for k in range(turns):
            mine = steps[k * each : (k + 1) * each]
            if mine:

                @pl.when(i == first + k)
                def _(mine=mine):
                    for step in mine:
                        step()


def led(count, body, lists):
    @pl.loop(0, count)
    def _(i):
        for k, steps in enumerate(lists):

            @pl.when(i == k)
            def _(steps=steps):
                run(steps)

        body(i)


def gate_up(normed, wg, wu):
    gate = jnp.dot(normed, wg, preferred_element_type=F32)
    up = jnp.dot(normed, wu, preferred_element_type=F32)
    return (gate * jax.nn.sigmoid(gate) * up).astype(BF16), gate.astype(BF16), up.astype(BF16)


def cols_of(total):
    return max(128, 655360 // total // 128 * 128)


def mlp_kernel(grp, n_early, *refs):
    early, refs = refs[:n_early], refs[n_early:]
    (
        nm_ref,
        dyall_ref,
        wg_in,
        wu_in,
        down_all_ref,
        h_ref,
        dy_ref,
        gain_ref,
        down_ref,
        dh_ref,
        gm_ref,
        gdown_out,
        ggate_out,
        gup_out,
        branch_ref,
        out_ref,
        downgot_ref,
        gategot_ref,
        p,
        wd,
        tile_n,
        tsem,
        act,
        dgu,
        cols,
        csem,
        dsem,
        wg_ref,
        wu_ref,
        gdown_ref,
        ggate_ref,
        gup_ref,
        fsem,
        *rest,
    ) = refs
    scat_refs, rest = rest[:N_SCATTER], rest[N_SCATTER:]
    send, recv, sem, zs, zr = rest
    rows, width = h_ref.shape
    size = 2 * rows
    n = len(grp.masks)
    units = wd.shape[0]
    step = cols.shape[2]

    def at(j):
        return pl.ds(pl.multiple_of(grp.chip_at(j) * size, size), size)

    def load(src, buf, k, j):
        return pltpu.make_async_copy(src.at[at(j)], buf.at[j % 2], tsem.at[k, j % 2])

    def load_cols(src, c):
        part = pl.ds(pl.multiple_of(c * step, step), step)
        return pltpu.make_async_copy(src.at[:, part], cols.at[c % 2], csem.at[c % 2])

    fetch = Fetch(fsem, (wg_in, wg_ref), (wu_in, wu_ref))
    takes = []
    if n_early:
        takes = [
            pltpu.make_async_copy(src, dst, tsem.at[0, i])
            for i, (src, dst) in enumerate(zip(early, (act, dgu)))
        ]
        for c in takes:
            c.start()
    else:
        load(nm_ref, tile_n, 0, 0).start()
    grp.greet()
    spread = Spread(grp, zs, zr)
    spread.to(0, lambda: (down_all_ref, wd))

    def forward(j):
        @pl.when(j + 1 < n)
        def _():
            load(nm_ref, tile_n, 0, j + 1).start()

        load(nm_ref, tile_n, 0, j).wait()
        here = at(j)
        act[here], dgu[here, :units], dgu[here, units:] = gate_up(
            tile_n[j % 2], wg_ref[...], wu_ref[...]
        )

    load_cols(dyall_ref, 0).start()
    if n_early:
        for c in takes:
            c.wait()
    else:
        fetch.wait()
        paced(n, forward, [])
    blocks = width // step

    def down_cols(c):
        @pl.when(c + 1 < blocks)
        def _():
            load_cols(dyall_ref, c + 1).start()

        load_cols(dyall_ref, c).wait()
        part = pl.ds(pl.multiple_of(c * step, step), step)
        gdown_ref[:, part] = dot_tn(cols[c % 2], act[...]).T.astype(BF16)

    load(dyall_ref, tile_n, 1, 0).start()
    paced(blocks, down_cols, [])
    outs = [pltpu.make_async_copy(gdown_ref, gdown_out, fsem.at[2])]
    outs[0].start()
    if n_early:
        fetch.wait()
    spread.wait()
    spread_grad(grp, spread, gdown_ref, downgot_ref, 1)

    scat = Scatter(grp, p, rows, *scat_refs)
    chunk = min(512, width)

    def backward(j):
        @pl.when(j + 1 < n)
        def _():
            load(dyall_ref, tile_n, 1, j + 1).start()

        load(dyall_ref, tile_n, 1, j).wait()
        here = at(j)
        grad_act = dot_nt(tile_n[j % 2], wd[...])
        gate, up = dgu[here, :units].astype(F32), dgu[here, units:].astype(F32)
        sigma = jax.nn.sigmoid(gate)
        grad_gate = (grad_act * up * (sigma * (1.0 + gate * (1.0 - sigma)))).astype(BF16)
        grad_up = (grad_act * (gate * sigma)).astype(BF16)
        dgu[here, :units] = grad_gate
        dgu[here, units:] = grad_up
        for c in range(0, width, chunk):
            p[here, c : c + chunk] = (
                dot_nt(grad_gate, wg_ref[c : c + chunk]) + dot_nt(grad_up, wu_ref[c : c + chunk])
            ).astype(BF16)
        scat.begin_tile(j)

    core = scat.core_steps(True) + scat.core_steps(False)
    pair_links = scat.link_steps(True)
    todo = []
    late = n // 2
    share = -(-len(pair_links) // max(1, late - 1))
    for j in range(1, n):
        todo.append([core[j - 1]])
        if j > late:
            k = (j - late - 1) * share
            todo[-1] += pair_links[k : k + share]
    done = share * max(0, late - 1)
    paced(n, backward, [functools.partial(run, x) for x in todo], 1)
    rest_steps = [core[n - 1]] + pair_links[done:] + scat.link_steps(False)

    def gate_up_cols(c):
        @pl.when(c + 1 < blocks)
        def _():
            load_cols(nm_ref, c + 1).start()

        load_cols(nm_ref, c).wait()
        part = pl.ds(pl.multiple_of(c * step, step), step)
        grads = dot_tn(cols[c % 2], dgu[...]).astype(BF16)
        ggate_ref[part] = grads[:, :units]
        gup_ref[part] = grads[:, units:]

    load_cols(nm_ref, 0).start()
    paced(blocks, gate_up_cols, rest_steps)
    for i, pair in enumerate(((ggate_ref, ggate_out), (gup_ref, gup_out))):
        outs.append(pltpu.make_async_copy(*pair, fsem.at[3 + i]))
        outs[-1].start()
    dy = scat_refs[0].at[n - 1]
    fetches = [
        pltpu.make_async_copy(dy_ref, dy, dsem.at[0]),
        pltpu.make_async_copy(h_ref, dh_ref, dsem.at[1]),
    ]
    for fetch in fetches:
        fetch.start()
    scat.finish()
    summed = scat.block(0)
    for fetch in fetches:
        fetch.wait()
    gm_ref[...] = jnp.zeros_like(gm_ref)

    def back(part):
        dn, gain_part = norm_back_tile(dh_ref[part], gain_ref[1:2].astype(F32), summed[part].astype(F32))
        gm_ref[...] += gain_part
        dh = dy[part].astype(F32) + dn
        dh_ref[part] = dh
        summed[part] = dh.astype(BF16)

    tiles(rows, back)
    gather = Gather(grp, summed, branch_ref, send, recv, sem)
    steps = gather.begin()
    spread_grad(grp, spread, ggate_ref, gategot_ref, 0, grp.far)
    scat.drain()

    def save(j):
        return pltpu.make_async_copy(tile_n.at[j % 2], out_ref.at[at(j)], tsem.at[0, j % 2])

    def branch(j):
        @pl.when(j > 1)
        def _():
            save(j - 2).wait()

        tile_n[j % 2] = jnp.dot(act[at(j)], wd[...], preferred_element_type=F32).astype(BF16)
        save(j).start()

    near = functools.partial(spread_grad, grp, spread, ggate_ref, gategot_ref, 0, (1,))
    paced(n, branch, steps[:6] + [near] + steps[6:], 1)
    for c in outs:
        c.wait()
    save(n - 2).wait()
    save(n - 1).wait()
    gather.finish()
    spread.wait()


def mlp(grp, early, normed, dy_all, wg, wu, wd, hidden, dy, gain, w_down, cid):
    rows, width = hidden.shape
    total = rows * grp.size
    n = len(grp.masks)
    units = wg.shape[1]
    gdown, ggate = sds((units, width), BF16), sds((width, units), BF16)
    return pl.pallas_call(
        functools.partial(mlp_kernel, grp, len(early)),
        out_shape=[
            sds((rows, width), F32),
            sds((1, width), F32),
            gdown,
            ggate,
            ggate,
            sds((total, width), BF16),
            sds((total, width), BF16),
            got_shape(grp, gdown, 1),
            got_shape(grp, ggate, 0),
        ],
        in_specs=[ANY] * (len(early) + 7) + [VMEM, ANY],
        out_specs=[VMEM] * 2 + [ANY] * 7,
        scratch_shapes=[
            pltpu.VMEM((total, width), BF16),
            pltpu.VMEM((units, width), BF16),
            pltpu.VMEM((2, 2 * rows, width), BF16),
            pltpu.SemaphoreType.DMA((2, 2)),
            pltpu.VMEM((total, units), BF16),
            pltpu.VMEM((total, 2 * units), BF16),
            pltpu.VMEM((2, total, cols_of(total)), BF16),
            pltpu.SemaphoreType.DMA((2,)),
            pltpu.SemaphoreType.DMA((2,)),
            pltpu.VMEM((width, units), BF16),
            pltpu.VMEM((width, units), BF16),
            pltpu.VMEM((units, width), BF16),
            pltpu.VMEM((width, units), BF16),
            pltpu.VMEM((width, units), BF16),
            pltpu.SemaphoreType.DMA((5,)),
        ]
        + scatter_scratch(grp, rows, width)
        + gather_scratch(grp)
        + spread_sems(grp, 4),
        compiler_params=params(cid),
        name="mlp",
    )(*early, normed, dy_all, wg, wu, wd, hidden, dy, gain, w_down)


def fifth_kernel(grp, p_ref, h_ref, gup_ref, out_ref, up_ref, *rest):
    p, psem, rest = rest[0], rest[1], rest[2:]
    scat, rest = rest[:N_SCATTER], rest[N_SCATTER:]
    zs, zr = rest
    pltpu.make_async_copy(p_ref, p, psem).start()
    grp.greet()
    spread = Spread(grp, zs, zr)
    spread_grad(grp, spread, gup_ref, up_ref, 0)
    pltpu.make_async_copy(p_ref, p, psem).wait()
    acc = plain_scatter(grp, p, h_ref.shape[0], scat)

    def finish(rows):
        out_ref[rows] = (h_ref[rows] + acc[rows].astype(F32)).astype(BF16)

    tiles(h_ref.shape[0], finish)
    spread.wait()


def fifth(grp, part, hidden, grad_up, cid):
    rows, width = hidden.shape
    return pl.pallas_call(
        functools.partial(fifth_kernel, grp),
        out_shape=[sds((rows, width), BF16), got_shape(grp, grad_up, 0)],
        in_specs=[ANY, VMEM, ANY],
        out_specs=[VMEM, ANY],
        scratch_shapes=[pltpu.VMEM((rows * grp.size, width), BF16), pltpu.SemaphoreType.DMA]
        + scatter_scratch(grp, rows, width)
        + spread_sems(grp, 1),
        compiler_params=params(cid),
        name="fifth",
    )(part, hidden, grad_up)


def sixth_kernel(
    grp, p_ref, x_ref, dh_ref, gain_ref, gm_ref, gout_ref, gqkv_ref, tok_ref, gains_ref, o_ref, qkv_ref, *rest
):
    p, psem, rest = rest[0], rest[1], rest[2:]
    scat, rest = rest[:N_SCATTER], rest[N_SCATTER:]
    buf, gs, gr, zs, zr = rest
    pltpu.make_async_copy(p_ref, p, psem).start()
    grp.greet(everyone=True)
    spread = Spread(grp, zs, zr)
    spread_grad(grp, spread, gout_ref, o_ref, 1)
    spread_grad(grp, spread, gqkv_ref, qkv_ref, 0)
    pltpu.make_async_copy(p_ref, p, psem).wait()
    acc = plain_scatter(grp, p, x_ref.shape[0], scat)
    buf[0, 0:1] = jnp.zeros_like(gm_ref)
    buf[0, 1:2] = gm_ref[...]

    def back(rows):
        dn, gain_part = norm_back_tile(
            x_ref[rows].astype(F32), gain_ref[0:1].astype(F32), acc[rows].astype(F32)
        )
        buf[0, 0:1] += gain_part
        tok_ref[rows] = (dh_ref[rows] + dn).astype(BF16)

    tiles(x_ref.shape[0], back)
    sum_gains(grp, buf, gs, gr)
    gains_ref[...] = buf[buf.shape[0] - 1]
    spread.wait()


def sixth(grp, part, x, dh, gain, gain_m, grad_out, grad_qkv, cid):
    rows, width = x.shape
    return pl.pallas_call(
        functools.partial(sixth_kernel, grp),
        out_shape=[
            sds((rows, width), BF16),
            sds((2, width), F32),
            got_shape(grp, grad_out, 1),
            got_shape(grp, grad_qkv, 0),
        ],
        in_specs=[ANY, VMEM, VMEM, VMEM, VMEM, ANY, ANY],
        out_specs=[VMEM, VMEM, ANY, ANY],
        scratch_shapes=[pltpu.VMEM((rows * grp.size, width), BF16), pltpu.SemaphoreType.DMA]
        + scatter_scratch(grp, rows, width)
        + gain_scratch(grp, width)
        + spread_sems(grp, 2),
        compiler_params=params(cid),
        name="sixth",
    )(part, x, dh, gain, gain_m, grad_out, grad_qkv)


def swap_halves(value):
    half = HEAD // 2
    width = value.shape[1]
    pieces = []
    for at in range(0, width, HEAD):
        pieces.append(value[:, at + half : at + HEAD])
        pieces.append(value[:, at : at + half])
    if width % 128:
        return jnp.concatenate(pieces, axis=1)
    lane = lax.broadcasted_iota(jnp.int32, value.shape, 1)
    return jnp.where(
        lane % HEAD < half, pltpu.roll(value, width - half, 1), pltpu.roll(value, half, 1)
    )


QB = 256


def bands(length):
    for at in range(0, length, QB):
        first = max(0, at - SAMPLE)
        yield at, min(QB, length - at), first, at + min(QB, length - at) - first


def kept(start_row, at, size, first, width):
    key = first + lax.broadcasted_iota(jnp.int32, (width, size), 0)
    query = at + lax.broadcasted_iota(jnp.int32, (width, size), 1)
    return (key >= start_row) & (key <= query)


def attend_back_kernel(
    heads, q_ref, k_ref, v_ref, do_ref, lse_ref, cos_ref, sin_ref, start_ref, out_ref, dq, dk, dv
):
    wide = heads * HEAD
    length = q_ref.shape[0]
    dk[...] = jnp.zeros_like(dk)
    dv[...] = jnp.zeros_like(dv)
    for h in range(heads):
        lanes = slice(h * HEAD, (h + 1) * HEAD)
        for at, size, first, width in bands(length):
            query = q_ref[at : at + size, lanes]
            key = k_ref[first : first + width, lanes]
            value = v_ref[first : first + width, lanes]
            grad = do_ref[at : at + size, lanes]
            scores = dot_nt(key, query * BF16(HEAD**-0.5))
            mask = kept(start_ref[0, :, at : at + size], at, size, first, width)
            weights = jnp.where(
                mask, jnp.exp(jnp.where(mask, scores, -1e9) - lse_ref[0, h : h + 1, at : at + size]), 0.0
            )
            dv[first : first + width, lanes] += jnp.dot(
                weights.astype(BF16), grad, preferred_element_type=F32
            )
            grad_weights = dot_nt(value, grad)
            inner = jnp.sum(weights * grad_weights, axis=0, keepdims=True)
            grad_scores = (weights * (grad_weights - inner)).astype(BF16)
            dq[at : at + size, lanes] = dot_tn(grad_scores, key)
            dk[first : first + width, lanes] += jnp.dot(
                grad_scores, query, preferred_element_type=F32
            )

    @pl.loop(0, length // QB)
    def _(i):
        rows = pl.ds(pl.multiple_of(i * QB, QB), QB)
        cosine, sine = cos_ref[rows], sin_ref[rows]
        query, key = dq[rows] * HEAD**-0.5, dk[rows] * HEAD**-0.5
        out_ref[rows, :wide] = (query * cosine - swap_halves(query) * sine).astype(BF16)
        out_ref[rows, wide : 2 * wide] = (key * cosine - swap_halves(key) * sine).astype(BF16)
        out_ref[rows, 2 * wide :] = dv[rows].astype(BF16)


def attend_back(query, key, value, grad, lse, cosine, sine, start, heads):
    rows, _, length = start.shape
    wide = heads * HEAD

    def tall(width):
        return pl.BlockSpec((length, width), lambda r: (r, 0))

    return pl.pallas_call(
        functools.partial(attend_back_kernel, heads),
        grid=(rows,),
        out_shape=jax.ShapeDtypeStruct((rows * length, 3 * wide), BF16),
        in_specs=[tall(wide)] * 4
        + [pl.BlockSpec((1, heads, length), lambda r: (r, 0, 0)), tall(wide), tall(wide)]
        + [pl.BlockSpec((1, 1, length), lambda r: (r, 0, 0))],
        out_specs=tall(3 * wide),
        scratch_shapes=[pltpu.VMEM((length, wide), F32)] * 3,
        compiler_params=pltpu.CompilerParams(vmem_limit_bytes=48 << 20),
        name="attend_back",
    )(query, key, value, grad, lse, cosine, sine, start)


def finish_kernel(z_size, parts, z_ref, *refs):
    low = z_ref[0] % 2
    n = len(parts)
    owns, gots, outs = refs[:n], refs[n : 2 * n], list(refs[2 * n :])
    for own, got, (axis, count) in zip(owns, gots, parts):
        sums = [own[...].astype(F32), None]
        for m in range(1, z_size):
            term = got[m - 1].astype(F32)
            sums[m % 2] = term if sums[m % 2] is None else sums[m % 2] + term
        if axis == 0:
            out = outs.pop(0)
            out[low] = sums[0]
            out[1 - low] = sums[1]
            continue
        width = sums[0].shape[1] // count
        for i in range(count):
            out = outs.pop(0)
            for which, total in ((low, sums[0]), (1 - low, sums[1])):
                place = pl.ds(pl.multiple_of(which * width, width), width)
                out[:, place] = total[:, i * width : (i + 1) * width]


def finish(z_size, z, grads, gots, axes):
    steps = 2
    owns, blocks, outs, shapes = [], [], [], []
    for grad, got, (axis, count) in zip(grads, gots, axes):
        rows, cols = got.shape[1] // steps, got.shape[2]
        if axis == 0:
            owns.append(pl.BlockSpec((rows, cols), lambda i, z_ref: (i, z_ref[0])))
            outs.append(pl.BlockSpec((2, rows, cols), lambda i, z_ref: (0, i, 0)))
            shapes.append(sds((2, rows * steps, cols), F32))
        else:
            owns.append(pl.BlockSpec((rows, cols), lambda i, z_ref: (z_ref[0] * steps + i, 0)))
            wide = 2 * cols // count
            outs += [pl.BlockSpec((rows, wide), lambda i, z_ref: (i, 0))] * count
            shapes += [sds((rows * steps, wide), F32)] * count
        blocks.append(pl.BlockSpec((z_size - 1, rows, cols), lambda i, z_ref: (0, i, 0)))
    return pl.pallas_call(
        functools.partial(finish_kernel, z_size, axes),
        out_shape=shapes,
        grid_spec=pltpu.PrefetchScalarGridSpec(
            num_scalar_prefetch=1, grid=(steps,), in_specs=owns + blocks, out_specs=outs
        ),
        compiler_params=pltpu.CompilerParams(vmem_limit_bytes=56 << 20),
        name="finish",
    )(jnp.reshape(z, (1,)), *grads, *gots)


def shards(
    z_size,
    t_size,
    tokens,
    gain_attn,
    gain_mlp,
    w_query,
    w_key,
    w_value,
    w_out,
    w_gate,
    w_up,
    w_down,
    segment_ids,
    out_grad,
):
    grp = Group(z_size, t_size)
    z = lax.axis_index("fsdp")
    low = z % 2

    def deliver(grad, got, half_axis, axis, parts=1):
        size = grad.shape[axis] // z_size
        sums = [lax.dynamic_slice_in_dim(grad, z * size, size, axis).astype(F32), None]
        for m in range(1, z_size):
            term = got[m - 1].astype(F32)
            sums[m % 2] = term if sums[m % 2] is None else sums[m % 2] + term
        outs = []
        piece = sums[0].shape[half_axis] // parts
        for i in range(parts):
            a, b = (lax.slice_in_dim(s, i * piece, (i + 1) * piece, axis=half_axis) for s in sums)
            outs.append(
                jnp.where(
                    low == 0,
                    jnp.concatenate([a, b], axis=half_axis),
                    jnp.concatenate([b, a], axis=half_axis),
                )
            )
        return outs

    wide = w_query.shape[1] // 2
    heads = wide // HEAD

    gains_in = jnp.stack([gain_attn, gain_mlp])
    normed_a, wqkv, wo, start, cosine, sine = first(
        grp, low, tokens, gains_in, w_query, w_key, w_value, w_out, segment_ids, 0
    )
    query, key, value, attended, lse, hidden, normed_m, grad_all, wg, wu, wd, *early = middle(
        grp,
        heads,
        normed_a,
        wqkv,
        wo,
        cosine,
        sine,
        start,
        out_grad,
        tokens,
        gains_in,
        w_gate,
        w_up,
        w_down,
        1,
    )
    grad_hidden, gain_m_part, grad_down, grad_wg, grad_wu, branch_all, out_part, got_down, got_gate = mlp(
        grp, early, normed_m, grad_all, wg, wu, wd, hidden, out_grad, gains_in, w_down, 3
    )
    if grp.size <= 16:
        output, tokens_grad, gains, grad_wout, grad_wqkv, got_up, got_out, got_qkv = last(
            grp, heads, branch_all, normed_a, out_part, grad_wu, query, key, value, attended, lse,
            cosine, sine, start, wqkv, wo, hidden, tokens, grad_hidden, gains_in, gain_m_part, 4,
        )
    else:
        output, got_up = fifth(grp, out_part, hidden, grad_wu, 4)
        grad_wout = dot_tn(attended, branch_all).astype(BF16)
        grad_attended = dot_nt(branch_all, wo).astype(BF16)
        grad_qkv = attend_back(query, key, value, grad_attended, lse, cosine, sine, start, heads)
        grad_wqkv = dot_tn(normed_a, grad_qkv).astype(BF16)
        grad_na = dot_nt(grad_qkv, wqkv).astype(BF16)
        tokens_grad, gains, got_out, got_qkv = sixth(
            grp, grad_na, tokens, grad_hidden, gains_in, gain_m_part, grad_wout, grad_wqkv, 5
        )
    grads = (grad_down, grad_wg, grad_wu, grad_wout, grad_wqkv)
    gots = (got_down, got_gate, got_up, got_out, got_qkv)
    axes = ((0, 1), (1, 1), (1, 1), (0, 1), (1, 3))
    if wide % LANES == 0:
        outs = finish(z_size, z, grads, gots, axes)
        down_out, out_out = (x.reshape(-1, x.shape[2]) for x in (outs[0], outs[3]))
        gate_out, up_out = outs[1:3]
        query_out, key_out, value_out = outs[4:]
    else:
        (down_out,) = deliver(grad_down, got_down, 0, 1)
        (gate_out,) = deliver(grad_wg, got_gate, 1, 0)
        (up_out,) = deliver(grad_wu, got_up, 1, 0)
        (out_out,) = deliver(grad_wout, got_out, 0, 1)
        query_out, key_out, value_out = deliver(grad_wqkv, got_qkv, 1, 0, 3)
    return (
        output,
        tokens_grad,
        gains[0],
        gains[1],
        query_out,
        key_out,
        value_out,
        out_out,
        gate_out,
        up_out,
        down_out,
    )


def solution(mesh):
    return jax.shard_map(
        functools.partial(shards, mesh.shape["fsdp"], mesh.shape["tensor"]),
        mesh=mesh,
        in_specs=(
            P(("fsdp", "tensor"), None),
            P(),
            P(),
            P("fsdp", "tensor"),
            P("fsdp", "tensor"),
            P("fsdp", "tensor"),
            P("tensor", "fsdp"),
            P("fsdp", "tensor"),
            P("fsdp", "tensor"),
            P("tensor", "fsdp"),
            P("fsdp", None),
            P(("fsdp", "tensor"), None),
        ),
        out_specs=(
            P(("fsdp", "tensor"), None),
            P(("fsdp", "tensor"), None),
            P(),
            P(),
            P("fsdp", "tensor"),
            P("fsdp", "tensor"),
            P("fsdp", "tensor"),
            P("tensor", "fsdp"),
            P("fsdp", "tensor"),
            P("fsdp", "tensor"),
            P("tensor", "fsdp"),
        ),
        check_vma=False,
    )
```

```python
import functools
import math

import jax
import jax.numpy as jnp
from jax import lax
from jax.experimental import pallas as pl
from jax.experimental.pallas import tpu as pltpu
from jax.sharding import PartitionSpec as P

HEAD = 64
SAMPLE = 512
EPS = 1e-05
LANES = 128
ROPE_BASE = 130000.0
MESH = pl.DeviceIdType.MESH
BF16 = jnp.bfloat16
F32 = jnp.float32
ANY = pl.BlockSpec(memory_space=pl.ANY)
VMEM = pl.BlockSpec(memory_space=pltpu.VMEM)


def flip(index, bit):
    return index + bit - 2 * bit * ((index // bit) % 2)


def dot_nt(left, right):
    return lax.dot_general(left, right, (((1,), (1,)), ((), ())), preferred_element_type=F32)


def dot_tn(left, right):
    return lax.dot_general(left, right, (((0,), (0,)), ((), ())), preferred_element_type=F32)


class Group:
    def __init__(self, z_size, t_size):
        self.z_size = z_size
        self.t_size = t_size
        self.size = 2 * t_size
        inner = []
        bit = 2
        while bit < t_size:
            inner.append(bit)
            bit *= 2
        self.core = 1
        self.pair = t_size
        self.orders = (tuple(inner) + (self.pair,), tuple(inner[::-1]) + (self.pair,))
        self.inner = (tuple(inner), tuple(inner[::-1]))
        self.bits = (self.core,) + tuple(inner) + (self.pair,)
        masks = [0]
        for b in self.orders[0]:
            masks = masks + [m + b for m in masks]
        self.masks = tuple(masks)
        self.far = tuple(range(2, z_size))

    def place(self):
        return lax.axis_index("fsdp"), lax.axis_index("tensor")

    def rank(self, mask=0):
        z, t = self.place()
        r = (z % 2) * self.t_size + t
        for b in self.bits:
            if mask & b:
                r = flip(r, b)
        return r

    def chip_at(self, j, near=False):
        chip = self.rank() // 2
        mask = j if near else len(self.masks) - 1 - j
        out = 0
        bit = 1
        while bit < len(self.masks):
            a, b = (chip // bit) % 2, (mask // bit) % 2
            out = out + (a + b - 2 * a * b) * bit
            bit *= 2
        return out

    def partner(self, bit):
        z, t = self.place()
        if bit == self.pair:
            return (flip(z, 1), t)
        return (z, flip(t, bit))

    def across(self, mask):
        z, t = self.place()
        bit = 1
        while bit < self.z_size:
            if mask & bit:
                z = flip(z, bit)
            bit *= 2
        return (z, t)

    def beside(self, mask):
        z, t = self.place()
        bit = 1
        while bit < self.t_size:
            if mask & bit:
                t = flip(t, bit)
            bit *= 2
        return (z, t)

    def greet(self, everyone=False):
        barrier = pltpu.get_barrier_semaphore()
        if everyone:
            peers = [self.beside(m) for m in range(1, self.t_size)]
        else:
            peers = [self.partner(b) for b in self.bits if b != self.pair]
        peers += [self.across(m) for m in range(1, self.z_size)]
        for peer in peers:
            pl.semaphore_signal(barrier, inc=1, device_id=peer, device_id_type=MESH)
        pl.semaphore_wait(barrier, len(peers))


def last_bit(mask, order):
    found = None
    for b in order:
        if mask & b:
            found = b
    return found


class Gather:
    def __init__(self, grp, x_ref, o_ref, send, recv, local):
        self.grp, self.x, self.o = grp, x_ref, o_ref
        self.send, self.recv = send, recv
        self.rows = x_ref.shape[0]
        self.half = self.rows // 2
        self.order = [(grp.pair,) + grp.inner[h] + (grp.core,) for h in range(2)]
        self.sent = []
        own = pl.ds(pl.multiple_of(grp.rank() * self.rows, self.rows), self.rows)
        self.own = pltpu.make_async_copy(x_ref, o_ref.at[own], local)

    def at(self, mask, h):
        first = self.grp.rank(mask) * self.rows + h * self.half
        return self.o.at[pl.ds(pl.multiple_of(first, self.half), self.half)]

    def copy(self, src, mask, h, key, bit):
        return pltpu.make_async_remote_copy(
            src_ref=src,
            dst_ref=self.at(mask, h),
            send_sem=self.send.at[h, key],
            recv_sem=self.recv.at[h, key],
            device_id=self.grp.partner(bit),
            device_id_type=MESH,
        )

    def forward(self, h, mask, bits=None):
        order = self.order[h]
        start = 0 if mask == 0 else order.index(last_bit(mask, order)) + 1
        for bit in order[start:] if bits is None else bits:
            self.own_copy(h, mask, bit).start()
            self.sent.append((h, mask, bit))

    def own_copy(self, h, mask, bit):
        src = self.x.at[pl.ds(h * self.half, self.half)] if mask == 0 else self.at(mask, h)
        return self.copy(src, mask, h, mask | bit, bit)

    def arrived(self, h, mask):
        bit = last_bit(mask, self.order[h])
        self.copy(self.at(mask, h), mask, h, mask, bit).wait_recv()

    def begin(self):
        self.own.start()
        for h in range(2):
            self.forward(h, 0, (self.grp.pair,))
        for k in range(1, len(self.order[0])):
            for h in range(2):
                self.forward(h, 0, (self.order[h][k],))
        grp = self.grp
        plain = sorted(
            (m for m in grp.masks if m), key=lambda m: (m & grp.pair, bin(m).count("1"))
        )
        if len(plain) > 3:
            plain.remove(grp.pair)
            plain.insert(2, grp.pair)
        self.plain = plain

        def step(h, m):
            self.arrived(h, m)
            self.forward(h, m)

        return [
            functools.partial(step, h, m if h == 0 else mirror(grp, m))
            for m in plain
            for h in range(2)
        ]

    def chip_arrived(self, mask):
        for h in range(2):
            self.arrived(h, mask | self.grp.core)
        if mask == 0:
            self.own.wait()

    def needs(self, steps):
        plain = self.plain
        done = 0
        out = []
        for m in sorted(self.grp.masks):
            upto = done
            if m:
                other = next(k for k in plain if mirror(self.grp, k) == m)
                upto = 2 * (max(plain.index(m), plain.index(other)) + 1)
            out.append(steps[done : max(done, upto)] + [functools.partial(self.chip_arrived, m)])
            done = max(done, upto)
        return out

    def finish(self):
        for m in self.grp.masks:
            self.chip_arrived(m)
        self.drain()

    def drain(self):
        for sent in self.sent:
            self.own_copy(*sent).wait_send()


def mirror(grp, mask):
    out = mask & (grp.pair | grp.core)
    a, b = grp.inner
    for p, q in zip(a, b):
        if mask & p:
            out |= q
    return out


TILE = 16


def add_rows(dst, src, rows):
    count = rows // TILE

    @pl.loop(0, count, unroll=1 + (count + 1) % 2)
    def _(i):
        part = pl.ds(pl.multiple_of(i * TILE, TILE), TILE)
        dst[part] = (dst[part].astype(F32) + src[part].astype(F32)).astype(dst.dtype)


def scatter_scratch(grp, rows, width):
    n = len(grp.masks)
    return [
        pltpu.VMEM((n, rows, width), BF16),
        pltpu.VMEM((2, n - 1, rows // 2, width), BF16),
        pltpu.SemaphoreType.DMA((n,)),
        pltpu.SemaphoreType.DMA((n,)),
        pltpu.SemaphoreType.DMA((2, n)),
        pltpu.SemaphoreType.DMA((2, n)),
    ]


N_SCATTER = 6


class Scatter:
    def __init__(self, grp, p, rows, got, rbuf, csend, crecv, send, recv, own=None):
        self.grp, self.p, self.rows, self.half = grp, p, rows, rows // 2
        self.own = own
        self.got, self.rbuf = got, rbuf
        self.csend, self.crecv, self.send, self.recv = csend, crecv, send, recv
        self.index = {m: len(grp.masks) - 1 - m // 2 for m in grp.masks}
        self.started = []
        self.slots = []
        for h in range(2):
            s = {}
            order = grp.orders[h]
            for i in range(len(order)):
                later = order[i + 1 :]
                for m in grp.masks:
                    if all((not m & b) or b in later for b in order):
                        s[(i, m)] = len(s)
            self.slots.append(s)

    def masks(self, pair):
        chosen = [m for m in self.grp.masks if bool(m & self.grp.pair) == pair]
        return sorted(chosen, reverse=True)

    def begin_tile(self, j):
        _, t = self.grp.place()
        first = (self.grp.chip_at(j) * 2 + 1 - t % 2) * self.rows
        pltpu.make_async_remote_copy(
            src_ref=self.p.at[pl.ds(pl.multiple_of(first, self.rows), self.rows)],
            dst_ref=self.got.at[j],
            send_sem=self.csend.at[j],
            recv_sem=self.crecv.at[j],
            device_id=self.grp.partner(self.grp.core),
            device_id_type=MESH,
        ).start()

    def block(self, mask, h=None):
        if self.own is not None and not mask & self.grp.core:
            mine = self.own.at[self.index[mask]]
            return mine if h is None else mine.at[pl.ds(h * self.half, self.half)]
        first = self.grp.rank(mask) * self.rows
        if h is None:
            return self.p.at[pl.ds(pl.multiple_of(first, self.rows), self.rows)]
        return self.p.at[pl.ds(pl.multiple_of(first + h * self.half, self.half), self.half)]

    def core_copy(self, mask):
        i = self.index[mask]
        return pltpu.make_async_remote_copy(
            src_ref=self.block(mask | self.grp.core),
            dst_ref=self.got.at[i],
            send_sem=self.csend.at[i],
            recv_sem=self.crecv.at[i],
            device_id=self.grp.partner(self.grp.core),
            device_id_type=MESH,
        )

    def begin(self, masks):
        for m in masks:
            self.core_copy(m).start()

    def load(self, mask, sem):
        first = pl.multiple_of(self.grp.rank(mask) * self.rows, self.rows)
        i = self.index[mask]
        return pltpu.make_async_copy(self.p.at[pl.ds(first, self.rows)], self.own.at[i], sem.at[i])

    def core_step(self, mask):
        self.core_copy(mask).wait_recv()
        add_rows(self.block(mask), self.got.at[self.index[mask]], self.rows)
        for h in range(2):
            if mask & self.grp.orders[h][0]:
                self.ship(h, 0, mask)

    def link_copy(self, h, i, mask, k):
        return pltpu.make_async_remote_copy(
            src_ref=self.block(mask, h),
            dst_ref=self.rbuf.at[h, k],
            send_sem=self.send.at[h, k],
            recv_sem=self.recv.at[h, k],
            device_id=self.grp.partner(self.grp.orders[h][i]),
            device_id_type=MESH,
        )

    def ship(self, h, i, mask):
        self.out_copy(h, i, mask).start()
        self.started.append((h, i, mask))

    def out_copy(self, h, i, mask):
        return self.link_copy(h, i, mask, self.slots[h][(i, mask - self.grp.orders[h][i])])

    def take(self, h, i, mask):
        k = self.slots[h][(i, mask)]
        self.link_copy(h, i, mask, k).wait_recv()
        add_rows(self.block(mask, h), self.rbuf.at[h, k], self.half)

    def core_steps(self, pair):
        return [functools.partial(self.core_step, m) for m in self.masks(pair)]

    def link_steps(self, pair):
        steps = []
        for i in range(1, len(self.grp.orders[0])):
            for m in self.masks(pair):
                for h in range(2):
                    order = self.grp.orders[h]
                    mine = m if h == 0 else mirror(self.grp, m)
                    if any(mine & b for b in order[:i]):
                        continue

                    def step(h=h, i=i, mine=mine, order=order):
                        self.take(h, i - 1, mine)
                        if mine & order[i]:
                            self.ship(h, i, mine)

                    steps.append(step)
        return steps

    def finish(self):
        for h in range(2):
            self.take(h, len(self.grp.orders[h]) - 1, 0)

    def drain(self):
        for m in self.grp.masks:
            self.core_copy(m).wait_send()
        for sent in self.started:
            self.out_copy(*sent).wait_send()


def plain_scatter(grp, p, rows, refs):
    scat = Scatter(grp, p, rows, *refs)
    scat.begin(scat.masks(True) + scat.masks(False))
    run(scat.core_steps(True) + scat.core_steps(False))
    run(scat.link_steps(True) + scat.link_steps(False))
    scat.finish()
    scat.drain()
    return scat.block(0)


def run(*lists):
    for i in range(max(len(x) for x in lists)):
        for steps in lists:
            if i < len(steps):
                steps[i]()


class Spread:
    def __init__(self, grp, send, recv):
        self.grp, self.send, self.recv = grp, send, recv
        self.used = 0
        self.makers = []

    def to(self, mask, views, start=True):
        k = self.used
        self.used += 1

        def make():
            src, dst = views()
            if mask == 0:
                return pltpu.make_async_copy(src, dst, self.send.at[k])
            return pltpu.make_async_remote_copy(
                src_ref=src,
                dst_ref=dst,
                send_sem=self.send.at[k],
                recv_sem=self.recv.at[k],
                device_id=self.grp.across(mask),
                device_id_type=MESH,
            )

        if start:
            make().start()
        self.makers.append(make)
        return make

    def wait(self):
        self.wait_first(len(self.makers))

    def wait_first(self, count):
        for make in self.makers[:count]:
            make().wait()
        self.makers = self.makers[count:]


def spread_sems(grp, parts):
    return [pltpu.SemaphoreType.DMA((grp.z_size * parts,))] * 2


def spread_weight(grp, spread, shard, whole, half_axis, at, masks=None, start=True):
    axis = 1 - half_axis
    mine, other = shard
    makers = []
    for m in grp.far + (0, 1) if masks is None else masks:

        def views(src=other if m % 2 else mine):
            z, _ = grp.place()
            size, width = src.shape[axis], src.shape[half_axis]
            place = pl.ds(pl.multiple_of(z * size, size), size)
            if axis == 0:
                return src, whole.at[place, at : at + width]
            return src, whole.at[at : at + width, place]

        makers.append(spread.to(m, views, start))
    return makers


def halves_of(grp, ref, axis):
    z, _ = grp.place()
    size = ref.shape[axis] // 2
    out = []
    for which in (z % 2, 1 - z % 2):
        part = pl.ds(pl.multiple_of(which * size, size), size)
        out.append(ref.at[:, part] if axis == 1 else ref.at[part])
    return out


def weight_jobs(grp, spread, shard, whole, half_axis, pieces):
    axis = 1 - half_axis
    mine, other = shard
    jobs = {m: [] for m in range(grp.z_size)}
    for i in range(pieces):
        for m in range(grp.z_size):

            def views(i=i, src=other if m % 2 else mine):
                z, _ = grp.place()
                size, width = src.shape[0] // pieces, src.shape[1]
                piece = src.at[pl.ds(i * size, size)]
                if axis == 0:
                    first = pl.multiple_of(z * (size * pieces) + i * size, size)
                    return piece, whole.at[pl.ds(first, size)]
                place = pl.ds(pl.multiple_of(z * width, width), width)
                return piece, whole.at[pl.ds(i * size, size), place]

            jobs[m].append(functools.partial(spread.to, m, views))
    return by_distance(grp, jobs)


def grad_jobs(grp, spread, grad, got, axis, pieces):
    jobs = {m: [] for m in range(1, grp.z_size)}
    for i in range(pieces):
        for m in range(1, grp.z_size):

            def views(i=i, m=m):
                place = grp.across(m)[0]
                size = got.shape[1] // pieces
                land = got.at[m - 1, pl.ds(i * size, size)]
                if axis == 0:
                    first = pl.multiple_of(place * (size * pieces) + i * size, size)
                    return grad.at[pl.ds(first, size)], land
                width = got.shape[2]
                part = pl.ds(pl.multiple_of(place * width, width), width)
                return grad.at[pl.ds(i * size, size), part], land

            jobs[m].append(functools.partial(spread.to, m, views))
    return by_distance(grp, jobs)


def by_distance(grp, jobs):
    far = [job for jobs_i in zip(*(jobs[m] for m in grp.far)) for job in jobs_i]
    near = [job for jobs_i in zip(*(jobs[m] for m in (1, 0) if m in jobs)) for job in jobs_i]
    return far, near


def mixed(steps, jobs, first=0):
    out = list(steps[:first])
    tail = steps[first:]
    done = 0
    for i, step in enumerate(tail):
        upto = (i + 1) * len(jobs) // len(tail)
        out.append(functools.partial(run, [step] + jobs[done:upto]))
        done = upto
    return out + (jobs if not tail else [])


PIECES = 1


def spread_grad(grp, spread, grad, got, axis, masks=None, start=True):
    makers = []
    for m in grp.far + (1,) if masks is None else masks:

        def views(m=m):
            size = grad.shape[axis] // grp.z_size
            part = pl.ds(pl.multiple_of(grp.across(m)[0] * size, size), size)
            return (grad.at[part] if axis == 0 else grad.at[:, part]), got.at[m - 1]

        makers.append(spread.to(m, views, start))
    return makers


def launch(makers, where=None):
    if where is None:
        for make in makers:
            make().start()
    else:

        @pl.when(where)
        def _():
            for make in makers:
                make().start()


def inner_plane(grp):
    z, _ = grp.place()
    return (z * 4 >= grp.z_size) & (z * 4 < 3 * grp.z_size)


def staged_gather(gather, after_pair):
    steps = gather.begin()
    cut = 6 if len(steps) > 6 else len(steps)
    run(steps[:cut])
    after_pair()
    run(steps[cut:])
    gather.finish()


def tiles(rows, body):
    count = rows // TILE

    @pl.loop(0, count, unroll=1 + (count + 1) % 2)
    def _(i):
        body(pl.ds(pl.multiple_of(i * TILE, TILE), TILE))


def norm_scale(value):
    return lax.rsqrt(jnp.mean(value * value, axis=-1, keepdims=True) + EPS)


def gather_scratch(grp):
    return [
        pltpu.SemaphoreType.DMA((2, grp.size)),
        pltpu.SemaphoreType.DMA((2, grp.size)),
        pltpu.SemaphoreType.DMA,
    ]


def params(cid):
    return pltpu.CompilerParams(
        collective_id=cid, has_side_effects=True, vmem_limit_bytes=61952 << 10
    )


def sds(shape, dtype):
    return jax.ShapeDtypeStruct(shape, dtype)


def weight_views(grp, refs, axis, presliced):
    if presliced:
        return [(refs[2 * i], refs[2 * i + 1]) for i in range(len(refs) // 2)]
    return [tuple(halves_of(grp, r, axis)) for r in refs]


def shard_args(low, shards_, axis):
    aligned = shards_[0].shape[axis] // 2 % (128 if axis == 1 else 16) == 0
    if aligned:
        return False, list(shards_)
    out = []
    for w in shards_:
        size = w.shape[axis] // 2
        out += [
            lax.dynamic_slice_in_dim(w, low * size, size, axis),
            lax.dynamic_slice_in_dim(w, (1 - low) * size, size, axis),
        ]
    return True, out


def first_kernel(grp, flags, n_qkv, x_ref, gain_ref, *rest):
    pre_qkv, pre_o = flags
    qkv_refs, rest = rest[:n_qkv], rest[n_qkv:]
    n_o = 2 if pre_o else 1
    o_refs, rest = rest[:n_o], rest[n_o:]
    seg_ref, all_ref, wqkv_ref, wo_ref, start_ref, cos_ref, sin_ref, local, ids, send, recv, sem, zs, zr = rest
    grp.greet()
    spread = Spread(grp, zs, zr)
    z, _ = grp.place()
    spread.to(0, lambda: (seg_ref, ids.at[z % 2]))
    spread.to(1, lambda: (seg_ref, ids.at[z % 2]))

    def weights(masks):
        at = 0
        for pair in weight_views(grp, qkv_refs, 1, pre_qkv):
            spread_weight(grp, spread, pair, wqkv_ref, 1, at, masks)
            at += pair[0].shape[1]
        for pair in weight_views(grp, o_refs, 0, pre_o):
            spread_weight(grp, spread, pair, wo_ref, 0, 0, masks)

    def norm(rows):
        x = x_ref[rows].astype(F32)
        local[rows] = (x * norm_scale(x) * gain_ref[0:1].astype(F32)).astype(BF16)

    tiles(x_ref.shape[0], norm)
    gather = Gather(grp, local, all_ref, send, recv, sem)
    steps = gather.begin()
    weights((1,) + grp.far + (0,))
    spread.wait_first(2)
    places(ids, start_ref, cos_ref, sin_ref)
    run(steps[:6])
    run(steps[6:] or [lambda: None])
    gather.finish()
    spread.wait()


def places(ids, start_ref, cos_ref, sin_ref):
    planes, rows, length = ids.shape
    wide = cos_ref.shape[1]
    place = lax.broadcasted_iota(jnp.int32, (1, length), 1)
    lane = lax.broadcasted_iota(jnp.int32, (LANES, LANES), 1)
    pair = (lane % (HEAD // 2)).astype(F32)
    inverse = jnp.exp(pair * (-2.0 / HEAD) * math.log(ROPE_BASE))
    sign = jnp.where(lane % HEAD < HEAD // 2, -1.0, 1.0)
    for a in range(planes):
        for r in range(rows):
            row = a * rows + r
            own = ids[a, r : r + 1]
            change = (place == 0) | (own != pltpu.roll(own, 1, 1))
            start = jnp.where(change, place, 0)
            step = 1
            while step < length:
                start = jnp.maximum(start, jnp.where(place >= step, pltpu.roll(start, step, 1), 0))
                step *= 2
            start_ref[row] = start

    @pl.loop(0, planes * rows)
    def _(row):
        @pl.loop(0, length // LANES)
        def _(c):
            here = pl.ds(pl.multiple_of(c * LANES, LANES), LANES)
            token = c * LANES + lax.broadcasted_iota(jnp.int32, (1, LANES), 1)
            position = (token - start_ref[row, :, here]).astype(F32)
            angle = jnp.broadcast_to(position, (LANES, LANES)).T * inverse
            there = pl.ds(pl.multiple_of(row * length + c * LANES, LANES), LANES)
            cos_ref[there] = jnp.cos(angle)[:, :wide]
            sin_ref[there] = (sign * jnp.sin(angle))[:, :wide]


def first(grp, low, x, gain, w_query, w_key, w_value, w_out, ids, cid):
    pre_qkv, qkv = shard_args(low, (w_query, w_key, w_value), 1)
    pre_o, out = shard_args(low, (w_out,), 0)
    rows, width = x.shape
    if pre_qkv:
        qkv = [jnp.concatenate(qkv[i::2], axis=1) for i in range(2)]
    deep = w_query.shape[0] * grp.z_size
    thin = 3 * w_query.shape[1] // 2
    table = sds((2 * ids.shape[0] * ids.shape[1], thin // 3), F32)
    return pl.pallas_call(
        functools.partial(first_kernel, grp, (pre_qkv, pre_o), len(qkv)),
        out_shape=[
            sds((rows * grp.size, width), BF16),
            sds((deep, thin), BF16),
            sds((w_out.shape[0] // 2, w_out.shape[1] * grp.z_size), BF16),
            sds((2 * ids.shape[0], 1, ids.shape[1]), jnp.int32),
            table,
            table,
        ],
        in_specs=[VMEM, VMEM] + [ANY] * (len(qkv) + len(out)) + [VMEM],
        out_specs=[ANY] * 3 + [VMEM] * 3,
        scratch_shapes=[
            pltpu.VMEM((rows, width), BF16),
            pltpu.VMEM((2,) + ids.shape, jnp.int32),
        ]
        + gather_scratch(grp)
        + spread_sems(grp, 5),
        compiler_params=params(cid),
        name="first",
    )(x, gain, *qkv, *out, ids)


def attend_rows(length, heads, q_ref, k_ref, v_ref, start_ref, o_ref, lse_ref, row):
    base = row * length

    def band(h, at, first, width, size):
        lanes = slice(h * HEAD, (h + 1) * HEAD)
        mine = pl.ds(pl.multiple_of(base + at, QB), size)
        keys = pl.ds(pl.multiple_of(base + first, QB), width)
        cols = pl.ds(pl.multiple_of(at, QB), size)
        query = q_ref[mine, lanes] * BF16(HEAD**-0.5)
        scores = dot_nt(k_ref[keys, lanes], query)
        mask = kept(start_ref[row, :, cols], at, size, first, width)
        scores = jnp.where(mask, scores, -1e9)
        top = jnp.max(scores, axis=0, keepdims=True)
        expo = jnp.exp(scores - top)
        total = jnp.sum(expo, axis=0, keepdims=True)
        weights = (expo * (1.0 / total)).astype(BF16)
        o_ref[mine, lanes] = dot_tn(weights, v_ref[keys, lanes]).astype(BF16)
        lse_ref[row, h : h + 1, cols] = top + jnp.log(total)

    return banded(length, heads, band)


def banded(length, heads, band):
    parts = []
    for h in range(heads):
        whole = [b for b in bands(length) if b[3] == SAMPLE + QB]
        for at, size, first, width in bands(length):
            if width != SAMPLE + QB:
                parts.append(functools.partial(band, h, at, first, width, size))

        def loop(h=h, whole=whole):
            @pl.loop(0, len(whole))
            def _(i):
                at = whole[0][0] + i * QB
                band(h, at, at - SAMPLE, SAMPLE + QB, QB)

        if whole:
            parts.append(loop)
    return parts


def middle_kernel(
    grp,
    heads,
    fused,
    na_ref,
    wqkv_ref,
    wo_ref,
    cos_ref,
    sin_ref,
    start_ref,
    dy_ref,
    x_ref,
    gain_ref,
    gate_ref,
    up_ref,
    down_ref,
    q_ref,
    k_ref,
    v_ref,
    o_ref,
    lse_ref,
    h_ref,
    nm_ref,
    dyall_ref,
    wg_ref,
    wu_ref,
    wd_ref,
    *rest,
):
    early, rest = (rest[:2], rest[2:]) if fused else (None, rest)
    p, rowbuf, rowsem, local = rest[:4]
    rest = rest[4:]
    if fused:
        wg, wu, tile, tilesem, stage_a, stage_g, stagesem = rest[:7]
        rest = rest[7:]
    scat_refs, rest = rest[:N_SCATTER], rest[N_SCATTER:]
    dsend, drecv, dsem, send, recv, sem, zs, zr = rest
    rows_all, _, length = start_ref.shape
    wide = heads * HEAD
    z, _ = grp.place()
    n = rows_all // 2
    rows = [(1 - z % 2) * n + j for j in range(n)] + [(z % 2) * n + j for j in range(n)]

    blocks = length // QB

    def load(i, j):
        part = pl.ds(pl.multiple_of(rows[i] * length + j * QB, QB), QB)
        return pltpu.make_async_copy(na_ref.at[part], rowbuf.at[j % 2], rowsem.at[j % 2])

    load(0, 0).start()
    grp.greet()
    spread = Spread(grp, zs, zr)
    views = [
        (halves_of(grp, gate_ref, 1), wg_ref, 1),
        (halves_of(grp, up_ref, 1), wu_ref, 1),
        (halves_of(grp, down_ref, 0), wd_ref, 0),
    ]
    outer = Gather(grp, dy_ref, dyall_ref, dsend, drecv, dsem)
    outer_steps = outer.begin()
    for pair, whole, axis in views[:2]:
        spread_weight(grp, spread, pair, whole, axis, 0, (1, 0))
    far = []
    for pair, whole, axis in views[:2]:
        far += spread_weight(grp, spread, pair, whole, axis, 0, grp.far, start=False)
    inner = inner_plane(grp)
    outer_plane = jnp.logical_not(inner)
    cut = len(far) // 2
    launch(far[:cut])
    launch(far[cut:], inner)
    scat = Scatter(grp, p, x_ref.shape[0], *scat_refs)

    def project(i):
        base = rows[i] * length
        if i:
            load(i, 0).start()

        @pl.loop(0, blocks)
        def _(j):
            @pl.when(j + 1 < blocks)
            def _():
                load(i, j + 1).start()

            load(i, j).wait()
            there = pl.ds(pl.multiple_of(base + j * QB, QB), QB)
            qkv = jnp.dot(rowbuf[j % 2], wqkv_ref[...], preferred_element_type=F32)
            cosine, sine = cos_ref[there], sin_ref[there]
            query, key = qkv[:, :wide], qkv[:, wide : 2 * wide]
            q_ref[there] = (query * cosine + swap_halves(query) * sine).astype(BF16)
            k_ref[there] = (key * cosine + swap_halves(key) * sine).astype(BF16)
            v_ref[there] = qkv[:, 2 * wide :].astype(BF16)

    def branch(i):
        base = rows[i] * length

        @pl.loop(0, length // QB)
        def _(j):
            there = pl.ds(pl.multiple_of(base + j * QB, QB), QB)
            p[there] = jnp.dot(o_ref[there], wo_ref[...], preferred_element_type=F32).astype(BF16)

    def parts(i):
        return (
            [functools.partial(project, i)]
            + attend_rows(length, heads, q_ref, k_ref, v_ref, start_ref, o_ref, lse_ref, rows[i])
            + [functools.partial(branch, i)]
        )

    todo = [part for i in range(n) for part in parts(i)]
    wait = max(0, len(todo) - 4)
    run(todo[:wait])
    outer_steps = weave(todo[wait:], outer_steps)
    scat.begin(scat.masks(True))
    todo = [part for i in range(n, 2 * n) for part in parts(i)]
    links = scat.link_steps(True)
    beside = scat.core_steps(True) + links[:-2]
    beside = weave(todo, beside, -(-len(beside) // len(todo)))
    scat.begin(scat.masks(False))
    run(beside + scat.core_steps(False)[:1] + links[-2:])
    launch(far[cut:], outer_plane)
    run(scat.core_steps(False)[1:])
    run(scat.link_steps(False), outer_steps)
    scat.finish()
    summed = scat.block(0)

    def norm(part):
        h = x_ref[part].astype(F32) + summed[part].astype(F32)
        h_ref[part] = h
        local[part] = (h * norm_scale(h) * gain_ref[1:2].astype(F32)).astype(BF16)

    tiles(x_ref.shape[0], norm)
    gather = Gather(grp, local, nm_ref, send, recv, sem)
    steps = gather.begin()
    pair, whole, axis = views[2]
    spread_weight(grp, spread, pair, whole, axis, 0)
    if not fused:
        run(steps)
        scat.drain()
        outer.finish()
        gather.finish()
        spread.wait()
        return
    spread.wait_first(2 * grp.z_size)
    loads = [
        pltpu.make_async_copy(src, dst, tilesem.at[i])
        for i, (src, dst) in enumerate(((wg_ref, wg), (wu_ref, wu)))
    ]
    for c in loads:
        c.start()
    scat.drain()
    for c in loads:
        c.wait()
    size = tile.shape[0]
    units = wg.shape[1]

    def saves(j):
        here = pl.ds(pl.multiple_of(grp.chip_at(j, near=True) * size, size), size)
        return (
            pltpu.make_async_copy(stage_a.at[j % 2], early[0].at[here], stagesem.at[0, j % 2]),
            pltpu.make_async_copy(stage_g.at[j % 2], early[1].at[here], stagesem.at[1, j % 2]),
        )

    def forward(j):
        here = pl.ds(pl.multiple_of(grp.chip_at(j, near=True) * size, size), size)
        load = pltpu.make_async_copy(nm_ref.at[here], tile, tilesem.at[0])
        load.start()

        @pl.when(j > 1)
        def _():
            for c in saves(j - 2):
                c.wait()

        load.wait()
        act, gate, up = gate_up(tile[...], wg[...], wu[...])
        stage_a[j % 2] = act
        stage_g[j % 2, :, :units] = gate
        stage_g[j % 2, :, units:] = up
        for c in saves(j):
            c.start()

    count = len(grp.masks)
    led(count, forward, gather.needs(steps))
    for j in (count - 2, count - 1):
        for c in saves(j):
            c.wait()
    outer.finish()
    gather.drain()
    spread.wait()


def middle(grp, heads, normed, wqkv, wo, cosine, sine, start, dy, x, gain, w_gate, w_up, w_down, cid):
    rows, width = x.shape
    total = rows * grp.size
    wide = heads * HEAD
    rows_all, _, length = start.shape
    thin = sds((total, wide), BF16)
    fused = grp.size <= 16
    units = w_gate.shape[1] // 2
    early, beside = [], []
    if fused:
        early = [sds((total, units), BF16), sds((total, 2 * units), BF16)]
        beside = [
            pltpu.VMEM((width, units), BF16),
            pltpu.VMEM((width, units), BF16),
            pltpu.VMEM((2 * rows, width), BF16),
            pltpu.SemaphoreType.DMA((2,)),
            pltpu.VMEM((2, 2 * rows, units), BF16),
            pltpu.VMEM((2, 2 * rows, 2 * units), BF16),
            pltpu.SemaphoreType.DMA((2, 2)),
        ]
    return pl.pallas_call(
        functools.partial(middle_kernel, grp, heads, fused),
        out_shape=[thin] * 4
        + [
            sds((rows_all, heads, length), F32),
            sds((rows, width), F32),
            sds((total, width), BF16),
            sds((total, width), BF16),
            sds((w_gate.shape[0] * grp.z_size, w_gate.shape[1] // 2), BF16),
            sds((w_up.shape[0] * grp.z_size, w_up.shape[1] // 2), BF16),
            sds((w_down.shape[0] // 2, w_down.shape[1] * grp.z_size), BF16),
        ]
        + early,
        in_specs=[ANY, VMEM, VMEM, VMEM, VMEM, VMEM, ANY, VMEM, VMEM, ANY, ANY, ANY],
        out_specs=[VMEM] * 6 + [ANY] * (5 + len(early)),
        scratch_shapes=[
            pltpu.VMEM((total, width), BF16),
            pltpu.VMEM((2, QB, width), BF16),
            pltpu.SemaphoreType.DMA((2,)),
            pltpu.VMEM((rows, width), BF16),
        ]
        + beside
        + scatter_scratch(grp, rows, width)
        + gather_scratch(grp)
        + gather_scratch(grp)
        + spread_sems(grp, 3 * PIECES),
        compiler_params=params(cid),
        name="middle",
    )(normed, wqkv, wo, cosine, sine, start, dy, x, gain, w_gate, w_up, w_down)


def norm_back_tile(value, gain, grad):
    scale = norm_scale(value)
    scaled = grad * gain
    inner = jnp.mean(value * scaled, axis=-1, keepdims=True)
    back = scale * scaled - value * (scale * scale * scale * inner)
    return back, jnp.sum(grad * value * scale, axis=0, keepdims=True)


class Fetch:
    def __init__(self, sems, *pairs):
        self.copies = [
            pltpu.make_async_copy(src, dst, sems.at[i]) for i, (src, dst) in enumerate(pairs)
        ]
        for c in self.copies:
            c.start()

    def wait(self):
        for c in self.copies:
            c.wait()


def weave(parts, steps, each=1):
    for part in parts:
        part()
        for step in steps[:each]:
            step()
        steps = steps[each:]
    return steps


def last_kernel(
    grp,
    heads,
    branch_ref,
    na_ref,
    part_ref,
    gup_ref,
    q_ref,
    k_ref,
    v_ref,
    o_ref,
    lse_ref,
    cos_in,
    sin_in,
    start_ref,
    wqkv_in,
    wo_ref,
    h_in,
    x_in,
    dh_in,
    gain_ref,
    gm_ref,
    out_ref,
    tok_ref,
    gains_ref,
    gout_ref,
    gqkv_ref,
    upgot_ref,
    outgot_ref,
    qkvgot_ref,
    p,
    own,
    ownsem,
    rowbuf,
    rowsem,
    cols,
    csem,
    do,
    dqkv,
    dq,
    dk,
    dv,
    gacc,
    cos_ref,
    sin_ref,
    wqkv_ref,
    h_ref,
    x_ref,
    dh_ref,
    fsem,
    buf,
    gs,
    gr,
    *rest,
):
    na_scat, rest = rest[:N_SCATTER], rest[N_SCATTER:]
    out_scat, rest = rest[:N_SCATTER], rest[N_SCATTER:]
    zs, zr = rest
    rows_all, _, length = start_ref.shape
    rows, width = h_in.shape
    wide = heads * HEAD
    z, _ = grp.place()
    n = rows_all // 2
    order = [(1 - z % 2) * n + j for j in range(n)] + [(z % 2) * n + j for j in range(n)]
    blocks = length // QB
    step = cols.shape[2]

    def load(i, j):
        part = pl.ds(pl.multiple_of(order[i] * length + j * QB, QB), QB)
        return pltpu.make_async_copy(branch_ref.at[part], rowbuf.at[j % 2], rowsem.at[j % 2])

    def load_cols(c):
        part = pl.ds(pl.multiple_of(c * step, step), step)
        return pltpu.make_async_copy(na_ref.at[:, part], cols.at[c % 2], csem.at[c % 2])

    load(0, 0).start()
    fetch = Fetch(
        fsem,
        (cos_in, cos_ref),
        (sin_in, sin_ref),
        (wqkv_in, wqkv_ref),
        (h_in, h_ref),
        (x_in, x_ref),
        (dh_in, dh_ref),
    )
    load_cols(0).start()
    outer = Scatter(grp, part_ref, rows, *out_scat, own=own)
    for m in outer.masks(True) + outer.masks(False):
        outer.load(m, ownsem).start()
    grp.greet(everyone=True)
    outer.begin(outer.masks(True) + outer.masks(False))
    spread = Spread(grp, zs, zr)
    spread_grad(grp, spread, gup_ref, upgot_ref, 0, (1,) + grp.far)
    scat = Scatter(grp, p, rows, *na_scat)
    gacc[...] = jnp.zeros_like(gacc)

    def outer_core(m):
        outer.load(m, ownsem).wait()
        outer.core_step(m)

    outer_steps = [
        functools.partial(outer_core, m) for m in outer.masks(True) + outer.masks(False)
    ]
    outer_steps += outer.link_steps(True) + outer.link_steps(False)

    def prepare(i):
        base = order[i] * length
        if i:
            load(i, 0).start()
        dk[...] = jnp.zeros_like(dk)
        dv[...] = jnp.zeros_like(dv)

        @pl.loop(0, blocks)
        def _(j):
            @pl.when(j + 1 < blocks)
            def _():
                load(i, j + 1).start()

            load(i, j).wait()
            there = pl.ds(pl.multiple_of(base + j * QB, QB), QB)
            here = pl.ds(pl.multiple_of(j * QB, QB), QB)
            branch = rowbuf[j % 2]
            do[here] = dot_nt(branch, wo_ref[...]).astype(BF16)
            gacc[...] += dot_tn(o_ref[there], branch)

    def banded_back(i):
        row = order[i]
        base = row * length

        def band(h, at, first, width, size):
            lanes = slice(h * HEAD, (h + 1) * HEAD)
            cols_at = pl.ds(pl.multiple_of(at, QB), size)
            keys_at = pl.ds(pl.multiple_of(first, QB), width)
            mine = pl.ds(pl.multiple_of(base + at, QB), size)
            keys = pl.ds(pl.multiple_of(base + first, QB), width)
            query = q_ref[mine, lanes]
            key = k_ref[keys, lanes]
            grad = do[cols_at, lanes]
            scores = dot_nt(key, query * BF16(HEAD**-0.5))
            mask = kept(start_ref[row, :, cols_at], at, size, first, width)
            scores = jnp.where(mask, scores, -1e9)
            weights = jnp.exp(scores - lse_ref[row, h : h + 1, cols_at])
            dv[keys_at, lanes] += jnp.dot(weights.astype(BF16), grad, preferred_element_type=F32)
            grad_weights = dot_nt(v_ref[keys, lanes], grad)
            inner = jnp.sum(weights * grad_weights, axis=0, keepdims=True)
            grad_scores = (weights * (grad_weights - inner)).astype(BF16)
            dq[cols_at, lanes] = dot_tn(grad_scores, key)
            dk[keys_at, lanes] += jnp.dot(grad_scores, query, preferred_element_type=F32)

        return banded(length, heads, band)

    def turn_back(i):
        base = order[i] * length
        if i == 0:
            fetch.wait()

        @pl.loop(0, blocks)
        def _(j):
            there = pl.ds(pl.multiple_of(base + j * QB, QB), QB)
            here = pl.ds(pl.multiple_of(j * QB, QB), QB)
            cosine, sine = cos_ref[there], sin_ref[there]
            query, key = dq[here] * HEAD**-0.5, dk[here] * HEAD**-0.5
            dqkv[there, :wide] = (query * cosine - swap_halves(query) * sine).astype(BF16)
            dqkv[there, wide : 2 * wide] = (key * cosine - swap_halves(key) * sine).astype(BF16)
            dqkv[there, 2 * wide :] = dv[here].astype(BF16)
            p[there] = dot_nt(dqkv[there], wqkv_ref[...]).astype(BF16)

    def parts(i):
        return (
            [functools.partial(prepare, i)] + banded_back(i) + [functools.partial(turn_back, i)]
        )

    for i in range(n):
        outer_steps = weave(parts(i), outer_steps)
    scat.begin(scat.masks(True))
    pair_core = scat.core_steps(True)
    for i in range(n, 2 * n):
        todo = parts(i)
        beside = [
            functools.partial(run, pair_core[a : a + 1] + outer_steps[a : a + 1])
            for a in range(len(todo))
        ]
        outer_steps, pair_core = outer_steps[len(todo) :], pair_core[len(todo) :]
        weave(todo, beside)
    scat.begin(scat.masks(False))
    gout_ref[...] = gacc[...].astype(BF16)
    inner = inner_plane(grp)
    spread_grad(grp, spread, gout_ref, outgot_ref, 1, (1,) + grp.far)

    def qkv_cols(c):
        @pl.when(c + 1 < width // step)
        def _():
            load_cols(c + 1).start()

        load_cols(c).wait()
        part = pl.ds(pl.multiple_of(c * step, step), step)
        gqkv_ref[part] = dot_tn(cols[c % 2], dqkv[...]).astype(BF16)

    paced(width // step, qkv_cols, pair_core + scat.core_steps(False))
    spread_grad(grp, spread, gqkv_ref, qkvgot_ref, 0, (1,))
    far = spread_grad(grp, spread, gqkv_ref, qkvgot_ref, 0, grp.far, start=False)
    launch(far, inner)
    run(scat.link_steps(True))
    launch(far, jnp.logical_not(inner))
    run(scat.link_steps(False), outer_steps)
    outer.finish()
    whole = outer.block(0)

    def output(part):
        out_ref[part] = (h_ref[part] + whole[part].astype(F32)).astype(BF16)

    tiles(rows, output)
    scat.finish()
    summed = scat.block(0)
    buf[0, 0:1] = jnp.zeros_like(gm_ref)
    buf[0, 1:2] = gm_ref[...]

    def back(part):
        dn, gain_part = norm_back_tile(
            x_ref[part].astype(F32), gain_ref[0:1].astype(F32), summed[part].astype(F32)
        )
        buf[0, 0:1] += gain_part
        tok_ref[part] = (dh_ref[part] + dn).astype(BF16)

    tiles(rows, back)
    sum_gains(grp, buf, gs, gr)
    gains_ref[...] = buf[buf.shape[0] - 1]
    outer.drain()
    scat.drain()
    spread.wait()


def gain_scratch(grp, width):
    n = grp.t_size + grp.z_size - 2
    return [
        pltpu.VMEM((grp.t_size + grp.z_size + 3, 2, width), F32),
        pltpu.SemaphoreType.DMA((n,)),
        pltpu.SemaphoreType.DMA((n,)),
    ]


def sum_gains(grp, buf, send, recv):
    z, t = grp.place()
    at, sem = 0, 0
    for index, size, peer in ((t, grp.t_size, grp.beside), (z, grp.z_size, grp.across)):
        copies = []
        for m in range(1, size):
            c = pltpu.make_async_remote_copy(
                src_ref=buf.at[at],
                dst_ref=buf.at[at + 1 + index],
                send_sem=send.at[sem],
                recv_sem=recv.at[sem],
                device_id=peer(m),
                device_id_type=MESH,
            )
            c.start()
            copies.append(c)
            sem += 1
        buf[at + 1 + index] = buf[at]
        for c in copies:
            c.wait()
        total = buf[at + 1]
        for i in range(1, size):
            total = total + buf[at + 1 + i]
        at += size + 1
        buf[at] = total


def last(
    grp, heads, branch, normed, part, grad_up, query, key, value, attended, lse, cosine, sine, start,
    wqkv, wo, hidden, x, dh, gain, gain_m, cid,
):
    rows, width = x.shape
    total = rows * grp.size
    wide = heads * HEAD
    length = start.shape[2]
    n = len(grp.masks)
    gout, gqkv = sds((wide, width), BF16), sds((width, 3 * wide), BF16)
    return pl.pallas_call(
        functools.partial(last_kernel, grp, heads),
        out_shape=[
            sds((rows, width), BF16),
            sds((rows, width), BF16),
            sds((2, width), F32),
            gout,
            gqkv,
            got_shape(grp, grad_up, 0),
            got_shape(grp, gout, 1),
            got_shape(grp, gqkv, 0),
        ],
        in_specs=[ANY] * 4 + [VMEM] * 5 + [ANY] * 2 + [VMEM, ANY, VMEM] + [ANY] * 3 + [VMEM] * 2,
        out_specs=[VMEM] * 5 + [ANY] * 3,
        scratch_shapes=[
            pltpu.VMEM((total, width), BF16),
            pltpu.VMEM((n, rows, width), BF16),
            pltpu.SemaphoreType.DMA((n,)),
            pltpu.VMEM((2, QB, width), BF16),
            pltpu.SemaphoreType.DMA((2,)),
            pltpu.VMEM((2, total, cols_of(total)), BF16),
            pltpu.SemaphoreType.DMA((2,)),
            pltpu.VMEM((length, wide), BF16),
            pltpu.VMEM((total, 3 * wide), BF16),
            pltpu.VMEM((length, wide), F32),
            pltpu.VMEM((length, wide), F32),
            pltpu.VMEM((length, wide), F32),
            pltpu.VMEM((wide, width), F32),
            pltpu.VMEM((total, wide), F32),
            pltpu.VMEM((total, wide), F32),
            pltpu.VMEM((width, 3 * wide), BF16),
            pltpu.VMEM((rows, width), F32),
            pltpu.VMEM((rows, width), BF16),
            pltpu.VMEM((rows, width), F32),
            pltpu.SemaphoreType.DMA((6,)),
        ]
        + gain_scratch(grp, width)
        + scatter_scratch(grp, rows, width)
        + scatter_scratch(grp, rows, width)
        + spread_sems(grp, 3 * PIECES),
        compiler_params=params(cid),
        name="last",
    )(
        branch, normed, part, grad_up, query, key, value, attended, lse, cosine, sine, start,
        wqkv, wo, hidden, x, dh, gain, gain_m,
    )


def got_shape(grp, grad, axis):
    shape = list(grad.shape)
    shape[axis] //= grp.z_size
    return sds((grp.z_size - 1, *shape), BF16)


def paced(count, body, steps, first=0):
    turns = count - first
    each = -(-len(steps) // turns) if steps else 0

    @pl.loop(0, count)
    def _(i):
        body(i)
        for k in range(turns):
            mine = steps[k * each : (k + 1) * each]
            if mine:

                @pl.when(i == first + k)
                def _(mine=mine):
                    for step in mine:
                        step()


def led(count, body, lists):
    @pl.loop(0, count)
    def _(i):
        for k, steps in enumerate(lists):

            @pl.when(i == k)
            def _(steps=steps):
                run(steps)

        body(i)


def gate_up(normed, wg, wu):
    gate = jnp.dot(normed, wg, preferred_element_type=F32)
    up = jnp.dot(normed, wu, preferred_element_type=F32)
    return (gate * jax.nn.sigmoid(gate) * up).astype(BF16), gate.astype(BF16), up.astype(BF16)


def cols_of(total):
    return max(128, 655360 // total // 128 * 128)


def mlp_kernel(grp, n_early, *refs):
    early, refs = refs[:n_early], refs[n_early:]
    (
        nm_ref,
        dyall_ref,
        wg_in,
        wu_in,
        down_all_ref,
        h_ref,
        dy_ref,
        gain_ref,
        down_ref,
        dh_ref,
        gm_ref,
        gdown_out,
        ggate_out,
        gup_out,
        branch_ref,
        out_ref,
        downgot_ref,
        gategot_ref,
        p,
        wd,
        tile_n,
        tsem,
        act,
        dgu,
        cols,
        csem,
        dsem,
        wg_ref,
        wu_ref,
        gdown_ref,
        ggate_ref,
        gup_ref,
        fsem,
        *rest,
    ) = refs
    scat_refs, rest = rest[:N_SCATTER], rest[N_SCATTER:]
    send, recv, sem, zs, zr = rest
    rows, width = h_ref.shape
    size = 2 * rows
    n = len(grp.masks)
    units = wd.shape[0]
    step = cols.shape[2]

    def at(j):
        return pl.ds(pl.multiple_of(grp.chip_at(j) * size, size), size)

    def load(src, buf, k, j):
        return pltpu.make_async_copy(src.at[at(j)], buf.at[j % 2], tsem.at[k, j % 2])

    def load_cols(src, c):
        part = pl.ds(pl.multiple_of(c * step, step), step)
        return pltpu.make_async_copy(src.at[:, part], cols.at[c % 2], csem.at[c % 2])

    fetch = Fetch(fsem, (wg_in, wg_ref), (wu_in, wu_ref))
    takes = []
    if n_early:
        takes = [
            pltpu.make_async_copy(src, dst, tsem.at[0, i])
            for i, (src, dst) in enumerate(zip(early, (act, dgu)))
        ]
        for c in takes:
            c.start()
    else:
        load(nm_ref, tile_n, 0, 0).start()
    grp.greet()
    spread = Spread(grp, zs, zr)
    spread.to(0, lambda: (down_all_ref, wd))

    def forward(j):
        @pl.when(j + 1 < n)
        def _():
            load(nm_ref, tile_n, 0, j + 1).start()

        load(nm_ref, tile_n, 0, j).wait()
        here = at(j)
        act[here], dgu[here, :units], dgu[here, units:] = gate_up(
            tile_n[j % 2], wg_ref[...], wu_ref[...]
        )

    load_cols(dyall_ref, 0).start()
    if n_early:
        for c in takes:
            c.wait()
    else:
        fetch.wait()
        paced(n, forward, [])
    blocks = width // step

    def down_cols(c):
        @pl.when(c + 1 < blocks)
        def _():
            load_cols(dyall_ref, c + 1).start()

        load_cols(dyall_ref, c).wait()
        part = pl.ds(pl.multiple_of(c * step, step), step)
        gdown_ref[:, part] = dot_tn(act[...], cols[c % 2]).astype(BF16)

    load(dyall_ref, tile_n, 1, 0).start()
    paced(blocks, down_cols, [])
    outs = [pltpu.make_async_copy(gdown_ref, gdown_out, fsem.at[2])]
    outs[0].start()
    if n_early:
        fetch.wait()
    spread.wait()
    spread_grad(grp, spread, gdown_ref, downgot_ref, 1)

    scat = Scatter(grp, p, rows, *scat_refs)
    chunk = min(512, width)

    def backward(j):
        @pl.when(j + 1 < n)
        def _():
            load(dyall_ref, tile_n, 1, j + 1).start()

        load(dyall_ref, tile_n, 1, j).wait()
        here = at(j)
        grad_act = dot_nt(tile_n[j % 2], wd[...])
        gate, up = dgu[here, :units].astype(F32), dgu[here, units:].astype(F32)
        sigma = jax.nn.sigmoid(gate)
        grad_gate = (grad_act * up * (sigma * (1.0 + gate * (1.0 - sigma)))).astype(BF16)
        grad_up = (grad_act * (gate * sigma)).astype(BF16)
        dgu[here, :units] = grad_gate
        dgu[here, units:] = grad_up
        for c in range(0, width, chunk):
            p[here, c : c + chunk] = (
                dot_nt(grad_gate, wg_ref[c : c + chunk]) + dot_nt(grad_up, wu_ref[c : c + chunk])
            ).astype(BF16)
        scat.begin_tile(j)

    core = scat.core_steps(True) + scat.core_steps(False)
    pair_links = scat.link_steps(True)
    todo = []
    late = n // 2
    share = -(-len(pair_links) // max(1, late - 1))
    for j in range(1, n):
        todo.append([core[j - 1]])
        if j > late:
            k = (j - late - 1) * share
            todo[-1] += pair_links[k : k + share]
    done = share * max(0, late - 1)
    paced(n, backward, [functools.partial(run, x) for x in todo], 1)
    rest_steps = [core[n - 1]] + pair_links[done:] + scat.link_steps(False)

    def gate_up_cols(c):
        @pl.when(c + 1 < blocks)
        def _():
            load_cols(nm_ref, c + 1).start()

        load_cols(nm_ref, c).wait()
        part = pl.ds(pl.multiple_of(c * step, step), step)
        grads = dot_tn(cols[c % 2], dgu[...]).astype(BF16)
        ggate_ref[part] = grads[:, :units]
        gup_ref[part] = grads[:, units:]

    load_cols(nm_ref, 0).start()
    paced(blocks, gate_up_cols, rest_steps)
    for i, pair in enumerate(((ggate_ref, ggate_out), (gup_ref, gup_out))):
        outs.append(pltpu.make_async_copy(*pair, fsem.at[3 + i]))
        outs[-1].start()
    dy = scat_refs[0].at[n - 1]
    fetches = [
        pltpu.make_async_copy(dy_ref, dy, dsem.at[0]),
        pltpu.make_async_copy(h_ref, dh_ref, dsem.at[1]),
    ]
    for fetch in fetches:
        fetch.start()
    scat.finish()
    summed = scat.block(0)
    for fetch in fetches:
        fetch.wait()
    gm_ref[...] = jnp.zeros_like(gm_ref)

    def back(part):
        dn, gain_part = norm_back_tile(dh_ref[part], gain_ref[1:2].astype(F32), summed[part].astype(F32))
        gm_ref[...] += gain_part
        dh = dy[part].astype(F32) + dn
        dh_ref[part] = dh
        summed[part] = dh.astype(BF16)

    tiles(rows, back)
    gather = Gather(grp, summed, branch_ref, send, recv, sem)
    steps = gather.begin()
    spread_grad(grp, spread, ggate_ref, gategot_ref, 0, grp.far)
    scat.drain()

    def save(j):
        return pltpu.make_async_copy(tile_n.at[j % 2], out_ref.at[at(j)], tsem.at[0, j % 2])

    def branch(j):
        @pl.when(j > 1)
        def _():
            save(j - 2).wait()

        tile_n[j % 2] = jnp.dot(act[at(j)], wd[...], preferred_element_type=F32).astype(BF16)
        save(j).start()

    near = functools.partial(spread_grad, grp, spread, ggate_ref, gategot_ref, 0, (1,))
    paced(n, branch, steps[:6] + [near] + steps[6:], 1)
    for c in outs:
        c.wait()
    save(n - 2).wait()
    save(n - 1).wait()
    gather.finish()
    spread.wait()


def mlp(grp, early, normed, dy_all, wg, wu, wd, hidden, dy, gain, w_down, cid):
    rows, width = hidden.shape
    total = rows * grp.size
    n = len(grp.masks)
    units = wg.shape[1]
    gdown, ggate = sds((units, width), BF16), sds((width, units), BF16)
    return pl.pallas_call(
        functools.partial(mlp_kernel, grp, len(early)),
        out_shape=[
            sds((rows, width), F32),
            sds((1, width), F32),
            gdown,
            ggate,
            ggate,
            sds((total, width), BF16),
            sds((total, width), BF16),
            got_shape(grp, gdown, 1),
            got_shape(grp, ggate, 0),
        ],
        in_specs=[ANY] * (len(early) + 7) + [VMEM, ANY],
        out_specs=[VMEM] * 2 + [ANY] * 7,
        scratch_shapes=[
            pltpu.VMEM((total, width), BF16),
            pltpu.VMEM((units, width), BF16),
            pltpu.VMEM((2, 2 * rows, width), BF16),
            pltpu.SemaphoreType.DMA((2, 2)),
            pltpu.VMEM((total, units), BF16),
            pltpu.VMEM((total, 2 * units), BF16),
            pltpu.VMEM((2, total, cols_of(total)), BF16),
            pltpu.SemaphoreType.DMA((2,)),
            pltpu.SemaphoreType.DMA((2,)),
            pltpu.VMEM((width, units), BF16),
            pltpu.VMEM((width, units), BF16),
            pltpu.VMEM((units, width), BF16),
            pltpu.VMEM((width, units), BF16),
            pltpu.VMEM((width, units), BF16),
            pltpu.SemaphoreType.DMA((5,)),
        ]
        + scatter_scratch(grp, rows, width)
        + gather_scratch(grp)
        + spread_sems(grp, 4),
        compiler_params=params(cid),
        name="mlp",
    )(*early, normed, dy_all, wg, wu, wd, hidden, dy, gain, w_down)


def fifth_kernel(grp, p_ref, h_ref, gup_ref, out_ref, up_ref, *rest):
    p, psem, rest = rest[0], rest[1], rest[2:]
    scat, rest = rest[:N_SCATTER], rest[N_SCATTER:]
    zs, zr = rest
    pltpu.make_async_copy(p_ref, p, psem).start()
    grp.greet()
    spread = Spread(grp, zs, zr)
    spread_grad(grp, spread, gup_ref, up_ref, 0)
    pltpu.make_async_copy(p_ref, p, psem).wait()
    acc = plain_scatter(grp, p, h_ref.shape[0], scat)

    def finish(rows):
        out_ref[rows] = (h_ref[rows] + acc[rows].astype(F32)).astype(BF16)

    tiles(h_ref.shape[0], finish)
    spread.wait()


def fifth(grp, part, hidden, grad_up, cid):
    rows, width = hidden.shape
    return pl.pallas_call(
        functools.partial(fifth_kernel, grp),
        out_shape=[sds((rows, width), BF16), got_shape(grp, grad_up, 0)],
        in_specs=[ANY, VMEM, ANY],
        out_specs=[VMEM, ANY],
        scratch_shapes=[pltpu.VMEM((rows * grp.size, width), BF16), pltpu.SemaphoreType.DMA]
        + scatter_scratch(grp, rows, width)
        + spread_sems(grp, 1),
        compiler_params=params(cid),
        name="fifth",
    )(part, hidden, grad_up)


def sixth_kernel(
    grp, p_ref, x_ref, dh_ref, gain_ref, gm_ref, gout_ref, gqkv_ref, tok_ref, gains_ref, o_ref, qkv_ref, *rest
):
    p, psem, rest = rest[0], rest[1], rest[2:]
    scat, rest = rest[:N_SCATTER], rest[N_SCATTER:]
    buf, gs, gr, zs, zr = rest
    pltpu.make_async_copy(p_ref, p, psem).start()
    grp.greet(everyone=True)
    spread = Spread(grp, zs, zr)
    spread_grad(grp, spread, gout_ref, o_ref, 1)
    spread_grad(grp, spread, gqkv_ref, qkv_ref, 0)
    pltpu.make_async_copy(p_ref, p, psem).wait()
    acc = plain_scatter(grp, p, x_ref.shape[0], scat)
    buf[0, 0:1] = jnp.zeros_like(gm_ref)
    buf[0, 1:2] = gm_ref[...]

    def back(rows):
        dn, gain_part = norm_back_tile(
            x_ref[rows].astype(F32), gain_ref[0:1].astype(F32), acc[rows].astype(F32)
        )
        buf[0, 0:1] += gain_part
        tok_ref[rows] = (dh_ref[rows] + dn).astype(BF16)

    tiles(x_ref.shape[0], back)
    sum_gains(grp, buf, gs, gr)
    gains_ref[...] = buf[buf.shape[0] - 1]
    spread.wait()


def sixth(grp, part, x, dh, gain, gain_m, grad_out, grad_qkv, cid):
    rows, width = x.shape
    return pl.pallas_call(
        functools.partial(sixth_kernel, grp),
        out_shape=[
            sds((rows, width), BF16),
            sds((2, width), F32),
            got_shape(grp, grad_out, 1),
            got_shape(grp, grad_qkv, 0),
        ],
        in_specs=[ANY, VMEM, VMEM, VMEM, VMEM, ANY, ANY],
        out_specs=[VMEM, VMEM, ANY, ANY],
        scratch_shapes=[pltpu.VMEM((rows * grp.size, width), BF16), pltpu.SemaphoreType.DMA]
        + scatter_scratch(grp, rows, width)
        + gain_scratch(grp, width)
        + spread_sems(grp, 2),
        compiler_params=params(cid),
        name="sixth",
    )(part, x, dh, gain, gain_m, grad_out, grad_qkv)


def swap_halves(value):
    half = HEAD // 2
    width = value.shape[1]
    pieces = []
    for at in range(0, width, HEAD):
        pieces.append(value[:, at + half : at + HEAD])
        pieces.append(value[:, at : at + half])
    if width % 128:
        return jnp.concatenate(pieces, axis=1)
    lane = lax.broadcasted_iota(jnp.int32, value.shape, 1)
    return jnp.where(
        lane % HEAD < half, pltpu.roll(value, width - half, 1), pltpu.roll(value, half, 1)
    )


QB = 256


def bands(length):
    for at in range(0, length, QB):
        first = max(0, at - SAMPLE)
        yield at, min(QB, length - at), first, at + min(QB, length - at) - first


def kept(start_row, at, size, first, width):
    key = first + lax.broadcasted_iota(jnp.int32, (width, size), 0)
    query = at + lax.broadcasted_iota(jnp.int32, (width, size), 1)
    return (key >= start_row) & (key <= query)


def attend_back_kernel(
    heads, q_ref, k_ref, v_ref, do_ref, lse_ref, cos_ref, sin_ref, start_ref, out_ref, dq, dk, dv
):
    wide = heads * HEAD
    length = q_ref.shape[0]
    dk[...] = jnp.zeros_like(dk)
    dv[...] = jnp.zeros_like(dv)
    for h in range(heads):
        lanes = slice(h * HEAD, (h + 1) * HEAD)
        for at, size, first, width in bands(length):
            query = q_ref[at : at + size, lanes]
            key = k_ref[first : first + width, lanes]
            value = v_ref[first : first + width, lanes]
            grad = do_ref[at : at + size, lanes]
            scores = dot_nt(key, query * BF16(HEAD**-0.5))
            mask = kept(start_ref[0, :, at : at + size], at, size, first, width)
            weights = jnp.where(
                mask, jnp.exp(jnp.where(mask, scores, -1e9) - lse_ref[0, h : h + 1, at : at + size]), 0.0
            )
            dv[first : first + width, lanes] += jnp.dot(
                weights.astype(BF16), grad, preferred_element_type=F32
            )
            grad_weights = dot_nt(value, grad)
            inner = jnp.sum(weights * grad_weights, axis=0, keepdims=True)
            grad_scores = (weights * (grad_weights - inner)).astype(BF16)
            dq[at : at + size, lanes] = dot_tn(grad_scores, key)
            dk[first : first + width, lanes] += jnp.dot(
                grad_scores, query, preferred_element_type=F32
            )

    @pl.loop(0, length // QB)
    def _(i):
        rows = pl.ds(pl.multiple_of(i * QB, QB), QB)
        cosine, sine = cos_ref[rows], sin_ref[rows]
        query, key = dq[rows] * HEAD**-0.5, dk[rows] * HEAD**-0.5
        out_ref[rows, :wide] = (query * cosine - swap_halves(query) * sine).astype(BF16)
        out_ref[rows, wide : 2 * wide] = (key * cosine - swap_halves(key) * sine).astype(BF16)
        out_ref[rows, 2 * wide :] = dv[rows].astype(BF16)


def attend_back(query, key, value, grad, lse, cosine, sine, start, heads):
    rows, _, length = start.shape
    wide = heads * HEAD

    def tall(width):
        return pl.BlockSpec((length, width), lambda r: (r, 0))

    return pl.pallas_call(
        functools.partial(attend_back_kernel, heads),
        grid=(rows,),
        out_shape=jax.ShapeDtypeStruct((rows * length, 3 * wide), BF16),
        in_specs=[tall(wide)] * 4
        + [pl.BlockSpec((1, heads, length), lambda r: (r, 0, 0)), tall(wide), tall(wide)]
        + [pl.BlockSpec((1, 1, length), lambda r: (r, 0, 0))],
        out_specs=tall(3 * wide),
        scratch_shapes=[pltpu.VMEM((length, wide), F32)] * 3,
        compiler_params=pltpu.CompilerParams(vmem_limit_bytes=48 << 20),
        name="attend_back",
    )(query, key, value, grad, lse, cosine, sine, start)


def finish_kernel(z_size, parts, z_ref, *refs):
    low = z_ref[0] % 2
    n = len(parts)
    owns, gots, outs = refs[:n], refs[n : 2 * n], list(refs[2 * n :])
    for own, got, (axis, count) in zip(owns, gots, parts):
        sums = [own[...].astype(F32), None]
        for m in range(1, z_size):
            term = got[m - 1].astype(F32)
            sums[m % 2] = term if sums[m % 2] is None else sums[m % 2] + term
        if axis == 0:
            out = outs.pop(0)
            out[low] = sums[0]
            out[1 - low] = sums[1]
            continue
        width = sums[0].shape[1] // count
        for i in range(count):
            out = outs.pop(0)
            for which, total in ((low, sums[0]), (1 - low, sums[1])):
                place = pl.ds(pl.multiple_of(which * width, width), width)
                out[:, place] = total[:, i * width : (i + 1) * width]


def finish(z_size, z, grads, gots, axes):
    steps = 2
    owns, blocks, outs, shapes = [], [], [], []
    for grad, got, (axis, count) in zip(grads, gots, axes):
        rows, cols = got.shape[1] // steps, got.shape[2]
        if axis == 0:
            owns.append(pl.BlockSpec((rows, cols), lambda i, z_ref: (i, z_ref[0])))
            outs.append(pl.BlockSpec((2, rows, cols), lambda i, z_ref: (0, i, 0)))
            shapes.append(sds((2, rows * steps, cols), F32))
        else:
            owns.append(pl.BlockSpec((rows, cols), lambda i, z_ref: (z_ref[0] * steps + i, 0)))
            wide = 2 * cols // count
            outs += [pl.BlockSpec((rows, wide), lambda i, z_ref: (i, 0))] * count
            shapes += [sds((rows * steps, wide), F32)] * count
        blocks.append(pl.BlockSpec((z_size - 1, rows, cols), lambda i, z_ref: (0, i, 0)))
    return pl.pallas_call(
        functools.partial(finish_kernel, z_size, axes),
        out_shape=shapes,
        grid_spec=pltpu.PrefetchScalarGridSpec(
            num_scalar_prefetch=1, grid=(steps,), in_specs=owns + blocks, out_specs=outs
        ),
        compiler_params=pltpu.CompilerParams(vmem_limit_bytes=56 << 20),
        name="finish",
    )(jnp.reshape(z, (1,)), *grads, *gots)


def shards(
    z_size,
    t_size,
    tokens,
    gain_attn,
    gain_mlp,
    w_query,
    w_key,
    w_value,
    w_out,
    w_gate,
    w_up,
    w_down,
    segment_ids,
    out_grad,
):
    grp = Group(z_size, t_size)
    z = lax.axis_index("fsdp")
    low = z % 2

    def deliver(grad, got, half_axis, axis, parts=1):
        size = grad.shape[axis] // z_size
        sums = [lax.dynamic_slice_in_dim(grad, z * size, size, axis).astype(F32), None]
        for m in range(1, z_size):
            term = got[m - 1].astype(F32)
            sums[m % 2] = term if sums[m % 2] is None else sums[m % 2] + term
        outs = []
        piece = sums[0].shape[half_axis] // parts
        for i in range(parts):
            a, b = (lax.slice_in_dim(s, i * piece, (i + 1) * piece, axis=half_axis) for s in sums)
            outs.append(
                jnp.where(
                    low == 0,
                    jnp.concatenate([a, b], axis=half_axis),
                    jnp.concatenate([b, a], axis=half_axis),
                )
            )
        return outs

    wide = w_query.shape[1] // 2
    heads = wide // HEAD

    gains_in = jnp.stack([gain_attn, gain_mlp])
    normed_a, wqkv, wo, start, cosine, sine = first(
        grp, low, tokens, gains_in, w_query, w_key, w_value, w_out, segment_ids, 0
    )
    query, key, value, attended, lse, hidden, normed_m, grad_all, wg, wu, wd, *early = middle(
        grp,
        heads,
        normed_a,
        wqkv,
        wo,
        cosine,
        sine,
        start,
        out_grad,
        tokens,
        gains_in,
        w_gate,
        w_up,
        w_down,
        1,
    )
    grad_hidden, gain_m_part, grad_down, grad_wg, grad_wu, branch_all, out_part, got_down, got_gate = mlp(
        grp, early, normed_m, grad_all, wg, wu, wd, hidden, out_grad, gains_in, w_down, 3
    )
    if grp.size <= 16:
        output, tokens_grad, gains, grad_wout, grad_wqkv, got_up, got_out, got_qkv = last(
            grp, heads, branch_all, normed_a, out_part, grad_wu, query, key, value, attended, lse,
            cosine, sine, start, wqkv, wo, hidden, tokens, grad_hidden, gains_in, gain_m_part, 4,
        )
    else:
        output, got_up = fifth(grp, out_part, hidden, grad_wu, 4)
        grad_wout = dot_tn(attended, branch_all).astype(BF16)
        grad_attended = dot_nt(branch_all, wo).astype(BF16)
        grad_qkv = attend_back(query, key, value, grad_attended, lse, cosine, sine, start, heads)
        grad_wqkv = dot_tn(normed_a, grad_qkv).astype(BF16)
        grad_na = dot_nt(grad_qkv, wqkv).astype(BF16)
        tokens_grad, gains, got_out, got_qkv = sixth(
            grp, grad_na, tokens, grad_hidden, gains_in, gain_m_part, grad_wout, grad_wqkv, 5
        )
    grads = (grad_down, grad_wg, grad_wu, grad_wout, grad_wqkv)
    gots = (got_down, got_gate, got_up, got_out, got_qkv)
    axes = ((0, 1), (1, 1), (1, 1), (0, 1), (1, 3))
    if wide % LANES == 0:
        outs = finish(z_size, z, grads, gots, axes)
        down_out, out_out = (x.reshape(-1, x.shape[2]) for x in (outs[0], outs[3]))
        gate_out, up_out = outs[1:3]
        query_out, key_out, value_out = outs[4:]
    else:
        (down_out,) = deliver(grad_down, got_down, 0, 1)
        (gate_out,) = deliver(grad_wg, got_gate, 1, 0)
        (up_out,) = deliver(grad_wu, got_up, 1, 0)
        (out_out,) = deliver(grad_wout, got_out, 0, 1)
        query_out, key_out, value_out = deliver(grad_wqkv, got_qkv, 1, 0, 3)
    return (
        output,
        tokens_grad,
        gains[0],
        gains[1],
        query_out,
        key_out,
        value_out,
        out_out,
        gate_out,
        up_out,
        down_out,
    )


def solution(mesh):
    return jax.shard_map(
        functools.partial(shards, mesh.shape["fsdp"], mesh.shape["tensor"]),
        mesh=mesh,
        in_specs=(
            P(("fsdp", "tensor"), None),
            P(),
            P(),
            P("fsdp", "tensor"),
            P("fsdp", "tensor"),
            P("fsdp", "tensor"),
            P("tensor", "fsdp"),
            P("fsdp", "tensor"),
            P("fsdp", "tensor"),
            P("tensor", "fsdp"),
            P("fsdp", None),
            P(("fsdp", "tensor"), None),
        ),
        out_specs=(
            P(("fsdp", "tensor"), None),
            P(("fsdp", "tensor"), None),
            P(),
            P(),
            P("fsdp", "tensor"),
            P("fsdp", "tensor"),
            P("fsdp", "tensor"),
            P("tensor", "fsdp"),
            P("fsdp", "tensor"),
            P("fsdp", "tensor"),
            P("tensor", "fsdp"),
        ),
        check_vma=False,
    )
```
